256 devices in a mesh: geo: 8 (over x, core), spec: 32 (over z, y).
Axes of the slice: x: 4, y: 4, z: 8, core: 2. Of those that a mesh axis runs over, the one named last changes fastest.
Arguments:
- spectrum: float32 [32, 36, 256, 512], P('spec', None, 'geo'), may hold values from 0.01 to 50, as said below
- land_sea: int32 [256, 512], P('geo'), may hold values from 0 to 1, as said below
- sea_index: int32 [8, 12288], P('geo'), may hold values from 0 to 16383, as said below
- sea_count: int32 [8], P('geo'), may hold values from 4096 to 12288, as said below
- wind_speed: float32 [256, 512], P('geo'), may hold values from 4 to 24
- wind_dir: float32 [256, 512], P('geo'), may hold values from -3.140625 to 3.140625
- slope_x: float32 [256, 512], P('geo'), may hold values from -0.5 to 0.5
- slope_y: float32 [256, 512], P('geo'), may hold values from -0.5 to 0.5
Outputs:
- next_spectrum: float32 [32, 36, 256, 512], P('spec', None, 'geo')
The draws below stay inside these ranges and needn't reach their ends.
Inputs may be any that keep to these rules, and one draw needn't show every extreme that they name: `spectrum`: A positive energy density. `land_sea`: land comes in aligned 8 x 8 blocks of cells. `sea_index`: row t lists the sea cells of tile t in increasing position, then its land cells in increasing position, all distinct; its first sea_count[t] entries are exactly the tile's sea cells. `sea_count`: the number of sea cells of each tile; at least one tile has exactly 12288.
All inputs are finite; a program needn't handle non-finite values.
Results may differ from the reference program's by a relative error of at most 0.0003.
Values sent between devices are 32-bit elements; how exact they have to be, the bound alone decides.
A program may use at most 64 MiB of HBM per device.

```python
import math
import jax
import jax.numpy as jnp
from jax import lax

NK = 32
NTH = 36
ROWS = 32
NY = 512
TILES = 8
NX = 256
CAP = 12288


def log_uniform(key, shape, low, high):
    return jnp.exp(jax.random.uniform(key, shape, jnp.float32, jnp.log(low), jnp.log(high)))


def draw_spectrum(key, part):
    base = jax.random.fold_in(key, 11)
    key_freq, key_dirs, key_rough = jax.random.split(base, 3)
    freq_scale = log_uniform(key_freq, (NK, 1, 1, 1), 0.3, 3.0)
    dir_scale = log_uniform(key_dirs, (1, NTH, 1, 1), 0.5, 2.0)
    rough = log_uniform(key_rough, (NK, NTH, NX, NY), 0.5, 2.0)
    return freq_scale * dir_scale * rough


def land_layout(key):
    base = jax.random.fold_in(key, 7)
    key_lands, key_full, key_order = jax.random.split(base, 3)
    block_rows = ROWS // 8
    block_cols = NY // 8
    block_count = block_rows * block_cols
    fewest = block_count // 4
    most_land = 3 * block_count // 4
    land_counts = jax.random.randint(key_lands, (TILES,), fewest, most_land + 1)
    full_tile = jax.random.randint(key_full, (), 0, TILES)
    land_counts = jnp.where(jnp.arange(TILES) == full_tile, fewest, land_counts)
    orders = jax.vmap(lambda one_key: jax.random.permutation(one_key, block_count))(jax.random.split(key_order, TILES))
    block_ranks = jnp.argsort(orders, axis=1, stable=True)
    land_blocks = (block_ranks < land_counts[:, None]).astype(jnp.int32).reshape(TILES, block_rows, block_cols)
    sea_tiles = 1 - jnp.repeat(jnp.repeat(land_blocks, 8, axis=1), 8, axis=2)
    flat_sea = sea_tiles.reshape(TILES, ROWS * NY)
    order_keys = (1 - flat_sea) * (ROWS * NY) + jnp.arange(ROWS * NY, dtype=jnp.int32)[None, :]
    listing = jnp.argsort(order_keys, axis=1, stable=True)[:, :CAP].astype(jnp.int32)
    counts = jnp.sum(flat_sea, axis=1).astype(jnp.int32)
    return (sea_tiles.reshape(TILES * ROWS, NY).astype(jnp.int32), listing, counts)


def draw_land_sea(key, part):
    return land_layout(key)[0]


def draw_sea_index(key, part):
    return land_layout(key)[1]


def draw_sea_count(key, part):
    return land_layout(key)[2]


def block_scale(rng, extent, cuts, low, largest):
    loudness, own = 1.0, jax.random.fold_in(rng, 6)
    for position, blocks in cuts:
        heights = jnp.exp(jax.random.uniform(jax.random.fold_in(own, position), (blocks,), jnp.float32, low / len(cuts), largest / len(cuts)))
        loudness = loudness * jnp.repeat(heights, extent[position] // blocks).reshape([-1 if axis == position else 1 for axis in range(len(extent))])
    return loudness


def setup_inputs(seed: int = 0) -> dict:
    seeds = jax.random.split(jax.random.key(seed), 9)
    spectrum = draw_spectrum(jax.random.fold_in(seeds[8], 71), 0)
    land_sea = draw_land_sea(jax.random.fold_in(seeds[8], 71), 0)
    sea_index = draw_sea_index(jax.random.fold_in(seeds[8], 71), 0)
    sea_count = draw_sea_count(jax.random.fold_in(seeds[8], 71), 0)
    wind_speed = jnp.clip(4.0 + 20.0 * jax.random.uniform(seeds[4], (NX, NY), jnp.float32) ** block_scale(seeds[4], (NX, NY), ((0, 8),), -0.2, 0.2), 4.0, 24.0)
    wind_dir = jnp.clip(jax.random.uniform(seeds[5], (NX, NY), jnp.float32, -3.140625, 3.140625), -3.140625, 3.140625)
    slope_x = jnp.clip(jax.random.uniform(seeds[6], (NX, NY), jnp.float32, -0.5, 0.5) * block_scale(seeds[6], (NX, NY), ((0, 8),), -0.4, 0.0), -0.5, 0.5)
    slope_y = jnp.clip(jax.random.uniform(seeds[7], (NX, NY), jnp.float32, -0.5, 0.5) * block_scale(seeds[7], (NX, NY), ((0, 8),), -0.4, 0.0), -0.5, 0.5)
    return {"spectrum": spectrum, "land_sea": land_sea, "sea_index": sea_index, "sea_count": sea_count, "wind_speed": wind_speed, "wind_dir": wind_dir, "slope_x": slope_x, "slope_y": slope_y}


GRAVITY = 9.81
BASE_FREQ = 0.035
GROWTH = 1.1
COURANT_TOP = 0.9
TURN_TOP = 1.2
SPACING = 0.1
USTAR_RATIO = 0.035
WIND_COEF = 0.0375
WHITECAP = 0.36
STEEP_REF = 1.6
EPSILON = 1e-06
QUAD_COEF = 100.0

def band_table(band_ids):
    growth_factor = jnp.power(GROWTH, band_ids)
    radian_freq = 2.0 * math.pi * BASE_FREQ * growth_factor
    wavenum = radian_freq * radian_freq / GRAVITY
    return (radian_freq, wavenum, COURANT_TOP / growth_factor, TURN_TOP / growth_factor, SPACING * radian_freq)

def quick_flux(far_left, near_left, near_right, far_right, courant):
    forward = courant >= 0
    upwind = jnp.where(forward, far_left, far_right)
    center = jnp.where(forward, near_left, near_right)
    downwind = jnp.where(forward, near_right, near_left)
    face_value = 0.5 * (center + downwind) - 0.5 * jnp.abs(courant) * (downwind - center) - (1.0 - courant * courant) / 6.0 * (downwind - 2.0 * center + upwind)
    return courant * face_value

def advect(padded, courant, along):
    face_count = padded.shape[along] - 4
    shifted = [lax.slice_in_dim(padded, offset, offset + face_count + 1, axis=along) for offset in range(4)]
    face_flux = quick_flux(shifted[0], shifted[1], shifted[2], shifted[3], courant)
    centre_cells = lax.slice_in_dim(padded, 2, 2 + face_count, axis=along)
    upper_flux = lax.slice_in_dim(face_flux, 1, face_count + 1, axis=along)
    lower_flux = lax.slice_in_dim(face_flux, 0, face_count, axis=along)
    return centre_cells - (upper_flux - lower_flux)

def quad_delta(center, above, below, energy, dir_axis):
    plus = jnp.roll(above, -1, axis=dir_axis)
    minus = jnp.roll(below, 3, axis=dir_axis)
    return QUAD_COEF * (center * center * (plus + minus) - 2.0 * center * plus * minus) / (energy * energy)

def quad_term(delta, delta_above, delta_below, dir_axis):
    return -2.0 * delta + jnp.roll(delta_below, 1, axis=dir_axis) + jnp.roll(delta_above, -3, axis=dir_axis)

def sources(density, energy_sum, first_sum, root_sum, radian_freq, wavenum, cosine, wind_speed):
    energy = energy_sum + EPSILON
    mean_sigma = energy / (first_sum + EPSILON)
    ratio_k = energy / (root_sum + EPSILON)
    mean_k = ratio_k * ratio_k
    steepness = energy * mean_k * mean_k / STEEP_REF
    decay_rate = WHITECAP * mean_sigma * (wavenum / mean_k) * steepness * steepness
    growth_rate = WIND_COEF * radian_freq * jnp.maximum(28.0 * USTAR_RATIO * wind_speed * radian_freq / GRAVITY * cosine - 1.0, 0.0)
    return density * (1.0 + growth_rate) / (1.0 + decay_rate)

def reference(spectrum, land_sea, sea_index, sea_count, wind_speed, wind_dir, slope_x, slope_y):
    wet_mask = land_sea.astype(jnp.float32)
    dtheta = 2.0 * math.pi / NTH
    angles = (jnp.arange(NTH).astype(jnp.float32) + 0.5) * dtheta
    face_angles = jnp.arange(NTH + 1).astype(jnp.float32) * dtheta
    cosine = jnp.cos(angles[:, None, None] - wind_dir[None])

    def propagate(member):
        density, band = member
        radian_freq, wavenum, courant, turn_rate, band_spread = band_table(band)
        density = density * wet_mask
        padded = jnp.pad(density, ((0, 0), (2, 2), (0, 0)))
        density = advect(padded, courant * jnp.cos(angles)[:, None, None], 1) * wet_mask
        padded = jnp.pad(density, ((0, 0), (0, 0), (2, 2)))
        density = advect(padded, courant * jnp.sin(angles)[:, None, None], 2) * wet_mask
        turning = turn_rate * (jnp.sin(face_angles)[:, None, None] * slope_x - jnp.cos(face_angles)[:, None, None] * slope_y)
        padded = jnp.concatenate([density[-2:], density, density[:2]], axis=0)
        floored = jnp.maximum(advect(padded, turning, 0), 0.0)
        scaled = floored * (band_spread * dtheta)
        return (floored, lax.optimization_barrier(jnp.sum(scaled, axis=0)), lax.optimization_barrier(jnp.sum(scaled / radian_freq, axis=0)), lax.optimization_barrier(jnp.sum(scaled / jnp.sqrt(wavenum), axis=0)))
    band_ids = jnp.arange(NK).astype(jnp.float32)
    band_slots = jnp.arange(NK).astype(jnp.int32)
    floored, energy_part, first_part, root_part = lax.map(propagate, (spectrum, band_ids))
    energy_sum = lax.optimization_barrier(jnp.sum(energy_part, axis=0))
    first_sum = lax.optimization_barrier(jnp.sum(first_part, axis=0))
    root_sum = lax.optimization_barrier(jnp.sum(root_part, axis=0))
    energy = energy_sum + EPSILON
    zero_band = jnp.zeros((1,) + floored.shape[1:], jnp.float32)
    padded_bands = jnp.concatenate([zero_band, floored, zero_band], axis=0)

    def pairing(index):
        return quad_delta(padded_bands[index + 1], padded_bands[index + 2], padded_bands[index], energy, 0)
    delta = lax.map(pairing, band_slots)
    padded_delta = jnp.concatenate([zero_band, delta, zero_band], axis=0)

    def update(member):
        density, band, index = member
        radian_freq, wavenum, courant, turn_rate, band_spread = band_table(band)
        extra = quad_term(padded_delta[index + 1], padded_delta[index + 2], padded_delta[index], 0)
        return sources(density, energy_sum, first_sum, root_sum, radian_freq, wavenum, cosine, wind_speed) + extra
    updated = lax.map(update, (floored, band_ids, band_slots))
    tile_ids = jnp.arange(TILES).astype(jnp.int32)[:, None]
    global_cells = (tile_ids * (ROWS * NY) + sea_index.astype(jnp.int32)).reshape(-1)
    live_slots = (jnp.arange(CAP).astype(jnp.int32)[None, :] < sea_count[:, None]).astype(jnp.float32).reshape(-1)
    active = jnp.zeros((NX * NY,), jnp.float32).at[global_cells].max(live_slots).reshape(NX, NY)
    return updated * active[None, None]
```

```python
import math

import jax
import jax.numpy as jnp
from jax import lax
from jax.sharding import PartitionSpec as P

GRAVITY = 9.81
BASE_FREQ = 0.035
GROWTH = 1.1
COURANT_TOP = 0.9
TURN_TOP = 1.2
SPACING = 0.1
USTAR_RATIO = 0.035
WIND_COEF = 0.0375
WHITECAP = 0.36
STEEP_REF = 1.6
EPSILON = 1e-06
QUAD_COEF = 100.0


def extended(cells, sides, width):
    for axis, dim in sides:
        count = lax.axis_size(axis)
        ends = count - 1
        head = lax.slice_in_dim(cells, 0, width, axis=dim)
        tail = lax.slice_in_dim(cells, cells.shape[dim] - width, cells.shape[dim], axis=dim)
        cells = jnp.concatenate(
            [
                lax.ppermute(tail, axis, [(i, (i + 1) % count) for i in range(ends)]),
                cells,
                lax.ppermute(head, axis, [((i + 1) % count, i) for i in range(ends)]),
            ],
            axis=dim,
        )
    return cells


def band_table(band_ids):
    growth_factor = jnp.power(GROWTH, band_ids)
    radian_freq = 2.0 * math.pi * BASE_FREQ * growth_factor
    wavenum = radian_freq * radian_freq / GRAVITY
    return (
        radian_freq,
        wavenum,
        COURANT_TOP / growth_factor,
        TURN_TOP / growth_factor,
        SPACING * radian_freq,
    )


def quick_flux(far_left, near_left, near_right, far_right, courant):
    forward = courant >= 0
    upwind = jnp.where(forward, far_left, far_right)
    center = jnp.where(forward, near_left, near_right)
    downwind = jnp.where(forward, near_right, near_left)
    face_value = (
        0.5 * (center + downwind)
        - 0.5 * jnp.abs(courant) * (downwind - center)
        - (1.0 - courant * courant) / 6.0 * (downwind - 2.0 * center + upwind)
    )
    return courant * face_value


def advect(padded, courant, along):
    face_count = padded.shape[along] - 4
    shifted = [
        lax.slice_in_dim(padded, offset, offset + face_count + 1, axis=along) for offset in range(4)
    ]
    face_flux = quick_flux(shifted[0], shifted[1], shifted[2], shifted[3], courant)
    centre_cells = lax.slice_in_dim(padded, 2, 2 + face_count, axis=along)
    upper_flux = lax.slice_in_dim(face_flux, 1, face_count + 1, axis=along)
    lower_flux = lax.slice_in_dim(face_flux, 0, face_count, axis=along)
    return centre_cells - (upper_flux - lower_flux)


def quad_delta(center, above, below, energy, dir_axis):
    plus = jnp.roll(above, -1, axis=dir_axis)
    minus = jnp.roll(below, 3, axis=dir_axis)
    return (
        QUAD_COEF
        * (center * center * (plus + minus) - 2.0 * center * plus * minus)
        / (energy * energy)
    )


def quad_term(delta, delta_above, delta_below, dir_axis):
    return (
        -2.0 * delta
        + jnp.roll(delta_below, 1, axis=dir_axis)
        + jnp.roll(delta_above, -3, axis=dir_axis)
    )


def band_neighbours(values):
    empty = jnp.zeros((1,) + values.shape[1:], jnp.float32)
    return (
        jnp.concatenate([values[1:], empty], axis=0),
        jnp.concatenate([empty, values[:-1]], axis=0),
    )


def sources(density, energy_sum, first_sum, root_sum, radian_freq, wavenum, cosine, wind_speed):
    energy = energy_sum + EPSILON
    mean_sigma = energy / (first_sum + EPSILON)
    ratio_k = energy / (root_sum + EPSILON)
    mean_k = ratio_k * ratio_k
    steepness = energy * mean_k * mean_k / STEEP_REF
    decay_rate = WHITECAP * mean_sigma * (wavenum / mean_k) * steepness * steepness
    growth_rate = (
        WIND_COEF
        * radian_freq
        * jnp.maximum(28.0 * USTAR_RATIO * wind_speed * radian_freq / GRAVITY * cosine - 1.0, 0.0)
    )
    return density * (1.0 + growth_rate) / (1.0 + decay_rate)


def local_sources(point_block, wind_block, wind_angle, angles, dtheta):
    band_total = point_block.shape[0]
    band_ids = jnp.arange(band_total).astype(jnp.float32)
    radian_freq, wavenum, courant, turn_rate, band_spread = band_table(band_ids)
    scaled = point_block * (band_spread * dtheta)[:, None, None]
    energy_sum = jnp.sum(scaled, axis=(0, 1))
    first_sum = jnp.sum(scaled / radian_freq[:, None, None], axis=(0, 1))
    root_sum = jnp.sum(scaled / jnp.sqrt(wavenum)[:, None, None], axis=(0, 1))
    energy = energy_sum + EPSILON
    above, below = band_neighbours(point_block)
    delta = quad_delta(point_block, above, below, energy, 1)
    delta_above, delta_below = band_neighbours(delta)
    extra = quad_term(delta, delta_above, delta_below, 1)
    cosine = jnp.cos(angles[:, None] - wind_angle[None, :])
    return (
        sources(
            point_block,
            energy_sum,
            first_sum,
            root_sum,
            radian_freq[:, None, None],
            wavenum[:, None, None],
            cosine,
            wind_block,
        )
        + extra
    )


Y_GROUP = 4


def shards(spectrum, land_sea, sea_index, sea_count, wind_speed, wind_dir, slope_x, slope_y):
    local_bands, dir_count, row_count, col_count = spectrum.shape
    z_count = lax.axis_size("z")
    y_count = lax.axis_size("y")
    z_pos = lax.axis_index("z")
    y_pos = lax.axis_index("y")
    spec_pos = z_pos * y_count + y_pos
    dtheta = 2.0 * math.pi / dir_count
    angles = (jnp.arange(dir_count).astype(jnp.float32) + 0.5) * dtheta
    face_angles = jnp.arange(dir_count + 1).astype(jnp.float32) * dtheta
    band_ids = (spec_pos * local_bands + jnp.arange(local_bands)).astype(jnp.float32)
    radian_freq, wavenum, courant, turn_rate, band_spread = band_table(band_ids)
    wet_mask = land_sea.astype(jnp.float32)
    density = spectrum * wet_mask
    padded = extended(density, (("geo", 2),), 2)
    density = (
        advect(padded, (courant[:, None] * jnp.cos(angles)[None, :])[:, :, None, None], 2)
        * wet_mask
    )
    padded = jnp.pad(density, ((0, 0), (0, 0), (0, 0), (2, 2)))
    density = (
        advect(padded, (courant[:, None] * jnp.sin(angles)[None, :])[:, :, None, None], 3)
        * wet_mask
    )
    turning = turn_rate[:, None, None, None] * (
        jnp.sin(face_angles)[None, :, None, None] * slope_x
        - jnp.cos(face_angles)[None, :, None, None] * slope_y
    )
    padded = jnp.concatenate([density[:, -2:], density, density[:, :2]], axis=1)
    floored = jnp.maximum(advect(padded, turning, 1), 0.0)
    point = lax.all_to_all(floored, "y", split_axis=2, concat_axis=0, tiled=True)
    group = point.shape[0]
    part_rows = point.shape[2]
    lower = lax.ppermute(point[group - 2 :], "z", [(i, i + 1) for i in range(z_count - 1)])
    upper = lax.ppermute(point[:2], "z", [(i + 1, i) for i in range(z_count - 1)])
    group_ids = (z_pos * group + jnp.arange(group)).astype(jnp.float32)
    radian_freq, wavenum, courant, turn_rate, band_spread = band_table(group_ids)
    scaled = point * (band_spread * dtheta)[:, None, None, None]
    sums = jnp.stack(
        [
            jnp.sum(scaled, axis=(0, 1)),
            jnp.sum(scaled / radian_freq[:, None, None, None], axis=(0, 1)),
            jnp.sum(scaled / jnp.sqrt(wavenum)[:, None, None, None], axis=(0, 1)),
        ]
    )
    sums = lax.psum(sums, "z")
    energy_sum, first_sum, root_sum = sums[0], sums[1], sums[2]
    energy = energy_sum + EPSILON
    ext = jnp.concatenate([lower, point, upper], axis=0)
    delta = quad_delta(ext[1:-1], ext[2:], ext[:-2], energy, 1)
    extra = (
        -2.0 * delta[1:-1]
        + jnp.roll(delta[:-2], 1, axis=1)
        + jnp.roll(delta[2:], -3, axis=1)
    )
    row_start = y_pos * part_rows
    wind_block = lax.dynamic_slice_in_dim(wind_speed, row_start, part_rows, axis=0)
    wind_angle = lax.dynamic_slice_in_dim(wind_dir, row_start, part_rows, axis=0)
    wet_block = lax.dynamic_slice_in_dim(wet_mask, row_start, part_rows, axis=0)
    cosine = jnp.cos(angles[:, None, None] - wind_angle[None])
    updated = (
        sources(
            point,
            energy_sum,
            first_sum,
            root_sum,
            radian_freq[:, None, None, None],
            wavenum[:, None, None, None],
            cosine,
            wind_block,
        )
        + extra
    ) * wet_block
    return lax.all_to_all(updated, "y", split_axis=0, concat_axis=2, tiled=True)


def solution(mesh):
    geo_count = mesh.shape["geo"]
    spec_count = mesh.shape["spec"]
    local = jax.sharding.Mesh(
        mesh.devices.reshape(geo_count, spec_count // Y_GROUP, Y_GROUP), ("geo", "z", "y")
    )
    spec = ("z", "y")
    placed = (
        P(spec, None, "geo", None),
        P("geo", None),
        P("geo", None),
        P("geo"),
        P("geo", None),
        P("geo", None),
        P("geo", None),
        P("geo", None),
    )
    return jax.shard_map(
        shards, mesh=local, in_specs=placed, out_specs=P(spec, None, "geo", None), check_vma=False
    )
```

```python
import math

import jax
import jax.numpy as jnp
from jax import lax
from jax.sharding import PartitionSpec as P

GRAVITY = 9.81
BASE_FREQ = 0.035
GROWTH = 1.1
COURANT_TOP = 0.9
TURN_TOP = 1.2
SPACING = 0.1
USTAR_RATIO = 0.035
WIND_COEF = 0.0375
WHITECAP = 0.36
STEEP_REF = 1.6
EPSILON = 1e-06
QUAD_COEF = 100.0


def extended(cells, sides, width):
    for axis, dim in sides:
        count = lax.axis_size(axis)
        ends = count - 1
        head = lax.slice_in_dim(cells, 0, width, axis=dim)
        tail = lax.slice_in_dim(cells, cells.shape[dim] - width, cells.shape[dim], axis=dim)
        cells = jnp.concatenate(
            [
                lax.ppermute(tail, axis, [(i, (i + 1) % count) for i in range(ends)]),
                cells,
                lax.ppermute(head, axis, [((i + 1) % count, i) for i in range(ends)]),
            ],
            axis=dim,
        )
    return cells


def band_table(band_ids):
    growth_factor = jnp.power(GROWTH, band_ids)
    radian_freq = 2.0 * math.pi * BASE_FREQ * growth_factor
    wavenum = radian_freq * radian_freq / GRAVITY
    return (
        radian_freq,
        wavenum,
        COURANT_TOP / growth_factor,
        TURN_TOP / growth_factor,
        SPACING * radian_freq,
    )


def quick_flux(far_left, near_left, near_right, far_right, courant):
    forward = courant >= 0
    upwind = jnp.where(forward, far_left, far_right)
    center = jnp.where(forward, near_left, near_right)
    downwind = jnp.where(forward, near_right, near_left)
    face_value = (
        0.5 * (center + downwind)
        - 0.5 * jnp.abs(courant) * (downwind - center)
        - (1.0 - courant * courant) / 6.0 * (downwind - 2.0 * center + upwind)
    )
    return courant * face_value


def advect(padded, courant, along):
    face_count = padded.shape[along] - 4
    shifted = [
        lax.slice_in_dim(padded, offset, offset + face_count + 1, axis=along) for offset in range(4)
    ]
    face_flux = quick_flux(shifted[0], shifted[1], shifted[2], shifted[3], courant)
    centre_cells = lax.slice_in_dim(padded, 2, 2 + face_count, axis=along)
    upper_flux = lax.slice_in_dim(face_flux, 1, face_count + 1, axis=along)
    lower_flux = lax.slice_in_dim(face_flux, 0, face_count, axis=along)
    return centre_cells - (upper_flux - lower_flux)


def quad_delta(center, above, below, energy, dir_axis):
    plus = jnp.roll(above, -1, axis=dir_axis)
    minus = jnp.roll(below, 3, axis=dir_axis)
    return (
        QUAD_COEF
        * (center * center * (plus + minus) - 2.0 * center * plus * minus)
        / (energy * energy)
    )


def quad_term(delta, delta_above, delta_below, dir_axis):
    return (
        -2.0 * delta
        + jnp.roll(delta_below, 1, axis=dir_axis)
        + jnp.roll(delta_above, -3, axis=dir_axis)
    )


def band_neighbours(values):
    empty = jnp.zeros((1,) + values.shape[1:], jnp.float32)
    return (
        jnp.concatenate([values[1:], empty], axis=0),
        jnp.concatenate([empty, values[:-1]], axis=0),
    )


def sources(density, energy_sum, first_sum, root_sum, radian_freq, wavenum, cosine, wind_speed):
    energy = energy_sum + EPSILON
    mean_sigma = energy / (first_sum + EPSILON)
    ratio_k = energy / (root_sum + EPSILON)
    mean_k = ratio_k * ratio_k
    steepness = energy * mean_k * mean_k / STEEP_REF
    decay_rate = WHITECAP * mean_sigma * (wavenum / mean_k) * steepness * steepness
    growth_rate = (
        WIND_COEF
        * radian_freq
        * jnp.maximum(28.0 * USTAR_RATIO * wind_speed * radian_freq / GRAVITY * cosine - 1.0, 0.0)
    )
    return density * (1.0 + growth_rate) / (1.0 + decay_rate)


def local_sources(point_block, wind_block, wind_angle, angles, dtheta):
    band_total = point_block.shape[0]
    band_ids = jnp.arange(band_total).astype(jnp.float32)
    radian_freq, wavenum, courant, turn_rate, band_spread = band_table(band_ids)
    scaled = point_block * (band_spread * dtheta)[:, None, None]
    energy_sum = jnp.sum(scaled, axis=(0, 1))
    first_sum = jnp.sum(scaled / radian_freq[:, None, None], axis=(0, 1))
    root_sum = jnp.sum(scaled / jnp.sqrt(wavenum)[:, None, None], axis=(0, 1))
    energy = energy_sum + EPSILON
    above, below = band_neighbours(point_block)
    delta = quad_delta(point_block, above, below, energy, 1)
    delta_above, delta_below = band_neighbours(delta)
    extra = quad_term(delta, delta_above, delta_below, 1)
    cosine = jnp.cos(angles[:, None] - wind_angle[None, :])
    return (
        sources(
            point_block,
            energy_sum,
            first_sum,
            root_sum,
            radian_freq[:, None, None],
            wavenum[:, None, None],
            cosine,
            wind_block,
        )
        + extra
    )


Y_GROUP = 4


def shards(spectrum, land_sea, sea_index, sea_count, wind_speed, wind_dir, slope_x, slope_y):
    local_bands, dir_count, row_count, col_count = spectrum.shape
    z_count = lax.axis_size("z")
    y_count = lax.axis_size("y")
    z_pos = lax.axis_index("z")
    y_pos = lax.axis_index("y")
    spec_pos = z_pos * y_count + y_pos
    dtheta = 2.0 * math.pi / dir_count
    angles = (jnp.arange(dir_count).astype(jnp.float32) + 0.5) * dtheta
    face_angles = jnp.arange(dir_count + 1).astype(jnp.float32) * dtheta
    band_ids = (spec_pos * local_bands + jnp.arange(local_bands)).astype(jnp.float32)
    radian_freq, wavenum, courant, turn_rate, band_spread = band_table(band_ids)
    wet_mask = land_sea.astype(jnp.float32)
    density = spectrum * wet_mask
    padded = extended(density, (("geo", 2),), 2)
    density = (
        advect(padded, (courant[:, None] * jnp.cos(angles)[None, :])[:, :, None, None], 2)
        * wet_mask
    )
    padded = jnp.pad(density, ((0, 0), (0, 0), (0, 0), (2, 2)))
    density = (
        advect(padded, (courant[:, None] * jnp.sin(angles)[None, :])[:, :, None, None], 3)
        * wet_mask
    )
    turning = turn_rate[:, None, None, None] * (
        jnp.sin(face_angles)[None, :, None, None] * slope_x
        - jnp.cos(face_angles)[None, :, None, None] * slope_y
    )
    padded = jnp.concatenate([density[:, -2:], density, density[:, :2]], axis=1)
    floored = jnp.maximum(advect(padded, turning, 1), 0.0)
    point = lax.all_to_all(floored, "y", split_axis=2, concat_axis=0, tiled=True)
    group = point.shape[0]
    part_rows = point.shape[2]
    lower = lax.ppermute(point[group - 2 :], "z", [(i, i + 1) for i in range(z_count - 1)])
    upper = lax.ppermute(point[:2], "z", [(i + 1, i) for i in range(z_count - 1)])
    group_ids = (z_pos * group + jnp.arange(group)).astype(jnp.float32)
    radian_freq, wavenum, courant, turn_rate, band_spread = band_table(group_ids)
    scaled = point * (band_spread * dtheta)[:, None, None, None]
    sums = jnp.stack(
        [
            jnp.sum(scaled, axis=(0, 1)),
            jnp.sum(scaled / radian_freq[:, None, None, None], axis=(0, 1)),
            jnp.sum(scaled / jnp.sqrt(wavenum)[:, None, None, None], axis=(0, 1)),
        ]
    )
    sums = jnp.sum(lax.all_gather(sums, "z"), axis=0)
    energy_sum, first_sum, root_sum = sums[0], sums[1], sums[2]
    energy = energy_sum + EPSILON
    ext = jnp.concatenate([lower, point, upper], axis=0)
    center, plus, minus = ext[1:-1], jnp.roll(ext[2:], -1, axis=1), jnp.roll(ext[:-2], 3, axis=1)
    cubic = center * center * (plus + minus) - 2.0 * center * plus * minus
    extra = (
        -2.0 * cubic[1:-1] + jnp.roll(cubic[:-2], 1, axis=1) + jnp.roll(cubic[2:], -3, axis=1)
    ) * (QUAD_COEF / (energy * energy))
    row_start = y_pos * part_rows
    wind_block = lax.dynamic_slice_in_dim(wind_speed, row_start, part_rows, axis=0)
    wind_angle = lax.dynamic_slice_in_dim(wind_dir, row_start, part_rows, axis=0)
    wet_block = lax.dynamic_slice_in_dim(wet_mask, row_start, part_rows, axis=0)
    cosine = jnp.cos(angles[:, None, None] - wind_angle[None])
    updated = (
        sources(
            point,
            energy_sum,
            first_sum,
            root_sum,
            radian_freq[:, None, None, None],
            wavenum[:, None, None, None],
            cosine,
            wind_block,
        )
        + extra
    ) * wet_block
    return lax.all_to_all(updated, "y", split_axis=0, concat_axis=2, tiled=True)


def solution(mesh):
    geo_count = mesh.shape["geo"]
    spec_count = mesh.shape["spec"]
    local = jax.sharding.Mesh(
        mesh.devices.reshape(geo_count, spec_count // Y_GROUP, Y_GROUP), ("geo", "z", "y")
    )
    spec = ("z", "y")
    placed = (
        P(spec, None, "geo", None),
        P("geo", None),
        P("geo", None),
        P("geo"),
        P("geo", None),
        P("geo", None),
        P("geo", None),
        P("geo", None),
    )
    return jax.shard_map(
        shards, mesh=local, in_specs=placed, out_specs=P(spec, None, "geo", None), check_vma=False
    )
```

```python
import math

import jax
import jax.numpy as jnp
from jax import lax
from jax.sharding import PartitionSpec as P

GRAVITY = 9.81
BASE_FREQ = 0.035
GROWTH = 1.1
COURANT_TOP = 0.9
TURN_TOP = 1.2
SPACING = 0.1
USTAR_RATIO = 0.035
WIND_COEF = 0.0375
WHITECAP = 0.36
STEEP_REF = 1.6
EPSILON = 1e-06
QUAD_COEF = 100.0


def extended(cells, sides, width):
    for axis, dim in sides:
        count = lax.axis_size(axis)
        ends = count - 1
        head = lax.slice_in_dim(cells, 0, width, axis=dim)
        tail = lax.slice_in_dim(cells, cells.shape[dim] - width, cells.shape[dim], axis=dim)
        cells = jnp.concatenate(
            [
                lax.ppermute(tail, axis, [(i, (i + 1) % count) for i in range(ends)]),
                cells,
                lax.ppermute(head, axis, [((i + 1) % count, i) for i in range(ends)]),
            ],
            axis=dim,
        )
    return cells


def band_table(band_ids):
    growth_factor = jnp.power(GROWTH, band_ids)
    radian_freq = 2.0 * math.pi * BASE_FREQ * growth_factor
    wavenum = radian_freq * radian_freq / GRAVITY
    return (
        radian_freq,
        wavenum,
        COURANT_TOP / growth_factor,
        TURN_TOP / growth_factor,
        SPACING * radian_freq,
    )


def quick_flux(far_left, near_left, near_right, far_right, courant):
    forward = courant >= 0
    upwind = jnp.where(forward, far_left, far_right)
    center = jnp.where(forward, near_left, near_right)
    downwind = jnp.where(forward, near_right, near_left)
    face_value = (
        0.5 * (center + downwind)
        - 0.5 * jnp.abs(courant) * (downwind - center)
        - (1.0 - courant * courant) / 6.0 * (downwind - 2.0 * center + upwind)
    )
    return courant * face_value


def advect(padded, courant, along):
    face_count = padded.shape[along] - 4
    shifted = [
        lax.slice_in_dim(padded, offset, offset + face_count + 1, axis=along) for offset in range(4)
    ]
    face_flux = quick_flux(shifted[0], shifted[1], shifted[2], shifted[3], courant)
    centre_cells = lax.slice_in_dim(padded, 2, 2 + face_count, axis=along)
    upper_flux = lax.slice_in_dim(face_flux, 1, face_count + 1, axis=along)
    lower_flux = lax.slice_in_dim(face_flux, 0, face_count, axis=along)
    return centre_cells - (upper_flux - lower_flux)


def quad_delta(center, above, below, energy, dir_axis):
    plus = jnp.roll(above, -1, axis=dir_axis)
    minus = jnp.roll(below, 3, axis=dir_axis)
    return (
        QUAD_COEF
        * (center * center * (plus + minus) - 2.0 * center * plus * minus)
        / (energy * energy)
    )


def quad_term(delta, delta_above, delta_below, dir_axis):
    return (
        -2.0 * delta
        + jnp.roll(delta_below, 1, axis=dir_axis)
        + jnp.roll(delta_above, -3, axis=dir_axis)
    )


def band_neighbours(values):
    empty = jnp.zeros((1,) + values.shape[1:], jnp.float32)
    return (
        jnp.concatenate([values[1:], empty], axis=0),
        jnp.concatenate([empty, values[:-1]], axis=0),
    )


def sources(density, energy_sum, first_sum, root_sum, radian_freq, wavenum, cosine, wind_speed):
    energy = energy_sum + EPSILON
    mean_sigma = energy / (first_sum + EPSILON)
    ratio_k = energy / (root_sum + EPSILON)
    mean_k = ratio_k * ratio_k
    steepness = energy * mean_k * mean_k / STEEP_REF
    decay_rate = WHITECAP * mean_sigma * (wavenum / mean_k) * steepness * steepness
    growth_rate = (
        WIND_COEF
        * radian_freq
        * jnp.maximum(28.0 * USTAR_RATIO * wind_speed * radian_freq / GRAVITY * cosine - 1.0, 0.0)
    )
    return density * (1.0 + growth_rate) / (1.0 + decay_rate)


def local_sources(point_block, wind_block, wind_angle, angles, dtheta):
    band_total = point_block.shape[0]
    band_ids = jnp.arange(band_total).astype(jnp.float32)
    radian_freq, wavenum, courant, turn_rate, band_spread = band_table(band_ids)
    scaled = point_block * (band_spread * dtheta)[:, None, None]
    energy_sum = jnp.sum(scaled, axis=(0, 1))
    first_sum = jnp.sum(scaled / radian_freq[:, None, None], axis=(0, 1))
    root_sum = jnp.sum(scaled / jnp.sqrt(wavenum)[:, None, None], axis=(0, 1))
    energy = energy_sum + EPSILON
    above, below = band_neighbours(point_block)
    delta = quad_delta(point_block, above, below, energy, 1)
    delta_above, delta_below = band_neighbours(delta)
    extra = quad_term(delta, delta_above, delta_below, 1)
    cosine = jnp.cos(angles[:, None] - wind_angle[None, :])
    return (
        sources(
            point_block,
            energy_sum,
            first_sum,
            root_sum,
            radian_freq[:, None, None],
            wavenum[:, None, None],
            cosine,
            wind_block,
        )
        + extra
    )


Y_GROUP = 4


def shards(spectrum, land_sea, sea_index, sea_count, wind_speed, wind_dir, slope_x, slope_y):
    local_bands, dir_count, row_count, col_count = spectrum.shape
    z_count = lax.axis_size("z")
    y_count = lax.axis_size("y")
    z_pos = lax.axis_index("z")
    y_pos = lax.axis_index("y")
    spec_pos = z_pos * y_count + y_pos
    dtheta = 2.0 * math.pi / dir_count
    angles = (jnp.arange(dir_count).astype(jnp.float32) + 0.5) * dtheta
    face_angles = jnp.arange(dir_count + 1).astype(jnp.float32) * dtheta
    band_ids = (spec_pos * local_bands + jnp.arange(local_bands)).astype(jnp.float32)
    radian_freq, wavenum, courant, turn_rate, band_spread = band_table(band_ids)
    wet_mask = land_sea.astype(jnp.float32)
    density = spectrum * wet_mask
    padded = extended(density, (("geo", 2),), 2)
    density = (
        advect(padded, (courant[:, None] * jnp.cos(angles)[None, :])[:, :, None, None], 2)
        * wet_mask
    )
    padded = jnp.pad(density, ((0, 0), (0, 0), (0, 0), (2, 2)))
    density = (
        advect(padded, (courant[:, None] * jnp.sin(angles)[None, :])[:, :, None, None], 3)
        * wet_mask
    )
    turning = turn_rate[:, None, None, None] * (
        jnp.sin(face_angles)[None, :, None, None] * slope_x
        - jnp.cos(face_angles)[None, :, None, None] * slope_y
    )
    padded = jnp.concatenate([density[:, -2:], density, density[:, :2]], axis=1)
    floored = jnp.maximum(advect(padded, turning, 1), 0.0)
    point = lax.all_to_all(floored, "y", split_axis=2, concat_axis=0, tiled=True)
    group = point.shape[0]
    part_rows = point.shape[2]
    lower = lax.ppermute(point[group - 2 :], "z", [(i, i + 1) for i in range(z_count - 1)])
    upper = lax.ppermute(point[:2], "z", [(i + 1, i) for i in range(z_count - 1)])
    group_ids = (z_pos * group + jnp.arange(group)).astype(jnp.float32)
    radian_freq, wavenum, courant, turn_rate, band_spread = band_table(group_ids)
    scaled = point * (band_spread * dtheta)[:, None, None, None]
    sums = jnp.stack(
        [
            jnp.sum(scaled, axis=(0, 1)),
            jnp.sum(scaled / radian_freq[:, None, None, None], axis=(0, 1)),
            jnp.sum(scaled / jnp.sqrt(wavenum)[:, None, None, None], axis=(0, 1)),
        ]
    )
    step = 1
    while step < z_count:
        sums = sums + lax.ppermute(sums, "z", [(i, i ^ step) for i in range(z_count)])
        step *= 2
    energy_sum, first_sum, root_sum = sums[0], sums[1], sums[2]
    energy = energy_sum + EPSILON
    ext = jnp.concatenate([lower, point, upper], axis=0)
    center, plus, minus = ext[1:-1], jnp.roll(ext[2:], -1, axis=1), jnp.roll(ext[:-2], 3, axis=1)
    cubic = center * center * (plus + minus) - 2.0 * center * plus * minus
    extra = (
        -2.0 * cubic[1:-1] + jnp.roll(cubic[:-2], 1, axis=1) + jnp.roll(cubic[2:], -3, axis=1)
    ) * (QUAD_COEF / (energy * energy))
    row_start = y_pos * part_rows
    wind_block = lax.dynamic_slice_in_dim(wind_speed, row_start, part_rows, axis=0)
    wind_angle = lax.dynamic_slice_in_dim(wind_dir, row_start, part_rows, axis=0)
    wet_block = lax.dynamic_slice_in_dim(wet_mask, row_start, part_rows, axis=0)
    cosine = jnp.cos(angles[:, None, None] - wind_angle[None])
    updated = (
        sources(
            point,
            energy_sum,
            first_sum,
            root_sum,
            radian_freq[:, None, None, None],
            wavenum[:, None, None, None],
            cosine,
            wind_block,
        )
        + extra
    ) * wet_block
    return lax.all_to_all(updated, "y", split_axis=0, concat_axis=2, tiled=True)


def solution(mesh):
    geo_count = mesh.shape["geo"]
    spec_count = mesh.shape["spec"]
    local = jax.sharding.Mesh(
        mesh.devices.reshape(geo_count, spec_count // Y_GROUP, Y_GROUP), ("geo", "z", "y")
    )
    spec = ("z", "y")
    placed = (
        P(spec, None, "geo", None),
        P("geo", None),
        P("geo", None),
        P("geo"),
        P("geo", None),
        P("geo", None),
        P("geo", None),
        P("geo", None),
    )
    return jax.shard_map(
        shards, mesh=local, in_specs=placed, out_specs=P(spec, None, "geo", None), check_vma=False
    )
```

```python
import math

import jax
import jax.numpy as jnp
from jax import lax
from jax.sharding import PartitionSpec as P

GRAVITY = 9.81
BASE_FREQ = 0.035
GROWTH = 1.1
COURANT_TOP = 0.9
TURN_TOP = 1.2
SPACING = 0.1
USTAR_RATIO = 0.035
WIND_COEF = 0.0375
WHITECAP = 0.36
STEEP_REF = 1.6
EPSILON = 1e-06
QUAD_COEF = 100.0


def extended(cells, sides, width):
    for axis, dim in sides:
        count = lax.axis_size(axis)
        ends = count - 1
        head = lax.slice_in_dim(cells, 0, width, axis=dim)
        tail = lax.slice_in_dim(cells, cells.shape[dim] - width, cells.shape[dim], axis=dim)
        cells = jnp.concatenate(
            [
                lax.ppermute(tail, axis, [(i, (i + 1) % count) for i in range(ends)]),
                cells,
                lax.ppermute(head, axis, [((i + 1) % count, i) for i in range(ends)]),
            ],
            axis=dim,
        )
    return cells


def band_table(band_ids):
    growth_factor = jnp.power(GROWTH, band_ids)
    radian_freq = 2.0 * math.pi * BASE_FREQ * growth_factor
    wavenum = radian_freq * radian_freq / GRAVITY
    return (
        radian_freq,
        wavenum,
        COURANT_TOP / growth_factor,
        TURN_TOP / growth_factor,
        SPACING * radian_freq,
    )


def quick_flux(far_left, near_left, near_right, far_right, courant):
    forward = courant >= 0
    upwind = jnp.where(forward, far_left, far_right)
    center = jnp.where(forward, near_left, near_right)
    downwind = jnp.where(forward, near_right, near_left)
    face_value = (
        0.5 * (center + downwind)
        - 0.5 * jnp.abs(courant) * (downwind - center)
        - (1.0 - courant * courant) / 6.0 * (downwind - 2.0 * center + upwind)
    )
    return courant * face_value


def advect(padded, courant, along):
    face_count = padded.shape[along] - 4
    shifted = [
        lax.slice_in_dim(padded, offset, offset + face_count + 1, axis=along) for offset in range(4)
    ]
    face_flux = quick_flux(shifted[0], shifted[1], shifted[2], shifted[3], courant)
    centre_cells = lax.slice_in_dim(padded, 2, 2 + face_count, axis=along)
    upper_flux = lax.slice_in_dim(face_flux, 1, face_count + 1, axis=along)
    lower_flux = lax.slice_in_dim(face_flux, 0, face_count, axis=along)
    return centre_cells - (upper_flux - lower_flux)


def quad_delta(center, above, below, energy, dir_axis):
    plus = jnp.roll(above, -1, axis=dir_axis)
    minus = jnp.roll(below, 3, axis=dir_axis)
    return (
        QUAD_COEF
        * (center * center * (plus + minus) - 2.0 * center * plus * minus)
        / (energy * energy)
    )


def quad_term(delta, delta_above, delta_below, dir_axis):
    return (
        -2.0 * delta
        + jnp.roll(delta_below, 1, axis=dir_axis)
        + jnp.roll(delta_above, -3, axis=dir_axis)
    )


def band_neighbours(values):
    empty = jnp.zeros((1,) + values.shape[1:], jnp.float32)
    return (
        jnp.concatenate([values[1:], empty], axis=0),
        jnp.concatenate([empty, values[:-1]], axis=0),
    )


def sources(density, energy_sum, first_sum, root_sum, radian_freq, wavenum, cosine, wind_speed):
    energy = energy_sum + EPSILON
    mean_sigma = energy / (first_sum + EPSILON)
    ratio_k = energy / (root_sum + EPSILON)
    mean_k = ratio_k * ratio_k
    steepness = energy * mean_k * mean_k / STEEP_REF
    decay_rate = WHITECAP * mean_sigma * (wavenum / mean_k) * steepness * steepness
    growth_rate = (
        WIND_COEF
        * radian_freq
        * jnp.maximum(28.0 * USTAR_RATIO * wind_speed * radian_freq / GRAVITY * cosine - 1.0, 0.0)
    )
    return density * (1.0 + growth_rate) / (1.0 + decay_rate)


def local_sources(point_block, wind_block, wind_angle, angles, dtheta):
    band_total = point_block.shape[0]
    band_ids = jnp.arange(band_total).astype(jnp.float32)
    radian_freq, wavenum, courant, turn_rate, band_spread = band_table(band_ids)
    scaled = point_block * (band_spread * dtheta)[:, None, None]
    energy_sum = jnp.sum(scaled, axis=(0, 1))
    first_sum = jnp.sum(scaled / radian_freq[:, None, None], axis=(0, 1))
    root_sum = jnp.sum(scaled / jnp.sqrt(wavenum)[:, None, None], axis=(0, 1))
    energy = energy_sum + EPSILON
    above, below = band_neighbours(point_block)
    delta = quad_delta(point_block, above, below, energy, 1)
    delta_above, delta_below = band_neighbours(delta)
    extra = quad_term(delta, delta_above, delta_below, 1)
    cosine = jnp.cos(angles[:, None] - wind_angle[None, :])
    return (
        sources(
            point_block,
            energy_sum,
            first_sum,
            root_sum,
            radian_freq[:, None, None],
            wavenum[:, None, None],
            cosine,
            wind_block,
        )
        + extra
    )


Y_GROUP = 4
COLUMN_CHUNKS = 2


def shards(spectrum, land_sea, sea_index, sea_count, wind_speed, wind_dir, slope_x, slope_y):
    local_bands, dir_count, row_count, col_count = spectrum.shape
    z_count = lax.axis_size("z")
    y_count = lax.axis_size("y")
    z_pos = lax.axis_index("z")
    y_pos = lax.axis_index("y")
    spec_pos = z_pos * y_count + y_pos
    dtheta = 2.0 * math.pi / dir_count
    angles = (jnp.arange(dir_count).astype(jnp.float32) + 0.5) * dtheta
    face_angles = jnp.arange(dir_count + 1).astype(jnp.float32) * dtheta
    band_ids = (spec_pos * local_bands + jnp.arange(local_bands)).astype(jnp.float32)
    radian_freq, wavenum, courant, turn_rate, band_spread = band_table(band_ids)
    wet_mask = land_sea.astype(jnp.float32)
    density = spectrum * wet_mask
    padded = extended(density, (("geo", 2),), 2)
    density = (
        advect(padded, (courant[:, None] * jnp.cos(angles)[None, :])[:, :, None, None], 2)
        * wet_mask
    )
    padded = jnp.pad(density, ((0, 0), (0, 0), (0, 0), (2, 2)))
    density = (
        advect(padded, (courant[:, None] * jnp.sin(angles)[None, :])[:, :, None, None], 3)
        * wet_mask
    )
    turning = turn_rate[:, None, None, None] * (
        jnp.sin(face_angles)[None, :, None, None] * slope_x
        - jnp.cos(face_angles)[None, :, None, None] * slope_y
    )
    padded = jnp.concatenate([density[:, -2:], density, density[:, :2]], axis=1)
    floored = jnp.maximum(advect(padded, turning, 1), 0.0)
    chunk_width = col_count // COLUMN_CHUNKS
    pieces = []
    for chunk in range(COLUMN_CHUNKS):
        columns = slice(chunk * chunk_width, (chunk + 1) * chunk_width)
        pieces.append(
            source_chunk(
                floored[..., columns],
                wind_speed[:, columns],
                wind_dir[:, columns],
                wet_mask[:, columns],
                angles,
                dtheta,
            )
        )
    return jnp.concatenate(pieces, axis=3)


def source_chunk(floored, wind_speed, wind_dir, wet_mask, angles, dtheta):
    z_count = lax.axis_size("z")
    z_pos = lax.axis_index("z")
    y_pos = lax.axis_index("y")
    point = lax.all_to_all(floored, "y", split_axis=2, concat_axis=0, tiled=True)
    group = point.shape[0]
    part_rows = point.shape[2]
    lower = lax.ppermute(point[group - 2 :], "z", [(i, i + 1) for i in range(z_count - 1)])
    upper = lax.ppermute(point[:2], "z", [(i + 1, i) for i in range(z_count - 1)])
    group_ids = (z_pos * group + jnp.arange(group)).astype(jnp.float32)
    radian_freq, wavenum, courant, turn_rate, band_spread = band_table(group_ids)
    scaled = point * (band_spread * dtheta)[:, None, None, None]
    sums = jnp.stack(
        [
            jnp.sum(scaled, axis=(0, 1)),
            jnp.sum(scaled / radian_freq[:, None, None, None], axis=(0, 1)),
            jnp.sum(scaled / jnp.sqrt(wavenum)[:, None, None, None], axis=(0, 1)),
        ]
    )
    step = 1
    while step < z_count:
        sums = sums + lax.ppermute(sums, "z", [(i, i ^ step) for i in range(z_count)])
        step *= 2
    energy_sum, first_sum, root_sum = sums[0], sums[1], sums[2]
    energy = energy_sum + EPSILON
    ext = jnp.concatenate([lower, point, upper], axis=0)
    center, plus, minus = ext[1:-1], jnp.roll(ext[2:], -1, axis=1), jnp.roll(ext[:-2], 3, axis=1)
    cubic = center * center * (plus + minus) - 2.0 * center * plus * minus
    extra = (
        -2.0 * cubic[1:-1] + jnp.roll(cubic[:-2], 1, axis=1) + jnp.roll(cubic[2:], -3, axis=1)
    ) * (QUAD_COEF / (energy * energy))
    row_start = y_pos * part_rows
    wind_block = lax.dynamic_slice_in_dim(wind_speed, row_start, part_rows, axis=0)
    wind_angle = lax.dynamic_slice_in_dim(wind_dir, row_start, part_rows, axis=0)
    wet_block = lax.dynamic_slice_in_dim(wet_mask, row_start, part_rows, axis=0)
    cosine = jnp.cos(angles[:, None, None] - wind_angle[None])
    updated = (
        sources(
            point,
            energy_sum,
            first_sum,
            root_sum,
            radian_freq[:, None, None, None],
            wavenum[:, None, None, None],
            cosine,
            wind_block,
        )
        + extra
    ) * wet_block
    return lax.all_to_all(updated, "y", split_axis=0, concat_axis=2, tiled=True)


def solution(mesh):
    geo_count = mesh.shape["geo"]
    spec_count = mesh.shape["spec"]
    local = jax.sharding.Mesh(
        mesh.devices.reshape(geo_count, spec_count // Y_GROUP, Y_GROUP), ("geo", "z", "y")
    )
    spec = ("z", "y")
    placed = (
        P(spec, None, "geo", None),
        P("geo", None),
        P("geo", None),
        P("geo"),
        P("geo", None),
        P("geo", None),
        P("geo", None),
        P("geo", None),
    )
    return jax.shard_map(
        shards, mesh=local, in_specs=placed, out_specs=P(spec, None, "geo", None), check_vma=False
    )
```

```python
import functools
import math

import jax
import jax.numpy as jnp
from jax import lax
from jax.experimental import pallas as pl
from jax.experimental.pallas import tpu as pltpu
from jax.sharding import PartitionSpec as P

GRAVITY = 9.81
BASE_FREQ = 0.035
GROWTH = 1.1
COURANT_TOP = 0.9
TURN_TOP = 1.2
SPACING = 0.1
USTAR_RATIO = 0.035
WIND_COEF = 0.0375
WHITECAP = 0.36
STEEP_REF = 1.6
EPSILON = 1e-06
QUAD_COEF = 100.0


def extended(cells, sides, width):
    for axis, dim in sides:
        count = lax.axis_size(axis)
        ends = count - 1
        head = lax.slice_in_dim(cells, 0, width, axis=dim)
        tail = lax.slice_in_dim(cells, cells.shape[dim] - width, cells.shape[dim], axis=dim)
        cells = jnp.concatenate(
            [
                lax.ppermute(tail, axis, [(i, (i + 1) % count) for i in range(ends)]),
                cells,
                lax.ppermute(head, axis, [((i + 1) % count, i) for i in range(ends)]),
            ],
            axis=dim,
        )
    return cells


def band_table(band_ids):
    growth_factor = jnp.power(GROWTH, band_ids)
    radian_freq = 2.0 * math.pi * BASE_FREQ * growth_factor
    wavenum = radian_freq * radian_freq / GRAVITY
    return (
        radian_freq,
        wavenum,
        COURANT_TOP / growth_factor,
        TURN_TOP / growth_factor,
        SPACING * radian_freq,
    )


def quick_flux(far_left, near_left, near_right, far_right, courant):
    forward = courant >= 0
    upwind = jnp.where(forward, far_left, far_right)
    center = jnp.where(forward, near_left, near_right)
    downwind = jnp.where(forward, near_right, near_left)
    face_value = (
        0.5 * (center + downwind)
        - 0.5 * jnp.abs(courant) * (downwind - center)
        - (1.0 - courant * courant) / 6.0 * (downwind - 2.0 * center + upwind)
    )
    return courant * face_value


def advect(padded, courant, along):
    face_count = padded.shape[along] - 4
    shifted = [
        lax.slice_in_dim(padded, offset, offset + face_count + 1, axis=along) for offset in range(4)
    ]
    face_flux = quick_flux(shifted[0], shifted[1], shifted[2], shifted[3], courant)
    centre_cells = lax.slice_in_dim(padded, 2, 2 + face_count, axis=along)
    upper_flux = lax.slice_in_dim(face_flux, 1, face_count + 1, axis=along)
    lower_flux = lax.slice_in_dim(face_flux, 0, face_count, axis=along)
    return centre_cells - (upper_flux - lower_flux)


def quad_delta(center, above, below, energy, dir_axis):
    plus = jnp.roll(above, -1, axis=dir_axis)
    minus = jnp.roll(below, 3, axis=dir_axis)
    return (
        QUAD_COEF
        * (center * center * (plus + minus) - 2.0 * center * plus * minus)
        / (energy * energy)
    )


def quad_term(delta, delta_above, delta_below, dir_axis):
    return (
        -2.0 * delta
        + jnp.roll(delta_below, 1, axis=dir_axis)
        + jnp.roll(delta_above, -3, axis=dir_axis)
    )


def band_neighbours(values):
    empty = jnp.zeros((1,) + values.shape[1:], jnp.float32)
    return (
        jnp.concatenate([values[1:], empty], axis=0),
        jnp.concatenate([empty, values[:-1]], axis=0),
    )


def sources(density, energy_sum, first_sum, root_sum, radian_freq, wavenum, cosine, wind_speed):
    energy = energy_sum + EPSILON
    mean_sigma = energy / (first_sum + EPSILON)
    ratio_k = energy / (root_sum + EPSILON)
    mean_k = ratio_k * ratio_k
    steepness = energy * mean_k * mean_k / STEEP_REF
    decay_rate = WHITECAP * mean_sigma * (wavenum / mean_k) * steepness * steepness
    growth_rate = (
        WIND_COEF
        * radian_freq
        * jnp.maximum(28.0 * USTAR_RATIO * wind_speed * radian_freq / GRAVITY * cosine - 1.0, 0.0)
    )
    return density * (1.0 + growth_rate) / (1.0 + decay_rate)


def local_sources(point_block, wind_block, wind_angle, angles, dtheta):
    band_total = point_block.shape[0]
    band_ids = jnp.arange(band_total).astype(jnp.float32)
    radian_freq, wavenum, courant, turn_rate, band_spread = band_table(band_ids)
    scaled = point_block * (band_spread * dtheta)[:, None, None]
    energy_sum = jnp.sum(scaled, axis=(0, 1))
    first_sum = jnp.sum(scaled / radian_freq[:, None, None], axis=(0, 1))
    root_sum = jnp.sum(scaled / jnp.sqrt(wavenum)[:, None, None], axis=(0, 1))
    energy = energy_sum + EPSILON
    above, below = band_neighbours(point_block)
    delta = quad_delta(point_block, above, below, energy, 1)
    delta_above, delta_below = band_neighbours(delta)
    extra = quad_term(delta, delta_above, delta_below, 1)
    cosine = jnp.cos(angles[:, None] - wind_angle[None, :])
    return (
        sources(
            point_block,
            energy_sum,
            first_sum,
            root_sum,
            radian_freq[:, None, None],
            wavenum[:, None, None],
            cosine,
            wind_block,
        )
        + extra
    )


Y_GROUP = 4


def _z_exchange_kernel(z_count, point_ref, part_ref, lower_ref, upper_ref, gathered_ref,
                       halo_send, halo_recv, gather_send, gather_recv):
    geo = lax.axis_index("geo")
    z_pos = lax.axis_index("z")
    y_pos = lax.axis_index("y")
    group = point_ref.shape[0]
    barrier = pltpu.get_barrier_semaphore()
    for offset in range(1, z_count):
        target = lax.rem(z_pos + offset, z_count)
        pl.semaphore_signal(barrier, inc=1, device_id=(geo, target, y_pos),
                            device_id_type=pl.DeviceIdType.MESH)
    pl.semaphore_wait(barrier, z_count - 1)

    def halo_copy(src_lo, dst_ref, slot, target):
        return pltpu.make_async_remote_copy(
            src_ref=point_ref.at[pl.ds(src_lo, 2)],
            dst_ref=dst_ref,
            send_sem=halo_send.at[slot],
            recv_sem=halo_recv.at[slot],
            device_id=(geo, target, y_pos),
            device_id_type=pl.DeviceIdType.MESH,
        )

    up = halo_copy(group - 2, lower_ref, 0, z_pos + 1)
    down = halo_copy(0, upper_ref, 1, z_pos - 1)

    @pl.when(z_pos < z_count - 1)
    def _():
        up.start()

    @pl.when(z_pos > 0)
    def _():
        down.start()

    copies = []
    for offset in range(1, z_count):
        target = lax.rem(z_pos + offset, z_count)
        copy = pltpu.make_async_remote_copy(
            src_ref=part_ref,
            dst_ref=gathered_ref.at[z_pos],
            send_sem=gather_send.at[offset],
            recv_sem=gather_recv.at[offset],
            device_id=(geo, target, y_pos),
            device_id_type=pl.DeviceIdType.MESH,
        )
        copy.start()
        copies.append(copy)
    gathered_ref[z_pos] = part_ref[...]

    @pl.when(z_pos == 0)
    def _():
        lower_ref[...] = jnp.zeros(lower_ref.shape, lower_ref.dtype)

    @pl.when(z_pos == z_count - 1)
    def _():
        upper_ref[...] = jnp.zeros(upper_ref.shape, upper_ref.dtype)

    for copy in copies:
        copy.wait_send()
        copy.wait_recv()

    @pl.when(z_pos < z_count - 1)
    def _():
        up.wait_send()
        down.wait_recv()

    @pl.when(z_pos > 0)
    def _():
        down.wait_send()
        up.wait_recv()


def z_exchange(point, part, z_count):
    group, dirs, rows, cols = point.shape
    halo = jax.ShapeDtypeStruct((2, dirs, rows, cols), point.dtype)
    vmem = pl.BlockSpec(memory_space=pltpu.VMEM)
    return pl.pallas_call(
        functools.partial(_z_exchange_kernel, z_count),
        out_shape=(halo, halo, jax.ShapeDtypeStruct((z_count,) + part.shape, part.dtype)),
        in_specs=[vmem, vmem],
        out_specs=(vmem, vmem, vmem),
        scratch_shapes=[
            pltpu.SemaphoreType.DMA((2,)),
            pltpu.SemaphoreType.DMA((2,)),
            pltpu.SemaphoreType.DMA((z_count,)),
            pltpu.SemaphoreType.DMA((z_count,)),
        ],
        compiler_params=pltpu.CompilerParams(collective_id=0, has_side_effects=True),
    )(point, part)


def shards(spectrum, land_sea, sea_index, sea_count, wind_speed, wind_dir, slope_x, slope_y):
    local_bands, dir_count, row_count, col_count = spectrum.shape
    z_count = lax.axis_size("z")
    y_count = lax.axis_size("y")
    z_pos = lax.axis_index("z")
    y_pos = lax.axis_index("y")
    spec_pos = z_pos * y_count + y_pos
    dtheta = 2.0 * math.pi / dir_count
    angles = (jnp.arange(dir_count).astype(jnp.float32) + 0.5) * dtheta
    face_angles = jnp.arange(dir_count + 1).astype(jnp.float32) * dtheta
    band_ids = (spec_pos * local_bands + jnp.arange(local_bands)).astype(jnp.float32)
    radian_freq, wavenum, courant, turn_rate, band_spread = band_table(band_ids)
    wet_mask = land_sea.astype(jnp.float32)
    density = spectrum * wet_mask
    padded = extended(density, (("geo", 2),), 2)
    density = (
        advect(padded, (courant[:, None] * jnp.cos(angles)[None, :])[:, :, None, None], 2)
        * wet_mask
    )
    padded = jnp.pad(density, ((0, 0), (0, 0), (0, 0), (2, 2)))
    density = (
        advect(padded, (courant[:, None] * jnp.sin(angles)[None, :])[:, :, None, None], 3)
        * wet_mask
    )
    turning = turn_rate[:, None, None, None] * (
        jnp.sin(face_angles)[None, :, None, None] * slope_x
        - jnp.cos(face_angles)[None, :, None, None] * slope_y
    )
    padded = jnp.concatenate([density[:, -2:], density, density[:, :2]], axis=1)
    floored = jnp.maximum(advect(padded, turning, 1), 0.0)
    point = lax.all_to_all(floored, "y", split_axis=2, concat_axis=0, tiled=True)
    group = point.shape[0]
    part_rows = point.shape[2]
    group_ids = (z_pos * group + jnp.arange(group)).astype(jnp.float32)
    radian_freq, wavenum, courant, turn_rate, band_spread = band_table(group_ids)
    scaled = point * (band_spread * dtheta)[:, None, None, None]
    sums = jnp.stack(
        [
            jnp.sum(scaled, axis=(0, 1)),
            jnp.sum(scaled / radian_freq[:, None, None, None], axis=(0, 1)),
            jnp.sum(scaled / jnp.sqrt(wavenum)[:, None, None, None], axis=(0, 1)),
        ]
    )
    lower, upper, gathered = z_exchange(point, sums, z_count)
    sums = jnp.sum(gathered, axis=0)
    energy_sum, first_sum, root_sum = sums[0], sums[1], sums[2]
    energy = energy_sum + EPSILON
    ext = jnp.concatenate([lower, point, upper], axis=0)
    center, plus, minus = ext[1:-1], jnp.roll(ext[2:], -1, axis=1), jnp.roll(ext[:-2], 3, axis=1)
    cubic = center * center * (plus + minus) - 2.0 * center * plus * minus
    extra = (
        -2.0 * cubic[1:-1] + jnp.roll(cubic[:-2], 1, axis=1) + jnp.roll(cubic[2:], -3, axis=1)
    ) * (QUAD_COEF / (energy * energy))
    row_start = y_pos * part_rows
    wind_block = lax.dynamic_slice_in_dim(wind_speed, row_start, part_rows, axis=0)
    wind_angle = lax.dynamic_slice_in_dim(wind_dir, row_start, part_rows, axis=0)
    wet_block = lax.dynamic_slice_in_dim(wet_mask, row_start, part_rows, axis=0)
    cosine = jnp.cos(angles[:, None, None] - wind_angle[None])
    updated = (
        sources(
            point,
            energy_sum,
            first_sum,
            root_sum,
            radian_freq[:, None, None, None],
            wavenum[:, None, None, None],
            cosine,
            wind_block,
        )
        + extra
    ) * wet_block
    return lax.all_to_all(updated, "y", split_axis=0, concat_axis=2, tiled=True)


def solution(mesh):
    geo_count = mesh.shape["geo"]
    spec_count = mesh.shape["spec"]
    local = jax.sharding.Mesh(
        mesh.devices.reshape(geo_count, spec_count // Y_GROUP, Y_GROUP), ("geo", "z", "y")
    )
    spec = ("z", "y")
    placed = (
        P(spec, None, "geo", None),
        P("geo", None),
        P("geo", None),
        P("geo"),
        P("geo", None),
        P("geo", None),
        P("geo", None),
        P("geo", None),
    )
    return jax.shard_map(
        shards, mesh=local, in_specs=placed, out_specs=P(spec, None, "geo", None), check_vma=False
    )
```

```python
import functools
import math

import jax
import jax.numpy as jnp
from jax import lax
from jax.experimental import pallas as pl
from jax.experimental.pallas import tpu as pltpu
from jax.sharding import PartitionSpec as P

GRAVITY = 9.81
BASE_FREQ = 0.035
GROWTH = 1.1
COURANT_TOP = 0.9
TURN_TOP = 1.2
SPACING = 0.1
USTAR_RATIO = 0.035
WIND_COEF = 0.0375
WHITECAP = 0.36
STEEP_REF = 1.6
EPSILON = 1e-06
QUAD_COEF = 100.0


def extended(cells, sides, width):
    for axis, dim in sides:
        count = lax.axis_size(axis)
        ends = count - 1
        head = lax.slice_in_dim(cells, 0, width, axis=dim)
        tail = lax.slice_in_dim(cells, cells.shape[dim] - width, cells.shape[dim], axis=dim)
        cells = jnp.concatenate(
            [
                lax.ppermute(tail, axis, [(i, (i + 1) % count) for i in range(ends)]),
                cells,
                lax.ppermute(head, axis, [((i + 1) % count, i) for i in range(ends)]),
            ],
            axis=dim,
        )
    return cells


def band_table(band_ids):
    growth_factor = jnp.power(GROWTH, band_ids)
    radian_freq = 2.0 * math.pi * BASE_FREQ * growth_factor
    wavenum = radian_freq * radian_freq / GRAVITY
    return (
        radian_freq,
        wavenum,
        COURANT_TOP / growth_factor,
        TURN_TOP / growth_factor,
        SPACING * radian_freq,
    )


def quick_flux(far_left, near_left, near_right, far_right, courant):
    forward = courant >= 0
    upwind = jnp.where(forward, far_left, far_right)
    center = jnp.where(forward, near_left, near_right)
    downwind = jnp.where(forward, near_right, near_left)
    face_value = (
        0.5 * (center + downwind)
        - 0.5 * jnp.abs(courant) * (downwind - center)
        - (1.0 - courant * courant) / 6.0 * (downwind - 2.0 * center + upwind)
    )
    return courant * face_value


def advect(padded, courant, along):
    face_count = padded.shape[along] - 4
    shifted = [
        lax.slice_in_dim(padded, offset, offset + face_count + 1, axis=along) for offset in range(4)
    ]
    face_flux = quick_flux(shifted[0], shifted[1], shifted[2], shifted[3], courant)
    centre_cells = lax.slice_in_dim(padded, 2, 2 + face_count, axis=along)
    upper_flux = lax.slice_in_dim(face_flux, 1, face_count + 1, axis=along)
    lower_flux = lax.slice_in_dim(face_flux, 0, face_count, axis=along)
    return centre_cells - (upper_flux - lower_flux)


def quad_delta(center, above, below, energy, dir_axis):
    plus = jnp.roll(above, -1, axis=dir_axis)
    minus = jnp.roll(below, 3, axis=dir_axis)
    return (
        QUAD_COEF
        * (center * center * (plus + minus) - 2.0 * center * plus * minus)
        / (energy * energy)
    )


def quad_term(delta, delta_above, delta_below, dir_axis):
    return (
        -2.0 * delta
        + jnp.roll(delta_below, 1, axis=dir_axis)
        + jnp.roll(delta_above, -3, axis=dir_axis)
    )


def band_neighbours(values):
    empty = jnp.zeros((1,) + values.shape[1:], jnp.float32)
    return (
        jnp.concatenate([values[1:], empty], axis=0),
        jnp.concatenate([empty, values[:-1]], axis=0),
    )


def sources(density, energy_sum, first_sum, root_sum, radian_freq, wavenum, cosine, wind_speed):
    energy = energy_sum + EPSILON
    mean_sigma = energy / (first_sum + EPSILON)
    ratio_k = energy / (root_sum + EPSILON)
    mean_k = ratio_k * ratio_k
    steepness = energy * mean_k * mean_k / STEEP_REF
    decay_rate = WHITECAP * mean_sigma * (wavenum / mean_k) * steepness * steepness
    growth_rate = (
        WIND_COEF
        * radian_freq
        * jnp.maximum(28.0 * USTAR_RATIO * wind_speed * radian_freq / GRAVITY * cosine - 1.0, 0.0)
    )
    return density * (1.0 + growth_rate) / (1.0 + decay_rate)


def local_sources(point_block, wind_block, wind_angle, angles, dtheta):
    band_total = point_block.shape[0]
    band_ids = jnp.arange(band_total).astype(jnp.float32)
    radian_freq, wavenum, courant, turn_rate, band_spread = band_table(band_ids)
    scaled = point_block * (band_spread * dtheta)[:, None, None]
    energy_sum = jnp.sum(scaled, axis=(0, 1))
    first_sum = jnp.sum(scaled / radian_freq[:, None, None], axis=(0, 1))
    root_sum = jnp.sum(scaled / jnp.sqrt(wavenum)[:, None, None], axis=(0, 1))
    energy = energy_sum + EPSILON
    above, below = band_neighbours(point_block)
    delta = quad_delta(point_block, above, below, energy, 1)
    delta_above, delta_below = band_neighbours(delta)
    extra = quad_term(delta, delta_above, delta_below, 1)
    cosine = jnp.cos(angles[:, None] - wind_angle[None, :])
    return (
        sources(
            point_block,
            energy_sum,
            first_sum,
            root_sum,
            radian_freq[:, None, None],
            wavenum[:, None, None],
            cosine,
            wind_block,
        )
        + extra
    )


Y_GROUP = 4
HALO = 2


def _z_gather_kernel(z_count, part_ref, gathered_ref, gather_send, gather_recv):
    geo = lax.axis_index("geo")
    z_pos = lax.axis_index("z")
    y_pos = lax.axis_index("y")
    barrier = pltpu.get_barrier_semaphore()
    for offset in range(1, z_count):
        target = lax.rem(z_pos + offset, z_count)
        pl.semaphore_signal(barrier, inc=1, device_id=(geo, target, y_pos),
                            device_id_type=pl.DeviceIdType.MESH)
    pl.semaphore_wait(barrier, z_count - 1)
    copies = []
    for offset in range(1, z_count):
        target = lax.rem(z_pos + offset, z_count)
        copy = pltpu.make_async_remote_copy(
            src_ref=part_ref,
            dst_ref=gathered_ref.at[z_pos],
            send_sem=gather_send.at[offset],
            recv_sem=gather_recv.at[offset],
            device_id=(geo, target, y_pos),
            device_id_type=pl.DeviceIdType.MESH,
        )
        copy.start()
        copies.append(copy)
    gathered_ref[z_pos] = part_ref[...]
    for copy in copies:
        copy.wait_send()
        copy.wait_recv()


def z_gather(part, z_count):
    vmem = pl.BlockSpec(memory_space=pltpu.VMEM)
    return pl.pallas_call(
        functools.partial(_z_gather_kernel, z_count),
        out_shape=jax.ShapeDtypeStruct((z_count,) + part.shape, part.dtype),
        in_specs=[vmem],
        out_specs=vmem,
        scratch_shapes=[
            pltpu.SemaphoreType.DMA((z_count,)),
            pltpu.SemaphoreType.DMA((z_count,)),
        ],
        compiler_params=pltpu.CompilerParams(collective_id=0, has_side_effects=True),
    )(part)


def _spread_kernel(z_count, y_count, floored_ref, ext_ref, y_send, local_sem, slot_recv, z_send):
    geo = lax.axis_index("geo")
    z_pos = lax.axis_index("z")
    y_pos = lax.axis_index("y")
    rows = ext_ref.shape[2]
    mesh_id = pl.DeviceIdType.MESH
    barrier = pltpu.get_barrier_semaphore()
    for offset in range(1, y_count):
        pl.semaphore_signal(barrier, inc=1, device_id=(geo, z_pos, lax.rem(y_pos + offset, y_count)),
                            device_id_type=mesh_id)

    for step in (1, z_count - 1):
        pl.semaphore_signal(barrier, inc=1, device_id=(geo, lax.rem(z_pos + step, z_count), y_pos),
                            device_id_type=mesh_id)
    pl.semaphore_wait(barrier, y_count + 1)

    own_slot = HALO + y_pos
    sends = []
    for offset in range(1, y_count):
        target = lax.rem(y_pos + offset, y_count)
        copy = pltpu.make_async_remote_copy(
            src_ref=floored_ref.at[0, :, pl.ds(pl.multiple_of(target * rows, rows), rows)],
            dst_ref=ext_ref.at[own_slot],
            send_sem=y_send.at[offset],
            recv_sem=slot_recv.at[own_slot],
            device_id=(geo, z_pos, target),
            device_id_type=mesh_id,
        )
        copy.start()
        sends.append(copy)
    local = pltpu.make_async_copy(
        floored_ref.at[0, :, pl.ds(pl.multiple_of(y_pos * rows, rows), rows)],
        ext_ref.at[own_slot],
        local_sem.at[0],
    )
    local.start()

    @pl.when(z_pos == 0)
    def _():
        ext_ref[pl.ds(0, HALO)] = jnp.zeros((HALO,) + ext_ref.shape[1:], ext_ref.dtype)

    @pl.when(z_pos == z_count - 1)
    def _():
        ext_ref[pl.ds(HALO + y_count, HALO)] = jnp.zeros((HALO,) + ext_ref.shape[1:], ext_ref.dtype)

    def forward(slot, dst_slot, target_z):
        return pltpu.make_async_remote_copy(
            src_ref=ext_ref.at[slot],
            dst_ref=ext_ref.at[dst_slot],
            send_sem=z_send.at[slot - HALO],
            recv_sem=slot_recv.at[dst_slot],
            device_id=(geo, target_z, y_pos),
            device_id_type=mesh_id,
        )

    forwards = []
    for band in range(y_count):
        slot = HALO + band
        arrival = pltpu.make_async_remote_copy(
            src_ref=ext_ref.at[slot],
            dst_ref=ext_ref.at[slot],
            send_sem=y_send.at[0],
            recv_sem=slot_recv.at[slot],
            device_id=(geo, z_pos, lax.rem(y_pos + 1, y_count)),
            device_id_type=mesh_id,
        )

        @pl.when(y_pos == band)
        def _():
            local.wait()

        @pl.when(y_pos != band)
        def _():
            arrival.wait_recv()

        if band < HALO:
            fwd = forward(slot, slot + y_count, z_pos - 1)
            live = z_pos > 0
        elif band >= y_count - HALO:
            fwd = forward(slot, slot - y_count, z_pos + 1)
            live = z_pos < z_count - 1
        else:
            continue

        @pl.when(live)
        def _():
            fwd.start()

        forwards.append((fwd, live))
    for copy in sends:
        copy.wait_send()
    for fwd, live in forwards:

        @pl.when(live)
        def _():
            fwd.wait_send()

    for slot, live in ((0, z_pos > 0), (1, z_pos > 0),
                       (HALO + y_count, z_pos < z_count - 1), (HALO + y_count + 1, z_pos < z_count - 1)):
        incoming = pltpu.make_async_remote_copy(
            src_ref=ext_ref.at[slot],
            dst_ref=ext_ref.at[slot],
            send_sem=z_send.at[0],
            recv_sem=slot_recv.at[slot],
            device_id=(geo, lax.rem(z_pos + 1, z_count), y_pos),
            device_id_type=mesh_id,
        )

        @pl.when(live)
        def _():
            incoming.wait_recv()


def spread(floored, z_count, y_count):
    _, dirs, rows, cols = floored.shape
    part_rows = rows // y_count
    vmem = pl.BlockSpec(memory_space=pltpu.VMEM)
    slots = y_count + 2 * HALO
    return pl.pallas_call(
        functools.partial(_spread_kernel, z_count, y_count),
        out_shape=jax.ShapeDtypeStruct((slots, dirs, part_rows, cols), floored.dtype),
        in_specs=[vmem],
        out_specs=vmem,
        scratch_shapes=[
            pltpu.SemaphoreType.DMA((y_count,)),
            pltpu.SemaphoreType.DMA((1,)),
            pltpu.SemaphoreType.DMA((slots,)),
            pltpu.SemaphoreType.DMA((y_count,)),
        ],
        compiler_params=pltpu.CompilerParams(collective_id=1, has_side_effects=True),
    )(floored)


def shards(spectrum, land_sea, sea_index, sea_count, wind_speed, wind_dir, slope_x, slope_y):
    local_bands, dir_count, row_count, col_count = spectrum.shape
    z_count = lax.axis_size("z")
    y_count = lax.axis_size("y")
    z_pos = lax.axis_index("z")
    y_pos = lax.axis_index("y")
    spec_pos = z_pos * y_count + y_pos
    dtheta = 2.0 * math.pi / dir_count
    angles = (jnp.arange(dir_count).astype(jnp.float32) + 0.5) * dtheta
    face_angles = jnp.arange(dir_count + 1).astype(jnp.float32) * dtheta
    band_ids = (spec_pos * local_bands + jnp.arange(local_bands)).astype(jnp.float32)
    radian_freq, wavenum, courant, turn_rate, band_spread = band_table(band_ids)
    wet_mask = land_sea.astype(jnp.float32)
    density = spectrum * wet_mask
    padded = extended(density, (("geo", 2),), 2)
    density = (
        advect(padded, (courant[:, None] * jnp.cos(angles)[None, :])[:, :, None, None], 2)
        * wet_mask
    )
    padded = jnp.pad(density, ((0, 0), (0, 0), (0, 0), (2, 2)))
    density = (
        advect(padded, (courant[:, None] * jnp.sin(angles)[None, :])[:, :, None, None], 3)
        * wet_mask
    )
    turning = turn_rate[:, None, None, None] * (
        jnp.sin(face_angles)[None, :, None, None] * slope_x
        - jnp.cos(face_angles)[None, :, None, None] * slope_y
    )
    padded = jnp.concatenate([density[:, -2:], density, density[:, :2]], axis=1)
    floored = jnp.maximum(advect(padded, turning, 1), 0.0)
    ext = spread(floored, z_count, lax.axis_size("y"))
    point = ext[HALO:-HALO]
    group = point.shape[0]
    part_rows = point.shape[2]
    group_ids = (z_pos * group + jnp.arange(group)).astype(jnp.float32)
    radian_freq, wavenum, courant, turn_rate, band_spread = band_table(group_ids)
    scaled = point * (band_spread * dtheta)[:, None, None, None]
    sums = jnp.stack(
        [
            jnp.sum(scaled, axis=(0, 1)),
            jnp.sum(scaled / radian_freq[:, None, None, None], axis=(0, 1)),
            jnp.sum(scaled / jnp.sqrt(wavenum)[:, None, None, None], axis=(0, 1)),
        ]
    )
    sums = jnp.sum(z_gather(sums, z_count), axis=0)
    energy_sum, first_sum, root_sum = sums[0], sums[1], sums[2]
    energy = energy_sum + EPSILON
    center, plus, minus = ext[1:-1], jnp.roll(ext[2:], -1, axis=1), jnp.roll(ext[:-2], 3, axis=1)
    cubic = center * center * (plus + minus) - 2.0 * center * plus * minus
    extra = (
        -2.0 * cubic[1:-1] + jnp.roll(cubic[:-2], 1, axis=1) + jnp.roll(cubic[2:], -3, axis=1)
    ) * (QUAD_COEF / (energy * energy))
    row_start = y_pos * part_rows
    wind_block = lax.dynamic_slice_in_dim(wind_speed, row_start, part_rows, axis=0)
    wind_angle = lax.dynamic_slice_in_dim(wind_dir, row_start, part_rows, axis=0)
    wet_block = lax.dynamic_slice_in_dim(wet_mask, row_start, part_rows, axis=0)
    cosine = jnp.cos(angles[:, None, None] - wind_angle[None])
    updated = (
        sources(
            point,
            energy_sum,
            first_sum,
            root_sum,
            radian_freq[:, None, None, None],
            wavenum[:, None, None, None],
            cosine,
            wind_block,
        )
        + extra
    ) * wet_block
    return lax.all_to_all(updated, "y", split_axis=0, concat_axis=2, tiled=True)


def solution(mesh):
    geo_count = mesh.shape["geo"]
    spec_count = mesh.shape["spec"]
    local = jax.sharding.Mesh(
        mesh.devices.reshape(geo_count, spec_count // Y_GROUP, Y_GROUP), ("geo", "z", "y")
    )
    spec = ("z", "y")
    placed = (
        P(spec, None, "geo", None),
        P("geo", None),
        P("geo", None),
        P("geo"),
        P("geo", None),
        P("geo", None),
        P("geo", None),
        P("geo", None),
    )
    return jax.shard_map(
        shards, mesh=local, in_specs=placed, out_specs=P(spec, None, "geo", None), check_vma=False
    )
```

```python
import functools
import math

import jax
import jax.numpy as jnp
from jax import lax
from jax.experimental import pallas as pl
from jax.experimental.pallas import tpu as pltpu
from jax.sharding import PartitionSpec as P

GRAVITY = 9.81
BASE_FREQ = 0.035
GROWTH = 1.1
COURANT_TOP = 0.9
TURN_TOP = 1.2
SPACING = 0.1
USTAR_RATIO = 0.035
WIND_COEF = 0.0375
WHITECAP = 0.36
STEEP_REF = 1.6
EPSILON = 1e-06
QUAD_COEF = 100.0


def extended(cells, sides, width):
    for axis, dim in sides:
        count = lax.axis_size(axis)
        ends = count - 1
        head = lax.slice_in_dim(cells, 0, width, axis=dim)
        tail = lax.slice_in_dim(cells, cells.shape[dim] - width, cells.shape[dim], axis=dim)
        cells = jnp.concatenate(
            [
                lax.ppermute(tail, axis, [(i, (i + 1) % count) for i in range(ends)]),
                cells,
                lax.ppermute(head, axis, [((i + 1) % count, i) for i in range(ends)]),
            ],
            axis=dim,
        )
    return cells


def band_table(band_ids):
    growth_factor = jnp.power(GROWTH, band_ids)
    radian_freq = 2.0 * math.pi * BASE_FREQ * growth_factor
    wavenum = radian_freq * radian_freq / GRAVITY
    return (
        radian_freq,
        wavenum,
        COURANT_TOP / growth_factor,
        TURN_TOP / growth_factor,
        SPACING * radian_freq,
    )


def quick_flux(far_left, near_left, near_right, far_right, courant):
    forward = courant >= 0
    upwind = jnp.where(forward, far_left, far_right)
    center = jnp.where(forward, near_left, near_right)
    downwind = jnp.where(forward, near_right, near_left)
    face_value = (
        0.5 * (center + downwind)
        - 0.5 * jnp.abs(courant) * (downwind - center)
        - (1.0 - courant * courant) / 6.0 * (downwind - 2.0 * center + upwind)
    )
    return courant * face_value


def advect(padded, courant, along):
    face_count = padded.shape[along] - 4
    shifted = [
        lax.slice_in_dim(padded, offset, offset + face_count + 1, axis=along) for offset in range(4)
    ]
    face_flux = quick_flux(shifted[0], shifted[1], shifted[2], shifted[3], courant)
    centre_cells = lax.slice_in_dim(padded, 2, 2 + face_count, axis=along)
    upper_flux = lax.slice_in_dim(face_flux, 1, face_count + 1, axis=along)
    lower_flux = lax.slice_in_dim(face_flux, 0, face_count, axis=along)
    return centre_cells - (upper_flux - lower_flux)


def quad_delta(center, above, below, energy, dir_axis):
    plus = jnp.roll(above, -1, axis=dir_axis)
    minus = jnp.roll(below, 3, axis=dir_axis)
    return (
        QUAD_COEF
        * (center * center * (plus + minus) - 2.0 * center * plus * minus)
        / (energy * energy)
    )


def quad_term(delta, delta_above, delta_below, dir_axis):
    return (
        -2.0 * delta
        + jnp.roll(delta_below, 1, axis=dir_axis)
        + jnp.roll(delta_above, -3, axis=dir_axis)
    )


def band_neighbours(values):
    empty = jnp.zeros((1,) + values.shape[1:], jnp.float32)
    return (
        jnp.concatenate([values[1:], empty], axis=0),
        jnp.concatenate([empty, values[:-1]], axis=0),
    )


def sources(density, energy_sum, first_sum, root_sum, radian_freq, wavenum, cosine, wind_speed):
    energy = energy_sum + EPSILON
    mean_sigma = energy / (first_sum + EPSILON)
    ratio_k = energy / (root_sum + EPSILON)
    mean_k = ratio_k * ratio_k
    steepness = energy * mean_k * mean_k / STEEP_REF
    decay_rate = WHITECAP * mean_sigma * (wavenum / mean_k) * steepness * steepness
    growth_rate = (
        WIND_COEF
        * radian_freq
        * jnp.maximum(28.0 * USTAR_RATIO * wind_speed * radian_freq / GRAVITY * cosine - 1.0, 0.0)
    )
    return density * (1.0 + growth_rate) / (1.0 + decay_rate)


def local_sources(point_block, wind_block, wind_angle, angles, dtheta):
    band_total = point_block.shape[0]
    band_ids = jnp.arange(band_total).astype(jnp.float32)
    radian_freq, wavenum, courant, turn_rate, band_spread = band_table(band_ids)
    scaled = point_block * (band_spread * dtheta)[:, None, None]
    energy_sum = jnp.sum(scaled, axis=(0, 1))
    first_sum = jnp.sum(scaled / radian_freq[:, None, None], axis=(0, 1))
    root_sum = jnp.sum(scaled / jnp.sqrt(wavenum)[:, None, None], axis=(0, 1))
    energy = energy_sum + EPSILON
    above, below = band_neighbours(point_block)
    delta = quad_delta(point_block, above, below, energy, 1)
    delta_above, delta_below = band_neighbours(delta)
    extra = quad_term(delta, delta_above, delta_below, 1)
    cosine = jnp.cos(angles[:, None] - wind_angle[None, :])
    return (
        sources(
            point_block,
            energy_sum,
            first_sum,
            root_sum,
            radian_freq[:, None, None],
            wavenum[:, None, None],
            cosine,
            wind_block,
        )
        + extra
    )


Y_GROUP = 4
HALO = 2


def _z_gather_kernel(z_count, part_ref, gathered_ref, gather_send, gather_recv):
    geo = lax.axis_index("geo")
    z_pos = lax.axis_index("z")
    y_pos = lax.axis_index("y")
    barrier = pltpu.get_barrier_semaphore()
    for offset in range(1, z_count):
        target = lax.rem(z_pos + offset, z_count)
        pl.semaphore_signal(barrier, inc=1, device_id=(geo, target, y_pos),
                            device_id_type=pl.DeviceIdType.MESH)
    pl.semaphore_wait(barrier, z_count - 1)
    copies = []
    for offset in range(1, z_count):
        target = lax.rem(z_pos + offset, z_count)
        copy = pltpu.make_async_remote_copy(
            src_ref=part_ref,
            dst_ref=gathered_ref.at[z_pos],
            send_sem=gather_send.at[offset],
            recv_sem=gather_recv.at[offset],
            device_id=(geo, target, y_pos),
            device_id_type=pl.DeviceIdType.MESH,
        )
        copy.start()
        copies.append(copy)
    gathered_ref[z_pos] = part_ref[...]
    for copy in copies:
        copy.wait_send()
        copy.wait_recv()


def z_gather(part, z_count):
    vmem = pl.BlockSpec(memory_space=pltpu.VMEM)
    return pl.pallas_call(
        functools.partial(_z_gather_kernel, z_count),
        out_shape=jax.ShapeDtypeStruct((z_count,) + part.shape, part.dtype),
        in_specs=[vmem],
        out_specs=vmem,
        scratch_shapes=[
            pltpu.SemaphoreType.DMA((z_count,)),
            pltpu.SemaphoreType.DMA((z_count,)),
        ],
        compiler_params=pltpu.CompilerParams(collective_id=0, has_side_effects=True),
    )(part)


def _spread_kernel(z_count, y_count, floored_ref, ext_ref, y_send, local_sem, slot_recv, z_send):
    geo = lax.axis_index("geo")
    z_pos = lax.axis_index("z")
    y_pos = lax.axis_index("y")
    rows = ext_ref.shape[2]
    mesh_id = pl.DeviceIdType.MESH
    barrier = pltpu.get_barrier_semaphore()
    for offset in range(1, y_count):
        pl.semaphore_signal(barrier, inc=1, device_id=(geo, z_pos, lax.rem(y_pos + offset, y_count)),
                            device_id_type=mesh_id)

    for step in (1, z_count - 1):
        pl.semaphore_signal(barrier, inc=1, device_id=(geo, lax.rem(z_pos + step, z_count), y_pos),
                            device_id_type=mesh_id)
    pl.semaphore_wait(barrier, y_count + 1)

    own_slot = HALO + y_pos
    sends = []
    for offset in range(1, y_count):
        target = lax.rem(y_pos + offset, y_count)
        copy = pltpu.make_async_remote_copy(
            src_ref=floored_ref.at[0, :, pl.ds(pl.multiple_of(target * rows, rows), rows)],
            dst_ref=ext_ref.at[own_slot],
            send_sem=y_send.at[offset],
            recv_sem=slot_recv.at[own_slot],
            device_id=(geo, z_pos, target),
            device_id_type=mesh_id,
        )
        copy.start()
        sends.append(copy)
    local = pltpu.make_async_copy(
        floored_ref.at[0, :, pl.ds(pl.multiple_of(y_pos * rows, rows), rows)],
        ext_ref.at[own_slot],
        local_sem.at[0],
    )
    local.start()

    @pl.when(z_pos == 0)
    def _():
        ext_ref[pl.ds(0, HALO)] = jnp.zeros((HALO,) + ext_ref.shape[1:], ext_ref.dtype)

    @pl.when(z_pos == z_count - 1)
    def _():
        ext_ref[pl.ds(HALO + y_count, HALO)] = jnp.zeros((HALO,) + ext_ref.shape[1:], ext_ref.dtype)

    def forward(slot, dst_slot, target_z):
        return pltpu.make_async_remote_copy(
            src_ref=ext_ref.at[slot],
            dst_ref=ext_ref.at[dst_slot],
            send_sem=z_send.at[slot - HALO],
            recv_sem=slot_recv.at[dst_slot],
            device_id=(geo, target_z, y_pos),
            device_id_type=mesh_id,
        )

    forwards = []
    for band in range(y_count):
        slot = HALO + band
        arrival = pltpu.make_async_remote_copy(
            src_ref=ext_ref.at[slot],
            dst_ref=ext_ref.at[slot],
            send_sem=y_send.at[0],
            recv_sem=slot_recv.at[slot],
            device_id=(geo, z_pos, lax.rem(y_pos + 1, y_count)),
            device_id_type=mesh_id,
        )

        @pl.when(y_pos == band)
        def _():
            local.wait()

        @pl.when(y_pos != band)
        def _():
            arrival.wait_recv()

        if band < HALO:
            fwd = forward(slot, slot + y_count, z_pos - 1)
            live = z_pos > 0
        elif band >= y_count - HALO:
            fwd = forward(slot, slot - y_count, z_pos + 1)
            live = z_pos < z_count - 1
        else:
            continue

        @pl.when(live)
        def _():
            fwd.start()

        forwards.append((fwd, live))
    for copy in sends:
        copy.wait_send()
    for fwd, live in forwards:

        @pl.when(live)
        def _():
            fwd.wait_send()

    for slot, live in ((0, z_pos > 0), (1, z_pos > 0),
                       (HALO + y_count, z_pos < z_count - 1), (HALO + y_count + 1, z_pos < z_count - 1)):
        incoming = pltpu.make_async_remote_copy(
            src_ref=ext_ref.at[slot],
            dst_ref=ext_ref.at[slot],
            send_sem=z_send.at[0],
            recv_sem=slot_recv.at[slot],
            device_id=(geo, lax.rem(z_pos + 1, z_count), y_pos),
            device_id_type=mesh_id,
        )

        @pl.when(live)
        def _():
            incoming.wait_recv()


def spread(floored, z_count, y_count):
    _, dirs, rows, cols = floored.shape
    part_rows = rows // y_count
    vmem = pl.BlockSpec(memory_space=pltpu.VMEM)
    slots = y_count + 2 * HALO
    return pl.pallas_call(
        functools.partial(_spread_kernel, z_count, y_count),
        out_shape=jax.ShapeDtypeStruct((slots, dirs, part_rows, cols), floored.dtype),
        in_specs=[vmem],
        out_specs=vmem,
        scratch_shapes=[
            pltpu.SemaphoreType.DMA((y_count,)),
            pltpu.SemaphoreType.DMA((1,)),
            pltpu.SemaphoreType.DMA((slots,)),
            pltpu.SemaphoreType.DMA((y_count,)),
        ],
        compiler_params=pltpu.CompilerParams(collective_id=1, has_side_effects=True),
        cost_estimate=pl.CostEstimate(
            flops=0, transcendentals=0, bytes_accessed=40 * floored.size * floored.dtype.itemsize
        ),
    )(floored)


def shards(spectrum, land_sea, sea_index, sea_count, wind_speed, wind_dir, slope_x, slope_y):
    local_bands, dir_count, row_count, col_count = spectrum.shape
    z_count = lax.axis_size("z")
    y_count = lax.axis_size("y")
    z_pos = lax.axis_index("z")
    y_pos = lax.axis_index("y")
    spec_pos = z_pos * y_count + y_pos
    dtheta = 2.0 * math.pi / dir_count
    angles = (jnp.arange(dir_count).astype(jnp.float32) + 0.5) * dtheta
    face_angles = jnp.arange(dir_count + 1).astype(jnp.float32) * dtheta
    band_ids = (spec_pos * local_bands + jnp.arange(local_bands)).astype(jnp.float32)
    radian_freq, wavenum, courant, turn_rate, band_spread = band_table(band_ids)
    wet_mask = land_sea.astype(jnp.float32)
    density = spectrum * wet_mask
    padded = extended(density, (("geo", 2),), 2)
    density = (
        advect(padded, (courant[:, None] * jnp.cos(angles)[None, :])[:, :, None, None], 2)
        * wet_mask
    )
    padded = jnp.pad(density, ((0, 0), (0, 0), (0, 0), (2, 2)))
    density = (
        advect(padded, (courant[:, None] * jnp.sin(angles)[None, :])[:, :, None, None], 3)
        * wet_mask
    )
    turning = turn_rate[:, None, None, None] * (
        jnp.sin(face_angles)[None, :, None, None] * slope_x
        - jnp.cos(face_angles)[None, :, None, None] * slope_y
    )
    padded = jnp.concatenate([density[:, -2:], density, density[:, :2]], axis=1)
    floored = jnp.maximum(advect(padded, turning, 1), 0.0)
    own_freq, own_wavenum, _, _, own_spread = band_table(band_ids)
    own_scaled = floored * (own_spread * dtheta)[:, None, None, None]
    total_sums = lax.psum(
        jnp.stack(
            [
                jnp.sum(own_scaled, axis=(0, 1)),
                jnp.sum(own_scaled / own_freq[:, None, None, None], axis=(0, 1)),
                jnp.sum(own_scaled / jnp.sqrt(own_wavenum)[:, None, None, None], axis=(0, 1)),
            ]
        ),
        ("z", "y"),
    )
    ext = spread(floored, z_count, lax.axis_size("y"))
    point = ext[HALO:-HALO]
    group = point.shape[0]
    part_rows = point.shape[2]
    group_ids = (z_pos * group + jnp.arange(group)).astype(jnp.float32)
    radian_freq, wavenum, courant, turn_rate, band_spread = band_table(group_ids)
    row_start = y_pos * part_rows
    sums = lax.dynamic_slice_in_dim(total_sums, row_start, part_rows, axis=1)
    energy_sum, first_sum, root_sum = sums[0], sums[1], sums[2]
    energy = energy_sum + EPSILON
    center, plus, minus = ext[1:-1], jnp.roll(ext[2:], -1, axis=1), jnp.roll(ext[:-2], 3, axis=1)
    cubic = center * center * (plus + minus) - 2.0 * center * plus * minus
    extra = (
        -2.0 * cubic[1:-1] + jnp.roll(cubic[:-2], 1, axis=1) + jnp.roll(cubic[2:], -3, axis=1)
    ) * (QUAD_COEF / (energy * energy))
    wind_block = lax.dynamic_slice_in_dim(wind_speed, row_start, part_rows, axis=0)
    wind_angle = lax.dynamic_slice_in_dim(wind_dir, row_start, part_rows, axis=0)
    wet_block = lax.dynamic_slice_in_dim(wet_mask, row_start, part_rows, axis=0)
    cosine = jnp.cos(angles[:, None, None] - wind_angle[None])
    updated = (
        sources(
            point,
            energy_sum,
            first_sum,
            root_sum,
            radian_freq[:, None, None, None],
            wavenum[:, None, None, None],
            cosine,
            wind_block,
        )
        + extra
    ) * wet_block
    return lax.all_to_all(updated, "y", split_axis=0, concat_axis=2, tiled=True)


def solution(mesh):
    geo_count = mesh.shape["geo"]
    spec_count = mesh.shape["spec"]
    local = jax.sharding.Mesh(
        mesh.devices.reshape(geo_count, spec_count // Y_GROUP, Y_GROUP), ("geo", "z", "y")
    )
    spec = ("z", "y")
    placed = (
        P(spec, None, "geo", None),
        P("geo", None),
        P("geo", None),
        P("geo"),
        P("geo", None),
        P("geo", None),
        P("geo", None),
        P("geo", None),
    )
    return jax.shard_map(
        shards, mesh=local, in_specs=placed, out_specs=P(spec, None, "geo", None), check_vma=False
    )
```

```python
import functools
import math

import jax
import jax.numpy as jnp
from jax import lax
from jax.experimental import pallas as pl
from jax.experimental.pallas import tpu as pltpu
from jax.sharding import PartitionSpec as P

GRAVITY = 9.81
BASE_FREQ = 0.035
GROWTH = 1.1
COURANT_TOP = 0.9
TURN_TOP = 1.2
SPACING = 0.1
USTAR_RATIO = 0.035
WIND_COEF = 0.0375
WHITECAP = 0.36
STEEP_REF = 1.6
EPSILON = 1e-06
QUAD_COEF = 100.0


def extended(cells, sides, width):
    for axis, dim in sides:
        count = lax.axis_size(axis)
        ends = count - 1
        head = lax.slice_in_dim(cells, 0, width, axis=dim)
        tail = lax.slice_in_dim(cells, cells.shape[dim] - width, cells.shape[dim], axis=dim)
        cells = jnp.concatenate(
            [
                lax.ppermute(tail, axis, [(i, (i + 1) % count) for i in range(ends)]),
                cells,
                lax.ppermute(head, axis, [((i + 1) % count, i) for i in range(ends)]),
            ],
            axis=dim,
        )
    return cells


def band_table(band_ids):
    growth_factor = jnp.power(GROWTH, band_ids)
    radian_freq = 2.0 * math.pi * BASE_FREQ * growth_factor
    wavenum = radian_freq * radian_freq / GRAVITY
    return (
        radian_freq,
        wavenum,
        COURANT_TOP / growth_factor,
        TURN_TOP / growth_factor,
        SPACING * radian_freq,
    )


def quick_flux(far_left, near_left, near_right, far_right, courant):
    forward = courant >= 0
    upwind = jnp.where(forward, far_left, far_right)
    center = jnp.where(forward, near_left, near_right)
    downwind = jnp.where(forward, near_right, near_left)
    face_value = (
        0.5 * (center + downwind)
        - 0.5 * jnp.abs(courant) * (downwind - center)
        - (1.0 - courant * courant) / 6.0 * (downwind - 2.0 * center + upwind)
    )
    return courant * face_value


def advect(padded, courant, along):
    face_count = padded.shape[along] - 4
    shifted = [
        lax.slice_in_dim(padded, offset, offset + face_count + 1, axis=along) for offset in range(4)
    ]
    face_flux = quick_flux(shifted[0], shifted[1], shifted[2], shifted[3], courant)
    centre_cells = lax.slice_in_dim(padded, 2, 2 + face_count, axis=along)
    upper_flux = lax.slice_in_dim(face_flux, 1, face_count + 1, axis=along)
    lower_flux = lax.slice_in_dim(face_flux, 0, face_count, axis=along)
    return centre_cells - (upper_flux - lower_flux)


def quad_delta(center, above, below, energy, dir_axis):
    plus = jnp.roll(above, -1, axis=dir_axis)
    minus = jnp.roll(below, 3, axis=dir_axis)
    return (
        QUAD_COEF
        * (center * center * (plus + minus) - 2.0 * center * plus * minus)
        / (energy * energy)
    )


def quad_term(delta, delta_above, delta_below, dir_axis):
    return (
        -2.0 * delta
        + jnp.roll(delta_below, 1, axis=dir_axis)
        + jnp.roll(delta_above, -3, axis=dir_axis)
    )


def band_neighbours(values):
    empty = jnp.zeros((1,) + values.shape[1:], jnp.float32)
    return (
        jnp.concatenate([values[1:], empty], axis=0),
        jnp.concatenate([empty, values[:-1]], axis=0),
    )


def sources(density, energy_sum, first_sum, root_sum, radian_freq, wavenum, cosine, wind_speed):
    energy = energy_sum + EPSILON
    mean_sigma = energy / (first_sum + EPSILON)
    ratio_k = energy / (root_sum + EPSILON)
    mean_k = ratio_k * ratio_k
    steepness = energy * mean_k * mean_k / STEEP_REF
    decay_rate = WHITECAP * mean_sigma * (wavenum / mean_k) * steepness * steepness
    growth_rate = (
        WIND_COEF
        * radian_freq
        * jnp.maximum(28.0 * USTAR_RATIO * wind_speed * radian_freq / GRAVITY * cosine - 1.0, 0.0)
    )
    return density * (1.0 + growth_rate) / (1.0 + decay_rate)


def local_sources(point_block, wind_block, wind_angle, angles, dtheta):
    band_total = point_block.shape[0]
    band_ids = jnp.arange(band_total).astype(jnp.float32)
    radian_freq, wavenum, courant, turn_rate, band_spread = band_table(band_ids)
    scaled = point_block * (band_spread * dtheta)[:, None, None]
    energy_sum = jnp.sum(scaled, axis=(0, 1))
    first_sum = jnp.sum(scaled / radian_freq[:, None, None], axis=(0, 1))
    root_sum = jnp.sum(scaled / jnp.sqrt(wavenum)[:, None, None], axis=(0, 1))
    energy = energy_sum + EPSILON
    above, below = band_neighbours(point_block)
    delta = quad_delta(point_block, above, below, energy, 1)
    delta_above, delta_below = band_neighbours(delta)
    extra = quad_term(delta, delta_above, delta_below, 1)
    cosine = jnp.cos(angles[:, None] - wind_angle[None, :])
    return (
        sources(
            point_block,
            energy_sum,
            first_sum,
            root_sum,
            radian_freq[:, None, None],
            wavenum[:, None, None],
            cosine,
            wind_block,
        )
        + extra
    )


Y_GROUP = 4
HALO = 2


def _z_gather_kernel(z_count, part_ref, gathered_ref, gather_send, gather_recv):
    geo = lax.axis_index("geo")
    z_pos = lax.axis_index("z")
    y_pos = lax.axis_index("y")
    barrier = pltpu.get_barrier_semaphore()
    for offset in range(1, z_count):
        target = lax.rem(z_pos + offset, z_count)
        pl.semaphore_signal(barrier, inc=1, device_id=(geo, target, y_pos),
                            device_id_type=pl.DeviceIdType.MESH)
    pl.semaphore_wait(barrier, z_count - 1)
    copies = []
    for offset in range(1, z_count):
        target = lax.rem(z_pos + offset, z_count)
        copy = pltpu.make_async_remote_copy(
            src_ref=part_ref,
            dst_ref=gathered_ref.at[z_pos],
            send_sem=gather_send.at[offset],
            recv_sem=gather_recv.at[offset],
            device_id=(geo, target, y_pos),
            device_id_type=pl.DeviceIdType.MESH,
        )
        copy.start()
        copies.append(copy)
    gathered_ref[z_pos] = part_ref[...]
    for copy in copies:
        copy.wait_send()
        copy.wait_recv()


def z_gather(part, z_count):
    vmem = pl.BlockSpec(memory_space=pltpu.VMEM)
    return pl.pallas_call(
        functools.partial(_z_gather_kernel, z_count),
        out_shape=jax.ShapeDtypeStruct((z_count,) + part.shape, part.dtype),
        in_specs=[vmem],
        out_specs=vmem,
        scratch_shapes=[
            pltpu.SemaphoreType.DMA((z_count,)),
            pltpu.SemaphoreType.DMA((z_count,)),
        ],
        compiler_params=pltpu.CompilerParams(collective_id=0, has_side_effects=True),
    )(part)


def _spread_kernel(z_count, y_count, floored_ref, ext_ref, y_send, local_sem, slot_recv, z_send):
    geo = lax.axis_index("geo")
    z_pos = lax.axis_index("z")
    y_pos = lax.axis_index("y")
    rows = ext_ref.shape[2]
    mesh_id = pl.DeviceIdType.MESH
    barrier = pltpu.get_barrier_semaphore()
    for offset in range(1, y_count):
        pl.semaphore_signal(barrier, inc=1, device_id=(geo, z_pos, lax.rem(y_pos + offset, y_count)),
                            device_id_type=mesh_id)

    for step in (1, z_count - 1):
        pl.semaphore_signal(barrier, inc=1, device_id=(geo, lax.rem(z_pos + step, z_count), y_pos),
                            device_id_type=mesh_id)
    pl.semaphore_wait(barrier, y_count + 1)

    own_slot = HALO + y_pos
    sends = []
    for offset in range(1, y_count):
        target = lax.rem(y_pos + offset, y_count)
        copy = pltpu.make_async_remote_copy(
            src_ref=floored_ref.at[0, :, pl.ds(pl.multiple_of(target * rows, rows), rows)],
            dst_ref=ext_ref.at[own_slot],
            send_sem=y_send.at[offset],
            recv_sem=slot_recv.at[own_slot],
            device_id=(geo, z_pos, target),
            device_id_type=mesh_id,
        )
        copy.start()
        sends.append(copy)
    local = pltpu.make_async_copy(
        floored_ref.at[0, :, pl.ds(pl.multiple_of(y_pos * rows, rows), rows)],
        ext_ref.at[own_slot],
        local_sem.at[0],
    )
    local.start()

    @pl.when(z_pos == 0)
    def _():
        ext_ref[pl.ds(0, HALO)] = jnp.zeros((HALO,) + ext_ref.shape[1:], ext_ref.dtype)

    @pl.when(z_pos == z_count - 1)
    def _():
        ext_ref[pl.ds(HALO + y_count, HALO)] = jnp.zeros((HALO,) + ext_ref.shape[1:], ext_ref.dtype)

    def forward(slot, dst_slot, target_z):
        return pltpu.make_async_remote_copy(
            src_ref=ext_ref.at[slot],
            dst_ref=ext_ref.at[dst_slot],
            send_sem=z_send.at[slot - HALO],
            recv_sem=slot_recv.at[dst_slot],
            device_id=(geo, target_z, y_pos),
            device_id_type=mesh_id,
        )

    forwards = []
    for band in range(y_count):
        slot = HALO + band
        arrival = pltpu.make_async_remote_copy(
            src_ref=ext_ref.at[slot],
            dst_ref=ext_ref.at[slot],
            send_sem=y_send.at[0],
            recv_sem=slot_recv.at[slot],
            device_id=(geo, z_pos, lax.rem(y_pos + 1, y_count)),
            device_id_type=mesh_id,
        )

        @pl.when(y_pos == band)
        def _():
            local.wait()

        @pl.when(y_pos != band)
        def _():
            arrival.wait_recv()

        if band < HALO:
            fwd = forward(slot, slot + y_count, z_pos - 1)
            live = z_pos > 0
        elif band >= y_count - HALO:
            fwd = forward(slot, slot - y_count, z_pos + 1)
            live = z_pos < z_count - 1
        else:
            continue

        @pl.when(live)
        def _():
            fwd.start()

        forwards.append((fwd, live))
    for copy in sends:
        copy.wait_send()
    for fwd, live in forwards:

        @pl.when(live)
        def _():
            fwd.wait_send()

    for slot, live in ((0, z_pos > 0), (1, z_pos > 0),
                       (HALO + y_count, z_pos < z_count - 1), (HALO + y_count + 1, z_pos < z_count - 1)):
        incoming = pltpu.make_async_remote_copy(
            src_ref=ext_ref.at[slot],
            dst_ref=ext_ref.at[slot],
            send_sem=z_send.at[0],
            recv_sem=slot_recv.at[slot],
            device_id=(geo, lax.rem(z_pos + 1, z_count), y_pos),
            device_id_type=mesh_id,
        )

        @pl.when(live)
        def _():
            incoming.wait_recv()


def spread(floored, z_count, y_count):
    _, dirs, rows, cols = floored.shape
    part_rows = rows // y_count
    vmem = pl.BlockSpec(memory_space=pltpu.VMEM)
    slots = y_count + 2 * HALO
    return pl.pallas_call(
        functools.partial(_spread_kernel, z_count, y_count),
        out_shape=jax.ShapeDtypeStruct((slots, dirs, part_rows, cols), floored.dtype),
        in_specs=[vmem],
        out_specs=vmem,
        scratch_shapes=[
            pltpu.SemaphoreType.DMA((y_count,)),
            pltpu.SemaphoreType.DMA((1,)),
            pltpu.SemaphoreType.DMA((slots,)),
            pltpu.SemaphoreType.DMA((y_count,)),
        ],
        compiler_params=pltpu.CompilerParams(collective_id=1, has_side_effects=True),
    )(floored)


def shards(spectrum, land_sea, sea_index, sea_count, wind_speed, wind_dir, slope_x, slope_y):
    local_bands, dir_count, row_count, col_count = spectrum.shape
    z_count = lax.axis_size("z")
    y_count = lax.axis_size("y")
    z_pos = lax.axis_index("z")
    y_pos = lax.axis_index("y")
    spec_pos = z_pos * y_count + y_pos
    dtheta = 2.0 * math.pi / dir_count
    angles = (jnp.arange(dir_count).astype(jnp.float32) + 0.5) * dtheta
    face_angles = jnp.arange(dir_count + 1).astype(jnp.float32) * dtheta
    band_ids = (spec_pos * local_bands + jnp.arange(local_bands)).astype(jnp.float32)
    radian_freq, wavenum, courant, turn_rate, band_spread = band_table(band_ids)
    wet_mask = land_sea.astype(jnp.float32)
    density = spectrum * wet_mask
    padded = extended(density, (("geo", 2),), 2)
    density = (
        advect(padded, (courant[:, None] * jnp.cos(angles)[None, :])[:, :, None, None], 2)
        * wet_mask
    )
    padded = jnp.pad(density, ((0, 0), (0, 0), (0, 0), (2, 2)))
    density = (
        advect(padded, (courant[:, None] * jnp.sin(angles)[None, :])[:, :, None, None], 3)
        * wet_mask
    )
    turning = turn_rate[:, None, None, None] * (
        jnp.sin(face_angles)[None, :, None, None] * slope_x
        - jnp.cos(face_angles)[None, :, None, None] * slope_y
    )
    padded = jnp.concatenate([density[:, -2:], density, density[:, :2]], axis=1)
    floored = jnp.maximum(advect(padded, turning, 1), 0.0)
    ext = spread(floored, z_count, lax.axis_size("y"))
    point = ext[HALO:-HALO]
    group = point.shape[0]
    part_rows = point.shape[2]
    group_ids = (z_pos * group + jnp.arange(group)).astype(jnp.float32)
    radian_freq, wavenum, courant, turn_rate, band_spread = band_table(group_ids)
    scaled = point * (band_spread * dtheta)[:, None, None, None]
    sums = jnp.stack(
        [
            jnp.sum(scaled, axis=(0, 1)),
            jnp.sum(scaled / radian_freq[:, None, None, None], axis=(0, 1)),
            jnp.sum(scaled / jnp.sqrt(wavenum)[:, None, None, None], axis=(0, 1)),
        ]
    )
    step = 1
    while step < z_count:
        sums = sums + lax.ppermute(sums, "z", [(i, i ^ step) for i in range(z_count)])
        step *= 2
    energy_sum, first_sum, root_sum = sums[0], sums[1], sums[2]
    energy = energy_sum + EPSILON
    center, plus, minus = ext[1:-1], jnp.roll(ext[2:], -1, axis=1), jnp.roll(ext[:-2], 3, axis=1)
    cubic = center * center * (plus + minus) - 2.0 * center * plus * minus
    extra = (
        -2.0 * cubic[1:-1] + jnp.roll(cubic[:-2], 1, axis=1) + jnp.roll(cubic[2:], -3, axis=1)
    ) * (QUAD_COEF / (energy * energy))
    row_start = y_pos * part_rows
    wind_block = lax.dynamic_slice_in_dim(wind_speed, row_start, part_rows, axis=0)
    wind_angle = lax.dynamic_slice_in_dim(wind_dir, row_start, part_rows, axis=0)
    wet_block = lax.dynamic_slice_in_dim(wet_mask, row_start, part_rows, axis=0)
    cosine = jnp.cos(angles[:, None, None] - wind_angle[None])
    updated = (
        sources(
            point,
            energy_sum,
            first_sum,
            root_sum,
            radian_freq[:, None, None, None],
            wavenum[:, None, None, None],
            cosine,
            wind_block,
        )
        + extra
    ) * wet_block
    return lax.all_to_all(updated, "y", split_axis=0, concat_axis=2, tiled=True)


def solution(mesh):
    geo_count = mesh.shape["geo"]
    spec_count = mesh.shape["spec"]
    local = jax.sharding.Mesh(
        mesh.devices.reshape(geo_count, spec_count // Y_GROUP, Y_GROUP), ("geo", "z", "y")
    )
    spec = ("z", "y")
    placed = (
        P(spec, None, "geo", None),
        P("geo", None),
        P("geo", None),
        P("geo"),
        P("geo", None),
        P("geo", None),
        P("geo", None),
        P("geo", None),
    )
    return jax.shard_map(
        shards, mesh=local, in_specs=placed, out_specs=P(spec, None, "geo", None), check_vma=False
    )
```

```python
import functools
import math

import jax
import jax.numpy as jnp
from jax import lax
from jax.experimental import pallas as pl
from jax.experimental.pallas import tpu as pltpu
from jax.sharding import PartitionSpec as P

GRAVITY = 9.81
BASE_FREQ = 0.035
GROWTH = 1.1
COURANT_TOP = 0.9
TURN_TOP = 1.2
SPACING = 0.1
USTAR_RATIO = 0.035
WIND_COEF = 0.0375
WHITECAP = 0.36
STEEP_REF = 1.6
EPSILON = 1e-06
QUAD_COEF = 100.0


def extended(cells, sides, width):
    for axis, dim in sides:
        count = lax.axis_size(axis)
        ends = count - 1
        head = lax.slice_in_dim(cells, 0, width, axis=dim)
        tail = lax.slice_in_dim(cells, cells.shape[dim] - width, cells.shape[dim], axis=dim)
        cells = jnp.concatenate(
            [
                lax.ppermute(tail, axis, [(i, (i + 1) % count) for i in range(ends)]),
                cells,
                lax.ppermute(head, axis, [((i + 1) % count, i) for i in range(ends)]),
            ],
            axis=dim,
        )
    return cells


def band_table(band_ids):
    growth_factor = jnp.power(GROWTH, band_ids)
    radian_freq = 2.0 * math.pi * BASE_FREQ * growth_factor
    wavenum = radian_freq * radian_freq / GRAVITY
    return (
        radian_freq,
        wavenum,
        COURANT_TOP / growth_factor,
        TURN_TOP / growth_factor,
        SPACING * radian_freq,
    )


def quick_flux(far_left, near_left, near_right, far_right, courant):
    forward = courant >= 0
    upwind = jnp.where(forward, far_left, far_right)
    center = jnp.where(forward, near_left, near_right)
    downwind = jnp.where(forward, near_right, near_left)
    face_value = (
        0.5 * (center + downwind)
        - 0.5 * jnp.abs(courant) * (downwind - center)
        - (1.0 - courant * courant) / 6.0 * (downwind - 2.0 * center + upwind)
    )
    return courant * face_value


def advect(padded, courant, along):
    face_count = padded.shape[along] - 4
    shifted = [
        lax.slice_in_dim(padded, offset, offset + face_count + 1, axis=along) for offset in range(4)
    ]
    face_flux = quick_flux(shifted[0], shifted[1], shifted[2], shifted[3], courant)
    centre_cells = lax.slice_in_dim(padded, 2, 2 + face_count, axis=along)
    upper_flux = lax.slice_in_dim(face_flux, 1, face_count + 1, axis=along)
    lower_flux = lax.slice_in_dim(face_flux, 0, face_count, axis=along)
    return centre_cells - (upper_flux - lower_flux)


def quad_delta(center, above, below, energy, dir_axis):
    plus = jnp.roll(above, -1, axis=dir_axis)
    minus = jnp.roll(below, 3, axis=dir_axis)
    return (
        QUAD_COEF
        * (center * center * (plus + minus) - 2.0 * center * plus * minus)
        / (energy * energy)
    )


def quad_term(delta, delta_above, delta_below, dir_axis):
    return (
        -2.0 * delta
        + jnp.roll(delta_below, 1, axis=dir_axis)
        + jnp.roll(delta_above, -3, axis=dir_axis)
    )


def band_neighbours(values):
    empty = jnp.zeros((1,) + values.shape[1:], jnp.float32)
    return (
        jnp.concatenate([values[1:], empty], axis=0),
        jnp.concatenate([empty, values[:-1]], axis=0),
    )


def sources(density, energy_sum, first_sum, root_sum, radian_freq, wavenum, cosine, wind_speed):
    energy = energy_sum + EPSILON
    mean_sigma = energy / (first_sum + EPSILON)
    ratio_k = energy / (root_sum + EPSILON)
    mean_k = ratio_k * ratio_k
    steepness = energy * mean_k * mean_k / STEEP_REF
    decay_rate = WHITECAP * mean_sigma * (wavenum / mean_k) * steepness * steepness
    growth_rate = (
        WIND_COEF
        * radian_freq
        * jnp.maximum(28.0 * USTAR_RATIO * wind_speed * radian_freq / GRAVITY * cosine - 1.0, 0.0)
    )
    return density * (1.0 + growth_rate) / (1.0 + decay_rate)


def local_sources(point_block, wind_block, wind_angle, angles, dtheta):
    band_total = point_block.shape[0]
    band_ids = jnp.arange(band_total).astype(jnp.float32)
    radian_freq, wavenum, courant, turn_rate, band_spread = band_table(band_ids)
    scaled = point_block * (band_spread * dtheta)[:, None, None]
    energy_sum = jnp.sum(scaled, axis=(0, 1))
    first_sum = jnp.sum(scaled / radian_freq[:, None, None], axis=(0, 1))
    root_sum = jnp.sum(scaled / jnp.sqrt(wavenum)[:, None, None], axis=(0, 1))
    energy = energy_sum + EPSILON
    above, below = band_neighbours(point_block)
    delta = quad_delta(point_block, above, below, energy, 1)
    delta_above, delta_below = band_neighbours(delta)
    extra = quad_term(delta, delta_above, delta_below, 1)
    cosine = jnp.cos(angles[:, None] - wind_angle[None, :])
    return (
        sources(
            point_block,
            energy_sum,
            first_sum,
            root_sum,
            radian_freq[:, None, None],
            wavenum[:, None, None],
            cosine,
            wind_block,
        )
        + extra
    )


Y_GROUP = 4
HALO = 2


def _z_gather_kernel(z_count, part_ref, gathered_ref, gather_send, gather_recv):
    geo = lax.axis_index("geo")
    z_pos = lax.axis_index("z")
    y_pos = lax.axis_index("y")
    barrier = pltpu.get_barrier_semaphore()
    for offset in range(1, z_count):
        target = lax.rem(z_pos + offset, z_count)
        pl.semaphore_signal(barrier, inc=1, device_id=(geo, target, y_pos),
                            device_id_type=pl.DeviceIdType.MESH)
    pl.semaphore_wait(barrier, z_count - 1)
    copies = []
    for offset in range(1, z_count):
        target = lax.rem(z_pos + offset, z_count)
        copy = pltpu.make_async_remote_copy(
            src_ref=part_ref,
            dst_ref=gathered_ref.at[z_pos],
            send_sem=gather_send.at[offset],
            recv_sem=gather_recv.at[offset],
            device_id=(geo, target, y_pos),
            device_id_type=pl.DeviceIdType.MESH,
        )
        copy.start()
        copies.append(copy)
    gathered_ref[z_pos] = part_ref[...]
    for copy in copies:
        copy.wait_send()
        copy.wait_recv()


def z_gather(part, z_count):
    vmem = pl.BlockSpec(memory_space=pltpu.VMEM)
    return pl.pallas_call(
        functools.partial(_z_gather_kernel, z_count),
        out_shape=jax.ShapeDtypeStruct((z_count,) + part.shape, part.dtype),
        in_specs=[vmem],
        out_specs=vmem,
        scratch_shapes=[
            pltpu.SemaphoreType.DMA((z_count,)),
            pltpu.SemaphoreType.DMA((z_count,)),
        ],
        compiler_params=pltpu.CompilerParams(collective_id=0, has_side_effects=True),
    )(part)


def _spread_kernel(z_count, y_count, floored_ref, ext_ref, relay_ref, y_send, local_sem, slot_recv,
                   z_send, relay_send, relay_recv, pass_send, pass_recv):
    geo = lax.axis_index("geo")
    z_pos = lax.axis_index("z")
    y_pos = lax.axis_index("y")
    rows = ext_ref.shape[2]
    half = relay_ref.shape[1]
    mesh_id = pl.DeviceIdType.MESH
    up_y = lax.rem(y_pos + 1, y_count)
    down_y = lax.rem(y_pos + y_count - 1, y_count)
    barrier = pltpu.get_barrier_semaphore()
    for offset in range(1, y_count):
        pl.semaphore_signal(barrier, inc=1, device_id=(geo, z_pos, lax.rem(y_pos + offset, y_count)),
                            device_id_type=mesh_id)
    for step in (1, z_count - 1):
        pl.semaphore_signal(barrier, inc=1, device_id=(geo, lax.rem(z_pos + step, z_count), y_pos),
                            device_id_type=mesh_id)
    pl.semaphore_wait(barrier, y_count + 1)

    def quarter(target):
        return floored_ref.at[0, :, pl.ds(pl.multiple_of(target * rows, rows), rows)]

    own_slot = HALO + y_pos
    sends = []
    for offset in (1, y_count - 1):
        target = lax.rem(y_pos + offset, y_count)
        copy = pltpu.make_async_remote_copy(
            src_ref=quarter(target),
            dst_ref=ext_ref.at[own_slot],
            send_sem=y_send.at[offset],
            recv_sem=slot_recv.at[own_slot],
            device_id=(geo, z_pos, target),
            device_id_type=mesh_id,
        )
        copy.start()
        sends.append(copy)
    far = lax.rem(y_pos + 2, y_count)
    for side, via in ((0, up_y), (1, down_y)):
        copy = pltpu.make_async_remote_copy(
            src_ref=quarter(far).at[pl.ds(side * half, half)],
            dst_ref=relay_ref.at[side],
            send_sem=relay_send.at[side],
            recv_sem=relay_recv.at[side],
            device_id=(geo, z_pos, via),
            device_id_type=mesh_id,
        )
        copy.start()
        sends.append(copy)
    local = pltpu.make_async_copy(quarter(y_pos), ext_ref.at[own_slot], local_sem.at[0])
    local.start()

    @pl.when(z_pos == 0)
    def _():
        ext_ref[pl.ds(0, HALO)] = jnp.zeros((HALO,) + ext_ref.shape[1:], ext_ref.dtype)

    @pl.when(z_pos == z_count - 1)
    def _():
        ext_ref[pl.ds(HALO + y_count, HALO)] = jnp.zeros((HALO,) + ext_ref.shape[1:], ext_ref.dtype)

    passes = []
    for side, origin, onward in ((0, down_y, up_y), (1, up_y, down_y)):
        relay_in = pltpu.make_async_remote_copy(
            src_ref=relay_ref.at[side],
            dst_ref=relay_ref.at[side],
            send_sem=relay_send.at[side],
            recv_sem=relay_recv.at[side],
            device_id=(geo, z_pos, onward),
            device_id_type=mesh_id,
        )
        relay_in.wait_recv()
        onward_copy = pltpu.make_async_remote_copy(
            src_ref=relay_ref.at[side],
            dst_ref=ext_ref.at[HALO + origin, pl.ds(side * half, half)],
            send_sem=pass_send.at[side],
            recv_sem=pass_recv.at[side],
            device_id=(geo, z_pos, onward),
            device_id_type=mesh_id,
        )
        onward_copy.start()
        passes.append(onward_copy)

    def forward(slot, dst_slot, target_z):
        return pltpu.make_async_remote_copy(
            src_ref=ext_ref.at[slot],
            dst_ref=ext_ref.at[dst_slot],
            send_sem=z_send.at[slot - HALO],
            recv_sem=slot_recv.at[dst_slot],
            device_id=(geo, target_z, y_pos),
            device_id_type=mesh_id,
        )

    forwards = []
    for band in range(y_count):
        slot = HALO + band
        distance = lax.rem(band - y_pos + y_count, y_count)
        arrival = pltpu.make_async_remote_copy(
            src_ref=ext_ref.at[slot],
            dst_ref=ext_ref.at[slot],
            send_sem=y_send.at[0],
            recv_sem=slot_recv.at[slot],
            device_id=(geo, z_pos, up_y),
            device_id_type=mesh_id,
        )
        relayed = [
            pltpu.make_async_remote_copy(
                src_ref=ext_ref.at[slot, pl.ds(side * half, half)],
                dst_ref=ext_ref.at[slot, pl.ds(side * half, half)],
                send_sem=pass_send.at[side],
                recv_sem=pass_recv.at[side],
                device_id=(geo, z_pos, up_y),
                device_id_type=mesh_id,
            )
            for side in (0, 1)
        ]

        @pl.when(distance == 0)
        def _():
            local.wait()

        @pl.when((distance == 1) | (distance == y_count - 1))
        def _():
            arrival.wait_recv()

        @pl.when(distance == 2)
        def _():
            for copy in relayed:
                copy.wait_recv()

        if band < HALO:
            fwd = forward(slot, slot + y_count, z_pos - 1)
            live = z_pos > 0
        elif band >= y_count - HALO:
            fwd = forward(slot, slot - y_count, z_pos + 1)
            live = z_pos < z_count - 1
        else:
            continue

        @pl.when(live)
        def _():
            fwd.start()

        forwards.append((fwd, live))
    for copy in sends + passes:
        copy.wait_send()
    for fwd, live in forwards:

        @pl.when(live)
        def _():
            fwd.wait_send()

    for slot, live in ((0, z_pos > 0), (1, z_pos > 0),
                       (HALO + y_count, z_pos < z_count - 1), (HALO + y_count + 1, z_pos < z_count - 1)):
        incoming = pltpu.make_async_remote_copy(
            src_ref=ext_ref.at[slot],
            dst_ref=ext_ref.at[slot],
            send_sem=z_send.at[0],
            recv_sem=slot_recv.at[slot],
            device_id=(geo, lax.rem(z_pos + 1, z_count), y_pos),
            device_id_type=mesh_id,
        )

        @pl.when(live)
        def _():
            incoming.wait_recv()


def spread(floored, z_count, y_count):
    _, dirs, rows, cols = floored.shape
    part_rows = rows // y_count
    vmem = pl.BlockSpec(memory_space=pltpu.VMEM)
    slots = y_count + 2 * HALO
    half = dirs // 2
    assert 2 * half == dirs
    return pl.pallas_call(
        functools.partial(_spread_kernel, z_count, y_count),
        out_shape=jax.ShapeDtypeStruct((slots, dirs, part_rows, cols), floored.dtype),
        in_specs=[vmem],
        out_specs=vmem,
        scratch_shapes=[
            pltpu.VMEM((2, half, part_rows, cols), floored.dtype),
            pltpu.SemaphoreType.DMA((y_count,)),
            pltpu.SemaphoreType.DMA((1,)),
            pltpu.SemaphoreType.DMA((slots,)),
            pltpu.SemaphoreType.DMA((y_count,)),
            pltpu.SemaphoreType.DMA((2,)),
            pltpu.SemaphoreType.DMA((2,)),
            pltpu.SemaphoreType.DMA((2,)),
            pltpu.SemaphoreType.DMA((2,)),
        ],
        compiler_params=pltpu.CompilerParams(collective_id=1, has_side_effects=True),
    )(floored)


def extended(cells, sides, width):
    for axis, dim in sides:
        count = lax.axis_size(axis)
        ends = count - 1
        head = lax.slice_in_dim(cells, 0, width, axis=dim)
        tail = lax.slice_in_dim(cells, cells.shape[dim] - width, cells.shape[dim], axis=dim)
        cells = jnp.concatenate(
            [
                lax.ppermute(tail, axis, [(i, (i + 1) % count) for i in range(ends)]),
                cells,
                lax.ppermute(head, axis, [((i + 1) % count, i) for i in range(ends)]),
            ],
            axis=dim,
        )
    return cells


def band_table(band_ids):
    growth_factor = jnp.power(GROWTH, band_ids)
    radian_freq = 2.0 * math.pi * BASE_FREQ * growth_factor
    wavenum = radian_freq * radian_freq / GRAVITY
    return (
        radian_freq,
        wavenum,
        COURANT_TOP / growth_factor,
        TURN_TOP / growth_factor,
        SPACING * radian_freq,
    )


def quick_flux(far_left, near_left, near_right, far_right, courant):
    forward = courant >= 0
    upwind = jnp.where(forward, far_left, far_right)
    center = jnp.where(forward, near_left, near_right)
    downwind = jnp.where(forward, near_right, near_left)
    face_value = (
        0.5 * (center + downwind)
        - 0.5 * jnp.abs(courant) * (downwind - center)
        - (1.0 - courant * courant) / 6.0 * (downwind - 2.0 * center + upwind)
    )
    return courant * face_value


def advect(padded, courant, along):
    face_count = padded.shape[along] - 4
    shifted = [
        lax.slice_in_dim(padded, offset, offset + face_count + 1, axis=along) for offset in range(4)
    ]
    face_flux = quick_flux(shifted[0], shifted[1], shifted[2], shifted[3], courant)
    centre_cells = lax.slice_in_dim(padded, 2, 2 + face_count, axis=along)
    upper_flux = lax.slice_in_dim(face_flux, 1, face_count + 1, axis=along)
    lower_flux = lax.slice_in_dim(face_flux, 0, face_count, axis=along)
    return centre_cells - (upper_flux - lower_flux)


def quad_delta(center, above, below, energy, dir_axis):
    plus = jnp.roll(above, -1, axis=dir_axis)
    minus = jnp.roll(below, 3, axis=dir_axis)
    return (
        QUAD_COEF
        * (center * center * (plus + minus) - 2.0 * center * plus * minus)
        / (energy * energy)
    )


def quad_term(delta, delta_above, delta_below, dir_axis):
    return (
        -2.0 * delta
        + jnp.roll(delta_below, 1, axis=dir_axis)
        + jnp.roll(delta_above, -3, axis=dir_axis)
    )


def band_neighbours(values):
    empty = jnp.zeros((1,) + values.shape[1:], jnp.float32)
    return (
        jnp.concatenate([values[1:], empty], axis=0),
        jnp.concatenate([empty, values[:-1]], axis=0),
    )


def sources(density, energy_sum, first_sum, root_sum, radian_freq, wavenum, cosine, wind_speed):
    energy = energy_sum + EPSILON
    mean_sigma = energy / (first_sum + EPSILON)
    ratio_k = energy / (root_sum + EPSILON)
    mean_k = ratio_k * ratio_k
    steepness = energy * mean_k * mean_k / STEEP_REF
    decay_rate = WHITECAP * mean_sigma * (wavenum / mean_k) * steepness * steepness
    growth_rate = (
        WIND_COEF
        * radian_freq
        * jnp.maximum(28.0 * USTAR_RATIO * wind_speed * radian_freq / GRAVITY * cosine - 1.0, 0.0)
    )
    return density * (1.0 + growth_rate) / (1.0 + decay_rate)


def local_sources(point_block, wind_block, wind_angle, angles, dtheta):
    band_total = point_block.shape[0]
    band_ids = jnp.arange(band_total).astype(jnp.float32)
    radian_freq, wavenum, courant, turn_rate, band_spread = band_table(band_ids)
    scaled = point_block * (band_spread * dtheta)[:, None, None]
    energy_sum = jnp.sum(scaled, axis=(0, 1))
    first_sum = jnp.sum(scaled / radian_freq[:, None, None], axis=(0, 1))
    root_sum = jnp.sum(scaled / jnp.sqrt(wavenum)[:, None, None], axis=(0, 1))
    energy = energy_sum + EPSILON
    above, below = band_neighbours(point_block)
    delta = quad_delta(point_block, above, below, energy, 1)
    delta_above, delta_below = band_neighbours(delta)
    extra = quad_term(delta, delta_above, delta_below, 1)
    cosine = jnp.cos(angles[:, None] - wind_angle[None, :])
    return (
        sources(
            point_block,
            energy_sum,
            first_sum,
            root_sum,
            radian_freq[:, None, None],
            wavenum[:, None, None],
            cosine,
            wind_block,
        )
        + extra
    )


Y_GROUP = 4
HALO = 2


def _z_gather_kernel(z_count, part_ref, gathered_ref, gather_send, gather_recv):
    geo = lax.axis_index("geo")
    z_pos = lax.axis_index("z")
    y_pos = lax.axis_index("y")
    barrier = pltpu.get_barrier_semaphore()
    for offset in range(1, z_count):
        target = lax.rem(z_pos + offset, z_count)
        pl.semaphore_signal(barrier, inc=1, device_id=(geo, target, y_pos),
                            device_id_type=pl.DeviceIdType.MESH)
    pl.semaphore_wait(barrier, z_count - 1)
    copies = []
    for offset in range(1, z_count):
        target = lax.rem(z_pos + offset, z_count)
        copy = pltpu.make_async_remote_copy(
            src_ref=part_ref,
            dst_ref=gathered_ref.at[z_pos],
            send_sem=gather_send.at[offset],
            recv_sem=gather_recv.at[offset],
            device_id=(geo, target, y_pos),
            device_id_type=pl.DeviceIdType.MESH,
        )
        copy.start()
        copies.append(copy)
    gathered_ref[z_pos] = part_ref[...]
    for copy in copies:
        copy.wait_send()
        copy.wait_recv()


def z_gather(part, z_count):
    vmem = pl.BlockSpec(memory_space=pltpu.VMEM)
    return pl.pallas_call(
        functools.partial(_z_gather_kernel, z_count),
        out_shape=jax.ShapeDtypeStruct((z_count,) + part.shape, part.dtype),
        in_specs=[vmem],
        out_specs=vmem,
        scratch_shapes=[
            pltpu.SemaphoreType.DMA((z_count,)),
            pltpu.SemaphoreType.DMA((z_count,)),
        ],
        compiler_params=pltpu.CompilerParams(collective_id=0, has_side_effects=True),
    )(part)


def _spread_kernel(z_count, y_count, floored_ref, ext_ref, y_send, local_sem, slot_recv, z_send):
    geo = lax.axis_index("geo")
    z_pos = lax.axis_index("z")
    y_pos = lax.axis_index("y")
    rows = ext_ref.shape[2]
    mesh_id = pl.DeviceIdType.MESH
    barrier = pltpu.get_barrier_semaphore()
    for offset in range(1, y_count):
        pl.semaphore_signal(barrier, inc=1, device_id=(geo, z_pos, lax.rem(y_pos + offset, y_count)),
                            device_id_type=mesh_id)

    for step in (1, z_count - 1):
        pl.semaphore_signal(barrier, inc=1, device_id=(geo, lax.rem(z_pos + step, z_count), y_pos),
                            device_id_type=mesh_id)
    pl.semaphore_wait(barrier, y_count + 1)

    own_slot = HALO + y_pos
    sends = []
    for offset in range(1, y_count):
        target = lax.rem(y_pos + offset, y_count)
        copy = pltpu.make_async_remote_copy(
            src_ref=floored_ref.at[0, :, pl.ds(pl.multiple_of(target * rows, rows), rows)],
            dst_ref=ext_ref.at[own_slot],
            send_sem=y_send.at[offset],
            recv_sem=slot_recv.at[own_slot],
            device_id=(geo, z_pos, target),
            device_id_type=mesh_id,
        )
        copy.start()
        sends.append(copy)
    local = pltpu.make_async_copy(
        floored_ref.at[0, :, pl.ds(pl.multiple_of(y_pos * rows, rows), rows)],
        ext_ref.at[own_slot],
        local_sem.at[0],
    )
    local.start()

    @pl.when(z_pos == 0)
    def _():
        ext_ref[pl.ds(0, HALO)] = jnp.zeros((HALO,) + ext_ref.shape[1:], ext_ref.dtype)

    @pl.when(z_pos == z_count - 1)
    def _():
        ext_ref[pl.ds(HALO + y_count, HALO)] = jnp.zeros((HALO,) + ext_ref.shape[1:], ext_ref.dtype)

    def forward(slot, dst_slot, target_z):
        return pltpu.make_async_remote_copy(
            src_ref=ext_ref.at[slot],
            dst_ref=ext_ref.at[dst_slot],
            send_sem=z_send.at[slot - HALO],
            recv_sem=slot_recv.at[dst_slot],
            device_id=(geo, target_z, y_pos),
            device_id_type=mesh_id,
        )

    forwards = []
    for band in range(y_count):
        slot = HALO + band
        arrival = pltpu.make_async_remote_copy(
            src_ref=ext_ref.at[slot],
            dst_ref=ext_ref.at[slot],
            send_sem=y_send.at[0],
            recv_sem=slot_recv.at[slot],
            device_id=(geo, z_pos, lax.rem(y_pos + 1, y_count)),
            device_id_type=mesh_id,
        )

        @pl.when(y_pos == band)
        def _():
            local.wait()

        @pl.when(y_pos != band)
        def _():
            arrival.wait_recv()

        if band < HALO:
            fwd = forward(slot, slot + y_count, z_pos - 1)
            live = z_pos > 0
        elif band >= y_count - HALO:
            fwd = forward(slot, slot - y_count, z_pos + 1)
            live = z_pos < z_count - 1
        else:
            continue

        @pl.when(live)
        def _():
            fwd.start()

        forwards.append((fwd, live))
    for copy in sends:
        copy.wait_send()
    for fwd, live in forwards:

        @pl.when(live)
        def _():
            fwd.wait_send()

    for slot, live in ((0, z_pos > 0), (1, z_pos > 0),
                       (HALO + y_count, z_pos < z_count - 1), (HALO + y_count + 1, z_pos < z_count - 1)):
        incoming = pltpu.make_async_remote_copy(
            src_ref=ext_ref.at[slot],
            dst_ref=ext_ref.at[slot],
            send_sem=z_send.at[0],
            recv_sem=slot_recv.at[slot],
            device_id=(geo, lax.rem(z_pos + 1, z_count), y_pos),
            device_id_type=mesh_id,
        )

        @pl.when(live)
        def _():
            incoming.wait_recv()


def spread(floored, z_count, y_count):
    _, dirs, rows, cols = floored.shape
    part_rows = rows // y_count
    vmem = pl.BlockSpec(memory_space=pltpu.VMEM)
    slots = y_count + 2 * HALO
    return pl.pallas_call(
        functools.partial(_spread_kernel, z_count, y_count),
        out_shape=jax.ShapeDtypeStruct((slots, dirs, part_rows, cols), floored.dtype),
        in_specs=[vmem],
        out_specs=vmem,
        scratch_shapes=[
            pltpu.SemaphoreType.DMA((y_count,)),
            pltpu.SemaphoreType.DMA((1,)),
            pltpu.SemaphoreType.DMA((slots,)),
            pltpu.SemaphoreType.DMA((y_count,)),
        ],
        compiler_params=pltpu.CompilerParams(collective_id=1, has_side_effects=True),
    )(floored)


def shards(spectrum, land_sea, sea_index, sea_count, wind_speed, wind_dir, slope_x, slope_y):
    local_bands, dir_count, row_count, col_count = spectrum.shape
    z_count = lax.axis_size("z")
    y_count = lax.axis_size("y")
    z_pos = lax.axis_index("z")
    y_pos = lax.axis_index("y")
    spec_pos = z_pos * y_count + y_pos
    dtheta = 2.0 * math.pi / dir_count
    angles = (jnp.arange(dir_count).astype(jnp.float32) + 0.5) * dtheta
    face_angles = jnp.arange(dir_count + 1).astype(jnp.float32) * dtheta
    band_ids = (spec_pos * local_bands + jnp.arange(local_bands)).astype(jnp.float32)
    radian_freq, wavenum, courant, turn_rate, band_spread = band_table(band_ids)
    wet_mask = land_sea.astype(jnp.float32)
    density = spectrum * wet_mask
    padded = extended(density, (("geo", 2),), 2)
    density = (
        advect(padded, (courant[:, None] * jnp.cos(angles)[None, :])[:, :, None, None], 2)
        * wet_mask
    )
    padded = jnp.pad(density, ((0, 0), (0, 0), (0, 0), (2, 2)))
    density = (
        advect(padded, (courant[:, None] * jnp.sin(angles)[None, :])[:, :, None, None], 3)
        * wet_mask
    )
    turning = turn_rate[:, None, None, None] * (
        jnp.sin(face_angles)[None, :, None, None] * slope_x
        - jnp.cos(face_angles)[None, :, None, None] * slope_y
    )
    padded = jnp.concatenate([density[:, -2:], density, density[:, :2]], axis=1)
    floored = jnp.maximum(advect(padded, turning, 1), 0.0)
    ext = spread(floored, z_count, lax.axis_size("y"))
    point = ext[HALO:-HALO]
    group = point.shape[0]
    part_rows = point.shape[2]
    group_ids = (z_pos * group + jnp.arange(group)).astype(jnp.float32)
    radian_freq, wavenum, courant, turn_rate, band_spread = band_table(group_ids)
    scaled = point * (band_spread * dtheta)[:, None, None, None]
    sums = jnp.stack(
        [
            jnp.sum(scaled, axis=(0, 1)),
            jnp.sum(scaled / radian_freq[:, None, None, None], axis=(0, 1)),
            jnp.sum(scaled / jnp.sqrt(wavenum)[:, None, None, None], axis=(0, 1)),
        ]
    )
    step = 1
    while step < z_count:
        sums = sums + lax.ppermute(sums, "z", [(i, i ^ step) for i in range(z_count)])
        step *= 2
    energy_sum, first_sum, root_sum = sums[0], sums[1], sums[2]
    energy = energy_sum + EPSILON
    center, plus, minus = ext[1:-1], jnp.roll(ext[2:], -1, axis=1), jnp.roll(ext[:-2], 3, axis=1)
    cubic = center * center * (plus + minus) - 2.0 * center * plus * minus
    extra = (
        -2.0 * cubic[1:-1] + jnp.roll(cubic[:-2], 1, axis=1) + jnp.roll(cubic[2:], -3, axis=1)
    ) * (QUAD_COEF / (energy * energy))
    row_start = y_pos * part_rows
    wind_block = lax.dynamic_slice_in_dim(wind_speed, row_start, part_rows, axis=0)
    wind_angle = lax.dynamic_slice_in_dim(wind_dir, row_start, part_rows, axis=0)
    wet_block = lax.dynamic_slice_in_dim(wet_mask, row_start, part_rows, axis=0)
    cosine = jnp.cos(angles[:, None, None] - wind_angle[None])
    updated = (
        sources(
            point,
            energy_sum,
            first_sum,
            root_sum,
            radian_freq[:, None, None, None],
            wavenum[:, None, None, None],
            cosine,
            wind_block,
        )
        + extra
    ) * wet_block
    return lax.all_to_all(updated, "y", split_axis=0, concat_axis=2, tiled=True)


def solution(mesh):
    geo_count = mesh.shape["geo"]
    spec_count = mesh.shape["spec"]
    local = jax.sharding.Mesh(
        mesh.devices.reshape(geo_count, spec_count // Y_GROUP, Y_GROUP), ("geo", "z", "y")
    )
    spec = ("z", "y")
    placed = (
        P(spec, None, "geo", None),
        P("geo", None),
        P("geo", None),
        P("geo"),
        P("geo", None),
        P("geo", None),
        P("geo", None),
        P("geo", None),
    )
    return jax.shard_map(
        shards, mesh=local, in_specs=placed, out_specs=P(spec, None, "geo", None), check_vma=False
    )
```

```python
import functools
import math

import jax
import jax.numpy as jnp
from jax import lax
from jax.experimental import pallas as pl
from jax.experimental.pallas import tpu as pltpu
from jax.sharding import PartitionSpec as P

GRAVITY = 9.81
BASE_FREQ = 0.035
GROWTH = 1.1
COURANT_TOP = 0.9
TURN_TOP = 1.2
SPACING = 0.1
USTAR_RATIO = 0.035
WIND_COEF = 0.0375
WHITECAP = 0.36
STEEP_REF = 1.6
EPSILON = 1e-06
QUAD_COEF = 100.0


def extended(cells, sides, width):
    for axis, dim in sides:
        count = lax.axis_size(axis)
        ends = count - 1
        head = lax.slice_in_dim(cells, 0, width, axis=dim)
        tail = lax.slice_in_dim(cells, cells.shape[dim] - width, cells.shape[dim], axis=dim)
        cells = jnp.concatenate(
            [
                lax.ppermute(tail, axis, [(i, (i + 1) % count) for i in range(ends)]),
                cells,
                lax.ppermute(head, axis, [((i + 1) % count, i) for i in range(ends)]),
            ],
            axis=dim,
        )
    return cells


def band_table(band_ids):
    growth_factor = jnp.power(GROWTH, band_ids)
    radian_freq = 2.0 * math.pi * BASE_FREQ * growth_factor
    wavenum = radian_freq * radian_freq / GRAVITY
    return (
        radian_freq,
        wavenum,
        COURANT_TOP / growth_factor,
        TURN_TOP / growth_factor,
        SPACING * radian_freq,
    )


def quick_flux(far_left, near_left, near_right, far_right, courant):
    forward = courant >= 0
    upwind = jnp.where(forward, far_left, far_right)
    center = jnp.where(forward, near_left, near_right)
    downwind = jnp.where(forward, near_right, near_left)
    face_value = (
        0.5 * (center + downwind)
        - 0.5 * jnp.abs(courant) * (downwind - center)
        - (1.0 - courant * courant) / 6.0 * (downwind - 2.0 * center + upwind)
    )
    return courant * face_value


def advect(padded, courant, along):
    face_count = padded.shape[along] - 4
    shifted = [
        lax.slice_in_dim(padded, offset, offset + face_count + 1, axis=along) for offset in range(4)
    ]
    face_flux = quick_flux(shifted[0], shifted[1], shifted[2], shifted[3], courant)
    centre_cells = lax.slice_in_dim(padded, 2, 2 + face_count, axis=along)
    upper_flux = lax.slice_in_dim(face_flux, 1, face_count + 1, axis=along)
    lower_flux = lax.slice_in_dim(face_flux, 0, face_count, axis=along)
    return centre_cells - (upper_flux - lower_flux)


def quad_delta(center, above, below, energy, dir_axis):
    plus = jnp.roll(above, -1, axis=dir_axis)
    minus = jnp.roll(below, 3, axis=dir_axis)
    return (
        QUAD_COEF
        * (center * center * (plus + minus) - 2.0 * center * plus * minus)
        / (energy * energy)
    )


def quad_term(delta, delta_above, delta_below, dir_axis):
    return (
        -2.0 * delta
        + jnp.roll(delta_below, 1, axis=dir_axis)
        + jnp.roll(delta_above, -3, axis=dir_axis)
    )


def band_neighbours(values):
    empty = jnp.zeros((1,) + values.shape[1:], jnp.float32)
    return (
        jnp.concatenate([values[1:], empty], axis=0),
        jnp.concatenate([empty, values[:-1]], axis=0),
    )


def sources(density, energy_sum, first_sum, root_sum, radian_freq, wavenum, cosine, wind_speed):
    energy = energy_sum + EPSILON
    mean_sigma = energy / (first_sum + EPSILON)
    ratio_k = energy / (root_sum + EPSILON)
    mean_k = ratio_k * ratio_k
    steepness = energy * mean_k * mean_k / STEEP_REF
    decay_rate = WHITECAP * mean_sigma * (wavenum / mean_k) * steepness * steepness
    growth_rate = (
        WIND_COEF
        * radian_freq
        * jnp.maximum(28.0 * USTAR_RATIO * wind_speed * radian_freq / GRAVITY * cosine - 1.0, 0.0)
    )
    return density * (1.0 + growth_rate) / (1.0 + decay_rate)


def local_sources(point_block, wind_block, wind_angle, angles, dtheta):
    band_total = point_block.shape[0]
    band_ids = jnp.arange(band_total).astype(jnp.float32)
    radian_freq, wavenum, courant, turn_rate, band_spread = band_table(band_ids)
    scaled = point_block * (band_spread * dtheta)[:, None, None]
    energy_sum = jnp.sum(scaled, axis=(0, 1))
    first_sum = jnp.sum(scaled / radian_freq[:, None, None], axis=(0, 1))
    root_sum = jnp.sum(scaled / jnp.sqrt(wavenum)[:, None, None], axis=(0, 1))
    energy = energy_sum + EPSILON
    above, below = band_neighbours(point_block)
    delta = quad_delta(point_block, above, below, energy, 1)
    delta_above, delta_below = band_neighbours(delta)
    extra = quad_term(delta, delta_above, delta_below, 1)
    cosine = jnp.cos(angles[:, None] - wind_angle[None, :])
    return (
        sources(
            point_block,
            energy_sum,
            first_sum,
            root_sum,
            radian_freq[:, None, None],
            wavenum[:, None, None],
            cosine,
            wind_block,
        )
        + extra
    )


Y_GROUP = 4
HALO = 2
SPREAD_CHUNKS = 4


def _z_gather_kernel(z_count, part_ref, gathered_ref, gather_send, gather_recv):
    geo = lax.axis_index("geo")
    z_pos = lax.axis_index("z")
    y_pos = lax.axis_index("y")
    barrier = pltpu.get_barrier_semaphore()
    for offset in range(1, z_count):
        target = lax.rem(z_pos + offset, z_count)
        pl.semaphore_signal(barrier, inc=1, device_id=(geo, target, y_pos),
                            device_id_type=pl.DeviceIdType.MESH)
    pl.semaphore_wait(barrier, z_count - 1)
    copies = []
    for offset in range(1, z_count):
        target = lax.rem(z_pos + offset, z_count)
        copy = pltpu.make_async_remote_copy(
            src_ref=part_ref,
            dst_ref=gathered_ref.at[z_pos],
            send_sem=gather_send.at[offset],
            recv_sem=gather_recv.at[offset],
            device_id=(geo, target, y_pos),
            device_id_type=pl.DeviceIdType.MESH,
        )
        copy.start()
        copies.append(copy)
    gathered_ref[z_pos] = part_ref[...]
    for copy in copies:
        copy.wait_send()
        copy.wait_recv()


def z_gather(part, z_count):
    vmem = pl.BlockSpec(memory_space=pltpu.VMEM)
    return pl.pallas_call(
        functools.partial(_z_gather_kernel, z_count),
        out_shape=jax.ShapeDtypeStruct((z_count,) + part.shape, part.dtype),
        in_specs=[vmem],
        out_specs=vmem,
        scratch_shapes=[
            pltpu.SemaphoreType.DMA((z_count,)),
            pltpu.SemaphoreType.DMA((z_count,)),
        ],
        compiler_params=pltpu.CompilerParams(collective_id=0, has_side_effects=True),
    )(part)


def _spread_kernel(z_count, y_count, chunks, floored_ref, ext_ref, y_send, local_sem, slot_recv, z_send):
    geo = lax.axis_index("geo")
    z_pos = lax.axis_index("z")
    y_pos = lax.axis_index("y")
    rows = ext_ref.shape[2]
    width = ext_ref.shape[1] // chunks
    mesh_id = pl.DeviceIdType.MESH
    barrier = pltpu.get_barrier_semaphore()
    for offset in range(1, y_count):
        pl.semaphore_signal(barrier, inc=1, device_id=(geo, z_pos, lax.rem(y_pos + offset, y_count)),
                            device_id_type=mesh_id)
    for step in (1, z_count - 1):
        pl.semaphore_signal(barrier, inc=1, device_id=(geo, lax.rem(z_pos + step, z_count), y_pos),
                            device_id_type=mesh_id)
    pl.semaphore_wait(barrier, y_count + 1)

    own_slot = HALO + y_pos

    def planes(chunk):
        return pl.ds(chunk * width, width)

    def y_sends(chunk):
        copies = []
        for offset in range(1, y_count):
            target = lax.rem(y_pos + offset, y_count)
            copies.append(pltpu.make_async_remote_copy(
                src_ref=floored_ref.at[0, planes(chunk), pl.ds(pl.multiple_of(target * rows, rows), rows)],
                dst_ref=ext_ref.at[own_slot, planes(chunk)],
                send_sem=y_send.at[offset * chunks + chunk],
                recv_sem=slot_recv.at[own_slot * chunks + chunk],
                device_id=(geo, z_pos, target),
                device_id_type=mesh_id,
            ))
        copies.append(pltpu.make_async_copy(
            floored_ref.at[0, planes(chunk), pl.ds(pl.multiple_of(y_pos * rows, rows), rows)],
            ext_ref.at[own_slot, planes(chunk)],
            local_sem.at[chunk],
        ))
        return copies

    def forward(slot, dst_slot, target_z, chunk):
        return pltpu.make_async_remote_copy(
            src_ref=ext_ref.at[slot, planes(chunk)],
            dst_ref=ext_ref.at[dst_slot, planes(chunk)],
            send_sem=z_send.at[(slot - HALO) * chunks + chunk],
            recv_sem=slot_recv.at[dst_slot * chunks + chunk],
            device_id=(geo, target_z, y_pos),
            device_id_type=mesh_id,
        )

    @pl.when(z_pos == 0)
    def _():
        ext_ref[pl.ds(0, HALO)] = jnp.zeros((HALO,) + ext_ref.shape[1:], ext_ref.dtype)

    @pl.when(z_pos == z_count - 1)
    def _():
        ext_ref[pl.ds(HALO + y_count, HALO)] = jnp.zeros((HALO,) + ext_ref.shape[1:], ext_ref.dtype)

    pending = y_sends(0)
    for copy in pending:
        copy.start()
    forwards = []
    for chunk in range(chunks):
        for band in range(y_count):
            slot = HALO + band
            arrival = pltpu.make_async_remote_copy(
                src_ref=ext_ref.at[slot, planes(chunk)],
                dst_ref=ext_ref.at[slot, planes(chunk)],
                send_sem=y_send.at[chunk],
                recv_sem=slot_recv.at[slot * chunks + chunk],
                device_id=(geo, z_pos, lax.rem(y_pos + 1, y_count)),
                device_id_type=mesh_id,
            )
            local = pending[-1]

            @pl.when(y_pos == band)
            def _():
                local.wait()

            @pl.when(y_pos != band)
            def _():
                arrival.wait_recv()

            if band < HALO:
                fwd = forward(slot, slot + y_count, z_pos - 1, chunk)
                live = z_pos > 0
            elif band >= y_count - HALO:
                fwd = forward(slot, slot - y_count, z_pos + 1, chunk)
                live = z_pos < z_count - 1
            else:
                continue

            @pl.when(live)
            def _():
                fwd.start()

            forwards.append((fwd, live))
        for copy in pending[:-1]:
            copy.wait_send()
        if chunk + 1 < chunks:
            pending = y_sends(chunk + 1)
            for copy in pending:
                copy.start()
    for fwd, live in forwards:

        @pl.when(live)
        def _():
            fwd.wait_send()

    for chunk in range(chunks):
        for slot, live in ((0, z_pos > 0), (1, z_pos > 0),
                           (HALO + y_count, z_pos < z_count - 1), (HALO + y_count + 1, z_pos < z_count - 1)):
            incoming = pltpu.make_async_remote_copy(
                src_ref=ext_ref.at[slot, planes(chunk)],
                dst_ref=ext_ref.at[slot, planes(chunk)],
                send_sem=z_send.at[chunk],
                recv_sem=slot_recv.at[slot * chunks + chunk],
                device_id=(geo, lax.rem(z_pos + 1, z_count), y_pos),
                device_id_type=mesh_id,
            )

            @pl.when(live)
            def _():
                incoming.wait_recv()


def spread(floored, z_count, y_count):
    _, dirs, rows, cols = floored.shape
    part_rows = rows // y_count
    chunks = SPREAD_CHUNKS
    assert dirs % chunks == 0
    vmem = pl.BlockSpec(memory_space=pltpu.VMEM)
    slots = y_count + 2 * HALO
    return pl.pallas_call(
        functools.partial(_spread_kernel, z_count, y_count, chunks),
        out_shape=jax.ShapeDtypeStruct((slots, dirs, part_rows, cols), floored.dtype),
        in_specs=[vmem],
        out_specs=vmem,
        scratch_shapes=[
            pltpu.SemaphoreType.DMA((y_count * chunks,)),
            pltpu.SemaphoreType.DMA((chunks,)),
            pltpu.SemaphoreType.DMA((slots * chunks,)),
            pltpu.SemaphoreType.DMA((y_count * chunks,)),
        ],
        compiler_params=pltpu.CompilerParams(collective_id=1, has_side_effects=True),
    )(floored)


def extended(cells, sides, width):
    for axis, dim in sides:
        count = lax.axis_size(axis)
        ends = count - 1
        head = lax.slice_in_dim(cells, 0, width, axis=dim)
        tail = lax.slice_in_dim(cells, cells.shape[dim] - width, cells.shape[dim], axis=dim)
        cells = jnp.concatenate(
            [
                lax.ppermute(tail, axis, [(i, (i + 1) % count) for i in range(ends)]),
                cells,
                lax.ppermute(head, axis, [((i + 1) % count, i) for i in range(ends)]),
            ],
            axis=dim,
        )
    return cells


def band_table(band_ids):
    growth_factor = jnp.power(GROWTH, band_ids)
    radian_freq = 2.0 * math.pi * BASE_FREQ * growth_factor
    wavenum = radian_freq * radian_freq / GRAVITY
    return (
        radian_freq,
        wavenum,
        COURANT_TOP / growth_factor,
        TURN_TOP / growth_factor,
        SPACING * radian_freq,
    )


def quick_flux(far_left, near_left, near_right, far_right, courant):
    forward = courant >= 0
    upwind = jnp.where(forward, far_left, far_right)
    center = jnp.where(forward, near_left, near_right)
    downwind = jnp.where(forward, near_right, near_left)
    face_value = (
        0.5 * (center + downwind)
        - 0.5 * jnp.abs(courant) * (downwind - center)
        - (1.0 - courant * courant) / 6.0 * (downwind - 2.0 * center + upwind)
    )
    return courant * face_value


def advect(padded, courant, along):
    face_count = padded.shape[along] - 4
    shifted = [
        lax.slice_in_dim(padded, offset, offset + face_count + 1, axis=along) for offset in range(4)
    ]
    face_flux = quick_flux(shifted[0], shifted[1], shifted[2], shifted[3], courant)
    centre_cells = lax.slice_in_dim(padded, 2, 2 + face_count, axis=along)
    upper_flux = lax.slice_in_dim(face_flux, 1, face_count + 1, axis=along)
    lower_flux = lax.slice_in_dim(face_flux, 0, face_count, axis=along)
    return centre_cells - (upper_flux - lower_flux)


def quad_delta(center, above, below, energy, dir_axis):
    plus = jnp.roll(above, -1, axis=dir_axis)
    minus = jnp.roll(below, 3, axis=dir_axis)
    return (
        QUAD_COEF
        * (center * center * (plus + minus) - 2.0 * center * plus * minus)
        / (energy * energy)
    )


def quad_term(delta, delta_above, delta_below, dir_axis):
    return (
        -2.0 * delta
        + jnp.roll(delta_below, 1, axis=dir_axis)
        + jnp.roll(delta_above, -3, axis=dir_axis)
    )


def band_neighbours(values):
    empty = jnp.zeros((1,) + values.shape[1:], jnp.float32)
    return (
        jnp.concatenate([values[1:], empty], axis=0),
        jnp.concatenate([empty, values[:-1]], axis=0),
    )


def sources(density, energy_sum, first_sum, root_sum, radian_freq, wavenum, cosine, wind_speed):
    energy = energy_sum + EPSILON
    mean_sigma = energy / (first_sum + EPSILON)
    ratio_k = energy / (root_sum + EPSILON)
    mean_k = ratio_k * ratio_k
    steepness = energy * mean_k * mean_k / STEEP_REF
    decay_rate = WHITECAP * mean_sigma * (wavenum / mean_k) * steepness * steepness
    growth_rate = (
        WIND_COEF
        * radian_freq
        * jnp.maximum(28.0 * USTAR_RATIO * wind_speed * radian_freq / GRAVITY * cosine - 1.0, 0.0)
    )
    return density * (1.0 + growth_rate) / (1.0 + decay_rate)


def local_sources(point_block, wind_block, wind_angle, angles, dtheta):
    band_total = point_block.shape[0]
    band_ids = jnp.arange(band_total).astype(jnp.float32)
    radian_freq, wavenum, courant, turn_rate, band_spread = band_table(band_ids)
    scaled = point_block * (band_spread * dtheta)[:, None, None]
    energy_sum = jnp.sum(scaled, axis=(0, 1))
    first_sum = jnp.sum(scaled / radian_freq[:, None, None], axis=(0, 1))
    root_sum = jnp.sum(scaled / jnp.sqrt(wavenum)[:, None, None], axis=(0, 1))
    energy = energy_sum + EPSILON
    above, below = band_neighbours(point_block)
    delta = quad_delta(point_block, above, below, energy, 1)
    delta_above, delta_below = band_neighbours(delta)
    extra = quad_term(delta, delta_above, delta_below, 1)
    cosine = jnp.cos(angles[:, None] - wind_angle[None, :])
    return (
        sources(
            point_block,
            energy_sum,
            first_sum,
            root_sum,
            radian_freq[:, None, None],
            wavenum[:, None, None],
            cosine,
            wind_block,
        )
        + extra
    )


Y_GROUP = 4
HALO = 2


def _z_gather_kernel(z_count, part_ref, gathered_ref, gather_send, gather_recv):
    geo = lax.axis_index("geo")
    z_pos = lax.axis_index("z")
    y_pos = lax.axis_index("y")
    barrier = pltpu.get_barrier_semaphore()
    for offset in range(1, z_count):
        target = lax.rem(z_pos + offset, z_count)
        pl.semaphore_signal(barrier, inc=1, device_id=(geo, target, y_pos),
                            device_id_type=pl.DeviceIdType.MESH)
    pl.semaphore_wait(barrier, z_count - 1)
    copies = []
    for offset in range(1, z_count):
        target = lax.rem(z_pos + offset, z_count)
        copy = pltpu.make_async_remote_copy(
            src_ref=part_ref,
            dst_ref=gathered_ref.at[z_pos],
            send_sem=gather_send.at[offset],
            recv_sem=gather_recv.at[offset],
            device_id=(geo, target, y_pos),
            device_id_type=pl.DeviceIdType.MESH,
        )
        copy.start()
        copies.append(copy)
    gathered_ref[z_pos] = part_ref[...]
    for copy in copies:
        copy.wait_send()
        copy.wait_recv()


def z_gather(part, z_count):
    vmem = pl.BlockSpec(memory_space=pltpu.VMEM)
    return pl.pallas_call(
        functools.partial(_z_gather_kernel, z_count),
        out_shape=jax.ShapeDtypeStruct((z_count,) + part.shape, part.dtype),
        in_specs=[vmem],
        out_specs=vmem,
        scratch_shapes=[
            pltpu.SemaphoreType.DMA((z_count,)),
            pltpu.SemaphoreType.DMA((z_count,)),
        ],
        compiler_params=pltpu.CompilerParams(collective_id=0, has_side_effects=True),
    )(part)


def _spread_kernel(z_count, y_count, floored_ref, ext_ref, relay_ref, y_send, local_sem, slot_recv,
                   z_send, relay_send, relay_recv, pass_send, pass_recv):
    geo = lax.axis_index("geo")
    z_pos = lax.axis_index("z")
    y_pos = lax.axis_index("y")
    rows = ext_ref.shape[2]
    half = relay_ref.shape[1]
    mesh_id = pl.DeviceIdType.MESH
    up_y = lax.rem(y_pos + 1, y_count)
    down_y = lax.rem(y_pos + y_count - 1, y_count)
    barrier = pltpu.get_barrier_semaphore()
    for offset in range(1, y_count):
        pl.semaphore_signal(barrier, inc=1, device_id=(geo, z_pos, lax.rem(y_pos + offset, y_count)),
                            device_id_type=mesh_id)
    for step in (1, z_count - 1):
        pl.semaphore_signal(barrier, inc=1, device_id=(geo, lax.rem(z_pos + step, z_count), y_pos),
                            device_id_type=mesh_id)
    pl.semaphore_wait(barrier, y_count + 1)

    def quarter(target):
        return floored_ref.at[0, :, pl.ds(pl.multiple_of(target * rows, rows), rows)]

    own_slot = HALO + y_pos
    sends = []
    for offset in (1, y_count - 1):
        target = lax.rem(y_pos + offset, y_count)
        copy = pltpu.make_async_remote_copy(
            src_ref=quarter(target),
            dst_ref=ext_ref.at[own_slot],
            send_sem=y_send.at[offset],
            recv_sem=slot_recv.at[own_slot],
            device_id=(geo, z_pos, target),
            device_id_type=mesh_id,
        )
        copy.start()
        sends.append(copy)
    far = lax.rem(y_pos + 2, y_count)
    for side, via in ((0, up_y), (1, down_y)):
        copy = pltpu.make_async_remote_copy(
            src_ref=quarter(far).at[pl.ds(side * half, half)],
            dst_ref=relay_ref.at[side],
            send_sem=relay_send.at[side],
            recv_sem=relay_recv.at[side],
            device_id=(geo, z_pos, via),
            device_id_type=mesh_id,
        )
        copy.start()
        sends.append(copy)
    local = pltpu.make_async_copy(quarter(y_pos), ext_ref.at[own_slot], local_sem.at[0])
    local.start()

    @pl.when(z_pos == 0)
    def _():
        ext_ref[pl.ds(0, HALO)] = jnp.zeros((HALO,) + ext_ref.shape[1:], ext_ref.dtype)

    @pl.when(z_pos == z_count - 1)
    def _():
        ext_ref[pl.ds(HALO + y_count, HALO)] = jnp.zeros((HALO,) + ext_ref.shape[1:], ext_ref.dtype)

    passes = []
    for side, origin, onward in ((0, down_y, up_y), (1, up_y, down_y)):
        relay_in = pltpu.make_async_remote_copy(
            src_ref=relay_ref.at[side],
            dst_ref=relay_ref.at[side],
            send_sem=relay_send.at[side],
            recv_sem=relay_recv.at[side],
            device_id=(geo, z_pos, onward),
            device_id_type=mesh_id,
        )
        relay_in.wait_recv()
        onward_copy = pltpu.make_async_remote_copy(
            src_ref=relay_ref.at[side],
            dst_ref=ext_ref.at[HALO + origin, pl.ds(side * half, half)],
            send_sem=pass_send.at[side],
            recv_sem=pass_recv.at[side],
            device_id=(geo, z_pos, onward),
            device_id_type=mesh_id,
        )
        onward_copy.start()
        passes.append(onward_copy)

    def forward(slot, dst_slot, target_z):
        return pltpu.make_async_remote_copy(
            src_ref=ext_ref.at[slot],
            dst_ref=ext_ref.at[dst_slot],
            send_sem=z_send.at[slot - HALO],
            recv_sem=slot_recv.at[dst_slot],
            device_id=(geo, target_z, y_pos),
            device_id_type=mesh_id,
        )

    forwards = []
    for band in range(y_count):
        slot = HALO + band
        distance = lax.rem(band - y_pos + y_count, y_count)
        arrival = pltpu.make_async_remote_copy(
            src_ref=ext_ref.at[slot],
            dst_ref=ext_ref.at[slot],
            send_sem=y_send.at[0],
            recv_sem=slot_recv.at[slot],
            device_id=(geo, z_pos, up_y),
            device_id_type=mesh_id,
        )
        relayed = [
            pltpu.make_async_remote_copy(
                src_ref=ext_ref.at[slot, pl.ds(side * half, half)],
                dst_ref=ext_ref.at[slot, pl.ds(side * half, half)],
                send_sem=pass_send.at[side],
                recv_sem=pass_recv.at[side],
                device_id=(geo, z_pos, up_y),
                device_id_type=mesh_id,
            )
            for side in (0, 1)
        ]

        @pl.when(distance == 0)
        def _():
            local.wait()

        @pl.when((distance == 1) | (distance == y_count - 1))
        def _():
            arrival.wait_recv()

        @pl.when(distance == 2)
        def _():
            for copy in relayed:
                copy.wait_recv()

        if band < HALO:
            fwd = forward(slot, slot + y_count, z_pos - 1)
            live = z_pos > 0
        elif band >= y_count - HALO:
            fwd = forward(slot, slot - y_count, z_pos + 1)
            live = z_pos < z_count - 1
        else:
            continue

        @pl.when(live)
        def _():
            fwd.start()

        forwards.append((fwd, live))
    for copy in sends + passes:
        copy.wait_send()
    for fwd, live in forwards:

        @pl.when(live)
        def _():
            fwd.wait_send()

    for slot, live in ((0, z_pos > 0), (1, z_pos > 0),
                       (HALO + y_count, z_pos < z_count - 1), (HALO + y_count + 1, z_pos < z_count - 1)):
        incoming = pltpu.make_async_remote_copy(
            src_ref=ext_ref.at[slot],
            dst_ref=ext_ref.at[slot],
            send_sem=z_send.at[0],
            recv_sem=slot_recv.at[slot],
            device_id=(geo, lax.rem(z_pos + 1, z_count), y_pos),
            device_id_type=mesh_id,
        )

        @pl.when(live)
        def _():
            incoming.wait_recv()


def spread(floored, z_count, y_count):
    _, dirs, rows, cols = floored.shape
    part_rows = rows // y_count
    vmem = pl.BlockSpec(memory_space=pltpu.VMEM)
    slots = y_count + 2 * HALO
    half = dirs // 2
    assert 2 * half == dirs
    return pl.pallas_call(
        functools.partial(_spread_kernel, z_count, y_count),
        out_shape=jax.ShapeDtypeStruct((slots, dirs, part_rows, cols), floored.dtype),
        in_specs=[vmem],
        out_specs=vmem,
        scratch_shapes=[
            pltpu.VMEM((2, half, part_rows, cols), floored.dtype),
            pltpu.SemaphoreType.DMA((y_count,)),
            pltpu.SemaphoreType.DMA((1,)),
            pltpu.SemaphoreType.DMA((slots,)),
            pltpu.SemaphoreType.DMA((y_count,)),
            pltpu.SemaphoreType.DMA((2,)),
            pltpu.SemaphoreType.DMA((2,)),
            pltpu.SemaphoreType.DMA((2,)),
            pltpu.SemaphoreType.DMA((2,)),
        ],
        compiler_params=pltpu.CompilerParams(collective_id=1, has_side_effects=True),
    )(floored)


def extended(cells, sides, width):
    for axis, dim in sides:
        count = lax.axis_size(axis)
        ends = count - 1
        head = lax.slice_in_dim(cells, 0, width, axis=dim)
        tail = lax.slice_in_dim(cells, cells.shape[dim] - width, cells.shape[dim], axis=dim)
        cells = jnp.concatenate(
            [
                lax.ppermute(tail, axis, [(i, (i + 1) % count) for i in range(ends)]),
                cells,
                lax.ppermute(head, axis, [((i + 1) % count, i) for i in range(ends)]),
            ],
            axis=dim,
        )
    return cells


def band_table(band_ids):
    growth_factor = jnp.power(GROWTH, band_ids)
    radian_freq = 2.0 * math.pi * BASE_FREQ * growth_factor
    wavenum = radian_freq * radian_freq / GRAVITY
    return (
        radian_freq,
        wavenum,
        COURANT_TOP / growth_factor,
        TURN_TOP / growth_factor,
        SPACING * radian_freq,
    )


def quick_flux(far_left, near_left, near_right, far_right, courant):
    forward = courant >= 0
    upwind = jnp.where(forward, far_left, far_right)
    center = jnp.where(forward, near_left, near_right)
    downwind = jnp.where(forward, near_right, near_left)
    face_value = (
        0.5 * (center + downwind)
        - 0.5 * jnp.abs(courant) * (downwind - center)
        - (1.0 - courant * courant) / 6.0 * (downwind - 2.0 * center + upwind)
    )
    return courant * face_value


def advect(padded, courant, along):
    face_count = padded.shape[along] - 4
    shifted = [
        lax.slice_in_dim(padded, offset, offset + face_count + 1, axis=along) for offset in range(4)
    ]
    face_flux = quick_flux(shifted[0], shifted[1], shifted[2], shifted[3], courant)
    centre_cells = lax.slice_in_dim(padded, 2, 2 + face_count, axis=along)
    upper_flux = lax.slice_in_dim(face_flux, 1, face_count + 1, axis=along)
    lower_flux = lax.slice_in_dim(face_flux, 0, face_count, axis=along)
    return centre_cells - (upper_flux - lower_flux)


def quad_delta(center, above, below, energy, dir_axis):
    plus = jnp.roll(above, -1, axis=dir_axis)
    minus = jnp.roll(below, 3, axis=dir_axis)
    return (
        QUAD_COEF
        * (center * center * (plus + minus) - 2.0 * center * plus * minus)
        / (energy * energy)
    )


def quad_term(delta, delta_above, delta_below, dir_axis):
    return (
        -2.0 * delta
        + jnp.roll(delta_below, 1, axis=dir_axis)
        + jnp.roll(delta_above, -3, axis=dir_axis)
    )


def band_neighbours(values):
    empty = jnp.zeros((1,) + values.shape[1:], jnp.float32)
    return (
        jnp.concatenate([values[1:], empty], axis=0),
        jnp.concatenate([empty, values[:-1]], axis=0),
    )


def sources(density, energy_sum, first_sum, root_sum, radian_freq, wavenum, cosine, wind_speed):
    energy = energy_sum + EPSILON
    mean_sigma = energy / (first_sum + EPSILON)
    ratio_k = energy / (root_sum + EPSILON)
    mean_k = ratio_k * ratio_k
    steepness = energy * mean_k * mean_k / STEEP_REF
    decay_rate = WHITECAP * mean_sigma * (wavenum / mean_k) * steepness * steepness
    growth_rate = (
        WIND_COEF
        * radian_freq
        * jnp.maximum(28.0 * USTAR_RATIO * wind_speed * radian_freq / GRAVITY * cosine - 1.0, 0.0)
    )
    return density * (1.0 + growth_rate) / (1.0 + decay_rate)


def local_sources(point_block, wind_block, wind_angle, angles, dtheta):
    band_total = point_block.shape[0]
    band_ids = jnp.arange(band_total).astype(jnp.float32)
    radian_freq, wavenum, courant, turn_rate, band_spread = band_table(band_ids)
    scaled = point_block * (band_spread * dtheta)[:, None, None]
    energy_sum = jnp.sum(scaled, axis=(0, 1))
    first_sum = jnp.sum(scaled / radian_freq[:, None, None], axis=(0, 1))
    root_sum = jnp.sum(scaled / jnp.sqrt(wavenum)[:, None, None], axis=(0, 1))
    energy = energy_sum + EPSILON
    above, below = band_neighbours(point_block)
    delta = quad_delta(point_block, above, below, energy, 1)
    delta_above, delta_below = band_neighbours(delta)
    extra = quad_term(delta, delta_above, delta_below, 1)
    cosine = jnp.cos(angles[:, None] - wind_angle[None, :])
    return (
        sources(
            point_block,
            energy_sum,
            first_sum,
            root_sum,
            radian_freq[:, None, None],
            wavenum[:, None, None],
            cosine,
            wind_block,
        )
        + extra
    )


Y_GROUP = 4
HALO = 2


def _z_gather_kernel(z_count, part_ref, gathered_ref, gather_send, gather_recv):
    geo = lax.axis_index("geo")
    z_pos = lax.axis_index("z")
    y_pos = lax.axis_index("y")
    barrier = pltpu.get_barrier_semaphore()
    for offset in range(1, z_count):
        target = lax.rem(z_pos + offset, z_count)
        pl.semaphore_signal(barrier, inc=1, device_id=(geo, target, y_pos),
                            device_id_type=pl.DeviceIdType.MESH)
    pl.semaphore_wait(barrier, z_count - 1)
    copies = []
    for offset in range(1, z_count):
        target = lax.rem(z_pos + offset, z_count)
        copy = pltpu.make_async_remote_copy(
            src_ref=part_ref,
            dst_ref=gathered_ref.at[z_pos],
            send_sem=gather_send.at[offset],
            recv_sem=gather_recv.at[offset],
            device_id=(geo, target, y_pos),
            device_id_type=pl.DeviceIdType.MESH,
        )
        copy.start()
        copies.append(copy)
    gathered_ref[z_pos] = part_ref[...]
    for copy in copies:
        copy.wait_send()
        copy.wait_recv()


def z_gather(part, z_count):
    vmem = pl.BlockSpec(memory_space=pltpu.VMEM)
    return pl.pallas_call(
        functools.partial(_z_gather_kernel, z_count),
        out_shape=jax.ShapeDtypeStruct((z_count,) + part.shape, part.dtype),
        in_specs=[vmem],
        out_specs=vmem,
        scratch_shapes=[
            pltpu.SemaphoreType.DMA((z_count,)),
            pltpu.SemaphoreType.DMA((z_count,)),
        ],
        compiler_params=pltpu.CompilerParams(collective_id=0, has_side_effects=True),
    )(part)


def _spread_kernel(z_count, y_count, floored_ref, ext_ref, y_send, local_sem, slot_recv, z_send):
    geo = lax.axis_index("geo")
    z_pos = lax.axis_index("z")
    y_pos = lax.axis_index("y")
    rows = ext_ref.shape[2]
    mesh_id = pl.DeviceIdType.MESH
    barrier = pltpu.get_barrier_semaphore()
    for offset in range(1, y_count):
        pl.semaphore_signal(barrier, inc=1, device_id=(geo, z_pos, lax.rem(y_pos + offset, y_count)),
                            device_id_type=mesh_id)

    for step in (1, z_count - 1):
        pl.semaphore_signal(barrier, inc=1, device_id=(geo, lax.rem(z_pos + step, z_count), y_pos),
                            device_id_type=mesh_id)
    pl.semaphore_wait(barrier, y_count + 1)

    own_slot = HALO + y_pos
    sends = []
    for offset in range(1, y_count):
        target = lax.rem(y_pos + offset, y_count)
        copy = pltpu.make_async_remote_copy(
            src_ref=floored_ref.at[0, :, pl.ds(pl.multiple_of(target * rows, rows), rows)],
            dst_ref=ext_ref.at[own_slot],
            send_sem=y_send.at[offset],
            recv_sem=slot_recv.at[own_slot],
            device_id=(geo, z_pos, target),
            device_id_type=mesh_id,
        )
        copy.start()
        sends.append(copy)
    local = pltpu.make_async_copy(
        floored_ref.at[0, :, pl.ds(pl.multiple_of(y_pos * rows, rows), rows)],
        ext_ref.at[own_slot],
        local_sem.at[0],
    )
    local.start()

    @pl.when(z_pos == 0)
    def _():
        ext_ref[pl.ds(0, HALO)] = jnp.zeros((HALO,) + ext_ref.shape[1:], ext_ref.dtype)

    @pl.when(z_pos == z_count - 1)
    def _():
        ext_ref[pl.ds(HALO + y_count, HALO)] = jnp.zeros((HALO,) + ext_ref.shape[1:], ext_ref.dtype)

    def forward(slot, dst_slot, target_z):
        return pltpu.make_async_remote_copy(
            src_ref=ext_ref.at[slot],
            dst_ref=ext_ref.at[dst_slot],
            send_sem=z_send.at[slot - HALO],
            recv_sem=slot_recv.at[dst_slot],
            device_id=(geo, target_z, y_pos),
            device_id_type=mesh_id,
        )

    forwards = []
    for band in range(y_count):
        slot = HALO + band
        arrival = pltpu.make_async_remote_copy(
            src_ref=ext_ref.at[slot],
            dst_ref=ext_ref.at[slot],
            send_sem=y_send.at[0],
            recv_sem=slot_recv.at[slot],
            device_id=(geo, z_pos, lax.rem(y_pos + 1, y_count)),
            device_id_type=mesh_id,
        )

        @pl.when(y_pos == band)
        def _():
            local.wait()

        @pl.when(y_pos != band)
        def _():
            arrival.wait_recv()

        if band < HALO:
            fwd = forward(slot, slot + y_count, z_pos - 1)
            live = z_pos > 0
        elif band >= y_count - HALO:
            fwd = forward(slot, slot - y_count, z_pos + 1)
            live = z_pos < z_count - 1
        else:
            continue

        @pl.when(live)
        def _():
            fwd.start()

        forwards.append((fwd, live))
    for copy in sends:
        copy.wait_send()
    for fwd, live in forwards:

        @pl.when(live)
        def _():
            fwd.wait_send()

    for slot, live in ((0, z_pos > 0), (1, z_pos > 0),
                       (HALO + y_count, z_pos < z_count - 1), (HALO + y_count + 1, z_pos < z_count - 1)):
        incoming = pltpu.make_async_remote_copy(
            src_ref=ext_ref.at[slot],
            dst_ref=ext_ref.at[slot],
            send_sem=z_send.at[0],
            recv_sem=slot_recv.at[slot],
            device_id=(geo, lax.rem(z_pos + 1, z_count), y_pos),
            device_id_type=mesh_id,
        )

        @pl.when(live)
        def _():
            incoming.wait_recv()


def spread(floored, z_count, y_count):
    _, dirs, rows, cols = floored.shape
    part_rows = rows // y_count
    vmem = pl.BlockSpec(memory_space=pltpu.VMEM)
    slots = y_count + 2 * HALO
    return pl.pallas_call(
        functools.partial(_spread_kernel, z_count, y_count),
        out_shape=jax.ShapeDtypeStruct((slots, dirs, part_rows, cols), floored.dtype),
        in_specs=[vmem],
        out_specs=vmem,
        scratch_shapes=[
            pltpu.SemaphoreType.DMA((y_count,)),
            pltpu.SemaphoreType.DMA((1,)),
            pltpu.SemaphoreType.DMA((slots,)),
            pltpu.SemaphoreType.DMA((y_count,)),
        ],
        compiler_params=pltpu.CompilerParams(collective_id=1, has_side_effects=True),
    )(floored)


def shards(spectrum, land_sea, sea_index, sea_count, wind_speed, wind_dir, slope_x, slope_y):
    local_bands, dir_count, row_count, col_count = spectrum.shape
    z_count = lax.axis_size("z")
    y_count = lax.axis_size("y")
    z_pos = lax.axis_index("z")
    y_pos = lax.axis_index("y")
    spec_pos = z_pos * y_count + y_pos
    dtheta = 2.0 * math.pi / dir_count
    angles = (jnp.arange(dir_count).astype(jnp.float32) + 0.5) * dtheta
    face_angles = jnp.arange(dir_count + 1).astype(jnp.float32) * dtheta
    band_ids = (spec_pos * local_bands + jnp.arange(local_bands)).astype(jnp.float32)
    radian_freq, wavenum, courant, turn_rate, band_spread = band_table(band_ids)
    wet_mask = land_sea.astype(jnp.float32)
    density = spectrum * wet_mask
    padded = extended(density, (("geo", 2),), 2)
    density = (
        advect(padded, (courant[:, None] * jnp.cos(angles)[None, :])[:, :, None, None], 2)
        * wet_mask
    )
    padded = jnp.pad(density, ((0, 0), (0, 0), (0, 0), (2, 2)))
    density = (
        advect(padded, (courant[:, None] * jnp.sin(angles)[None, :])[:, :, None, None], 3)
        * wet_mask
    )
    turning = turn_rate[:, None, None, None] * (
        jnp.sin(face_angles)[None, :, None, None] * slope_x
        - jnp.cos(face_angles)[None, :, None, None] * slope_y
    )
    padded = jnp.concatenate([density[:, -2:], density, density[:, :2]], axis=1)
    floored = jnp.maximum(advect(padded, turning, 1), 0.0)
    ext = spread(floored, z_count, lax.axis_size("y"))
    point = ext[HALO:-HALO]
    group = point.shape[0]
    part_rows = point.shape[2]
    group_ids = (z_pos * group + jnp.arange(group)).astype(jnp.float32)
    radian_freq, wavenum, courant, turn_rate, band_spread = band_table(group_ids)
    scaled = point * (band_spread * dtheta)[:, None, None, None]
    sums = jnp.stack(
        [
            jnp.sum(scaled, axis=(0, 1)),
            jnp.sum(scaled / radian_freq[:, None, None, None], axis=(0, 1)),
            jnp.sum(scaled / jnp.sqrt(wavenum)[:, None, None, None], axis=(0, 1)),
        ]
    )
    step = 1
    while step < z_count:
        sums = sums + lax.ppermute(sums, "z", [(i, i ^ step) for i in range(z_count)])
        step *= 2
    energy_sum, first_sum, root_sum = sums[0], sums[1], sums[2]
    energy = energy_sum + EPSILON
    center, plus, minus = ext[1:-1], jnp.roll(ext[2:], -1, axis=1), jnp.roll(ext[:-2], 3, axis=1)
    cubic = center * center * (plus + minus) - 2.0 * center * plus * minus
    extra = (
        -2.0 * cubic[1:-1] + jnp.roll(cubic[:-2], 1, axis=1) + jnp.roll(cubic[2:], -3, axis=1)
    ) * (QUAD_COEF / (energy * energy))
    row_start = y_pos * part_rows
    wind_block = lax.dynamic_slice_in_dim(wind_speed, row_start, part_rows, axis=0)
    wind_angle = lax.dynamic_slice_in_dim(wind_dir, row_start, part_rows, axis=0)
    wet_block = lax.dynamic_slice_in_dim(wet_mask, row_start, part_rows, axis=0)
    cosine = jnp.cos(angles[:, None, None] - wind_angle[None])
    updated = (
        sources(
            point,
            energy_sum,
            first_sum,
            root_sum,
            radian_freq[:, None, None, None],
            wavenum[:, None, None, None],
            cosine,
            wind_block,
        )
        + extra
    ) * wet_block
    return lax.all_to_all(updated, "y", split_axis=0, concat_axis=2, tiled=True)


def solution(mesh):
    geo_count = mesh.shape["geo"]
    spec_count = mesh.shape["spec"]
    local = jax.sharding.Mesh(
        mesh.devices.reshape(geo_count, spec_count // Y_GROUP, Y_GROUP), ("geo", "z", "y")
    )
    spec = ("z", "y")
    placed = (
        P(spec, None, "geo", None),
        P("geo", None),
        P("geo", None),
        P("geo"),
        P("geo", None),
        P("geo", None),
        P("geo", None),
        P("geo", None),
    )
    return jax.shard_map(
        shards, mesh=local, in_specs=placed, out_specs=P(spec, None, "geo", None), check_vma=False
    )
```

```python
import functools
import math

import jax
import jax.numpy as jnp
from jax import lax
from jax.experimental import pallas as pl
from jax.experimental.pallas import tpu as pltpu
from jax.sharding import PartitionSpec as P

GRAVITY = 9.81
BASE_FREQ = 0.035
GROWTH = 1.1
COURANT_TOP = 0.9
TURN_TOP = 1.2
SPACING = 0.1
USTAR_RATIO = 0.035
WIND_COEF = 0.0375
WHITECAP = 0.36
STEEP_REF = 1.6
EPSILON = 1e-06
QUAD_COEF = 100.0


def extended(cells, sides, width):
    for axis, dim in sides:
        count = lax.axis_size(axis)
        ends = count - 1
        head = lax.slice_in_dim(cells, 0, width, axis=dim)
        tail = lax.slice_in_dim(cells, cells.shape[dim] - width, cells.shape[dim], axis=dim)
        cells = jnp.concatenate(
            [
                lax.ppermute(tail, axis, [(i, (i + 1) % count) for i in range(ends)]),
                cells,
                lax.ppermute(head, axis, [((i + 1) % count, i) for i in range(ends)]),
            ],
            axis=dim,
        )
    return cells


def band_table(band_ids):
    growth_factor = jnp.power(GROWTH, band_ids)
    radian_freq = 2.0 * math.pi * BASE_FREQ * growth_factor
    wavenum = radian_freq * radian_freq / GRAVITY
    return (
        radian_freq,
        wavenum,
        COURANT_TOP / growth_factor,
        TURN_TOP / growth_factor,
        SPACING * radian_freq,
    )


def quick_flux(far_left, near_left, near_right, far_right, courant):
    forward = courant >= 0
    upwind = jnp.where(forward, far_left, far_right)
    center = jnp.where(forward, near_left, near_right)
    downwind = jnp.where(forward, near_right, near_left)
    face_value = (
        0.5 * (center + downwind)
        - 0.5 * jnp.abs(courant) * (downwind - center)
        - (1.0 - courant * courant) / 6.0 * (downwind - 2.0 * center + upwind)
    )
    return courant * face_value


def advect(padded, courant, along):
    face_count = padded.shape[along] - 4
    shifted = [
        lax.slice_in_dim(padded, offset, offset + face_count + 1, axis=along) for offset in range(4)
    ]
    face_flux = quick_flux(shifted[0], shifted[1], shifted[2], shifted[3], courant)
    centre_cells = lax.slice_in_dim(padded, 2, 2 + face_count, axis=along)
    upper_flux = lax.slice_in_dim(face_flux, 1, face_count + 1, axis=along)
    lower_flux = lax.slice_in_dim(face_flux, 0, face_count, axis=along)
    return centre_cells - (upper_flux - lower_flux)


def quad_delta(center, above, below, energy, dir_axis):
    plus = jnp.roll(above, -1, axis=dir_axis)
    minus = jnp.roll(below, 3, axis=dir_axis)
    return (
        QUAD_COEF
        * (center * center * (plus + minus) - 2.0 * center * plus * minus)
        / (energy * energy)
    )


def quad_term(delta, delta_above, delta_below, dir_axis):
    return (
        -2.0 * delta
        + jnp.roll(delta_below, 1, axis=dir_axis)
        + jnp.roll(delta_above, -3, axis=dir_axis)
    )


def band_neighbours(values):
    empty = jnp.zeros((1,) + values.shape[1:], jnp.float32)
    return (
        jnp.concatenate([values[1:], empty], axis=0),
        jnp.concatenate([empty, values[:-1]], axis=0),
    )


def sources(density, energy_sum, first_sum, root_sum, radian_freq, wavenum, cosine, wind_speed):
    energy = energy_sum + EPSILON
    mean_sigma = energy / (first_sum + EPSILON)
    ratio_k = energy / (root_sum + EPSILON)
    mean_k = ratio_k * ratio_k
    steepness = energy * mean_k * mean_k / STEEP_REF
    decay_rate = WHITECAP * mean_sigma * (wavenum / mean_k) * steepness * steepness
    growth_rate = (
        WIND_COEF
        * radian_freq
        * jnp.maximum(28.0 * USTAR_RATIO * wind_speed * radian_freq / GRAVITY * cosine - 1.0, 0.0)
    )
    return density * (1.0 + growth_rate) / (1.0 + decay_rate)


def local_sources(point_block, wind_block, wind_angle, angles, dtheta):
    band_total = point_block.shape[0]
    band_ids = jnp.arange(band_total).astype(jnp.float32)
    radian_freq, wavenum, courant, turn_rate, band_spread = band_table(band_ids)
    scaled = point_block * (band_spread * dtheta)[:, None, None]
    energy_sum = jnp.sum(scaled, axis=(0, 1))
    first_sum = jnp.sum(scaled / radian_freq[:, None, None], axis=(0, 1))
    root_sum = jnp.sum(scaled / jnp.sqrt(wavenum)[:, None, None], axis=(0, 1))
    energy = energy_sum + EPSILON
    above, below = band_neighbours(point_block)
    delta = quad_delta(point_block, above, below, energy, 1)
    delta_above, delta_below = band_neighbours(delta)
    extra = quad_term(delta, delta_above, delta_below, 1)
    cosine = jnp.cos(angles[:, None] - wind_angle[None, :])
    return (
        sources(
            point_block,
            energy_sum,
            first_sum,
            root_sum,
            radian_freq[:, None, None],
            wavenum[:, None, None],
            cosine,
            wind_block,
        )
        + extra
    )


Y_GROUP = 4
HALO = 2
SPREAD_CHUNKS = 4


def _z_gather_kernel(z_count, part_ref, gathered_ref, gather_send, gather_recv):
    geo = lax.axis_index("geo")
    z_pos = lax.axis_index("z")
    y_pos = lax.axis_index("y")
    barrier = pltpu.get_barrier_semaphore()
    for offset in range(1, z_count):
        target = lax.rem(z_pos + offset, z_count)
        pl.semaphore_signal(barrier, inc=1, device_id=(geo, target, y_pos),
                            device_id_type=pl.DeviceIdType.MESH)
    pl.semaphore_wait(barrier, z_count - 1)
    copies = []
    for offset in range(1, z_count):
        target = lax.rem(z_pos + offset, z_count)
        copy = pltpu.make_async_remote_copy(
            src_ref=part_ref,
            dst_ref=gathered_ref.at[z_pos],
            send_sem=gather_send.at[offset],
            recv_sem=gather_recv.at[offset],
            device_id=(geo, target, y_pos),
            device_id_type=pl.DeviceIdType.MESH,
        )
        copy.start()
        copies.append(copy)
    gathered_ref[z_pos] = part_ref[...]
    for copy in copies:
        copy.wait_send()
        copy.wait_recv()


def z_gather(part, z_count):
    vmem = pl.BlockSpec(memory_space=pltpu.VMEM)
    return pl.pallas_call(
        functools.partial(_z_gather_kernel, z_count),
        out_shape=jax.ShapeDtypeStruct((z_count,) + part.shape, part.dtype),
        in_specs=[vmem],
        out_specs=vmem,
        scratch_shapes=[
            pltpu.SemaphoreType.DMA((z_count,)),
            pltpu.SemaphoreType.DMA((z_count,)),
        ],
        compiler_params=pltpu.CompilerParams(collective_id=0, has_side_effects=True),
    )(part)


def _spread_kernel(z_count, y_count, chunks, floored_ref, ext_ref, y_send, local_sem, slot_recv, z_send):
    geo = lax.axis_index("geo")
    z_pos = lax.axis_index("z")
    y_pos = lax.axis_index("y")
    rows = ext_ref.shape[2]
    width = ext_ref.shape[1] // chunks
    mesh_id = pl.DeviceIdType.MESH
    barrier = pltpu.get_barrier_semaphore()
    for offset in range(1, y_count):
        pl.semaphore_signal(barrier, inc=1, device_id=(geo, z_pos, lax.rem(y_pos + offset, y_count)),
                            device_id_type=mesh_id)
    for step in (1, z_count - 1):
        pl.semaphore_signal(barrier, inc=1, device_id=(geo, lax.rem(z_pos + step, z_count), y_pos),
                            device_id_type=mesh_id)
    pl.semaphore_wait(barrier, y_count + 1)

    own_slot = HALO + y_pos

    def planes(chunk):
        return pl.ds(chunk * width, width)

    def y_sends(chunk):
        copies = []
        for offset in range(1, y_count):
            target = lax.rem(y_pos + offset, y_count)
            copies.append(pltpu.make_async_remote_copy(
                src_ref=floored_ref.at[0, planes(chunk), pl.ds(pl.multiple_of(target * rows, rows), rows)],
                dst_ref=ext_ref.at[own_slot, planes(chunk)],
                send_sem=y_send.at[offset * chunks + chunk],
                recv_sem=slot_recv.at[own_slot * chunks + chunk],
                device_id=(geo, z_pos, target),
                device_id_type=mesh_id,
            ))
        copies.append(pltpu.make_async_copy(
            floored_ref.at[0, planes(chunk), pl.ds(pl.multiple_of(y_pos * rows, rows), rows)],
            ext_ref.at[own_slot, planes(chunk)],
            local_sem.at[chunk],
        ))
        return copies

    def forward(slot, dst_slot, target_z, chunk):
        return pltpu.make_async_remote_copy(
            src_ref=ext_ref.at[slot, planes(chunk)],
            dst_ref=ext_ref.at[dst_slot, planes(chunk)],
            send_sem=z_send.at[(slot - HALO) * chunks + chunk],
            recv_sem=slot_recv.at[dst_slot * chunks + chunk],
            device_id=(geo, target_z, y_pos),
            device_id_type=mesh_id,
        )

    @pl.when(z_pos == 0)
    def _():
        ext_ref[pl.ds(0, HALO)] = jnp.zeros((HALO,) + ext_ref.shape[1:], ext_ref.dtype)

    @pl.when(z_pos == z_count - 1)
    def _():
        ext_ref[pl.ds(HALO + y_count, HALO)] = jnp.zeros((HALO,) + ext_ref.shape[1:], ext_ref.dtype)

    pending = y_sends(0)
    for copy in pending:
        copy.start()
    forwards = []
    for chunk in range(chunks):
        for band in range(y_count):
            slot = HALO + band
            arrival = pltpu.make_async_remote_copy(
                src_ref=ext_ref.at[slot, planes(chunk)],
                dst_ref=ext_ref.at[slot, planes(chunk)],
                send_sem=y_send.at[chunk],
                recv_sem=slot_recv.at[slot * chunks + chunk],
                device_id=(geo, z_pos, lax.rem(y_pos + 1, y_count)),
                device_id_type=mesh_id,
            )
            local = pending[-1]

            @pl.when(y_pos == band)
            def _():
                local.wait()

            @pl.when(y_pos != band)
            def _():
                arrival.wait_recv()

            if band < HALO:
                fwd = forward(slot, slot + y_count, z_pos - 1, chunk)
                live = z_pos > 0
            elif band >= y_count - HALO:
                fwd = forward(slot, slot - y_count, z_pos + 1, chunk)
                live = z_pos < z_count - 1
            else:
                continue

            @pl.when(live)
            def _():
                fwd.start()

            forwards.append((fwd, live))
        for copy in pending[:-1]:
            copy.wait_send()
        if chunk + 1 < chunks:
            pending = y_sends(chunk + 1)
            for copy in pending:
                copy.start()
    for fwd, live in forwards:

        @pl.when(live)
        def _():
            fwd.wait_send()

    for chunk in range(chunks):
        for slot, live in ((0, z_pos > 0), (1, z_pos > 0),
                           (HALO + y_count, z_pos < z_count - 1), (HALO + y_count + 1, z_pos < z_count - 1)):
            incoming = pltpu.make_async_remote_copy(
                src_ref=ext_ref.at[slot, planes(chunk)],
                dst_ref=ext_ref.at[slot, planes(chunk)],
                send_sem=z_send.at[chunk],
                recv_sem=slot_recv.at[slot * chunks + chunk],
                device_id=(geo, lax.rem(z_pos + 1, z_count), y_pos),
                device_id_type=mesh_id,
            )

            @pl.when(live)
            def _():
                incoming.wait_recv()


def spread(floored, z_count, y_count):
    _, dirs, rows, cols = floored.shape
    part_rows = rows // y_count
    chunks = SPREAD_CHUNKS
    assert dirs % chunks == 0
    vmem = pl.BlockSpec(memory_space=pltpu.VMEM)
    slots = y_count + 2 * HALO
    return pl.pallas_call(
        functools.partial(_spread_kernel, z_count, y_count, chunks),
        out_shape=jax.ShapeDtypeStruct((slots, dirs, part_rows, cols), floored.dtype),
        in_specs=[vmem],
        out_specs=vmem,
        scratch_shapes=[
            pltpu.SemaphoreType.DMA((y_count * chunks,)),
            pltpu.SemaphoreType.DMA((chunks,)),
            pltpu.SemaphoreType.DMA((slots * chunks,)),
            pltpu.SemaphoreType.DMA((y_count * chunks,)),
        ],
        compiler_params=pltpu.CompilerParams(collective_id=1, has_side_effects=True),
    )(floored)


def extended(cells, sides, width):
    for axis, dim in sides:
        count = lax.axis_size(axis)
        ends = count - 1
        head = lax.slice_in_dim(cells, 0, width, axis=dim)
        tail = lax.slice_in_dim(cells, cells.shape[dim] - width, cells.shape[dim], axis=dim)
        cells = jnp.concatenate(
            [
                lax.ppermute(tail, axis, [(i, (i + 1) % count) for i in range(ends)]),
                cells,
                lax.ppermute(head, axis, [((i + 1) % count, i) for i in range(ends)]),
            ],
            axis=dim,
        )
    return cells


def band_table(band_ids):
    growth_factor = jnp.power(GROWTH, band_ids)
    radian_freq = 2.0 * math.pi * BASE_FREQ * growth_factor
    wavenum = radian_freq * radian_freq / GRAVITY
    return (
        radian_freq,
        wavenum,
        COURANT_TOP / growth_factor,
        TURN_TOP / growth_factor,
        SPACING * radian_freq,
    )


def quick_flux(far_left, near_left, near_right, far_right, courant):
    forward = courant >= 0
    upwind = jnp.where(forward, far_left, far_right)
    center = jnp.where(forward, near_left, near_right)
    downwind = jnp.where(forward, near_right, near_left)
    face_value = (
        0.5 * (center + downwind)
        - 0.5 * jnp.abs(courant) * (downwind - center)
        - (1.0 - courant * courant) / 6.0 * (downwind - 2.0 * center + upwind)
    )
    return courant * face_value


def advect(padded, courant, along):
    face_count = padded.shape[along] - 4
    shifted = [
        lax.slice_in_dim(padded, offset, offset + face_count + 1, axis=along) for offset in range(4)
    ]
    face_flux = quick_flux(shifted[0], shifted[1], shifted[2], shifted[3], courant)
    centre_cells = lax.slice_in_dim(padded, 2, 2 + face_count, axis=along)
    upper_flux = lax.slice_in_dim(face_flux, 1, face_count + 1, axis=along)
    lower_flux = lax.slice_in_dim(face_flux, 0, face_count, axis=along)
    return centre_cells - (upper_flux - lower_flux)


def quad_delta(center, above, below, energy, dir_axis):
    plus = jnp.roll(above, -1, axis=dir_axis)
    minus = jnp.roll(below, 3, axis=dir_axis)
    return (
        QUAD_COEF
        * (center * center * (plus + minus) - 2.0 * center * plus * minus)
        / (energy * energy)
    )


def quad_term(delta, delta_above, delta_below, dir_axis):
    return (
        -2.0 * delta
        + jnp.roll(delta_below, 1, axis=dir_axis)
        + jnp.roll(delta_above, -3, axis=dir_axis)
    )


def band_neighbours(values):
    empty = jnp.zeros((1,) + values.shape[1:], jnp.float32)
    return (
        jnp.concatenate([values[1:], empty], axis=0),
        jnp.concatenate([empty, values[:-1]], axis=0),
    )


def sources(density, energy_sum, first_sum, root_sum, radian_freq, wavenum, cosine, wind_speed):
    energy = energy_sum + EPSILON
    mean_sigma = energy / (first_sum + EPSILON)
    ratio_k = energy / (root_sum + EPSILON)
    mean_k = ratio_k * ratio_k
    steepness = energy * mean_k * mean_k / STEEP_REF
    decay_rate = WHITECAP * mean_sigma * (wavenum / mean_k) * steepness * steepness
    growth_rate = (
        WIND_COEF
        * radian_freq
        * jnp.maximum(28.0 * USTAR_RATIO * wind_speed * radian_freq / GRAVITY * cosine - 1.0, 0.0)
    )
    return density * (1.0 + growth_rate) / (1.0 + decay_rate)


def local_sources(point_block, wind_block, wind_angle, angles, dtheta):
    band_total = point_block.shape[0]
    band_ids = jnp.arange(band_total).astype(jnp.float32)
    radian_freq, wavenum, courant, turn_rate, band_spread = band_table(band_ids)
    scaled = point_block * (band_spread * dtheta)[:, None, None]
    energy_sum = jnp.sum(scaled, axis=(0, 1))
    first_sum = jnp.sum(scaled / radian_freq[:, None, None], axis=(0, 1))
    root_sum = jnp.sum(scaled / jnp.sqrt(wavenum)[:, None, None], axis=(0, 1))
    energy = energy_sum + EPSILON
    above, below = band_neighbours(point_block)
    delta = quad_delta(point_block, above, below, energy, 1)
    delta_above, delta_below = band_neighbours(delta)
    extra = quad_term(delta, delta_above, delta_below, 1)
    cosine = jnp.cos(angles[:, None] - wind_angle[None, :])
    return (
        sources(
            point_block,
            energy_sum,
            first_sum,
            root_sum,
            radian_freq[:, None, None],
            wavenum[:, None, None],
            cosine,
            wind_block,
        )
        + extra
    )


Y_GROUP = 4
HALO = 2


def _z_gather_kernel(z_count, part_ref, gathered_ref, gather_send, gather_recv):
    geo = lax.axis_index("geo")
    z_pos = lax.axis_index("z")
    y_pos = lax.axis_index("y")
    barrier = pltpu.get_barrier_semaphore()
    for offset in range(1, z_count):
        target = lax.rem(z_pos + offset, z_count)
        pl.semaphore_signal(barrier, inc=1, device_id=(geo, target, y_pos),
                            device_id_type=pl.DeviceIdType.MESH)
    pl.semaphore_wait(barrier, z_count - 1)
    copies = []
    for offset in range(1, z_count):
        target = lax.rem(z_pos + offset, z_count)
        copy = pltpu.make_async_remote_copy(
            src_ref=part_ref,
            dst_ref=gathered_ref.at[z_pos],
            send_sem=gather_send.at[offset],
            recv_sem=gather_recv.at[offset],
            device_id=(geo, target, y_pos),
            device_id_type=pl.DeviceIdType.MESH,
        )
        copy.start()
        copies.append(copy)
    gathered_ref[z_pos] = part_ref[...]
    for copy in copies:
        copy.wait_send()
        copy.wait_recv()


def z_gather(part, z_count):
    vmem = pl.BlockSpec(memory_space=pltpu.VMEM)
    return pl.pallas_call(
        functools.partial(_z_gather_kernel, z_count),
        out_shape=jax.ShapeDtypeStruct((z_count,) + part.shape, part.dtype),
        in_specs=[vmem],
        out_specs=vmem,
        scratch_shapes=[
            pltpu.SemaphoreType.DMA((z_count,)),
            pltpu.SemaphoreType.DMA((z_count,)),
        ],
        compiler_params=pltpu.CompilerParams(collective_id=0, has_side_effects=True),
    )(part)


def _spread_kernel(z_count, y_count, floored_ref, ext_ref, relay_ref, y_send, local_sem, slot_recv,
                   z_send, relay_send, relay_recv, pass_send, pass_recv):
    geo = lax.axis_index("geo")
    z_pos = lax.axis_index("z")
    y_pos = lax.axis_index("y")
    rows = ext_ref.shape[2]
    half = relay_ref.shape[1]
    mesh_id = pl.DeviceIdType.MESH
    up_y = lax.rem(y_pos + 1, y_count)
    down_y = lax.rem(y_pos + y_count - 1, y_count)
    barrier = pltpu.get_barrier_semaphore()
    for offset in range(1, y_count):
        pl.semaphore_signal(barrier, inc=1, device_id=(geo, z_pos, lax.rem(y_pos + offset, y_count)),
                            device_id_type=mesh_id)
    for step in (1, z_count - 1):
        pl.semaphore_signal(barrier, inc=1, device_id=(geo, lax.rem(z_pos + step, z_count), y_pos),
                            device_id_type=mesh_id)
    pl.semaphore_wait(barrier, y_count + 1)

    def quarter(target):
        return floored_ref.at[0, :, pl.ds(pl.multiple_of(target * rows, rows), rows)]

    own_slot = HALO + y_pos
    sends = []
    for offset in (1, y_count - 1):
        target = lax.rem(y_pos + offset, y_count)
        copy = pltpu.make_async_remote_copy(
            src_ref=quarter(target),
            dst_ref=ext_ref.at[own_slot],
            send_sem=y_send.at[offset],
            recv_sem=slot_recv.at[own_slot],
            device_id=(geo, z_pos, target),
            device_id_type=mesh_id,
        )
        copy.start()
        sends.append(copy)
    far = lax.rem(y_pos + 2, y_count)
    for side, via in ((0, up_y), (1, down_y)):
        copy = pltpu.make_async_remote_copy(
            src_ref=quarter(far).at[pl.ds(side * half, half)],
            dst_ref=relay_ref.at[side],
            send_sem=relay_send.at[side],
            recv_sem=relay_recv.at[side],
            device_id=(geo, z_pos, via),
            device_id_type=mesh_id,
        )
        copy.start()
        sends.append(copy)
    local = pltpu.make_async_copy(quarter(y_pos), ext_ref.at[own_slot], local_sem.at[0])
    local.start()

    @pl.when(z_pos == 0)
    def _():
        ext_ref[pl.ds(0, HALO)] = jnp.zeros((HALO,) + ext_ref.shape[1:], ext_ref.dtype)

    @pl.when(z_pos == z_count - 1)
    def _():
        ext_ref[pl.ds(HALO + y_count, HALO)] = jnp.zeros((HALO,) + ext_ref.shape[1:], ext_ref.dtype)

    passes = []
    for side, origin, onward in ((0, down_y, up_y), (1, up_y, down_y)):
        relay_in = pltpu.make_async_remote_copy(
            src_ref=relay_ref.at[side],
            dst_ref=relay_ref.at[side],
            send_sem=relay_send.at[side],
            recv_sem=relay_recv.at[side],
            device_id=(geo, z_pos, onward),
            device_id_type=mesh_id,
        )
        relay_in.wait_recv()
        onward_copy = pltpu.make_async_remote_copy(
            src_ref=relay_ref.at[side],
            dst_ref=ext_ref.at[HALO + origin, pl.ds(side * half, half)],
            send_sem=pass_send.at[side],
            recv_sem=pass_recv.at[side],
            device_id=(geo, z_pos, onward),
            device_id_type=mesh_id,
        )
        onward_copy.start()
        passes.append(onward_copy)

    def forward(slot, dst_slot, target_z):
        return pltpu.make_async_remote_copy(
            src_ref=ext_ref.at[slot],
            dst_ref=ext_ref.at[dst_slot],
            send_sem=z_send.at[slot - HALO],
            recv_sem=slot_recv.at[dst_slot],
            device_id=(geo, target_z, y_pos),
            device_id_type=mesh_id,
        )

    forwards = []
    for band in range(y_count):
        slot = HALO + band
        distance = lax.rem(band - y_pos + y_count, y_count)
        arrival = pltpu.make_async_remote_copy(
            src_ref=ext_ref.at[slot],
            dst_ref=ext_ref.at[slot],
            send_sem=y_send.at[0],
            recv_sem=slot_recv.at[slot],
            device_id=(geo, z_pos, up_y),
            device_id_type=mesh_id,
        )
        relayed = [
            pltpu.make_async_remote_copy(
                src_ref=ext_ref.at[slot, pl.ds(side * half, half)],
                dst_ref=ext_ref.at[slot, pl.ds(side * half, half)],
                send_sem=pass_send.at[side],
                recv_sem=pass_recv.at[side],
                device_id=(geo, z_pos, up_y),
                device_id_type=mesh_id,
            )
            for side in (0, 1)
        ]

        @pl.when(distance == 0)
        def _():
            local.wait()

        @pl.when((distance == 1) | (distance == y_count - 1))
        def _():
            arrival.wait_recv()

        @pl.when(distance == 2)
        def _():
            for copy in relayed:
                copy.wait_recv()

        if band < HALO:
            fwd = forward(slot, slot + y_count, z_pos - 1)
            live = z_pos > 0
        elif band >= y_count - HALO:
            fwd = forward(slot, slot - y_count, z_pos + 1)
            live = z_pos < z_count - 1
        else:
            continue

        @pl.when(live)
        def _():
            fwd.start()

        forwards.append((fwd, live))
    for copy in sends + passes:
        copy.wait_send()
    for fwd, live in forwards:

        @pl.when(live)
        def _():
            fwd.wait_send()

    for slot, live in ((0, z_pos > 0), (1, z_pos > 0),
                       (HALO + y_count, z_pos < z_count - 1), (HALO + y_count + 1, z_pos < z_count - 1)):
        incoming = pltpu.make_async_remote_copy(
            src_ref=ext_ref.at[slot],
            dst_ref=ext_ref.at[slot],
            send_sem=z_send.at[0],
            recv_sem=slot_recv.at[slot],
            device_id=(geo, lax.rem(z_pos + 1, z_count), y_pos),
            device_id_type=mesh_id,
        )

        @pl.when(live)
        def _():
            incoming.wait_recv()


def spread(floored, z_count, y_count):
    _, dirs, rows, cols = floored.shape
    part_rows = rows // y_count
    vmem = pl.BlockSpec(memory_space=pltpu.VMEM)
    slots = y_count + 2 * HALO
    half = dirs // 2
    assert 2 * half == dirs
    return pl.pallas_call(
        functools.partial(_spread_kernel, z_count, y_count),
        out_shape=jax.ShapeDtypeStruct((slots, dirs, part_rows, cols), floored.dtype),
        in_specs=[vmem],
        out_specs=vmem,
        scratch_shapes=[
            pltpu.VMEM((2, half, part_rows, cols), floored.dtype),
            pltpu.SemaphoreType.DMA((y_count,)),
            pltpu.SemaphoreType.DMA((1,)),
            pltpu.SemaphoreType.DMA((slots,)),
            pltpu.SemaphoreType.DMA((y_count,)),
            pltpu.SemaphoreType.DMA((2,)),
            pltpu.SemaphoreType.DMA((2,)),
            pltpu.SemaphoreType.DMA((2,)),
            pltpu.SemaphoreType.DMA((2,)),
        ],
        compiler_params=pltpu.CompilerParams(collective_id=1, has_side_effects=True),
    )(floored)


def extended(cells, sides, width):
    for axis, dim in sides:
        count = lax.axis_size(axis)
        ends = count - 1
        head = lax.slice_in_dim(cells, 0, width, axis=dim)
        tail = lax.slice_in_dim(cells, cells.shape[dim] - width, cells.shape[dim], axis=dim)
        cells = jnp.concatenate(
            [
                lax.ppermute(tail, axis, [(i, (i + 1) % count) for i in range(ends)]),
                cells,
                lax.ppermute(head, axis, [((i + 1) % count, i) for i in range(ends)]),
            ],
            axis=dim,
        )
    return cells


def band_table(band_ids):
    growth_factor = jnp.power(GROWTH, band_ids)
    radian_freq = 2.0 * math.pi * BASE_FREQ * growth_factor
    wavenum = radian_freq * radian_freq / GRAVITY
    return (
        radian_freq,
        wavenum,
        COURANT_TOP / growth_factor,
        TURN_TOP / growth_factor,
        SPACING * radian_freq,
    )


def quick_flux(far_left, near_left, near_right, far_right, courant):
    forward = courant >= 0
    upwind = jnp.where(forward, far_left, far_right)
    center = jnp.where(forward, near_left, near_right)
    downwind = jnp.where(forward, near_right, near_left)
    face_value = (
        0.5 * (center + downwind)
        - 0.5 * jnp.abs(courant) * (downwind - center)
        - (1.0 - courant * courant) / 6.0 * (downwind - 2.0 * center + upwind)
    )
    return courant * face_value


def advect(padded, courant, along):
    face_count = padded.shape[along] - 4
    shifted = [
        lax.slice_in_dim(padded, offset, offset + face_count + 1, axis=along) for offset in range(4)
    ]
    face_flux = quick_flux(shifted[0], shifted[1], shifted[2], shifted[3], courant)
    centre_cells = lax.slice_in_dim(padded, 2, 2 + face_count, axis=along)
    upper_flux = lax.slice_in_dim(face_flux, 1, face_count + 1, axis=along)
    lower_flux = lax.slice_in_dim(face_flux, 0, face_count, axis=along)
    return centre_cells - (upper_flux - lower_flux)


def quad_delta(center, above, below, energy, dir_axis):
    plus = jnp.roll(above, -1, axis=dir_axis)
    minus = jnp.roll(below, 3, axis=dir_axis)
    return (
        QUAD_COEF
        * (center * center * (plus + minus) - 2.0 * center * plus * minus)
        / (energy * energy)
    )


def quad_term(delta, delta_above, delta_below, dir_axis):
    return (
        -2.0 * delta
        + jnp.roll(delta_below, 1, axis=dir_axis)
        + jnp.roll(delta_above, -3, axis=dir_axis)
    )


def band_neighbours(values):
    empty = jnp.zeros((1,) + values.shape[1:], jnp.float32)
    return (
        jnp.concatenate([values[1:], empty], axis=0),
        jnp.concatenate([empty, values[:-1]], axis=0),
    )


def sources(density, energy_sum, first_sum, root_sum, radian_freq, wavenum, cosine, wind_speed):
    energy = energy_sum + EPSILON
    mean_sigma = energy / (first_sum + EPSILON)
    ratio_k = energy / (root_sum + EPSILON)
    mean_k = ratio_k * ratio_k
    steepness = energy * mean_k * mean_k / STEEP_REF
    decay_rate = WHITECAP * mean_sigma * (wavenum / mean_k) * steepness * steepness
    growth_rate = (
        WIND_COEF
        * radian_freq
        * jnp.maximum(28.0 * USTAR_RATIO * wind_speed * radian_freq / GRAVITY * cosine - 1.0, 0.0)
    )
    return density * (1.0 + growth_rate) / (1.0 + decay_rate)


def local_sources(point_block, wind_block, wind_angle, angles, dtheta):
    band_total = point_block.shape[0]
    band_ids = jnp.arange(band_total).astype(jnp.float32)
    radian_freq, wavenum, courant, turn_rate, band_spread = band_table(band_ids)
    scaled = point_block * (band_spread * dtheta)[:, None, None]
    energy_sum = jnp.sum(scaled, axis=(0, 1))
    first_sum = jnp.sum(scaled / radian_freq[:, None, None], axis=(0, 1))
    root_sum = jnp.sum(scaled / jnp.sqrt(wavenum)[:, None, None], axis=(0, 1))
    energy = energy_sum + EPSILON
    above, below = band_neighbours(point_block)
    delta = quad_delta(point_block, above, below, energy, 1)
    delta_above, delta_below = band_neighbours(delta)
    extra = quad_term(delta, delta_above, delta_below, 1)
    cosine = jnp.cos(angles[:, None] - wind_angle[None, :])
    return (
        sources(
            point_block,
            energy_sum,
            first_sum,
            root_sum,
            radian_freq[:, None, None],
            wavenum[:, None, None],
            cosine,
            wind_block,
        )
        + extra
    )


Y_GROUP = 4
HALO = 2


def _z_gather_kernel(z_count, part_ref, gathered_ref, gather_send, gather_recv):
    geo = lax.axis_index("geo")
    z_pos = lax.axis_index("z")
    y_pos = lax.axis_index("y")
    barrier = pltpu.get_barrier_semaphore()
    for offset in range(1, z_count):
        target = lax.rem(z_pos + offset, z_count)
        pl.semaphore_signal(barrier, inc=1, device_id=(geo, target, y_pos),
                            device_id_type=pl.DeviceIdType.MESH)
    pl.semaphore_wait(barrier, z_count - 1)
    copies = []
    for offset in range(1, z_count):
        target = lax.rem(z_pos + offset, z_count)
        copy = pltpu.make_async_remote_copy(
            src_ref=part_ref,
            dst_ref=gathered_ref.at[z_pos],
            send_sem=gather_send.at[offset],
            recv_sem=gather_recv.at[offset],
            device_id=(geo, target, y_pos),
            device_id_type=pl.DeviceIdType.MESH,
        )
        copy.start()
        copies.append(copy)
    gathered_ref[z_pos] = part_ref[...]
    for copy in copies:
        copy.wait_send()
        copy.wait_recv()


def z_gather(part, z_count):
    vmem = pl.BlockSpec(memory_space=pltpu.VMEM)
    return pl.pallas_call(
        functools.partial(_z_gather_kernel, z_count),
        out_shape=jax.ShapeDtypeStruct((z_count,) + part.shape, part.dtype),
        in_specs=[vmem],
        out_specs=vmem,
        scratch_shapes=[
            pltpu.SemaphoreType.DMA((z_count,)),
            pltpu.SemaphoreType.DMA((z_count,)),
        ],
        compiler_params=pltpu.CompilerParams(collective_id=0, has_side_effects=True),
    )(part)


def _spread_kernel(z_count, y_count, floored_ref, ext_ref, y_send, local_sem, slot_recv, z_send):
    geo = lax.axis_index("geo")
    z_pos = lax.axis_index("z")
    y_pos = lax.axis_index("y")
    rows = ext_ref.shape[2]
    mesh_id = pl.DeviceIdType.MESH
    barrier = pltpu.get_barrier_semaphore()
    for offset in range(1, y_count):
        pl.semaphore_signal(barrier, inc=1, device_id=(geo, z_pos, lax.rem(y_pos + offset, y_count)),
                            device_id_type=mesh_id)

    for step in (1, z_count - 1):
        pl.semaphore_signal(barrier, inc=1, device_id=(geo, lax.rem(z_pos + step, z_count), y_pos),
                            device_id_type=mesh_id)
    pl.semaphore_wait(barrier, y_count + 1)

    own_slot = HALO + y_pos
    sends = []
    for offset in range(1, y_count):
        target = lax.rem(y_pos + offset, y_count)
        copy = pltpu.make_async_remote_copy(
            src_ref=floored_ref.at[0, :, pl.ds(pl.multiple_of(target * rows, rows), rows)],
            dst_ref=ext_ref.at[own_slot],
            send_sem=y_send.at[offset],
            recv_sem=slot_recv.at[own_slot],
            device_id=(geo, z_pos, target),
            device_id_type=mesh_id,
        )
        copy.start()
        sends.append(copy)
    local = pltpu.make_async_copy(
        floored_ref.at[0, :, pl.ds(pl.multiple_of(y_pos * rows, rows), rows)],
        ext_ref.at[own_slot],
        local_sem.at[0],
    )
    local.start()

    @pl.when(z_pos == 0)
    def _():
        ext_ref[pl.ds(0, HALO)] = jnp.zeros((HALO,) + ext_ref.shape[1:], ext_ref.dtype)

    @pl.when(z_pos == z_count - 1)
    def _():
        ext_ref[pl.ds(HALO + y_count, HALO)] = jnp.zeros((HALO,) + ext_ref.shape[1:], ext_ref.dtype)

    def forward(slot, dst_slot, target_z):
        return pltpu.make_async_remote_copy(
            src_ref=ext_ref.at[slot],
            dst_ref=ext_ref.at[dst_slot],
            send_sem=z_send.at[slot - HALO],
            recv_sem=slot_recv.at[dst_slot],
            device_id=(geo, target_z, y_pos),
            device_id_type=mesh_id,
        )

    forwards = []
    for band in range(y_count):
        slot = HALO + band
        arrival = pltpu.make_async_remote_copy(
            src_ref=ext_ref.at[slot],
            dst_ref=ext_ref.at[slot],
            send_sem=y_send.at[0],
            recv_sem=slot_recv.at[slot],
            device_id=(geo, z_pos, lax.rem(y_pos + 1, y_count)),
            device_id_type=mesh_id,
        )

        @pl.when(y_pos == band)
        def _():
            local.wait()

        @pl.when(y_pos != band)
        def _():
            arrival.wait_recv()

        if band < HALO:
            fwd = forward(slot, slot + y_count, z_pos - 1)
            live = z_pos > 0
        elif band >= y_count - HALO:
            fwd = forward(slot, slot - y_count, z_pos + 1)
            live = z_pos < z_count - 1
        else:
            continue

        @pl.when(live)
        def _():
            fwd.start()

        forwards.append((fwd, live))
    for copy in sends:
        copy.wait_send()
    for fwd, live in forwards:

        @pl.when(live)
        def _():
            fwd.wait_send()

    for slot, live in ((0, z_pos > 0), (1, z_pos > 0),
                       (HALO + y_count, z_pos < z_count - 1), (HALO + y_count + 1, z_pos < z_count - 1)):
        incoming = pltpu.make_async_remote_copy(
            src_ref=ext_ref.at[slot],
            dst_ref=ext_ref.at[slot],
            send_sem=z_send.at[0],
            recv_sem=slot_recv.at[slot],
            device_id=(geo, lax.rem(z_pos + 1, z_count), y_pos),
            device_id_type=mesh_id,
        )

        @pl.when(live)
        def _():
            incoming.wait_recv()


def spread(floored, z_count, y_count):
    _, dirs, rows, cols = floored.shape
    part_rows = rows // y_count
    vmem = pl.BlockSpec(memory_space=pltpu.VMEM)
    slots = y_count + 2 * HALO
    return pl.pallas_call(
        functools.partial(_spread_kernel, z_count, y_count),
        out_shape=jax.ShapeDtypeStruct((slots, dirs, part_rows, cols), floored.dtype),
        in_specs=[vmem],
        out_specs=vmem,
        scratch_shapes=[
            pltpu.SemaphoreType.DMA((y_count,)),
            pltpu.SemaphoreType.DMA((1,)),
            pltpu.SemaphoreType.DMA((slots,)),
            pltpu.SemaphoreType.DMA((y_count,)),
        ],
        compiler_params=pltpu.CompilerParams(collective_id=1, has_side_effects=True),
    )(floored)


def shards(spectrum, land_sea, sea_index, sea_count, wind_speed, wind_dir, slope_x, slope_y):
    local_bands, dir_count, row_count, col_count = spectrum.shape
    z_count = lax.axis_size("z")
    y_count = lax.axis_size("y")
    z_pos = lax.axis_index("z")
    y_pos = lax.axis_index("y")
    spec_pos = z_pos * y_count + y_pos
    dtheta = 2.0 * math.pi / dir_count
    angles = (jnp.arange(dir_count).astype(jnp.float32) + 0.5) * dtheta
    face_angles = jnp.arange(dir_count + 1).astype(jnp.float32) * dtheta
    band_ids = (spec_pos * local_bands + jnp.arange(local_bands)).astype(jnp.float32)
    radian_freq, wavenum, courant, turn_rate, band_spread = band_table(band_ids)
    wet_mask = land_sea.astype(jnp.float32)
    density = spectrum * wet_mask
    padded = extended(density, (("geo", 2),), 2)
    density = (
        advect(padded, (courant[:, None] * jnp.cos(angles)[None, :])[:, :, None, None], 2)
        * wet_mask
    )
    padded = jnp.pad(density, ((0, 0), (0, 0), (0, 0), (2, 2)))
    density = (
        advect(padded, (courant[:, None] * jnp.sin(angles)[None, :])[:, :, None, None], 3)
        * wet_mask
    )
    turning = turn_rate[:, None, None, None] * (
        jnp.sin(face_angles)[None, :, None, None] * slope_x
        - jnp.cos(face_angles)[None, :, None, None] * slope_y
    )
    padded = jnp.concatenate([density[:, -2:], density, density[:, :2]], axis=1)
    floored = jnp.maximum(advect(padded, turning, 1), 0.0)
    ext = spread(floored, z_count, lax.axis_size("y"))
    point = ext[HALO:-HALO]
    group = point.shape[0]
    part_rows = point.shape[2]
    group_ids = (z_pos * group + jnp.arange(group)).astype(jnp.float32)
    radian_freq, wavenum, courant, turn_rate, band_spread = band_table(group_ids)
    scaled = point * (band_spread * dtheta)[:, None, None, None]
    sums = jnp.stack(
        [
            jnp.sum(scaled, axis=(0, 1)),
            jnp.sum(scaled / radian_freq[:, None, None, None], axis=(0, 1)),
            jnp.sum(scaled / jnp.sqrt(wavenum)[:, None, None, None], axis=(0, 1)),
        ]
    )
    sums = lax.psum(sums, "z")
    energy_sum, first_sum, root_sum = sums[0], sums[1], sums[2]
    energy = energy_sum + EPSILON
    center, plus, minus = ext[1:-1], jnp.roll(ext[2:], -1, axis=1), jnp.roll(ext[:-2], 3, axis=1)
    cubic = center * center * (plus + minus) - 2.0 * center * plus * minus
    extra = (
        -2.0 * cubic[1:-1] + jnp.roll(cubic[:-2], 1, axis=1) + jnp.roll(cubic[2:], -3, axis=1)
    ) * (QUAD_COEF / (energy * energy))
    row_start = y_pos * part_rows
    wind_block = lax.dynamic_slice_in_dim(wind_speed, row_start, part_rows, axis=0)
    wind_angle = lax.dynamic_slice_in_dim(wind_dir, row_start, part_rows, axis=0)
    wet_block = lax.dynamic_slice_in_dim(wet_mask, row_start, part_rows, axis=0)
    cosine = jnp.cos(angles[:, None, None] - wind_angle[None])
    updated = (
        sources(
            point,
            energy_sum,
            first_sum,
            root_sum,
            radian_freq[:, None, None, None],
            wavenum[:, None, None, None],
            cosine,
            wind_block,
        )
        + extra
    ) * wet_block
    return lax.all_to_all(updated, "y", split_axis=0, concat_axis=2, tiled=True)


def solution(mesh):
    geo_count = mesh.shape["geo"]
    spec_count = mesh.shape["spec"]
    local = jax.sharding.Mesh(
        mesh.devices.reshape(geo_count, spec_count // Y_GROUP, Y_GROUP), ("geo", "z", "y")
    )
    spec = ("z", "y")
    placed = (
        P(spec, None, "geo", None),
        P("geo", None),
        P("geo", None),
        P("geo"),
        P("geo", None),
        P("geo", None),
        P("geo", None),
        P("geo", None),
    )
    return jax.shard_map(
        shards, mesh=local, in_specs=placed, out_specs=P(spec, None, "geo", None), check_vma=False
    )
```

```python
import functools
import math

import jax
import jax.numpy as jnp
from jax import lax
from jax.experimental import pallas as pl
from jax.experimental.pallas import tpu as pltpu
from jax.sharding import PartitionSpec as P

GRAVITY = 9.81
BASE_FREQ = 0.035
GROWTH = 1.1
COURANT_TOP = 0.9
TURN_TOP = 1.2
SPACING = 0.1
USTAR_RATIO = 0.035
WIND_COEF = 0.0375
WHITECAP = 0.36
STEEP_REF = 1.6
EPSILON = 1e-06
QUAD_COEF = 100.0


def extended(cells, sides, width):
    for axis, dim in sides:
        count = lax.axis_size(axis)
        ends = count - 1
        head = lax.slice_in_dim(cells, 0, width, axis=dim)
        tail = lax.slice_in_dim(cells, cells.shape[dim] - width, cells.shape[dim], axis=dim)
        cells = jnp.concatenate(
            [
                lax.ppermute(tail, axis, [(i, (i + 1) % count) for i in range(ends)]),
                cells,
                lax.ppermute(head, axis, [((i + 1) % count, i) for i in range(ends)]),
            ],
            axis=dim,
        )
    return cells


def band_table(band_ids):
    growth_factor = jnp.power(GROWTH, band_ids)
    radian_freq = 2.0 * math.pi * BASE_FREQ * growth_factor
    wavenum = radian_freq * radian_freq / GRAVITY
    return (
        radian_freq,
        wavenum,
        COURANT_TOP / growth_factor,
        TURN_TOP / growth_factor,
        SPACING * radian_freq,
    )


def quick_flux(far_left, near_left, near_right, far_right, courant):
    forward = courant >= 0
    upwind = jnp.where(forward, far_left, far_right)
    center = jnp.where(forward, near_left, near_right)
    downwind = jnp.where(forward, near_right, near_left)
    face_value = (
        0.5 * (center + downwind)
        - 0.5 * jnp.abs(courant) * (downwind - center)
        - (1.0 - courant * courant) / 6.0 * (downwind - 2.0 * center + upwind)
    )
    return courant * face_value


def advect(padded, courant, along):
    face_count = padded.shape[along] - 4
    shifted = [
        lax.slice_in_dim(padded, offset, offset + face_count + 1, axis=along) for offset in range(4)
    ]
    face_flux = quick_flux(shifted[0], shifted[1], shifted[2], shifted[3], courant)
    centre_cells = lax.slice_in_dim(padded, 2, 2 + face_count, axis=along)
    upper_flux = lax.slice_in_dim(face_flux, 1, face_count + 1, axis=along)
    lower_flux = lax.slice_in_dim(face_flux, 0, face_count, axis=along)
    return centre_cells - (upper_flux - lower_flux)


def quad_delta(center, above, below, energy, dir_axis):
    plus = jnp.roll(above, -1, axis=dir_axis)
    minus = jnp.roll(below, 3, axis=dir_axis)
    return (
        QUAD_COEF
        * (center * center * (plus + minus) - 2.0 * center * plus * minus)
        / (energy * energy)
    )


def quad_term(delta, delta_above, delta_below, dir_axis):
    return (
        -2.0 * delta
        + jnp.roll(delta_below, 1, axis=dir_axis)
        + jnp.roll(delta_above, -3, axis=dir_axis)
    )


def band_neighbours(values):
    empty = jnp.zeros((1,) + values.shape[1:], jnp.float32)
    return (
        jnp.concatenate([values[1:], empty], axis=0),
        jnp.concatenate([empty, values[:-1]], axis=0),
    )


def sources(density, energy_sum, first_sum, root_sum, radian_freq, wavenum, cosine, wind_speed):
    energy = energy_sum + EPSILON
    mean_sigma = energy / (first_sum + EPSILON)
    ratio_k = energy / (root_sum + EPSILON)
    mean_k = ratio_k * ratio_k
    steepness = energy * mean_k * mean_k / STEEP_REF
    decay_rate = WHITECAP * mean_sigma * (wavenum / mean_k) * steepness * steepness
    growth_rate = (
        WIND_COEF
        * radian_freq
        * jnp.maximum(28.0 * USTAR_RATIO * wind_speed * radian_freq / GRAVITY * cosine - 1.0, 0.0)
    )
    return density * (1.0 + growth_rate) / (1.0 + decay_rate)


def local_sources(point_block, wind_block, wind_angle, angles, dtheta):
    band_total = point_block.shape[0]
    band_ids = jnp.arange(band_total).astype(jnp.float32)
    radian_freq, wavenum, courant, turn_rate, band_spread = band_table(band_ids)
    scaled = point_block * (band_spread * dtheta)[:, None, None]
    energy_sum = jnp.sum(scaled, axis=(0, 1))
    first_sum = jnp.sum(scaled / radian_freq[:, None, None], axis=(0, 1))
    root_sum = jnp.sum(scaled / jnp.sqrt(wavenum)[:, None, None], axis=(0, 1))
    energy = energy_sum + EPSILON
    above, below = band_neighbours(point_block)
    delta = quad_delta(point_block, above, below, energy, 1)
    delta_above, delta_below = band_neighbours(delta)
    extra = quad_term(delta, delta_above, delta_below, 1)
    cosine = jnp.cos(angles[:, None] - wind_angle[None, :])
    return (
        sources(
            point_block,
            energy_sum,
            first_sum,
            root_sum,
            radian_freq[:, None, None],
            wavenum[:, None, None],
            cosine,
            wind_block,
        )
        + extra
    )


Y_GROUP = 4


def _exchange_kernel(y_count, x_ref, out_ref, local_sem, send_sems, recv_sems):
    geo = lax.axis_index("geo")
    me = lax.axis_index("z") * y_count + lax.axis_index("y")
    count = x_ref.shape[0]
    mesh_id = pl.DeviceIdType.MESH
    barrier = pltpu.get_barrier_semaphore()
    for offset in range(1, count):
        target = lax.rem(me + offset, count)
        pl.semaphore_signal(barrier, inc=1, device_id=(geo, target // y_count, target % y_count),
                            device_id_type=mesh_id)
    pl.semaphore_wait(barrier, count - 1)
    local = pltpu.make_async_copy(x_ref.at[me], out_ref.at[me], local_sem.at[0])
    local.start()
    copies = []
    for offset in range(1, count):
        target = lax.rem(me + offset, count)
        copy = pltpu.make_async_remote_copy(
            src_ref=x_ref.at[target],
            dst_ref=out_ref.at[me],
            send_sem=send_sems.at[offset],
            recv_sem=recv_sems.at[offset],
            device_id=(geo, target // y_count, target % y_count),
            device_id_type=mesh_id,
        )
        copy.start()
        copies.append(copy)
    local.wait()
    for copy in copies:
        copy.wait_send()
        copy.wait_recv()


def exchange(x, y_count, collective_id):
    count = x.shape[0]
    vmem = pl.BlockSpec(memory_space=pltpu.VMEM)
    return pl.pallas_call(
        functools.partial(_exchange_kernel, y_count),
        out_shape=jax.ShapeDtypeStruct(x.shape, x.dtype),
        in_specs=[vmem],
        out_specs=vmem,
        scratch_shapes=[
            pltpu.SemaphoreType.DMA((1,)),
            pltpu.SemaphoreType.DMA((count,)),
            pltpu.SemaphoreType.DMA((count,)),
        ],
        compiler_params=pltpu.CompilerParams(collective_id=collective_id, has_side_effects=True),
    )(x)


def shards(spectrum, land_sea, sea_index, sea_count, wind_speed, wind_dir, slope_x, slope_y):
    local_bands, dir_count, row_count, col_count = spectrum.shape
    z_count = lax.axis_size("z")
    y_count = lax.axis_size("y")
    z_pos = lax.axis_index("z")
    y_pos = lax.axis_index("y")
    spec_pos = z_pos * y_count + y_pos
    dtheta = 2.0 * math.pi / dir_count
    angles = (jnp.arange(dir_count).astype(jnp.float32) + 0.5) * dtheta
    face_angles = jnp.arange(dir_count + 1).astype(jnp.float32) * dtheta
    band_ids = (spec_pos * local_bands + jnp.arange(local_bands)).astype(jnp.float32)
    radian_freq, wavenum, courant, turn_rate, band_spread = band_table(band_ids)
    wet_mask = land_sea.astype(jnp.float32)
    density = spectrum * wet_mask
    padded = extended(density, (("geo", 2),), 2)
    density = (
        advect(padded, (courant[:, None] * jnp.cos(angles)[None, :])[:, :, None, None], 2)
        * wet_mask
    )
    padded = jnp.pad(density, ((0, 0), (0, 0), (0, 0), (2, 2)))
    density = (
        advect(padded, (courant[:, None] * jnp.sin(angles)[None, :])[:, :, None, None], 3)
        * wet_mask
    )
    turning = turn_rate[:, None, None, None] * (
        jnp.sin(face_angles)[None, :, None, None] * slope_x
        - jnp.cos(face_angles)[None, :, None, None] * slope_y
    )
    padded = jnp.concatenate([density[:, -2:], density, density[:, :2]], axis=1)
    floored = jnp.maximum(advect(padded, turning, 1), 0.0)
    y_count = lax.axis_size("y")
    band_total = local_bands * z_count * y_count
    by_row = jnp.transpose(floored[0], (1, 0, 2))
    point_block = exchange(by_row, y_count, 0)
    row = lax.dynamic_slice_in_dim(wind_speed, spec_pos, 1, axis=0)[0]
    angle = lax.dynamic_slice_in_dim(wind_dir, spec_pos, 1, axis=0)[0]
    wet_row = lax.dynamic_slice_in_dim(wet_mask, spec_pos, 1, axis=0)[0]
    updated = local_sources(point_block, row, angle, angles, dtheta) * wet_row
    by_band = exchange(updated, y_count, 1)
    return jnp.transpose(by_band, (1, 0, 2))[None]


def solution(mesh):
    geo_count = mesh.shape["geo"]
    spec_count = mesh.shape["spec"]
    local = jax.sharding.Mesh(
        mesh.devices.reshape(geo_count, spec_count // Y_GROUP, Y_GROUP), ("geo", "z", "y")
    )
    spec = ("z", "y")
    placed = (
        P(spec, None, "geo", None),
        P("geo", None),
        P("geo", None),
        P("geo"),
        P("geo", None),
        P("geo", None),
        P("geo", None),
        P("geo", None),
    )
    return jax.shard_map(
        shards, mesh=local, in_specs=placed, out_specs=P(spec, None, "geo", None), check_vma=False
    )
```

```python
import functools
import math

import jax
import jax.numpy as jnp
from jax import lax
from jax.experimental import pallas as pl
from jax.experimental.pallas import tpu as pltpu
from jax.sharding import PartitionSpec as P

GRAVITY = 9.81
BASE_FREQ = 0.035
GROWTH = 1.1
COURANT_TOP = 0.9
TURN_TOP = 1.2
SPACING = 0.1
USTAR_RATIO = 0.035
WIND_COEF = 0.0375
WHITECAP = 0.36
STEEP_REF = 1.6
EPSILON = 1e-06
QUAD_COEF = 100.0


def _gather_rows_kernel(y_count, x_ref, out_ref, local_sem, send_sems, recv_sems):
    geo = lax.axis_index("geo")
    z_pos = lax.axis_index("z")
    y_pos = lax.axis_index("y")
    rows = x_ref.shape[2]
    mesh_id = pl.DeviceIdType.MESH
    barrier = pltpu.get_barrier_semaphore()
    for offset in range(1, y_count):
        pl.semaphore_signal(barrier, inc=1, device_id=(geo, z_pos, lax.rem(y_pos + offset, y_count)),
                            device_id_type=mesh_id)
    pl.semaphore_wait(barrier, y_count - 1)
    mine = out_ref.at[0, :, pl.ds(pl.multiple_of(y_pos * rows, rows), rows)]
    local = pltpu.make_async_copy(x_ref.at[y_pos], mine, local_sem.at[0])
    local.start()
    copies = []
    for offset in range(1, y_count):
        target = lax.rem(y_pos + offset, y_count)
        copy = pltpu.make_async_remote_copy(
            src_ref=x_ref.at[target],
            dst_ref=mine,
            send_sem=send_sems.at[offset],
            recv_sem=recv_sems.at[offset],
            device_id=(geo, z_pos, target),
            device_id_type=mesh_id,
        )
        copy.start()
        copies.append(copy)
    local.wait()
    for copy in copies:
        copy.wait_send()
        copy.wait_recv()


def gather_rows(x, y_count):
    group, dirs, rows, cols = x.shape
    vmem = pl.BlockSpec(memory_space=pltpu.VMEM)
    return pl.pallas_call(
        functools.partial(_gather_rows_kernel, y_count),
        out_shape=jax.ShapeDtypeStruct((1, dirs, rows * y_count, cols), x.dtype),
        in_specs=[vmem],
        out_specs=vmem,
        scratch_shapes=[
            pltpu.SemaphoreType.DMA((1,)),
            pltpu.SemaphoreType.DMA((y_count,)),
            pltpu.SemaphoreType.DMA((y_count,)),
        ],
        compiler_params=pltpu.CompilerParams(collective_id=2, has_side_effects=True),
    )(x)


def extended(cells, sides, width):
    for axis, dim in sides:
        count = lax.axis_size(axis)
        ends = count - 1
        head = lax.slice_in_dim(cells, 0, width, axis=dim)
        tail = lax.slice_in_dim(cells, cells.shape[dim] - width, cells.shape[dim], axis=dim)
        cells = jnp.concatenate(
            [
                lax.ppermute(tail, axis, [(i, (i + 1) % count) for i in range(ends)]),
                cells,
                lax.ppermute(head, axis, [((i + 1) % count, i) for i in range(ends)]),
            ],
            axis=dim,
        )
    return cells


def band_table(band_ids):
    growth_factor = jnp.power(GROWTH, band_ids)
    radian_freq = 2.0 * math.pi * BASE_FREQ * growth_factor
    wavenum = radian_freq * radian_freq / GRAVITY
    return (
        radian_freq,
        wavenum,
        COURANT_TOP / growth_factor,
        TURN_TOP / growth_factor,
        SPACING * radian_freq,
    )


def quick_flux(far_left, near_left, near_right, far_right, courant):
    forward = courant >= 0
    upwind = jnp.where(forward, far_left, far_right)
    center = jnp.where(forward, near_left, near_right)
    downwind = jnp.where(forward, near_right, near_left)
    face_value = (
        0.5 * (center + downwind)
        - 0.5 * jnp.abs(courant) * (downwind - center)
        - (1.0 - courant * courant) / 6.0 * (downwind - 2.0 * center + upwind)
    )
    return courant * face_value


def advect(padded, courant, along):
    face_count = padded.shape[along] - 4
    shifted = [
        lax.slice_in_dim(padded, offset, offset + face_count + 1, axis=along) for offset in range(4)
    ]
    face_flux = quick_flux(shifted[0], shifted[1], shifted[2], shifted[3], courant)
    centre_cells = lax.slice_in_dim(padded, 2, 2 + face_count, axis=along)
    upper_flux = lax.slice_in_dim(face_flux, 1, face_count + 1, axis=along)
    lower_flux = lax.slice_in_dim(face_flux, 0, face_count, axis=along)
    return centre_cells - (upper_flux - lower_flux)


def quad_delta(center, above, below, energy, dir_axis):
    plus = jnp.roll(above, -1, axis=dir_axis)
    minus = jnp.roll(below, 3, axis=dir_axis)
    return (
        QUAD_COEF
        * (center * center * (plus + minus) - 2.0 * center * plus * minus)
        / (energy * energy)
    )


def quad_term(delta, delta_above, delta_below, dir_axis):
    return (
        -2.0 * delta
        + jnp.roll(delta_below, 1, axis=dir_axis)
        + jnp.roll(delta_above, -3, axis=dir_axis)
    )


def band_neighbours(values):
    empty = jnp.zeros((1,) + values.shape[1:], jnp.float32)
    return (
        jnp.concatenate([values[1:], empty], axis=0),
        jnp.concatenate([empty, values[:-1]], axis=0),
    )


def sources(density, energy_sum, first_sum, root_sum, radian_freq, wavenum, cosine, wind_speed):
    energy = energy_sum + EPSILON
    mean_sigma = energy / (first_sum + EPSILON)
    ratio_k = energy / (root_sum + EPSILON)
    mean_k = ratio_k * ratio_k
    steepness = energy * mean_k * mean_k / STEEP_REF
    decay_rate = WHITECAP * mean_sigma * (wavenum / mean_k) * steepness * steepness
    growth_rate = (
        WIND_COEF
        * radian_freq
        * jnp.maximum(28.0 * USTAR_RATIO * wind_speed * radian_freq / GRAVITY * cosine - 1.0, 0.0)
    )
    return density * (1.0 + growth_rate) / (1.0 + decay_rate)


def local_sources(point_block, wind_block, wind_angle, angles, dtheta):
    band_total = point_block.shape[0]
    band_ids = jnp.arange(band_total).astype(jnp.float32)
    radian_freq, wavenum, courant, turn_rate, band_spread = band_table(band_ids)
    scaled = point_block * (band_spread * dtheta)[:, None, None]
    energy_sum = jnp.sum(scaled, axis=(0, 1))
    first_sum = jnp.sum(scaled / radian_freq[:, None, None], axis=(0, 1))
    root_sum = jnp.sum(scaled / jnp.sqrt(wavenum)[:, None, None], axis=(0, 1))
    energy = energy_sum + EPSILON
    above, below = band_neighbours(point_block)
    delta = quad_delta(point_block, above, below, energy, 1)
    delta_above, delta_below = band_neighbours(delta)
    extra = quad_term(delta, delta_above, delta_below, 1)
    cosine = jnp.cos(angles[:, None] - wind_angle[None, :])
    return (
        sources(
            point_block,
            energy_sum,
            first_sum,
            root_sum,
            radian_freq[:, None, None],
            wavenum[:, None, None],
            cosine,
            wind_block,
        )
        + extra
    )


Y_GROUP = 4
HALO = 2
SPREAD_CHUNKS = 4


def _z_gather_kernel(z_count, part_ref, gathered_ref, gather_send, gather_recv):
    geo = lax.axis_index("geo")
    z_pos = lax.axis_index("z")
    y_pos = lax.axis_index("y")
    barrier = pltpu.get_barrier_semaphore()
    for offset in range(1, z_count):
        target = lax.rem(z_pos + offset, z_count)
        pl.semaphore_signal(barrier, inc=1, device_id=(geo, target, y_pos),
                            device_id_type=pl.DeviceIdType.MESH)
    pl.semaphore_wait(barrier, z_count - 1)
    copies = []
    for offset in range(1, z_count):
        target = lax.rem(z_pos + offset, z_count)
        copy = pltpu.make_async_remote_copy(
            src_ref=part_ref,
            dst_ref=gathered_ref.at[z_pos],
            send_sem=gather_send.at[offset],
            recv_sem=gather_recv.at[offset],
            device_id=(geo, target, y_pos),
            device_id_type=pl.DeviceIdType.MESH,
        )
        copy.start()
        copies.append(copy)
    gathered_ref[z_pos] = part_ref[...]
    for copy in copies:
        copy.wait_send()
        copy.wait_recv()


def z_gather(part, z_count):
    vmem = pl.BlockSpec(memory_space=pltpu.VMEM)
    return pl.pallas_call(
        functools.partial(_z_gather_kernel, z_count),
        out_shape=jax.ShapeDtypeStruct((z_count,) + part.shape, part.dtype),
        in_specs=[vmem],
        out_specs=vmem,
        scratch_shapes=[
            pltpu.SemaphoreType.DMA((z_count,)),
            pltpu.SemaphoreType.DMA((z_count,)),
        ],
        compiler_params=pltpu.CompilerParams(collective_id=0, has_side_effects=True),
    )(part)


def _spread_kernel(z_count, y_count, chunks, floored_ref, ext_ref, y_send, local_sem, slot_recv, z_send):
    geo = lax.axis_index("geo")
    z_pos = lax.axis_index("z")
    y_pos = lax.axis_index("y")
    rows = ext_ref.shape[2]
    width = ext_ref.shape[1] // chunks
    mesh_id = pl.DeviceIdType.MESH
    barrier = pltpu.get_barrier_semaphore()
    for offset in range(1, y_count):
        pl.semaphore_signal(barrier, inc=1, device_id=(geo, z_pos, lax.rem(y_pos + offset, y_count)),
                            device_id_type=mesh_id)
    for step in (1, z_count - 1):
        pl.semaphore_signal(barrier, inc=1, device_id=(geo, lax.rem(z_pos + step, z_count), y_pos),
                            device_id_type=mesh_id)
    pl.semaphore_wait(barrier, y_count + 1)

    own_slot = HALO + y_pos

    def planes(chunk):
        return pl.ds(chunk * width, width)

    def y_sends(chunk):
        copies = []
        for offset in range(1, y_count):
            target = lax.rem(y_pos + offset, y_count)
            copies.append(pltpu.make_async_remote_copy(
                src_ref=floored_ref.at[0, planes(chunk), pl.ds(pl.multiple_of(target * rows, rows), rows)],
                dst_ref=ext_ref.at[own_slot, planes(chunk)],
                send_sem=y_send.at[offset * chunks + chunk],
                recv_sem=slot_recv.at[own_slot * chunks + chunk],
                device_id=(geo, z_pos, target),
                device_id_type=mesh_id,
            ))
        copies.append(pltpu.make_async_copy(
            floored_ref.at[0, planes(chunk), pl.ds(pl.multiple_of(y_pos * rows, rows), rows)],
            ext_ref.at[own_slot, planes(chunk)],
            local_sem.at[chunk],
        ))
        return copies

    def forward(slot, dst_slot, target_z, chunk):
        return pltpu.make_async_remote_copy(
            src_ref=ext_ref.at[slot, planes(chunk)],
            dst_ref=ext_ref.at[dst_slot, planes(chunk)],
            send_sem=z_send.at[(slot - HALO) * chunks + chunk],
            recv_sem=slot_recv.at[dst_slot * chunks + chunk],
            device_id=(geo, target_z, y_pos),
            device_id_type=mesh_id,
        )

    @pl.when(z_pos == 0)
    def _():
        ext_ref[pl.ds(0, HALO)] = jnp.zeros((HALO,) + ext_ref.shape[1:], ext_ref.dtype)

    @pl.when(z_pos == z_count - 1)
    def _():
        ext_ref[pl.ds(HALO + y_count, HALO)] = jnp.zeros((HALO,) + ext_ref.shape[1:], ext_ref.dtype)

    pending = y_sends(0)
    for copy in pending:
        copy.start()
    forwards = []
    for chunk in range(chunks):
        for band in range(y_count):
            slot = HALO + band
            arrival = pltpu.make_async_remote_copy(
                src_ref=ext_ref.at[slot, planes(chunk)],
                dst_ref=ext_ref.at[slot, planes(chunk)],
                send_sem=y_send.at[chunk],
                recv_sem=slot_recv.at[slot * chunks + chunk],
                device_id=(geo, z_pos, lax.rem(y_pos + 1, y_count)),
                device_id_type=mesh_id,
            )
            local = pending[-1]

            @pl.when(y_pos == band)
            def _():
                local.wait()

            @pl.when(y_pos != band)
            def _():
                arrival.wait_recv()

            if band < HALO:
                fwd = forward(slot, slot + y_count, z_pos - 1, chunk)
                live = z_pos > 0
            elif band >= y_count - HALO:
                fwd = forward(slot, slot - y_count, z_pos + 1, chunk)
                live = z_pos < z_count - 1
            else:
                continue

            @pl.when(live)
            def _():
                fwd.start()

            forwards.append((fwd, live))
        for copy in pending[:-1]:
            copy.wait_send()
        if chunk + 1 < chunks:
            pending = y_sends(chunk + 1)
            for copy in pending:
                copy.start()
    for fwd, live in forwards:

        @pl.when(live)
        def _():
            fwd.wait_send()

    for chunk in range(chunks):
        for slot, live in ((0, z_pos > 0), (1, z_pos > 0),
                           (HALO + y_count, z_pos < z_count - 1), (HALO + y_count + 1, z_pos < z_count - 1)):
            incoming = pltpu.make_async_remote_copy(
                src_ref=ext_ref.at[slot, planes(chunk)],
                dst_ref=ext_ref.at[slot, planes(chunk)],
                send_sem=z_send.at[chunk],
                recv_sem=slot_recv.at[slot * chunks + chunk],
                device_id=(geo, lax.rem(z_pos + 1, z_count), y_pos),
                device_id_type=mesh_id,
            )

            @pl.when(live)
            def _():
                incoming.wait_recv()


def spread(floored, z_count, y_count):
    _, dirs, rows, cols = floored.shape
    part_rows = rows // y_count
    chunks = SPREAD_CHUNKS
    assert dirs % chunks == 0
    vmem = pl.BlockSpec(memory_space=pltpu.VMEM)
    slots = y_count + 2 * HALO
    return pl.pallas_call(
        functools.partial(_spread_kernel, z_count, y_count, chunks),
        out_shape=jax.ShapeDtypeStruct((slots, dirs, part_rows, cols), floored.dtype),
        in_specs=[vmem],
        out_specs=vmem,
        scratch_shapes=[
            pltpu.SemaphoreType.DMA((y_count * chunks,)),
            pltpu.SemaphoreType.DMA((chunks,)),
            pltpu.SemaphoreType.DMA((slots * chunks,)),
            pltpu.SemaphoreType.DMA((y_count * chunks,)),
        ],
        compiler_params=pltpu.CompilerParams(collective_id=1, has_side_effects=True),
    )(floored)


def extended(cells, sides, width):
    for axis, dim in sides:
        count = lax.axis_size(axis)
        ends = count - 1
        head = lax.slice_in_dim(cells, 0, width, axis=dim)
        tail = lax.slice_in_dim(cells, cells.shape[dim] - width, cells.shape[dim], axis=dim)
        cells = jnp.concatenate(
            [
                lax.ppermute(tail, axis, [(i, (i + 1) % count) for i in range(ends)]),
                cells,
                lax.ppermute(head, axis, [((i + 1) % count, i) for i in range(ends)]),
            ],
            axis=dim,
        )
    return cells


def band_table(band_ids):
    growth_factor = jnp.power(GROWTH, band_ids)
    radian_freq = 2.0 * math.pi * BASE_FREQ * growth_factor
    wavenum = radian_freq * radian_freq / GRAVITY
    return (
        radian_freq,
        wavenum,
        COURANT_TOP / growth_factor,
        TURN_TOP / growth_factor,
        SPACING * radian_freq,
    )


def quick_flux(far_left, near_left, near_right, far_right, courant):
    forward = courant >= 0
    upwind = jnp.where(forward, far_left, far_right)
    center = jnp.where(forward, near_left, near_right)
    downwind = jnp.where(forward, near_right, near_left)
    face_value = (
        0.5 * (center + downwind)
        - 0.5 * jnp.abs(courant) * (downwind - center)
        - (1.0 - courant * courant) / 6.0 * (downwind - 2.0 * center + upwind)
    )
    return courant * face_value


def advect(padded, courant, along):
    face_count = padded.shape[along] - 4
    shifted = [
        lax.slice_in_dim(padded, offset, offset + face_count + 1, axis=along) for offset in range(4)
    ]
    face_flux = quick_flux(shifted[0], shifted[1], shifted[2], shifted[3], courant)
    centre_cells = lax.slice_in_dim(padded, 2, 2 + face_count, axis=along)
    upper_flux = lax.slice_in_dim(face_flux, 1, face_count + 1, axis=along)
    lower_flux = lax.slice_in_dim(face_flux, 0, face_count, axis=along)
    return centre_cells - (upper_flux - lower_flux)


def quad_delta(center, above, below, energy, dir_axis):
    plus = jnp.roll(above, -1, axis=dir_axis)
    minus = jnp.roll(below, 3, axis=dir_axis)
    return (
        QUAD_COEF
        * (center * center * (plus + minus) - 2.0 * center * plus * minus)
        / (energy * energy)
    )


def quad_term(delta, delta_above, delta_below, dir_axis):
    return (
        -2.0 * delta
        + jnp.roll(delta_below, 1, axis=dir_axis)
        + jnp.roll(delta_above, -3, axis=dir_axis)
    )


def band_neighbours(values):
    empty = jnp.zeros((1,) + values.shape[1:], jnp.float32)
    return (
        jnp.concatenate([values[1:], empty], axis=0),
        jnp.concatenate([empty, values[:-1]], axis=0),
    )


def sources(density, energy_sum, first_sum, root_sum, radian_freq, wavenum, cosine, wind_speed):
    energy = energy_sum + EPSILON
    mean_sigma = energy / (first_sum + EPSILON)
    ratio_k = energy / (root_sum + EPSILON)
    mean_k = ratio_k * ratio_k
    steepness = energy * mean_k * mean_k / STEEP_REF
    decay_rate = WHITECAP * mean_sigma * (wavenum / mean_k) * steepness * steepness
    growth_rate = (
        WIND_COEF
        * radian_freq
        * jnp.maximum(28.0 * USTAR_RATIO * wind_speed * radian_freq / GRAVITY * cosine - 1.0, 0.0)
    )
    return density * (1.0 + growth_rate) / (1.0 + decay_rate)


def local_sources(point_block, wind_block, wind_angle, angles, dtheta):
    band_total = point_block.shape[0]
    band_ids = jnp.arange(band_total).astype(jnp.float32)
    radian_freq, wavenum, courant, turn_rate, band_spread = band_table(band_ids)
    scaled = point_block * (band_spread * dtheta)[:, None, None]
    energy_sum = jnp.sum(scaled, axis=(0, 1))
    first_sum = jnp.sum(scaled / radian_freq[:, None, None], axis=(0, 1))
    root_sum = jnp.sum(scaled / jnp.sqrt(wavenum)[:, None, None], axis=(0, 1))
    energy = energy_sum + EPSILON
    above, below = band_neighbours(point_block)
    delta = quad_delta(point_block, above, below, energy, 1)
    delta_above, delta_below = band_neighbours(delta)
    extra = quad_term(delta, delta_above, delta_below, 1)
    cosine = jnp.cos(angles[:, None] - wind_angle[None, :])
    return (
        sources(
            point_block,
            energy_sum,
            first_sum,
            root_sum,
            radian_freq[:, None, None],
            wavenum[:, None, None],
            cosine,
            wind_block,
        )
        + extra
    )


Y_GROUP = 4
HALO = 2


def _z_gather_kernel(z_count, part_ref, gathered_ref, gather_send, gather_recv):
    geo = lax.axis_index("geo")
    z_pos = lax.axis_index("z")
    y_pos = lax.axis_index("y")
    barrier = pltpu.get_barrier_semaphore()
    for offset in range(1, z_count):
        target = lax.rem(z_pos + offset, z_count)
        pl.semaphore_signal(barrier, inc=1, device_id=(geo, target, y_pos),
                            device_id_type=pl.DeviceIdType.MESH)
    pl.semaphore_wait(barrier, z_count - 1)
    copies = []
    for offset in range(1, z_count):
        target = lax.rem(z_pos + offset, z_count)
        copy = pltpu.make_async_remote_copy(
            src_ref=part_ref,
            dst_ref=gathered_ref.at[z_pos],
            send_sem=gather_send.at[offset],
            recv_sem=gather_recv.at[offset],
            device_id=(geo, target, y_pos),
            device_id_type=pl.DeviceIdType.MESH,
        )
        copy.start()
        copies.append(copy)
    gathered_ref[z_pos] = part_ref[...]
    for copy in copies:
        copy.wait_send()
        copy.wait_recv()


def z_gather(part, z_count):
    vmem = pl.BlockSpec(memory_space=pltpu.VMEM)
    return pl.pallas_call(
        functools.partial(_z_gather_kernel, z_count),
        out_shape=jax.ShapeDtypeStruct((z_count,) + part.shape, part.dtype),
        in_specs=[vmem],
        out_specs=vmem,
        scratch_shapes=[
            pltpu.SemaphoreType.DMA((z_count,)),
            pltpu.SemaphoreType.DMA((z_count,)),
        ],
        compiler_params=pltpu.CompilerParams(collective_id=0, has_side_effects=True),
    )(part)


def _spread_kernel(z_count, y_count, floored_ref, ext_ref, relay_ref, y_send, local_sem, slot_recv,
                   z_send, relay_send, relay_recv, pass_send, pass_recv):
    geo = lax.axis_index("geo")
    z_pos = lax.axis_index("z")
    y_pos = lax.axis_index("y")
    rows = ext_ref.shape[2]
    half = relay_ref.shape[1]
    mesh_id = pl.DeviceIdType.MESH
    up_y = lax.rem(y_pos + 1, y_count)
    down_y = lax.rem(y_pos + y_count - 1, y_count)
    barrier = pltpu.get_barrier_semaphore()
    for offset in range(1, y_count):
        pl.semaphore_signal(barrier, inc=1, device_id=(geo, z_pos, lax.rem(y_pos + offset, y_count)),
                            device_id_type=mesh_id)
    for step in (1, z_count - 1):
        pl.semaphore_signal(barrier, inc=1, device_id=(geo, lax.rem(z_pos + step, z_count), y_pos),
                            device_id_type=mesh_id)
    pl.semaphore_wait(barrier, y_count + 1)

    def quarter(target):
        return floored_ref.at[0, :, pl.ds(pl.multiple_of(target * rows, rows), rows)]

    own_slot = HALO + y_pos
    sends = []
    for offset in (1, y_count - 1):
        target = lax.rem(y_pos + offset, y_count)
        copy = pltpu.make_async_remote_copy(
            src_ref=quarter(target),
            dst_ref=ext_ref.at[own_slot],
            send_sem=y_send.at[offset],
            recv_sem=slot_recv.at[own_slot],
            device_id=(geo, z_pos, target),
            device_id_type=mesh_id,
        )
        copy.start()
        sends.append(copy)
    far = lax.rem(y_pos + 2, y_count)
    for side, via in ((0, up_y), (1, down_y)):
        copy = pltpu.make_async_remote_copy(
            src_ref=quarter(far).at[pl.ds(side * half, half)],
            dst_ref=relay_ref.at[side],
            send_sem=relay_send.at[side],
            recv_sem=relay_recv.at[side],
            device_id=(geo, z_pos, via),
            device_id_type=mesh_id,
        )
        copy.start()
        sends.append(copy)
    local = pltpu.make_async_copy(quarter(y_pos), ext_ref.at[own_slot], local_sem.at[0])
    local.start()

    @pl.when(z_pos == 0)
    def _():
        ext_ref[pl.ds(0, HALO)] = jnp.zeros((HALO,) + ext_ref.shape[1:], ext_ref.dtype)

    @pl.when(z_pos == z_count - 1)
    def _():
        ext_ref[pl.ds(HALO + y_count, HALO)] = jnp.zeros((HALO,) + ext_ref.shape[1:], ext_ref.dtype)

    passes = []
    for side, origin, onward in ((0, down_y, up_y), (1, up_y, down_y)):
        relay_in = pltpu.make_async_remote_copy(
            src_ref=relay_ref.at[side],
            dst_ref=relay_ref.at[side],
            send_sem=relay_send.at[side],
            recv_sem=relay_recv.at[side],
            device_id=(geo, z_pos, onward),
            device_id_type=mesh_id,
        )
        relay_in.wait_recv()
        onward_copy = pltpu.make_async_remote_copy(
            src_ref=relay_ref.at[side],
            dst_ref=ext_ref.at[HALO + origin, pl.ds(side * half, half)],
            send_sem=pass_send.at[side],
            recv_sem=pass_recv.at[side],
            device_id=(geo, z_pos, onward),
            device_id_type=mesh_id,
        )
        onward_copy.start()
        passes.append(onward_copy)

    def forward(slot, dst_slot, target_z):
        return pltpu.make_async_remote_copy(
            src_ref=ext_ref.at[slot],
            dst_ref=ext_ref.at[dst_slot],
            send_sem=z_send.at[slot - HALO],
            recv_sem=slot_recv.at[dst_slot],
            device_id=(geo, target_z, y_pos),
            device_id_type=mesh_id,
        )

    forwards = []
    for band in range(y_count):
        slot = HALO + band
        distance = lax.rem(band - y_pos + y_count, y_count)
        arrival = pltpu.make_async_remote_copy(
            src_ref=ext_ref.at[slot],
            dst_ref=ext_ref.at[slot],
            send_sem=y_send.at[0],
            recv_sem=slot_recv.at[slot],
            device_id=(geo, z_pos, up_y),
            device_id_type=mesh_id,
        )
        relayed = [
            pltpu.make_async_remote_copy(
                src_ref=ext_ref.at[slot, pl.ds(side * half, half)],
                dst_ref=ext_ref.at[slot, pl.ds(side * half, half)],
                send_sem=pass_send.at[side],
                recv_sem=pass_recv.at[side],
                device_id=(geo, z_pos, up_y),
                device_id_type=mesh_id,
            )
            for side in (0, 1)
        ]

        @pl.when(distance == 0)
        def _():
            local.wait()

        @pl.when((distance == 1) | (distance == y_count - 1))
        def _():
            arrival.wait_recv()

        @pl.when(distance == 2)
        def _():
            for copy in relayed:
                copy.wait_recv()

        if band < HALO:
            fwd = forward(slot, slot + y_count, z_pos - 1)
            live = z_pos > 0
        elif band >= y_count - HALO:
            fwd = forward(slot, slot - y_count, z_pos + 1)
            live = z_pos < z_count - 1
        else:
            continue

        @pl.when(live)
        def _():
            fwd.start()

        forwards.append((fwd, live))
    for copy in sends + passes:
        copy.wait_send()
    for fwd, live in forwards:

        @pl.when(live)
        def _():
            fwd.wait_send()

    for slot, live in ((0, z_pos > 0), (1, z_pos > 0),
                       (HALO + y_count, z_pos < z_count - 1), (HALO + y_count + 1, z_pos < z_count - 1)):
        incoming = pltpu.make_async_remote_copy(
            src_ref=ext_ref.at[slot],
            dst_ref=ext_ref.at[slot],
            send_sem=z_send.at[0],
            recv_sem=slot_recv.at[slot],
            device_id=(geo, lax.rem(z_pos + 1, z_count), y_pos),
            device_id_type=mesh_id,
        )

        @pl.when(live)
        def _():
            incoming.wait_recv()


def spread(floored, z_count, y_count):
    _, dirs, rows, cols = floored.shape
    part_rows = rows // y_count
    vmem = pl.BlockSpec(memory_space=pltpu.VMEM)
    slots = y_count + 2 * HALO
    half = dirs // 2
    assert 2 * half == dirs
    return pl.pallas_call(
        functools.partial(_spread_kernel, z_count, y_count),
        out_shape=jax.ShapeDtypeStruct((slots, dirs, part_rows, cols), floored.dtype),
        in_specs=[vmem],
        out_specs=vmem,
        scratch_shapes=[
            pltpu.VMEM((2, half, part_rows, cols), floored.dtype),
            pltpu.SemaphoreType.DMA((y_count,)),
            pltpu.SemaphoreType.DMA((1,)),
            pltpu.SemaphoreType.DMA((slots,)),
            pltpu.SemaphoreType.DMA((y_count,)),
            pltpu.SemaphoreType.DMA((2,)),
            pltpu.SemaphoreType.DMA((2,)),
            pltpu.SemaphoreType.DMA((2,)),
            pltpu.SemaphoreType.DMA((2,)),
        ],
        compiler_params=pltpu.CompilerParams(collective_id=1, has_side_effects=True),
    )(floored)


def extended(cells, sides, width):
    for axis, dim in sides:
        count = lax.axis_size(axis)
        ends = count - 1
        head = lax.slice_in_dim(cells, 0, width, axis=dim)
        tail = lax.slice_in_dim(cells, cells.shape[dim] - width, cells.shape[dim], axis=dim)
        cells = jnp.concatenate(
            [
                lax.ppermute(tail, axis, [(i, (i + 1) % count) for i in range(ends)]),
                cells,
                lax.ppermute(head, axis, [((i + 1) % count, i) for i in range(ends)]),
            ],
            axis=dim,
        )
    return cells


def band_table(band_ids):
    growth_factor = jnp.power(GROWTH, band_ids)
    radian_freq = 2.0 * math.pi * BASE_FREQ * growth_factor
    wavenum = radian_freq * radian_freq / GRAVITY
    return (
        radian_freq,
        wavenum,
        COURANT_TOP / growth_factor,
        TURN_TOP / growth_factor,
        SPACING * radian_freq,
    )


def quick_flux(far_left, near_left, near_right, far_right, courant):
    forward = courant >= 0
    upwind = jnp.where(forward, far_left, far_right)
    center = jnp.where(forward, near_left, near_right)
    downwind = jnp.where(forward, near_right, near_left)
    face_value = (
        0.5 * (center + downwind)
        - 0.5 * jnp.abs(courant) * (downwind - center)
        - (1.0 - courant * courant) / 6.0 * (downwind - 2.0 * center + upwind)
    )
    return courant * face_value


def advect(padded, courant, along):
    face_count = padded.shape[along] - 4
    shifted = [
        lax.slice_in_dim(padded, offset, offset + face_count + 1, axis=along) for offset in range(4)
    ]
    face_flux = quick_flux(shifted[0], shifted[1], shifted[2], shifted[3], courant)
    centre_cells = lax.slice_in_dim(padded, 2, 2 + face_count, axis=along)
    upper_flux = lax.slice_in_dim(face_flux, 1, face_count + 1, axis=along)
    lower_flux = lax.slice_in_dim(face_flux, 0, face_count, axis=along)
    return centre_cells - (upper_flux - lower_flux)


def quad_delta(center, above, below, energy, dir_axis):
    plus = jnp.roll(above, -1, axis=dir_axis)
    minus = jnp.roll(below, 3, axis=dir_axis)
    return (
        QUAD_COEF
        * (center * center * (plus + minus) - 2.0 * center * plus * minus)
        / (energy * energy)
    )


def quad_term(delta, delta_above, delta_below, dir_axis):
    return (
        -2.0 * delta
        + jnp.roll(delta_below, 1, axis=dir_axis)
        + jnp.roll(delta_above, -3, axis=dir_axis)
    )


def band_neighbours(values):
    empty = jnp.zeros((1,) + values.shape[1:], jnp.float32)
    return (
        jnp.concatenate([values[1:], empty], axis=0),
        jnp.concatenate([empty, values[:-1]], axis=0),
    )


def sources(density, energy_sum, first_sum, root_sum, radian_freq, wavenum, cosine, wind_speed):
    energy = energy_sum + EPSILON
    mean_sigma = energy / (first_sum + EPSILON)
    ratio_k = energy / (root_sum + EPSILON)
    mean_k = ratio_k * ratio_k
    steepness = energy * mean_k * mean_k / STEEP_REF
    decay_rate = WHITECAP * mean_sigma * (wavenum / mean_k) * steepness * steepness
    growth_rate = (
        WIND_COEF
        * radian_freq
        * jnp.maximum(28.0 * USTAR_RATIO * wind_speed * radian_freq / GRAVITY * cosine - 1.0, 0.0)
    )
    return density * (1.0 + growth_rate) / (1.0 + decay_rate)


def local_sources(point_block, wind_block, wind_angle, angles, dtheta):
    band_total = point_block.shape[0]
    band_ids = jnp.arange(band_total).astype(jnp.float32)
    radian_freq, wavenum, courant, turn_rate, band_spread = band_table(band_ids)
    scaled = point_block * (band_spread * dtheta)[:, None, None]
    energy_sum = jnp.sum(scaled, axis=(0, 1))
    first_sum = jnp.sum(scaled / radian_freq[:, None, None], axis=(0, 1))
    root_sum = jnp.sum(scaled / jnp.sqrt(wavenum)[:, None, None], axis=(0, 1))
    energy = energy_sum + EPSILON
    above, below = band_neighbours(point_block)
    delta = quad_delta(point_block, above, below, energy, 1)
    delta_above, delta_below = band_neighbours(delta)
    extra = quad_term(delta, delta_above, delta_below, 1)
    cosine = jnp.cos(angles[:, None] - wind_angle[None, :])
    return (
        sources(
            point_block,
            energy_sum,
            first_sum,
            root_sum,
            radian_freq[:, None, None],
            wavenum[:, None, None],
            cosine,
            wind_block,
        )
        + extra
    )


Y_GROUP = 4
HALO = 2


def _z_gather_kernel(z_count, part_ref, gathered_ref, gather_send, gather_recv):
    geo = lax.axis_index("geo")
    z_pos = lax.axis_index("z")
    y_pos = lax.axis_index("y")
    barrier = pltpu.get_barrier_semaphore()
    for offset in range(1, z_count):
        target = lax.rem(z_pos + offset, z_count)
        pl.semaphore_signal(barrier, inc=1, device_id=(geo, target, y_pos),
                            device_id_type=pl.DeviceIdType.MESH)
    pl.semaphore_wait(barrier, z_count - 1)
    copies = []
    for offset in range(1, z_count):
        target = lax.rem(z_pos + offset, z_count)
        copy = pltpu.make_async_remote_copy(
            src_ref=part_ref,
            dst_ref=gathered_ref.at[z_pos],
            send_sem=gather_send.at[offset],
            recv_sem=gather_recv.at[offset],
            device_id=(geo, target, y_pos),
            device_id_type=pl.DeviceIdType.MESH,
        )
        copy.start()
        copies.append(copy)
    gathered_ref[z_pos] = part_ref[...]
    for copy in copies:
        copy.wait_send()
        copy.wait_recv()


def z_gather(part, z_count):
    vmem = pl.BlockSpec(memory_space=pltpu.VMEM)
    return pl.pallas_call(
        functools.partial(_z_gather_kernel, z_count),
        out_shape=jax.ShapeDtypeStruct((z_count,) + part.shape, part.dtype),
        in_specs=[vmem],
        out_specs=vmem,
        scratch_shapes=[
            pltpu.SemaphoreType.DMA((z_count,)),
            pltpu.SemaphoreType.DMA((z_count,)),
        ],
        compiler_params=pltpu.CompilerParams(collective_id=0, has_side_effects=True),
    )(part)


def _spread_kernel(z_count, y_count, floored_ref, ext_ref, y_send, local_sem, slot_recv, z_send):
    geo = lax.axis_index("geo")
    z_pos = lax.axis_index("z")
    y_pos = lax.axis_index("y")
    rows = ext_ref.shape[2]
    mesh_id = pl.DeviceIdType.MESH
    barrier = pltpu.get_barrier_semaphore()
    for offset in range(1, y_count):
        pl.semaphore_signal(barrier, inc=1, device_id=(geo, z_pos, lax.rem(y_pos + offset, y_count)),
                            device_id_type=mesh_id)

    for step in (1, z_count - 1):
        pl.semaphore_signal(barrier, inc=1, device_id=(geo, lax.rem(z_pos + step, z_count), y_pos),
                            device_id_type=mesh_id)
    pl.semaphore_wait(barrier, y_count + 1)

    own_slot = HALO + y_pos
    sends = []
    for offset in range(1, y_count):
        target = lax.rem(y_pos + offset, y_count)
        copy = pltpu.make_async_remote_copy(
            src_ref=floored_ref.at[0, :, pl.ds(pl.multiple_of(target * rows, rows), rows)],
            dst_ref=ext_ref.at[own_slot],
            send_sem=y_send.at[offset],
            recv_sem=slot_recv.at[own_slot],
            device_id=(geo, z_pos, target),
            device_id_type=mesh_id,
        )
        copy.start()
        sends.append(copy)
    local = pltpu.make_async_copy(
        floored_ref.at[0, :, pl.ds(pl.multiple_of(y_pos * rows, rows), rows)],
        ext_ref.at[own_slot],
        local_sem.at[0],
    )
    local.start()

    @pl.when(z_pos == 0)
    def _():
        ext_ref[pl.ds(0, HALO)] = jnp.zeros((HALO,) + ext_ref.shape[1:], ext_ref.dtype)

    @pl.when(z_pos == z_count - 1)
    def _():
        ext_ref[pl.ds(HALO + y_count, HALO)] = jnp.zeros((HALO,) + ext_ref.shape[1:], ext_ref.dtype)

    def forward(slot, dst_slot, target_z):
        return pltpu.make_async_remote_copy(
            src_ref=ext_ref.at[slot],
            dst_ref=ext_ref.at[dst_slot],
            send_sem=z_send.at[slot - HALO],
            recv_sem=slot_recv.at[dst_slot],
            device_id=(geo, target_z, y_pos),
            device_id_type=mesh_id,
        )

    forwards = []
    for band in range(y_count):
        slot = HALO + band
        arrival = pltpu.make_async_remote_copy(
            src_ref=ext_ref.at[slot],
            dst_ref=ext_ref.at[slot],
            send_sem=y_send.at[0],
            recv_sem=slot_recv.at[slot],
            device_id=(geo, z_pos, lax.rem(y_pos + 1, y_count)),
            device_id_type=mesh_id,
        )

        @pl.when(y_pos == band)
        def _():
            local.wait()

        @pl.when(y_pos != band)
        def _():
            arrival.wait_recv()

        if band < HALO:
            fwd = forward(slot, slot + y_count, z_pos - 1)
            live = z_pos > 0
        elif band >= y_count - HALO:
            fwd = forward(slot, slot - y_count, z_pos + 1)
            live = z_pos < z_count - 1
        else:
            continue

        @pl.when(live)
        def _():
            fwd.start()

        forwards.append((fwd, live))
    for copy in sends:
        copy.wait_send()
    for fwd, live in forwards:

        @pl.when(live)
        def _():
            fwd.wait_send()

    for slot, live in ((0, z_pos > 0), (1, z_pos > 0),
                       (HALO + y_count, z_pos < z_count - 1), (HALO + y_count + 1, z_pos < z_count - 1)):
        incoming = pltpu.make_async_remote_copy(
            src_ref=ext_ref.at[slot],
            dst_ref=ext_ref.at[slot],
            send_sem=z_send.at[0],
            recv_sem=slot_recv.at[slot],
            device_id=(geo, lax.rem(z_pos + 1, z_count), y_pos),
            device_id_type=mesh_id,
        )

        @pl.when(live)
        def _():
            incoming.wait_recv()


def spread(floored, z_count, y_count):
    _, dirs, rows, cols = floored.shape
    part_rows = rows // y_count
    vmem = pl.BlockSpec(memory_space=pltpu.VMEM)
    slots = y_count + 2 * HALO
    return pl.pallas_call(
        functools.partial(_spread_kernel, z_count, y_count),
        out_shape=jax.ShapeDtypeStruct((slots, dirs, part_rows, cols), floored.dtype),
        in_specs=[vmem],
        out_specs=vmem,
        scratch_shapes=[
            pltpu.SemaphoreType.DMA((y_count,)),
            pltpu.SemaphoreType.DMA((1,)),
            pltpu.SemaphoreType.DMA((slots,)),
            pltpu.SemaphoreType.DMA((y_count,)),
        ],
        compiler_params=pltpu.CompilerParams(collective_id=1, has_side_effects=True),
    )(floored)


def shards(spectrum, land_sea, sea_index, sea_count, wind_speed, wind_dir, slope_x, slope_y):
    local_bands, dir_count, row_count, col_count = spectrum.shape
    z_count = lax.axis_size("z")
    y_count = lax.axis_size("y")
    z_pos = lax.axis_index("z")
    y_pos = lax.axis_index("y")
    spec_pos = z_pos * y_count + y_pos
    dtheta = 2.0 * math.pi / dir_count
    angles = (jnp.arange(dir_count).astype(jnp.float32) + 0.5) * dtheta
    face_angles = jnp.arange(dir_count + 1).astype(jnp.float32) * dtheta
    band_ids = (spec_pos * local_bands + jnp.arange(local_bands)).astype(jnp.float32)
    radian_freq, wavenum, courant, turn_rate, band_spread = band_table(band_ids)
    wet_mask = land_sea.astype(jnp.float32)
    density = spectrum * wet_mask
    padded = extended(density, (("geo", 2),), 2)
    density = (
        advect(padded, (courant[:, None] * jnp.cos(angles)[None, :])[:, :, None, None], 2)
        * wet_mask
    )
    padded = jnp.pad(density, ((0, 0), (0, 0), (0, 0), (2, 2)))
    density = (
        advect(padded, (courant[:, None] * jnp.sin(angles)[None, :])[:, :, None, None], 3)
        * wet_mask
    )
    turning = turn_rate[:, None, None, None] * (
        jnp.sin(face_angles)[None, :, None, None] * slope_x
        - jnp.cos(face_angles)[None, :, None, None] * slope_y
    )
    padded = jnp.concatenate([density[:, -2:], density, density[:, :2]], axis=1)
    floored = jnp.maximum(advect(padded, turning, 1), 0.0)
    ext = spread(floored, z_count, lax.axis_size("y"))
    point = ext[HALO:-HALO]
    group = point.shape[0]
    part_rows = point.shape[2]
    group_ids = (z_pos * group + jnp.arange(group)).astype(jnp.float32)
    radian_freq, wavenum, courant, turn_rate, band_spread = band_table(group_ids)
    scaled = point * (band_spread * dtheta)[:, None, None, None]
    sums = jnp.stack(
        [
            jnp.sum(scaled, axis=(0, 1)),
            jnp.sum(scaled / radian_freq[:, None, None, None], axis=(0, 1)),
            jnp.sum(scaled / jnp.sqrt(wavenum)[:, None, None, None], axis=(0, 1)),
        ]
    )
    step = 1
    while step < z_count:
        sums = sums + lax.ppermute(sums, "z", [(i, i ^ step) for i in range(z_count)])
        step *= 2
    energy_sum, first_sum, root_sum = sums[0], sums[1], sums[2]
    energy = energy_sum + EPSILON
    center, plus, minus = ext[1:-1], jnp.roll(ext[2:], -1, axis=1), jnp.roll(ext[:-2], 3, axis=1)
    cubic = center * center * (plus + minus) - 2.0 * center * plus * minus
    extra = (
        -2.0 * cubic[1:-1] + jnp.roll(cubic[:-2], 1, axis=1) + jnp.roll(cubic[2:], -3, axis=1)
    ) * (QUAD_COEF / (energy * energy))
    row_start = y_pos * part_rows
    wind_block = lax.dynamic_slice_in_dim(wind_speed, row_start, part_rows, axis=0)
    wind_angle = lax.dynamic_slice_in_dim(wind_dir, row_start, part_rows, axis=0)
    wet_block = lax.dynamic_slice_in_dim(wet_mask, row_start, part_rows, axis=0)
    cosine = jnp.cos(angles[:, None, None] - wind_angle[None])
    updated = (
        sources(
            point,
            energy_sum,
            first_sum,
            root_sum,
            radian_freq[:, None, None, None],
            wavenum[:, None, None, None],
            cosine,
            wind_block,
        )
        + extra
    ) * wet_block
    return gather_rows(updated, lax.axis_size("y"))


def solution(mesh):
    geo_count = mesh.shape["geo"]
    spec_count = mesh.shape["spec"]
    local = jax.sharding.Mesh(
        mesh.devices.reshape(geo_count, spec_count // Y_GROUP, Y_GROUP), ("geo", "z", "y")
    )
    spec = ("z", "y")
    placed = (
        P(spec, None, "geo", None),
        P("geo", None),
        P("geo", None),
        P("geo"),
        P("geo", None),
        P("geo", None),
        P("geo", None),
        P("geo", None),
    )
    return jax.shard_map(
        shards, mesh=local, in_specs=placed, out_specs=P(spec, None, "geo", None), check_vma=False
    )
```

```python
import functools
import math

import jax
import jax.numpy as jnp
from jax import lax
from jax.experimental import pallas as pl
from jax.experimental.pallas import tpu as pltpu
from jax.sharding import PartitionSpec as P

GRAVITY = 9.81
BASE_FREQ = 0.035
GROWTH = 1.1
COURANT_TOP = 0.9
TURN_TOP = 1.2
SPACING = 0.1
USTAR_RATIO = 0.035
WIND_COEF = 0.0375
WHITECAP = 0.36
STEEP_REF = 1.6
EPSILON = 1e-06
QUAD_COEF = 100.0


def extended(cells, sides, width):
    for axis, dim in sides:
        count = lax.axis_size(axis)
        ends = count - 1
        head = lax.slice_in_dim(cells, 0, width, axis=dim)
        tail = lax.slice_in_dim(cells, cells.shape[dim] - width, cells.shape[dim], axis=dim)
        cells = jnp.concatenate(
            [
                lax.ppermute(tail, axis, [(i, (i + 1) % count) for i in range(ends)]),
                cells,
                lax.ppermute(head, axis, [((i + 1) % count, i) for i in range(ends)]),
            ],
            axis=dim,
        )
    return cells


def band_table(band_ids):
    growth_factor = jnp.power(GROWTH, band_ids)
    radian_freq = 2.0 * math.pi * BASE_FREQ * growth_factor
    wavenum = radian_freq * radian_freq / GRAVITY
    return (
        radian_freq,
        wavenum,
        COURANT_TOP / growth_factor,
        TURN_TOP / growth_factor,
        SPACING * radian_freq,
    )


def quick_flux(far_left, near_left, near_right, far_right, courant):
    forward = courant >= 0
    upwind = jnp.where(forward, far_left, far_right)
    center = jnp.where(forward, near_left, near_right)
    downwind = jnp.where(forward, near_right, near_left)
    face_value = (
        0.5 * (center + downwind)
        - 0.5 * jnp.abs(courant) * (downwind - center)
        - (1.0 - courant * courant) / 6.0 * (downwind - 2.0 * center + upwind)
    )
    return courant * face_value


def advect(padded, courant, along):
    face_count = padded.shape[along] - 4
    shifted = [
        lax.slice_in_dim(padded, offset, offset + face_count + 1, axis=along) for offset in range(4)
    ]
    face_flux = quick_flux(shifted[0], shifted[1], shifted[2], shifted[3], courant)
    centre_cells = lax.slice_in_dim(padded, 2, 2 + face_count, axis=along)
    upper_flux = lax.slice_in_dim(face_flux, 1, face_count + 1, axis=along)
    lower_flux = lax.slice_in_dim(face_flux, 0, face_count, axis=along)
    return centre_cells - (upper_flux - lower_flux)


def quad_delta(center, above, below, energy, dir_axis):
    plus = jnp.roll(above, -1, axis=dir_axis)
    minus = jnp.roll(below, 3, axis=dir_axis)
    return (
        QUAD_COEF
        * (center * center * (plus + minus) - 2.0 * center * plus * minus)
        / (energy * energy)
    )


def quad_term(delta, delta_above, delta_below, dir_axis):
    return (
        -2.0 * delta
        + jnp.roll(delta_below, 1, axis=dir_axis)
        + jnp.roll(delta_above, -3, axis=dir_axis)
    )


def band_neighbours(values):
    empty = jnp.zeros((1,) + values.shape[1:], jnp.float32)
    return (
        jnp.concatenate([values[1:], empty], axis=0),
        jnp.concatenate([empty, values[:-1]], axis=0),
    )


def sources(density, energy_sum, first_sum, root_sum, radian_freq, wavenum, cosine, wind_speed):
    energy = energy_sum + EPSILON
    mean_sigma = energy / (first_sum + EPSILON)
    ratio_k = energy / (root_sum + EPSILON)
    mean_k = ratio_k * ratio_k
    steepness = energy * mean_k * mean_k / STEEP_REF
    decay_rate = WHITECAP * mean_sigma * (wavenum / mean_k) * steepness * steepness
    growth_rate = (
        WIND_COEF
        * radian_freq
        * jnp.maximum(28.0 * USTAR_RATIO * wind_speed * radian_freq / GRAVITY * cosine - 1.0, 0.0)
    )
    return density * (1.0 + growth_rate) / (1.0 + decay_rate)


def local_sources(point_block, wind_block, wind_angle, angles, dtheta):
    band_total = point_block.shape[0]
    band_ids = jnp.arange(band_total).astype(jnp.float32)
    radian_freq, wavenum, courant, turn_rate, band_spread = band_table(band_ids)
    scaled = point_block * (band_spread * dtheta)[:, None, None]
    energy_sum = jnp.sum(scaled, axis=(0, 1))
    first_sum = jnp.sum(scaled / radian_freq[:, None, None], axis=(0, 1))
    root_sum = jnp.sum(scaled / jnp.sqrt(wavenum)[:, None, None], axis=(0, 1))
    energy = energy_sum + EPSILON
    above, below = band_neighbours(point_block)
    delta = quad_delta(point_block, above, below, energy, 1)
    delta_above, delta_below = band_neighbours(delta)
    extra = quad_term(delta, delta_above, delta_below, 1)
    cosine = jnp.cos(angles[:, None] - wind_angle[None, :])
    return (
        sources(
            point_block,
            energy_sum,
            first_sum,
            root_sum,
            radian_freq[:, None, None],
            wavenum[:, None, None],
            cosine,
            wind_block,
        )
        + extra
    )


Y_GROUP = 4
HALO = 2


def _z_halo_kernel(z_count, point_ref, lower_ref, upper_ref, halo_send, halo_recv):
    geo = lax.axis_index("geo")
    z_pos = lax.axis_index("z")
    y_pos = lax.axis_index("y")
    group = point_ref.shape[0]
    mesh_id = pl.DeviceIdType.MESH
    barrier = pltpu.get_barrier_semaphore()
    for step in (1, z_count - 1):
        pl.semaphore_signal(barrier, inc=1, device_id=(geo, lax.rem(z_pos + step, z_count), y_pos),
                            device_id_type=mesh_id)
    pl.semaphore_wait(barrier, 2)

    def halo_copy(src_lo, dst_ref, slot, target):
        return pltpu.make_async_remote_copy(
            src_ref=point_ref.at[pl.ds(src_lo, HALO)],
            dst_ref=dst_ref,
            send_sem=halo_send.at[slot],
            recv_sem=halo_recv.at[slot],
            device_id=(geo, target, y_pos),
            device_id_type=mesh_id,
        )

    up = halo_copy(group - HALO, lower_ref, 0, lax.rem(z_pos + 1, z_count))
    down = halo_copy(0, upper_ref, 1, lax.rem(z_pos + z_count - 1, z_count))

    @pl.when(z_pos < z_count - 1)
    def _():
        up.start()

    @pl.when(z_pos > 0)
    def _():
        down.start()

    @pl.when(z_pos == 0)
    def _():
        lower_ref[...] = jnp.zeros(lower_ref.shape, lower_ref.dtype)

    @pl.when(z_pos == z_count - 1)
    def _():
        upper_ref[...] = jnp.zeros(upper_ref.shape, upper_ref.dtype)

    @pl.when(z_pos < z_count - 1)
    def _():
        up.wait_send()
        down.wait_recv()

    @pl.when(z_pos > 0)
    def _():
        down.wait_send()
        up.wait_recv()


def z_halo(point, z_count):
    group, dirs, rows, cols = point.shape
    halo = jax.ShapeDtypeStruct((HALO, dirs, rows, cols), point.dtype)
    vmem = pl.BlockSpec(memory_space=pltpu.VMEM)
    return pl.pallas_call(
        functools.partial(_z_halo_kernel, z_count),
        out_shape=(halo, halo),
        in_specs=[vmem],
        out_specs=(vmem, vmem),
        scratch_shapes=[
            pltpu.SemaphoreType.DMA((2,)),
            pltpu.SemaphoreType.DMA((2,)),
        ],
        compiler_params=pltpu.CompilerParams(collective_id=0, has_side_effects=True),
    )(point)


def extended(cells, sides, width):
    for axis, dim in sides:
        count = lax.axis_size(axis)
        ends = count - 1
        head = lax.slice_in_dim(cells, 0, width, axis=dim)
        tail = lax.slice_in_dim(cells, cells.shape[dim] - width, cells.shape[dim], axis=dim)
        cells = jnp.concatenate(
            [
                lax.ppermute(tail, axis, [(i, (i + 1) % count) for i in range(ends)]),
                cells,
                lax.ppermute(head, axis, [((i + 1) % count, i) for i in range(ends)]),
            ],
            axis=dim,
        )
    return cells


def band_table(band_ids):
    growth_factor = jnp.power(GROWTH, band_ids)
    radian_freq = 2.0 * math.pi * BASE_FREQ * growth_factor
    wavenum = radian_freq * radian_freq / GRAVITY
    return (
        radian_freq,
        wavenum,
        COURANT_TOP / growth_factor,
        TURN_TOP / growth_factor,
        SPACING * radian_freq,
    )


def quick_flux(far_left, near_left, near_right, far_right, courant):
    forward = courant >= 0
    upwind = jnp.where(forward, far_left, far_right)
    center = jnp.where(forward, near_left, near_right)
    downwind = jnp.where(forward, near_right, near_left)
    face_value = (
        0.5 * (center + downwind)
        - 0.5 * jnp.abs(courant) * (downwind - center)
        - (1.0 - courant * courant) / 6.0 * (downwind - 2.0 * center + upwind)
    )
    return courant * face_value


def advect(padded, courant, along):
    face_count = padded.shape[along] - 4
    shifted = [
        lax.slice_in_dim(padded, offset, offset + face_count + 1, axis=along) for offset in range(4)
    ]
    face_flux = quick_flux(shifted[0], shifted[1], shifted[2], shifted[3], courant)
    centre_cells = lax.slice_in_dim(padded, 2, 2 + face_count, axis=along)
    upper_flux = lax.slice_in_dim(face_flux, 1, face_count + 1, axis=along)
    lower_flux = lax.slice_in_dim(face_flux, 0, face_count, axis=along)
    return centre_cells - (upper_flux - lower_flux)


def quad_delta(center, above, below, energy, dir_axis):
    plus = jnp.roll(above, -1, axis=dir_axis)
    minus = jnp.roll(below, 3, axis=dir_axis)
    return (
        QUAD_COEF
        * (center * center * (plus + minus) - 2.0 * center * plus * minus)
        / (energy * energy)
    )


def quad_term(delta, delta_above, delta_below, dir_axis):
    return (
        -2.0 * delta
        + jnp.roll(delta_below, 1, axis=dir_axis)
        + jnp.roll(delta_above, -3, axis=dir_axis)
    )


def band_neighbours(values):
    empty = jnp.zeros((1,) + values.shape[1:], jnp.float32)
    return (
        jnp.concatenate([values[1:], empty], axis=0),
        jnp.concatenate([empty, values[:-1]], axis=0),
    )


def sources(density, energy_sum, first_sum, root_sum, radian_freq, wavenum, cosine, wind_speed):
    energy = energy_sum + EPSILON
    mean_sigma = energy / (first_sum + EPSILON)
    ratio_k = energy / (root_sum + EPSILON)
    mean_k = ratio_k * ratio_k
    steepness = energy * mean_k * mean_k / STEEP_REF
    decay_rate = WHITECAP * mean_sigma * (wavenum / mean_k) * steepness * steepness
    growth_rate = (
        WIND_COEF
        * radian_freq
        * jnp.maximum(28.0 * USTAR_RATIO * wind_speed * radian_freq / GRAVITY * cosine - 1.0, 0.0)
    )
    return density * (1.0 + growth_rate) / (1.0 + decay_rate)


def local_sources(point_block, wind_block, wind_angle, angles, dtheta):
    band_total = point_block.shape[0]
    band_ids = jnp.arange(band_total).astype(jnp.float32)
    radian_freq, wavenum, courant, turn_rate, band_spread = band_table(band_ids)
    scaled = point_block * (band_spread * dtheta)[:, None, None]
    energy_sum = jnp.sum(scaled, axis=(0, 1))
    first_sum = jnp.sum(scaled / radian_freq[:, None, None], axis=(0, 1))
    root_sum = jnp.sum(scaled / jnp.sqrt(wavenum)[:, None, None], axis=(0, 1))
    energy = energy_sum + EPSILON
    above, below = band_neighbours(point_block)
    delta = quad_delta(point_block, above, below, energy, 1)
    delta_above, delta_below = band_neighbours(delta)
    extra = quad_term(delta, delta_above, delta_below, 1)
    cosine = jnp.cos(angles[:, None] - wind_angle[None, :])
    return (
        sources(
            point_block,
            energy_sum,
            first_sum,
            root_sum,
            radian_freq[:, None, None],
            wavenum[:, None, None],
            cosine,
            wind_block,
        )
        + extra
    )


Y_GROUP = 4


def _z_exchange_kernel(z_count, point_ref, part_ref, lower_ref, upper_ref, gathered_ref,
                       halo_send, halo_recv, gather_send, gather_recv):
    geo = lax.axis_index("geo")
    z_pos = lax.axis_index("z")
    y_pos = lax.axis_index("y")
    group = point_ref.shape[0]
    barrier = pltpu.get_barrier_semaphore()
    for offset in range(1, z_count):
        target = lax.rem(z_pos + offset, z_count)
        pl.semaphore_signal(barrier, inc=1, device_id=(geo, target, y_pos),
                            device_id_type=pl.DeviceIdType.MESH)
    pl.semaphore_wait(barrier, z_count - 1)

    def halo_copy(src_lo, dst_ref, slot, target):
        return pltpu.make_async_remote_copy(
            src_ref=point_ref.at[pl.ds(src_lo, 2)],
            dst_ref=dst_ref,
            send_sem=halo_send.at[slot],
            recv_sem=halo_recv.at[slot],
            device_id=(geo, target, y_pos),
            device_id_type=pl.DeviceIdType.MESH,
        )

    up = halo_copy(group - 2, lower_ref, 0, z_pos + 1)
    down = halo_copy(0, upper_ref, 1, z_pos - 1)

    @pl.when(z_pos < z_count - 1)
    def _():
        up.start()

    @pl.when(z_pos > 0)
    def _():
        down.start()

    copies = []
    for offset in range(1, z_count):
        target = lax.rem(z_pos + offset, z_count)
        copy = pltpu.make_async_remote_copy(
            src_ref=part_ref,
            dst_ref=gathered_ref.at[z_pos],
            send_sem=gather_send.at[offset],
            recv_sem=gather_recv.at[offset],
            device_id=(geo, target, y_pos),
            device_id_type=pl.DeviceIdType.MESH,
        )
        copy.start()
        copies.append(copy)
    gathered_ref[z_pos] = part_ref[...]

    @pl.when(z_pos == 0)
    def _():
        lower_ref[...] = jnp.zeros(lower_ref.shape, lower_ref.dtype)

    @pl.when(z_pos == z_count - 1)
    def _():
        upper_ref[...] = jnp.zeros(upper_ref.shape, upper_ref.dtype)

    for copy in copies:
        copy.wait_send()
        copy.wait_recv()

    @pl.when(z_pos < z_count - 1)
    def _():
        up.wait_send()
        down.wait_recv()

    @pl.when(z_pos > 0)
    def _():
        down.wait_send()
        up.wait_recv()


def z_exchange(point, part, z_count):
    group, dirs, rows, cols = point.shape
    halo = jax.ShapeDtypeStruct((2, dirs, rows, cols), point.dtype)
    vmem = pl.BlockSpec(memory_space=pltpu.VMEM)
    return pl.pallas_call(
        functools.partial(_z_exchange_kernel, z_count),
        out_shape=(halo, halo, jax.ShapeDtypeStruct((z_count,) + part.shape, part.dtype)),
        in_specs=[vmem, vmem],
        out_specs=(vmem, vmem, vmem),
        scratch_shapes=[
            pltpu.SemaphoreType.DMA((2,)),
            pltpu.SemaphoreType.DMA((2,)),
            pltpu.SemaphoreType.DMA((z_count,)),
            pltpu.SemaphoreType.DMA((z_count,)),
        ],
        compiler_params=pltpu.CompilerParams(collective_id=0, has_side_effects=True),
    )(point, part)


def shards(spectrum, land_sea, sea_index, sea_count, wind_speed, wind_dir, slope_x, slope_y):
    local_bands, dir_count, row_count, col_count = spectrum.shape
    z_count = lax.axis_size("z")
    y_count = lax.axis_size("y")
    z_pos = lax.axis_index("z")
    y_pos = lax.axis_index("y")
    spec_pos = z_pos * y_count + y_pos
    dtheta = 2.0 * math.pi / dir_count
    angles = (jnp.arange(dir_count).astype(jnp.float32) + 0.5) * dtheta
    face_angles = jnp.arange(dir_count + 1).astype(jnp.float32) * dtheta
    band_ids = (spec_pos * local_bands + jnp.arange(local_bands)).astype(jnp.float32)
    radian_freq, wavenum, courant, turn_rate, band_spread = band_table(band_ids)
    wet_mask = land_sea.astype(jnp.float32)
    density = spectrum * wet_mask
    padded = extended(density, (("geo", 2),), 2)
    density = (
        advect(padded, (courant[:, None] * jnp.cos(angles)[None, :])[:, :, None, None], 2)
        * wet_mask
    )
    padded = jnp.pad(density, ((0, 0), (0, 0), (0, 0), (2, 2)))
    density = (
        advect(padded, (courant[:, None] * jnp.sin(angles)[None, :])[:, :, None, None], 3)
        * wet_mask
    )
    turning = turn_rate[:, None, None, None] * (
        jnp.sin(face_angles)[None, :, None, None] * slope_x
        - jnp.cos(face_angles)[None, :, None, None] * slope_y
    )
    padded = jnp.concatenate([density[:, -2:], density, density[:, :2]], axis=1)
    floored = jnp.maximum(advect(padded, turning, 1), 0.0)
    point = lax.all_to_all(floored, "y", split_axis=2, concat_axis=0, tiled=True)
    group = point.shape[0]
    part_rows = point.shape[2]
    group_ids = (z_pos * group + jnp.arange(group)).astype(jnp.float32)
    radian_freq, wavenum, courant, turn_rate, band_spread = band_table(group_ids)
    scaled = point * (band_spread * dtheta)[:, None, None, None]
    sums = jnp.stack(
        [
            jnp.sum(scaled, axis=(0, 1)),
            jnp.sum(scaled / radian_freq[:, None, None, None], axis=(0, 1)),
            jnp.sum(scaled / jnp.sqrt(wavenum)[:, None, None, None], axis=(0, 1)),
        ]
    )
    lower, upper = z_halo(point, z_count)
    step = 1
    while step < z_count:
        sums = sums + lax.ppermute(sums, "z", [(i, i ^ step) for i in range(z_count)])
        step *= 2
    energy_sum, first_sum, root_sum = sums[0], sums[1], sums[2]
    energy = energy_sum + EPSILON
    ext = jnp.concatenate([lower, point, upper], axis=0)
    center, plus, minus = ext[1:-1], jnp.roll(ext[2:], -1, axis=1), jnp.roll(ext[:-2], 3, axis=1)
    cubic = center * center * (plus + minus) - 2.0 * center * plus * minus
    extra = (
        -2.0 * cubic[1:-1] + jnp.roll(cubic[:-2], 1, axis=1) + jnp.roll(cubic[2:], -3, axis=1)
    ) * (QUAD_COEF / (energy * energy))
    row_start = y_pos * part_rows
    wind_block = lax.dynamic_slice_in_dim(wind_speed, row_start, part_rows, axis=0)
    wind_angle = lax.dynamic_slice_in_dim(wind_dir, row_start, part_rows, axis=0)
    wet_block = lax.dynamic_slice_in_dim(wet_mask, row_start, part_rows, axis=0)
    cosine = jnp.cos(angles[:, None, None] - wind_angle[None])
    updated = (
        sources(
            point,
            energy_sum,
            first_sum,
            root_sum,
            radian_freq[:, None, None, None],
            wavenum[:, None, None, None],
            cosine,
            wind_block,
        )
        + extra
    ) * wet_block
    return lax.all_to_all(updated, "y", split_axis=0, concat_axis=2, tiled=True)


def solution(mesh):
    geo_count = mesh.shape["geo"]
    spec_count = mesh.shape["spec"]
    local = jax.sharding.Mesh(
        mesh.devices.reshape(geo_count, spec_count // Y_GROUP, Y_GROUP), ("geo", "z", "y")
    )
    spec = ("z", "y")
    placed = (
        P(spec, None, "geo", None),
        P("geo", None),
        P("geo", None),
        P("geo"),
        P("geo", None),
        P("geo", None),
        P("geo", None),
        P("geo", None),
    )
    return jax.shard_map(
        shards, mesh=local, in_specs=placed, out_specs=P(spec, None, "geo", None), check_vma=False
    )
```

```python
import functools
import math

import jax
import jax.numpy as jnp
from jax import lax
from jax.experimental import pallas as pl
from jax.experimental.pallas import tpu as pltpu
from jax.sharding import PartitionSpec as P

GRAVITY = 9.81
BASE_FREQ = 0.035
GROWTH = 1.1
COURANT_TOP = 0.9
TURN_TOP = 1.2
SPACING = 0.1
USTAR_RATIO = 0.035
WIND_COEF = 0.0375
WHITECAP = 0.36
STEEP_REF = 1.6
EPSILON = 1e-06
QUAD_COEF = 100.0


def extended(cells, sides, width):
    for axis, dim in sides:
        count = lax.axis_size(axis)
        ends = count - 1
        head = lax.slice_in_dim(cells, 0, width, axis=dim)
        tail = lax.slice_in_dim(cells, cells.shape[dim] - width, cells.shape[dim], axis=dim)
        cells = jnp.concatenate(
            [
                lax.ppermute(tail, axis, [(i, (i + 1) % count) for i in range(ends)]),
                cells,
                lax.ppermute(head, axis, [((i + 1) % count, i) for i in range(ends)]),
            ],
            axis=dim,
        )
    return cells


def band_table(band_ids):
    growth_factor = jnp.power(GROWTH, band_ids)
    radian_freq = 2.0 * math.pi * BASE_FREQ * growth_factor
    wavenum = radian_freq * radian_freq / GRAVITY
    return (
        radian_freq,
        wavenum,
        COURANT_TOP / growth_factor,
        TURN_TOP / growth_factor,
        SPACING * radian_freq,
    )


def quick_flux(far_left, near_left, near_right, far_right, courant):
    forward = courant >= 0
    upwind = jnp.where(forward, far_left, far_right)
    center = jnp.where(forward, near_left, near_right)
    downwind = jnp.where(forward, near_right, near_left)
    face_value = (
        0.5 * (center + downwind)
        - 0.5 * jnp.abs(courant) * (downwind - center)
        - (1.0 - courant * courant) / 6.0 * (downwind - 2.0 * center + upwind)
    )
    return courant * face_value


def advect(padded, courant, along):
    face_count = padded.shape[along] - 4
    shifted = [
        lax.slice_in_dim(padded, offset, offset + face_count + 1, axis=along) for offset in range(4)
    ]
    face_flux = quick_flux(shifted[0], shifted[1], shifted[2], shifted[3], courant)
    centre_cells = lax.slice_in_dim(padded, 2, 2 + face_count, axis=along)
    upper_flux = lax.slice_in_dim(face_flux, 1, face_count + 1, axis=along)
    lower_flux = lax.slice_in_dim(face_flux, 0, face_count, axis=along)
    return centre_cells - (upper_flux - lower_flux)


def quad_delta(center, above, below, energy, dir_axis):
    plus = jnp.roll(above, -1, axis=dir_axis)
    minus = jnp.roll(below, 3, axis=dir_axis)
    return (
        QUAD_COEF
        * (center * center * (plus + minus) - 2.0 * center * plus * minus)
        / (energy * energy)
    )


def quad_term(delta, delta_above, delta_below, dir_axis):
    return (
        -2.0 * delta
        + jnp.roll(delta_below, 1, axis=dir_axis)
        + jnp.roll(delta_above, -3, axis=dir_axis)
    )


def band_neighbours(values):
    empty = jnp.zeros((1,) + values.shape[1:], jnp.float32)
    return (
        jnp.concatenate([values[1:], empty], axis=0),
        jnp.concatenate([empty, values[:-1]], axis=0),
    )


def sources(density, energy_sum, first_sum, root_sum, radian_freq, wavenum, cosine, wind_speed):
    energy = energy_sum + EPSILON
    mean_sigma = energy / (first_sum + EPSILON)
    ratio_k = energy / (root_sum + EPSILON)
    mean_k = ratio_k * ratio_k
    steepness = energy * mean_k * mean_k / STEEP_REF
    decay_rate = WHITECAP * mean_sigma * (wavenum / mean_k) * steepness * steepness
    growth_rate = (
        WIND_COEF
        * radian_freq
        * jnp.maximum(28.0 * USTAR_RATIO * wind_speed * radian_freq / GRAVITY * cosine - 1.0, 0.0)
    )
    return density * (1.0 + growth_rate) / (1.0 + decay_rate)


def local_sources(point_block, wind_block, wind_angle, angles, dtheta):
    band_total = point_block.shape[0]
    band_ids = jnp.arange(band_total).astype(jnp.float32)
    radian_freq, wavenum, courant, turn_rate, band_spread = band_table(band_ids)
    scaled = point_block * (band_spread * dtheta)[:, None, None]
    energy_sum = jnp.sum(scaled, axis=(0, 1))
    first_sum = jnp.sum(scaled / radian_freq[:, None, None], axis=(0, 1))
    root_sum = jnp.sum(scaled / jnp.sqrt(wavenum)[:, None, None], axis=(0, 1))
    energy = energy_sum + EPSILON
    above, below = band_neighbours(point_block)
    delta = quad_delta(point_block, above, below, energy, 1)
    delta_above, delta_below = band_neighbours(delta)
    extra = quad_term(delta, delta_above, delta_below, 1)
    cosine = jnp.cos(angles[:, None] - wind_angle[None, :])
    return (
        sources(
            point_block,
            energy_sum,
            first_sum,
            root_sum,
            radian_freq[:, None, None],
            wavenum[:, None, None],
            cosine,
            wind_block,
        )
        + extra
    )


Y_GROUP = 4
HALO = 2


def _z_halo_kernel(z_count, point_ref, lower_ref, upper_ref, halo_send, halo_recv):
    geo = lax.axis_index("geo")
    z_pos = lax.axis_index("z")
    y_pos = lax.axis_index("y")
    group = point_ref.shape[0]
    mesh_id = pl.DeviceIdType.MESH
    barrier = pltpu.get_barrier_semaphore()
    for step in (1, z_count - 1):
        pl.semaphore_signal(barrier, inc=1, device_id=(geo, lax.rem(z_pos + step, z_count), y_pos),
                            device_id_type=mesh_id)
    pl.semaphore_wait(barrier, 2)

    def halo_copy(src_lo, dst_ref, slot, target):
        return pltpu.make_async_remote_copy(
            src_ref=point_ref.at[pl.ds(src_lo, HALO)],
            dst_ref=dst_ref,
            send_sem=halo_send.at[slot],
            recv_sem=halo_recv.at[slot],
            device_id=(geo, target, y_pos),
            device_id_type=mesh_id,
        )

    up = halo_copy(group - HALO, lower_ref, 0, lax.rem(z_pos + 1, z_count))
    down = halo_copy(0, upper_ref, 1, lax.rem(z_pos + z_count - 1, z_count))

    @pl.when(z_pos < z_count - 1)
    def _():
        up.start()

    @pl.when(z_pos > 0)
    def _():
        down.start()

    @pl.when(z_pos == 0)
    def _():
        lower_ref[...] = jnp.zeros(lower_ref.shape, lower_ref.dtype)

    @pl.when(z_pos == z_count - 1)
    def _():
        upper_ref[...] = jnp.zeros(upper_ref.shape, upper_ref.dtype)

    @pl.when(z_pos < z_count - 1)
    def _():
        up.wait_send()
        down.wait_recv()

    @pl.when(z_pos > 0)
    def _():
        down.wait_send()
        up.wait_recv()


def z_halo(point, z_count):
    group, dirs, rows, cols = point.shape
    halo = jax.ShapeDtypeStruct((HALO, dirs, rows, cols), point.dtype)
    vmem = pl.BlockSpec(memory_space=pltpu.VMEM)
    return pl.pallas_call(
        functools.partial(_z_halo_kernel, z_count),
        out_shape=(halo, halo),
        in_specs=[vmem],
        out_specs=(vmem, vmem),
        scratch_shapes=[
            pltpu.SemaphoreType.DMA((2,)),
            pltpu.SemaphoreType.DMA((2,)),
        ],
        compiler_params=pltpu.CompilerParams(collective_id=0, has_side_effects=True),
    )(point)


def extended(cells, sides, width):
    for axis, dim in sides:
        count = lax.axis_size(axis)
        ends = count - 1
        head = lax.slice_in_dim(cells, 0, width, axis=dim)
        tail = lax.slice_in_dim(cells, cells.shape[dim] - width, cells.shape[dim], axis=dim)
        cells = jnp.concatenate(
            [
                lax.ppermute(tail, axis, [(i, (i + 1) % count) for i in range(ends)]),
                cells,
                lax.ppermute(head, axis, [((i + 1) % count, i) for i in range(ends)]),
            ],
            axis=dim,
        )
    return cells


def band_table(band_ids):
    growth_factor = jnp.power(GROWTH, band_ids)
    radian_freq = 2.0 * math.pi * BASE_FREQ * growth_factor
    wavenum = radian_freq * radian_freq / GRAVITY
    return (
        radian_freq,
        wavenum,
        COURANT_TOP / growth_factor,
        TURN_TOP / growth_factor,
        SPACING * radian_freq,
    )


def quick_flux(far_left, near_left, near_right, far_right, courant):
    forward = courant >= 0
    upwind = jnp.where(forward, far_left, far_right)
    center = jnp.where(forward, near_left, near_right)
    downwind = jnp.where(forward, near_right, near_left)
    face_value = (
        0.5 * (center + downwind)
        - 0.5 * jnp.abs(courant) * (downwind - center)
        - (1.0 - courant * courant) / 6.0 * (downwind - 2.0 * center + upwind)
    )
    return courant * face_value


def advect(padded, courant, along):
    face_count = padded.shape[along] - 4
    shifted = [
        lax.slice_in_dim(padded, offset, offset + face_count + 1, axis=along) for offset in range(4)
    ]
    face_flux = quick_flux(shifted[0], shifted[1], shifted[2], shifted[3], courant)
    centre_cells = lax.slice_in_dim(padded, 2, 2 + face_count, axis=along)
    upper_flux = lax.slice_in_dim(face_flux, 1, face_count + 1, axis=along)
    lower_flux = lax.slice_in_dim(face_flux, 0, face_count, axis=along)
    return centre_cells - (upper_flux - lower_flux)


def quad_delta(center, above, below, energy, dir_axis):
    plus = jnp.roll(above, -1, axis=dir_axis)
    minus = jnp.roll(below, 3, axis=dir_axis)
    return (
        QUAD_COEF
        * (center * center * (plus + minus) - 2.0 * center * plus * minus)
        / (energy * energy)
    )


def quad_term(delta, delta_above, delta_below, dir_axis):
    return (
        -2.0 * delta
        + jnp.roll(delta_below, 1, axis=dir_axis)
        + jnp.roll(delta_above, -3, axis=dir_axis)
    )


def band_neighbours(values):
    empty = jnp.zeros((1,) + values.shape[1:], jnp.float32)
    return (
        jnp.concatenate([values[1:], empty], axis=0),
        jnp.concatenate([empty, values[:-1]], axis=0),
    )


def sources(density, energy_sum, first_sum, root_sum, radian_freq, wavenum, cosine, wind_speed):
    energy = energy_sum + EPSILON
    mean_sigma = energy / (first_sum + EPSILON)
    ratio_k = energy / (root_sum + EPSILON)
    mean_k = ratio_k * ratio_k
    steepness = energy * mean_k * mean_k / STEEP_REF
    decay_rate = WHITECAP * mean_sigma * (wavenum / mean_k) * steepness * steepness
    growth_rate = (
        WIND_COEF
        * radian_freq
        * jnp.maximum(28.0 * USTAR_RATIO * wind_speed * radian_freq / GRAVITY * cosine - 1.0, 0.0)
    )
    return density * (1.0 + growth_rate) / (1.0 + decay_rate)


def local_sources(point_block, wind_block, wind_angle, angles, dtheta):
    band_total = point_block.shape[0]
    band_ids = jnp.arange(band_total).astype(jnp.float32)
    radian_freq, wavenum, courant, turn_rate, band_spread = band_table(band_ids)
    scaled = point_block * (band_spread * dtheta)[:, None, None]
    energy_sum = jnp.sum(scaled, axis=(0, 1))
    first_sum = jnp.sum(scaled / radian_freq[:, None, None], axis=(0, 1))
    root_sum = jnp.sum(scaled / jnp.sqrt(wavenum)[:, None, None], axis=(0, 1))
    energy = energy_sum + EPSILON
    above, below = band_neighbours(point_block)
    delta = quad_delta(point_block, above, below, energy, 1)
    delta_above, delta_below = band_neighbours(delta)
    extra = quad_term(delta, delta_above, delta_below, 1)
    cosine = jnp.cos(angles[:, None] - wind_angle[None, :])
    return (
        sources(
            point_block,
            energy_sum,
            first_sum,
            root_sum,
            radian_freq[:, None, None],
            wavenum[:, None, None],
            cosine,
            wind_block,
        )
        + extra
    )


Y_GROUP = 4


def _z_exchange_kernel(z_count, point_ref, part_ref, lower_ref, upper_ref, gathered_ref,
                       halo_send, halo_recv, gather_send, gather_recv):
    geo = lax.axis_index("geo")
    z_pos = lax.axis_index("z")
    y_pos = lax.axis_index("y")
    group = point_ref.shape[0]
    barrier = pltpu.get_barrier_semaphore()
    for offset in range(1, z_count):
        target = lax.rem(z_pos + offset, z_count)
        pl.semaphore_signal(barrier, inc=1, device_id=(geo, target, y_pos),
                            device_id_type=pl.DeviceIdType.MESH)
    pl.semaphore_wait(barrier, z_count - 1)

    def halo_copy(src_lo, dst_ref, slot, target):
        return pltpu.make_async_remote_copy(
            src_ref=point_ref.at[pl.ds(src_lo, 2)],
            dst_ref=dst_ref,
            send_sem=halo_send.at[slot],
            recv_sem=halo_recv.at[slot],
            device_id=(geo, target, y_pos),
            device_id_type=pl.DeviceIdType.MESH,
        )

    up = halo_copy(group - 2, lower_ref, 0, z_pos + 1)
    down = halo_copy(0, upper_ref, 1, z_pos - 1)

    @pl.when(z_pos < z_count - 1)
    def _():
        up.start()

    @pl.when(z_pos > 0)
    def _():
        down.start()

    copies = []
    for offset in range(1, z_count):
        target = lax.rem(z_pos + offset, z_count)
        copy = pltpu.make_async_remote_copy(
            src_ref=part_ref,
            dst_ref=gathered_ref.at[z_pos],
            send_sem=gather_send.at[offset],
            recv_sem=gather_recv.at[offset],
            device_id=(geo, target, y_pos),
            device_id_type=pl.DeviceIdType.MESH,
        )
        copy.start()
        copies.append(copy)
    gathered_ref[z_pos] = part_ref[...]

    @pl.when(z_pos == 0)
    def _():
        lower_ref[...] = jnp.zeros(lower_ref.shape, lower_ref.dtype)

    @pl.when(z_pos == z_count - 1)
    def _():
        upper_ref[...] = jnp.zeros(upper_ref.shape, upper_ref.dtype)

    for copy in copies:
        copy.wait_send()
        copy.wait_recv()

    @pl.when(z_pos < z_count - 1)
    def _():
        up.wait_send()
        down.wait_recv()

    @pl.when(z_pos > 0)
    def _():
        down.wait_send()
        up.wait_recv()


def z_exchange(point, part, z_count):
    group, dirs, rows, cols = point.shape
    halo = jax.ShapeDtypeStruct((2, dirs, rows, cols), point.dtype)
    vmem = pl.BlockSpec(memory_space=pltpu.VMEM)
    return pl.pallas_call(
        functools.partial(_z_exchange_kernel, z_count),
        out_shape=(halo, halo, jax.ShapeDtypeStruct((z_count,) + part.shape, part.dtype)),
        in_specs=[vmem, vmem],
        out_specs=(vmem, vmem, vmem),
        scratch_shapes=[
            pltpu.SemaphoreType.DMA((2,)),
            pltpu.SemaphoreType.DMA((2,)),
            pltpu.SemaphoreType.DMA((z_count,)),
            pltpu.SemaphoreType.DMA((z_count,)),
        ],
        compiler_params=pltpu.CompilerParams(collective_id=0, has_side_effects=True),
    )(point, part)


def shards(spectrum, land_sea, sea_index, sea_count, wind_speed, wind_dir, slope_x, slope_y):
    local_bands, dir_count, row_count, col_count = spectrum.shape
    z_count = lax.axis_size("z")
    y_count = lax.axis_size("y")
    z_pos = lax.axis_index("z")
    y_pos = lax.axis_index("y")
    spec_pos = z_pos * y_count + y_pos
    dtheta = 2.0 * math.pi / dir_count
    angles = (jnp.arange(dir_count).astype(jnp.float32) + 0.5) * dtheta
    face_angles = jnp.arange(dir_count + 1).astype(jnp.float32) * dtheta
    band_ids = (spec_pos * local_bands + jnp.arange(local_bands)).astype(jnp.float32)
    radian_freq, wavenum, courant, turn_rate, band_spread = band_table(band_ids)
    wet_mask = land_sea.astype(jnp.float32)
    density = spectrum * wet_mask
    padded = extended(density, (("geo", 2),), 2)
    density = (
        advect(padded, (courant[:, None] * jnp.cos(angles)[None, :])[:, :, None, None], 2)
        * wet_mask
    )
    padded = jnp.pad(density, ((0, 0), (0, 0), (0, 0), (2, 2)))
    density = (
        advect(padded, (courant[:, None] * jnp.sin(angles)[None, :])[:, :, None, None], 3)
        * wet_mask
    )
    turning = turn_rate[:, None, None, None] * (
        jnp.sin(face_angles)[None, :, None, None] * slope_x
        - jnp.cos(face_angles)[None, :, None, None] * slope_y
    )
    padded = jnp.concatenate([density[:, -2:], density, density[:, :2]], axis=1)
    floored = jnp.maximum(advect(padded, turning, 1), 0.0)
    point = lax.all_to_all(floored, "y", split_axis=2, concat_axis=0, tiled=True)
    group = point.shape[0]
    part_rows = point.shape[2]
    group_ids = (z_pos * group + jnp.arange(group)).astype(jnp.float32)
    radian_freq, wavenum, courant, turn_rate, band_spread = band_table(group_ids)
    scaled = point * (band_spread * dtheta)[:, None, None, None]
    sums = jnp.stack(
        [
            jnp.sum(scaled, axis=(0, 1)),
            jnp.sum(scaled / radian_freq[:, None, None, None], axis=(0, 1)),
            jnp.sum(scaled / jnp.sqrt(wavenum)[:, None, None, None], axis=(0, 1)),
        ]
    )
    lower, upper = z_halo(point, z_count)
    shifted = [
        lax.ppermute(sums, "z", [(i, (i + shift) % z_count) for i in range(z_count)])
        for shift in range(1, z_count)
    ]
    sums = sums + sum(shifted)
    energy_sum, first_sum, root_sum = sums[0], sums[1], sums[2]
    energy = energy_sum + EPSILON
    ext = jnp.concatenate([lower, point, upper], axis=0)
    center, plus, minus = ext[1:-1], jnp.roll(ext[2:], -1, axis=1), jnp.roll(ext[:-2], 3, axis=1)
    cubic = center * center * (plus + minus) - 2.0 * center * plus * minus
    extra = (
        -2.0 * cubic[1:-1] + jnp.roll(cubic[:-2], 1, axis=1) + jnp.roll(cubic[2:], -3, axis=1)
    ) * (QUAD_COEF / (energy * energy))
    row_start = y_pos * part_rows
    wind_block = lax.dynamic_slice_in_dim(wind_speed, row_start, part_rows, axis=0)
    wind_angle = lax.dynamic_slice_in_dim(wind_dir, row_start, part_rows, axis=0)
    wet_block = lax.dynamic_slice_in_dim(wet_mask, row_start, part_rows, axis=0)
    cosine = jnp.cos(angles[:, None, None] - wind_angle[None])
    updated = (
        sources(
            point,
            energy_sum,
            first_sum,
            root_sum,
            radian_freq[:, None, None, None],
            wavenum[:, None, None, None],
            cosine,
            wind_block,
        )
        + extra
    ) * wet_block
    return lax.all_to_all(updated, "y", split_axis=0, concat_axis=2, tiled=True)


def solution(mesh):
    geo_count = mesh.shape["geo"]
    spec_count = mesh.shape["spec"]
    local = jax.sharding.Mesh(
        mesh.devices.reshape(geo_count, spec_count // Y_GROUP, Y_GROUP), ("geo", "z", "y")
    )
    spec = ("z", "y")
    placed = (
        P(spec, None, "geo", None),
        P("geo", None),
        P("geo", None),
        P("geo"),
        P("geo", None),
        P("geo", None),
        P("geo", None),
        P("geo", None),
    )
    return jax.shard_map(
        shards, mesh=local, in_specs=placed, out_specs=P(spec, None, "geo", None), check_vma=False
    )
```

```python
import functools
import math

import jax
import jax.numpy as jnp
from jax import lax
from jax.experimental import pallas as pl
from jax.experimental.pallas import tpu as pltpu
from jax.sharding import PartitionSpec as P

GRAVITY = 9.81
BASE_FREQ = 0.035
GROWTH = 1.1
COURANT_TOP = 0.9
TURN_TOP = 1.2
SPACING = 0.1
USTAR_RATIO = 0.035
WIND_COEF = 0.0375
WHITECAP = 0.36
STEEP_REF = 1.6
EPSILON = 1e-06
QUAD_COEF = 100.0


def extended(cells, sides, width):
    for axis, dim in sides:
        count = lax.axis_size(axis)
        ends = count - 1
        head = lax.slice_in_dim(cells, 0, width, axis=dim)
        tail = lax.slice_in_dim(cells, cells.shape[dim] - width, cells.shape[dim], axis=dim)
        cells = jnp.concatenate(
            [
                lax.ppermute(tail, axis, [(i, (i + 1) % count) for i in range(ends)]),
                cells,
                lax.ppermute(head, axis, [((i + 1) % count, i) for i in range(ends)]),
            ],
            axis=dim,
        )
    return cells


def band_table(band_ids):
    growth_factor = jnp.power(GROWTH, band_ids)
    radian_freq = 2.0 * math.pi * BASE_FREQ * growth_factor
    wavenum = radian_freq * radian_freq / GRAVITY
    return (
        radian_freq,
        wavenum,
        COURANT_TOP / growth_factor,
        TURN_TOP / growth_factor,
        SPACING * radian_freq,
    )


def quick_flux(far_left, near_left, near_right, far_right, courant):
    forward = courant >= 0
    upwind = jnp.where(forward, far_left, far_right)
    center = jnp.where(forward, near_left, near_right)
    downwind = jnp.where(forward, near_right, near_left)
    face_value = (
        0.5 * (center + downwind)
        - 0.5 * jnp.abs(courant) * (downwind - center)
        - (1.0 - courant * courant) / 6.0 * (downwind - 2.0 * center + upwind)
    )
    return courant * face_value


def advect(padded, courant, along):
    face_count = padded.shape[along] - 4
    shifted = [
        lax.slice_in_dim(padded, offset, offset + face_count + 1, axis=along) for offset in range(4)
    ]
    face_flux = quick_flux(shifted[0], shifted[1], shifted[2], shifted[3], courant)
    centre_cells = lax.slice_in_dim(padded, 2, 2 + face_count, axis=along)
    upper_flux = lax.slice_in_dim(face_flux, 1, face_count + 1, axis=along)
    lower_flux = lax.slice_in_dim(face_flux, 0, face_count, axis=along)
    return centre_cells - (upper_flux - lower_flux)


def quad_delta(center, above, below, energy, dir_axis):
    plus = jnp.roll(above, -1, axis=dir_axis)
    minus = jnp.roll(below, 3, axis=dir_axis)
    return (
        QUAD_COEF
        * (center * center * (plus + minus) - 2.0 * center * plus * minus)
        / (energy * energy)
    )


def quad_term(delta, delta_above, delta_below, dir_axis):
    return (
        -2.0 * delta
        + jnp.roll(delta_below, 1, axis=dir_axis)
        + jnp.roll(delta_above, -3, axis=dir_axis)
    )


def band_neighbours(values):
    empty = jnp.zeros((1,) + values.shape[1:], jnp.float32)
    return (
        jnp.concatenate([values[1:], empty], axis=0),
        jnp.concatenate([empty, values[:-1]], axis=0),
    )


def sources(density, energy_sum, first_sum, root_sum, radian_freq, wavenum, cosine, wind_speed):
    energy = energy_sum + EPSILON
    mean_sigma = energy / (first_sum + EPSILON)
    ratio_k = energy / (root_sum + EPSILON)
    mean_k = ratio_k * ratio_k
    steepness = energy * mean_k * mean_k / STEEP_REF
    decay_rate = WHITECAP * mean_sigma * (wavenum / mean_k) * steepness * steepness
    growth_rate = (
        WIND_COEF
        * radian_freq
        * jnp.maximum(28.0 * USTAR_RATIO * wind_speed * radian_freq / GRAVITY * cosine - 1.0, 0.0)
    )
    return density * (1.0 + growth_rate) / (1.0 + decay_rate)


def local_sources(point_block, wind_block, wind_angle, angles, dtheta):
    band_total = point_block.shape[0]
    band_ids = jnp.arange(band_total).astype(jnp.float32)
    radian_freq, wavenum, courant, turn_rate, band_spread = band_table(band_ids)
    scaled = point_block * (band_spread * dtheta)[:, None, None]
    energy_sum = jnp.sum(scaled, axis=(0, 1))
    first_sum = jnp.sum(scaled / radian_freq[:, None, None], axis=(0, 1))
    root_sum = jnp.sum(scaled / jnp.sqrt(wavenum)[:, None, None], axis=(0, 1))
    energy = energy_sum + EPSILON
    above, below = band_neighbours(point_block)
    delta = quad_delta(point_block, above, below, energy, 1)
    delta_above, delta_below = band_neighbours(delta)
    extra = quad_term(delta, delta_above, delta_below, 1)
    cosine = jnp.cos(angles[:, None] - wind_angle[None, :])
    return (
        sources(
            point_block,
            energy_sum,
            first_sum,
            root_sum,
            radian_freq[:, None, None],
            wavenum[:, None, None],
            cosine,
            wind_block,
        )
        + extra
    )


Y_GROUP = 4
HALO = 2


def _z_halo_kernel(z_count, point_ref, lower_ref, upper_ref, halo_send, halo_recv):
    geo = lax.axis_index("geo")
    z_pos = lax.axis_index("z")
    y_pos = lax.axis_index("y")
    group = point_ref.shape[0]
    mesh_id = pl.DeviceIdType.MESH
    barrier = pltpu.get_barrier_semaphore()
    for step in (1, z_count - 1):
        pl.semaphore_signal(barrier, inc=1, device_id=(geo, lax.rem(z_pos + step, z_count), y_pos),
                            device_id_type=mesh_id)
    pl.semaphore_wait(barrier, 2)

    def halo_copy(src_lo, dst_ref, slot, target):
        return pltpu.make_async_remote_copy(
            src_ref=point_ref.at[pl.ds(src_lo, HALO)],
            dst_ref=dst_ref,
            send_sem=halo_send.at[slot],
            recv_sem=halo_recv.at[slot],
            device_id=(geo, target, y_pos),
            device_id_type=mesh_id,
        )

    up = halo_copy(group - HALO, lower_ref, 0, lax.rem(z_pos + 1, z_count))
    down = halo_copy(0, upper_ref, 1, lax.rem(z_pos + z_count - 1, z_count))

    @pl.when(z_pos < z_count - 1)
    def _():
        up.start()

    @pl.when(z_pos > 0)
    def _():
        down.start()

    @pl.when(z_pos == 0)
    def _():
        lower_ref[...] = jnp.zeros(lower_ref.shape, lower_ref.dtype)

    @pl.when(z_pos == z_count - 1)
    def _():
        upper_ref[...] = jnp.zeros(upper_ref.shape, upper_ref.dtype)

    @pl.when(z_pos < z_count - 1)
    def _():
        up.wait_send()
        down.wait_recv()

    @pl.when(z_pos > 0)
    def _():
        down.wait_send()
        up.wait_recv()


def z_halo(point, z_count):
    group, dirs, rows, cols = point.shape
    halo = jax.ShapeDtypeStruct((HALO, dirs, rows, cols), point.dtype)
    vmem = pl.BlockSpec(memory_space=pltpu.VMEM)
    return pl.pallas_call(
        functools.partial(_z_halo_kernel, z_count),
        out_shape=(halo, halo),
        in_specs=[pl.BlockSpec(memory_space=pl.ANY)],
        out_specs=(vmem, vmem),
        scratch_shapes=[
            pltpu.SemaphoreType.DMA((2,)),
            pltpu.SemaphoreType.DMA((2,)),
        ],
        compiler_params=pltpu.CompilerParams(collective_id=0, has_side_effects=True),
    )(point)


def extended(cells, sides, width):
    for axis, dim in sides:
        count = lax.axis_size(axis)
        ends = count - 1
        head = lax.slice_in_dim(cells, 0, width, axis=dim)
        tail = lax.slice_in_dim(cells, cells.shape[dim] - width, cells.shape[dim], axis=dim)
        cells = jnp.concatenate(
            [
                lax.ppermute(tail, axis, [(i, (i + 1) % count) for i in range(ends)]),
                cells,
                lax.ppermute(head, axis, [((i + 1) % count, i) for i in range(ends)]),
            ],
            axis=dim,
        )
    return cells


def band_table(band_ids):
    growth_factor = jnp.power(GROWTH, band_ids)
    radian_freq = 2.0 * math.pi * BASE_FREQ * growth_factor
    wavenum = radian_freq * radian_freq / GRAVITY
    return (
        radian_freq,
        wavenum,
        COURANT_TOP / growth_factor,
        TURN_TOP / growth_factor,
        SPACING * radian_freq,
    )


def quick_flux(far_left, near_left, near_right, far_right, courant):
    forward = courant >= 0
    upwind = jnp.where(forward, far_left, far_right)
    center = jnp.where(forward, near_left, near_right)
    downwind = jnp.where(forward, near_right, near_left)
    face_value = (
        0.5 * (center + downwind)
        - 0.5 * jnp.abs(courant) * (downwind - center)
        - (1.0 - courant * courant) / 6.0 * (downwind - 2.0 * center + upwind)
    )
    return courant * face_value


def advect(padded, courant, along):
    face_count = padded.shape[along] - 4
    shifted = [
        lax.slice_in_dim(padded, offset, offset + face_count + 1, axis=along) for offset in range(4)
    ]
    face_flux = quick_flux(shifted[0], shifted[1], shifted[2], shifted[3], courant)
    centre_cells = lax.slice_in_dim(padded, 2, 2 + face_count, axis=along)
    upper_flux = lax.slice_in_dim(face_flux, 1, face_count + 1, axis=along)
    lower_flux = lax.slice_in_dim(face_flux, 0, face_count, axis=along)
    return centre_cells - (upper_flux - lower_flux)


def quad_delta(center, above, below, energy, dir_axis):
    plus = jnp.roll(above, -1, axis=dir_axis)
    minus = jnp.roll(below, 3, axis=dir_axis)
    return (
        QUAD_COEF
        * (center * center * (plus + minus) - 2.0 * center * plus * minus)
        / (energy * energy)
    )


def quad_term(delta, delta_above, delta_below, dir_axis):
    return (
        -2.0 * delta
        + jnp.roll(delta_below, 1, axis=dir_axis)
        + jnp.roll(delta_above, -3, axis=dir_axis)
    )


def band_neighbours(values):
    empty = jnp.zeros((1,) + values.shape[1:], jnp.float32)
    return (
        jnp.concatenate([values[1:], empty], axis=0),
        jnp.concatenate([empty, values[:-1]], axis=0),
    )


def sources(density, energy_sum, first_sum, root_sum, radian_freq, wavenum, cosine, wind_speed):
    energy = energy_sum + EPSILON
    mean_sigma = energy / (first_sum + EPSILON)
    ratio_k = energy / (root_sum + EPSILON)
    mean_k = ratio_k * ratio_k
    steepness = energy * mean_k * mean_k / STEEP_REF
    decay_rate = WHITECAP * mean_sigma * (wavenum / mean_k) * steepness * steepness
    growth_rate = (
        WIND_COEF
        * radian_freq
        * jnp.maximum(28.0 * USTAR_RATIO * wind_speed * radian_freq / GRAVITY * cosine - 1.0, 0.0)
    )
    return density * (1.0 + growth_rate) / (1.0 + decay_rate)


def local_sources(point_block, wind_block, wind_angle, angles, dtheta):
    band_total = point_block.shape[0]
    band_ids = jnp.arange(band_total).astype(jnp.float32)
    radian_freq, wavenum, courant, turn_rate, band_spread = band_table(band_ids)
    scaled = point_block * (band_spread * dtheta)[:, None, None]
    energy_sum = jnp.sum(scaled, axis=(0, 1))
    first_sum = jnp.sum(scaled / radian_freq[:, None, None], axis=(0, 1))
    root_sum = jnp.sum(scaled / jnp.sqrt(wavenum)[:, None, None], axis=(0, 1))
    energy = energy_sum + EPSILON
    above, below = band_neighbours(point_block)
    delta = quad_delta(point_block, above, below, energy, 1)
    delta_above, delta_below = band_neighbours(delta)
    extra = quad_term(delta, delta_above, delta_below, 1)
    cosine = jnp.cos(angles[:, None] - wind_angle[None, :])
    return (
        sources(
            point_block,
            energy_sum,
            first_sum,
            root_sum,
            radian_freq[:, None, None],
            wavenum[:, None, None],
            cosine,
            wind_block,
        )
        + extra
    )


Y_GROUP = 4


def _z_exchange_kernel(z_count, point_ref, part_ref, lower_ref, upper_ref, gathered_ref,
                       halo_send, halo_recv, gather_send, gather_recv):
    geo = lax.axis_index("geo")
    z_pos = lax.axis_index("z")
    y_pos = lax.axis_index("y")
    group = point_ref.shape[0]
    barrier = pltpu.get_barrier_semaphore()
    for offset in range(1, z_count):
        target = lax.rem(z_pos + offset, z_count)
        pl.semaphore_signal(barrier, inc=1, device_id=(geo, target, y_pos),
                            device_id_type=pl.DeviceIdType.MESH)
    pl.semaphore_wait(barrier, z_count - 1)

    def halo_copy(src_lo, dst_ref, slot, target):
        return pltpu.make_async_remote_copy(
            src_ref=point_ref.at[pl.ds(src_lo, 2)],
            dst_ref=dst_ref,
            send_sem=halo_send.at[slot],
            recv_sem=halo_recv.at[slot],
            device_id=(geo, target, y_pos),
            device_id_type=pl.DeviceIdType.MESH,
        )

    up = halo_copy(group - 2, lower_ref, 0, z_pos + 1)
    down = halo_copy(0, upper_ref, 1, z_pos - 1)

    @pl.when(z_pos < z_count - 1)
    def _():
        up.start()

    @pl.when(z_pos > 0)
    def _():
        down.start()

    copies = []
    for offset in range(1, z_count):
        target = lax.rem(z_pos + offset, z_count)
        copy = pltpu.make_async_remote_copy(
            src_ref=part_ref,
            dst_ref=gathered_ref.at[z_pos],
            send_sem=gather_send.at[offset],
            recv_sem=gather_recv.at[offset],
            device_id=(geo, target, y_pos),
            device_id_type=pl.DeviceIdType.MESH,
        )
        copy.start()
        copies.append(copy)
    gathered_ref[z_pos] = part_ref[...]

    @pl.when(z_pos == 0)
    def _():
        lower_ref[...] = jnp.zeros(lower_ref.shape, lower_ref.dtype)

    @pl.when(z_pos == z_count - 1)
    def _():
        upper_ref[...] = jnp.zeros(upper_ref.shape, upper_ref.dtype)

    for copy in copies:
        copy.wait_send()
        copy.wait_recv()

    @pl.when(z_pos < z_count - 1)
    def _():
        up.wait_send()
        down.wait_recv()

    @pl.when(z_pos > 0)
    def _():
        down.wait_send()
        up.wait_recv()


def z_exchange(point, part, z_count):
    group, dirs, rows, cols = point.shape
    halo = jax.ShapeDtypeStruct((2, dirs, rows, cols), point.dtype)
    vmem = pl.BlockSpec(memory_space=pltpu.VMEM)
    return pl.pallas_call(
        functools.partial(_z_exchange_kernel, z_count),
        out_shape=(halo, halo, jax.ShapeDtypeStruct((z_count,) + part.shape, part.dtype)),
        in_specs=[vmem, vmem],
        out_specs=(vmem, vmem, vmem),
        scratch_shapes=[
            pltpu.SemaphoreType.DMA((2,)),
            pltpu.SemaphoreType.DMA((2,)),
            pltpu.SemaphoreType.DMA((z_count,)),
            pltpu.SemaphoreType.DMA((z_count,)),
        ],
        compiler_params=pltpu.CompilerParams(collective_id=0, has_side_effects=True),
    )(point, part)


def shards(spectrum, land_sea, sea_index, sea_count, wind_speed, wind_dir, slope_x, slope_y):
    local_bands, dir_count, row_count, col_count = spectrum.shape
    z_count = lax.axis_size("z")
    y_count = lax.axis_size("y")
    z_pos = lax.axis_index("z")
    y_pos = lax.axis_index("y")
    spec_pos = z_pos * y_count + y_pos
    dtheta = 2.0 * math.pi / dir_count
    angles = (jnp.arange(dir_count).astype(jnp.float32) + 0.5) * dtheta
    face_angles = jnp.arange(dir_count + 1).astype(jnp.float32) * dtheta
    band_ids = (spec_pos * local_bands + jnp.arange(local_bands)).astype(jnp.float32)
    radian_freq, wavenum, courant, turn_rate, band_spread = band_table(band_ids)
    wet_mask = land_sea.astype(jnp.float32)
    density = spectrum * wet_mask
    padded = extended(density, (("geo", 2),), 2)
    density = (
        advect(padded, (courant[:, None] * jnp.cos(angles)[None, :])[:, :, None, None], 2)
        * wet_mask
    )
    padded = jnp.pad(density, ((0, 0), (0, 0), (0, 0), (2, 2)))
    density = (
        advect(padded, (courant[:, None] * jnp.sin(angles)[None, :])[:, :, None, None], 3)
        * wet_mask
    )
    turning = turn_rate[:, None, None, None] * (
        jnp.sin(face_angles)[None, :, None, None] * slope_x
        - jnp.cos(face_angles)[None, :, None, None] * slope_y
    )
    padded = jnp.concatenate([density[:, -2:], density, density[:, :2]], axis=1)
    floored = jnp.maximum(advect(padded, turning, 1), 0.0)
    point = lax.all_to_all(floored, "y", split_axis=2, concat_axis=0, tiled=True)
    group = point.shape[0]
    part_rows = point.shape[2]
    group_ids = (z_pos * group + jnp.arange(group)).astype(jnp.float32)
    radian_freq, wavenum, courant, turn_rate, band_spread = band_table(group_ids)
    scaled = point * (band_spread * dtheta)[:, None, None, None]
    sums = jnp.stack(
        [
            jnp.sum(scaled, axis=(0, 1)),
            jnp.sum(scaled / radian_freq[:, None, None, None], axis=(0, 1)),
            jnp.sum(scaled / jnp.sqrt(wavenum)[:, None, None, None], axis=(0, 1)),
        ]
    )
    lower, upper = z_halo(point, z_count)
    step = 1
    while step < z_count:
        sums = sums + lax.ppermute(sums, "z", [(i, i ^ step) for i in range(z_count)])
        step *= 2
    energy_sum, first_sum, root_sum = sums[0], sums[1], sums[2]
    energy = energy_sum + EPSILON
    ext = jnp.concatenate([lower, point, upper], axis=0)
    center, plus, minus = ext[1:-1], jnp.roll(ext[2:], -1, axis=1), jnp.roll(ext[:-2], 3, axis=1)
    cubic = center * center * (plus + minus) - 2.0 * center * plus * minus
    extra = (
        -2.0 * cubic[1:-1] + jnp.roll(cubic[:-2], 1, axis=1) + jnp.roll(cubic[2:], -3, axis=1)
    ) * (QUAD_COEF / (energy * energy))
    row_start = y_pos * part_rows
    wind_block = lax.dynamic_slice_in_dim(wind_speed, row_start, part_rows, axis=0)
    wind_angle = lax.dynamic_slice_in_dim(wind_dir, row_start, part_rows, axis=0)
    wet_block = lax.dynamic_slice_in_dim(wet_mask, row_start, part_rows, axis=0)
    cosine = jnp.cos(angles[:, None, None] - wind_angle[None])
    updated = (
        sources(
            point,
            energy_sum,
            first_sum,
            root_sum,
            radian_freq[:, None, None, None],
            wavenum[:, None, None, None],
            cosine,
            wind_block,
        )
        + extra
    ) * wet_block
    return lax.all_to_all(updated, "y", split_axis=0, concat_axis=2, tiled=True)


def solution(mesh):
    geo_count = mesh.shape["geo"]
    spec_count = mesh.shape["spec"]
    local = jax.sharding.Mesh(
        mesh.devices.reshape(geo_count, spec_count // Y_GROUP, Y_GROUP), ("geo", "z", "y")
    )
    spec = ("z", "y")
    placed = (
        P(spec, None, "geo", None),
        P("geo", None),
        P("geo", None),
        P("geo"),
        P("geo", None),
        P("geo", None),
        P("geo", None),
        P("geo", None),
    )
    return jax.shard_map(
        shards, mesh=local, in_specs=placed, out_specs=P(spec, None, "geo", None), check_vma=False
    )
```

```python
import functools
import math

import jax
import jax.numpy as jnp
from jax import lax
from jax.experimental import pallas as pl
from jax.experimental.pallas import tpu as pltpu
from jax.sharding import PartitionSpec as P

GRAVITY = 9.81
BASE_FREQ = 0.035
GROWTH = 1.1
COURANT_TOP = 0.9
TURN_TOP = 1.2
SPACING = 0.1
USTAR_RATIO = 0.035
WIND_COEF = 0.0375
WHITECAP = 0.36
STEEP_REF = 1.6
EPSILON = 1e-06
QUAD_COEF = 100.0


def extended(cells, sides, width):
    for axis, dim in sides:
        count = lax.axis_size(axis)
        ends = count - 1
        head = lax.slice_in_dim(cells, 0, width, axis=dim)
        tail = lax.slice_in_dim(cells, cells.shape[dim] - width, cells.shape[dim], axis=dim)
        cells = jnp.concatenate(
            [
                lax.ppermute(tail, axis, [(i, (i + 1) % count) for i in range(ends)]),
                cells,
                lax.ppermute(head, axis, [((i + 1) % count, i) for i in range(ends)]),
            ],
            axis=dim,
        )
    return cells


def band_table(band_ids):
    growth_factor = jnp.power(GROWTH, band_ids)
    radian_freq = 2.0 * math.pi * BASE_FREQ * growth_factor
    wavenum = radian_freq * radian_freq / GRAVITY
    return (
        radian_freq,
        wavenum,
        COURANT_TOP / growth_factor,
        TURN_TOP / growth_factor,
        SPACING * radian_freq,
    )


def quick_flux(far_left, near_left, near_right, far_right, courant):
    forward = courant >= 0
    upwind = jnp.where(forward, far_left, far_right)
    center = jnp.where(forward, near_left, near_right)
    downwind = jnp.where(forward, near_right, near_left)
    face_value = (
        0.5 * (center + downwind)
        - 0.5 * jnp.abs(courant) * (downwind - center)
        - (1.0 - courant * courant) / 6.0 * (downwind - 2.0 * center + upwind)
    )
    return courant * face_value


def advect(padded, courant, along):
    face_count = padded.shape[along] - 4
    shifted = [
        lax.slice_in_dim(padded, offset, offset + face_count + 1, axis=along) for offset in range(4)
    ]
    face_flux = quick_flux(shifted[0], shifted[1], shifted[2], shifted[3], courant)
    centre_cells = lax.slice_in_dim(padded, 2, 2 + face_count, axis=along)
    upper_flux = lax.slice_in_dim(face_flux, 1, face_count + 1, axis=along)
    lower_flux = lax.slice_in_dim(face_flux, 0, face_count, axis=along)
    return centre_cells - (upper_flux - lower_flux)


def quad_delta(center, above, below, energy, dir_axis):
    plus = jnp.roll(above, -1, axis=dir_axis)
    minus = jnp.roll(below, 3, axis=dir_axis)
    return (
        QUAD_COEF
        * (center * center * (plus + minus) - 2.0 * center * plus * minus)
        / (energy * energy)
    )


def quad_term(delta, delta_above, delta_below, dir_axis):
    return (
        -2.0 * delta
        + jnp.roll(delta_below, 1, axis=dir_axis)
        + jnp.roll(delta_above, -3, axis=dir_axis)
    )


def band_neighbours(values):
    empty = jnp.zeros((1,) + values.shape[1:], jnp.float32)
    return (
        jnp.concatenate([values[1:], empty], axis=0),
        jnp.concatenate([empty, values[:-1]], axis=0),
    )


def sources(density, energy_sum, first_sum, root_sum, radian_freq, wavenum, cosine, wind_speed):
    energy = energy_sum + EPSILON
    mean_sigma = energy / (first_sum + EPSILON)
    ratio_k = energy / (root_sum + EPSILON)
    mean_k = ratio_k * ratio_k
    steepness = energy * mean_k * mean_k / STEEP_REF
    decay_rate = WHITECAP * mean_sigma * (wavenum / mean_k) * steepness * steepness
    growth_rate = (
        WIND_COEF
        * radian_freq
        * jnp.maximum(28.0 * USTAR_RATIO * wind_speed * radian_freq / GRAVITY * cosine - 1.0, 0.0)
    )
    return density * (1.0 + growth_rate) / (1.0 + decay_rate)


def local_sources(point_block, wind_block, wind_angle, angles, dtheta):
    band_total = point_block.shape[0]
    band_ids = jnp.arange(band_total).astype(jnp.float32)
    radian_freq, wavenum, courant, turn_rate, band_spread = band_table(band_ids)
    scaled = point_block * (band_spread * dtheta)[:, None, None]
    energy_sum = jnp.sum(scaled, axis=(0, 1))
    first_sum = jnp.sum(scaled / radian_freq[:, None, None], axis=(0, 1))
    root_sum = jnp.sum(scaled / jnp.sqrt(wavenum)[:, None, None], axis=(0, 1))
    energy = energy_sum + EPSILON
    above, below = band_neighbours(point_block)
    delta = quad_delta(point_block, above, below, energy, 1)
    delta_above, delta_below = band_neighbours(delta)
    extra = quad_term(delta, delta_above, delta_below, 1)
    cosine = jnp.cos(angles[:, None] - wind_angle[None, :])
    return (
        sources(
            point_block,
            energy_sum,
            first_sum,
            root_sum,
            radian_freq[:, None, None],
            wavenum[:, None, None],
            cosine,
            wind_block,
        )
        + extra
    )


Y_GROUP = 4
HALO = 2


def _z_halo_kernel(z_count, point_ref, lower_ref, upper_ref, halo_send, halo_recv):
    geo = lax.axis_index("geo")
    z_pos = lax.axis_index("z")
    y_pos = lax.axis_index("y")
    group = point_ref.shape[0]
    mesh_id = pl.DeviceIdType.MESH
    barrier = pltpu.get_barrier_semaphore()
    for step in (1, z_count - 1):
        pl.semaphore_signal(barrier, inc=1, device_id=(geo, lax.rem(z_pos + step, z_count), y_pos),
                            device_id_type=mesh_id)
    pl.semaphore_wait(barrier, 2)

    def halo_copy(src_lo, dst_ref, slot, target):
        return pltpu.make_async_remote_copy(
            src_ref=point_ref.at[pl.ds(src_lo, HALO)],
            dst_ref=dst_ref,
            send_sem=halo_send.at[slot],
            recv_sem=halo_recv.at[slot],
            device_id=(geo, target, y_pos),
            device_id_type=mesh_id,
        )

    up = halo_copy(group - HALO, lower_ref, 0, lax.rem(z_pos + 1, z_count))
    down = halo_copy(0, upper_ref, 1, lax.rem(z_pos + z_count - 1, z_count))

    @pl.when(z_pos < z_count - 1)
    def _():
        up.start()

    @pl.when(z_pos > 0)
    def _():
        down.start()

    @pl.when(z_pos == 0)
    def _():
        lower_ref[...] = jnp.zeros(lower_ref.shape, lower_ref.dtype)

    @pl.when(z_pos == z_count - 1)
    def _():
        upper_ref[...] = jnp.zeros(upper_ref.shape, upper_ref.dtype)

    @pl.when(z_pos < z_count - 1)
    def _():
        up.wait_send()
        down.wait_recv()

    @pl.when(z_pos > 0)
    def _():
        down.wait_send()
        up.wait_recv()


def z_halo(point, z_count):
    group, dirs, rows, cols = point.shape
    halo = jax.ShapeDtypeStruct((HALO, dirs, rows, cols), point.dtype)
    vmem = pl.BlockSpec(memory_space=pltpu.VMEM)
    return pl.pallas_call(
        functools.partial(_z_halo_kernel, z_count),
        out_shape=(halo, halo),
        in_specs=[pl.BlockSpec(memory_space=pl.ANY)],
        out_specs=(vmem, vmem),
        scratch_shapes=[
            pltpu.SemaphoreType.DMA((2,)),
            pltpu.SemaphoreType.DMA((2,)),
        ],
        compiler_params=pltpu.CompilerParams(collective_id=0, has_side_effects=True),
    )(point)


def extended(cells, sides, width):
    for axis, dim in sides:
        count = lax.axis_size(axis)
        ends = count - 1
        head = lax.slice_in_dim(cells, 0, width, axis=dim)
        tail = lax.slice_in_dim(cells, cells.shape[dim] - width, cells.shape[dim], axis=dim)
        cells = jnp.concatenate(
            [
                lax.ppermute(tail, axis, [(i, (i + 1) % count) for i in range(ends)]),
                cells,
                lax.ppermute(head, axis, [((i + 1) % count, i) for i in range(ends)]),
            ],
            axis=dim,
        )
    return cells


def band_table(band_ids):
    growth_factor = jnp.power(GROWTH, band_ids)
    radian_freq = 2.0 * math.pi * BASE_FREQ * growth_factor
    wavenum = radian_freq * radian_freq / GRAVITY
    return (
        radian_freq,
        wavenum,
        COURANT_TOP / growth_factor,
        TURN_TOP / growth_factor,
        SPACING * radian_freq,
    )


def quick_flux(far_left, near_left, near_right, far_right, courant):
    forward = courant >= 0
    upwind = jnp.where(forward, far_left, far_right)
    center = jnp.where(forward, near_left, near_right)
    downwind = jnp.where(forward, near_right, near_left)
    face_value = (
        0.5 * (center + downwind)
        - 0.5 * jnp.abs(courant) * (downwind - center)
        - (1.0 - courant * courant) / 6.0 * (downwind - 2.0 * center + upwind)
    )
    return courant * face_value


def advect(padded, courant, along):
    face_count = padded.shape[along] - 4
    shifted = [
        lax.slice_in_dim(padded, offset, offset + face_count + 1, axis=along) for offset in range(4)
    ]
    face_flux = quick_flux(shifted[0], shifted[1], shifted[2], shifted[3], courant)
    centre_cells = lax.slice_in_dim(padded, 2, 2 + face_count, axis=along)
    upper_flux = lax.slice_in_dim(face_flux, 1, face_count + 1, axis=along)
    lower_flux = lax.slice_in_dim(face_flux, 0, face_count, axis=along)
    return centre_cells - (upper_flux - lower_flux)


def quad_delta(center, above, below, energy, dir_axis):
    plus = jnp.roll(above, -1, axis=dir_axis)
    minus = jnp.roll(below, 3, axis=dir_axis)
    return (
        QUAD_COEF
        * (center * center * (plus + minus) - 2.0 * center * plus * minus)
        / (energy * energy)
    )


def quad_term(delta, delta_above, delta_below, dir_axis):
    return (
        -2.0 * delta
        + jnp.roll(delta_below, 1, axis=dir_axis)
        + jnp.roll(delta_above, -3, axis=dir_axis)
    )


def band_neighbours(values):
    empty = jnp.zeros((1,) + values.shape[1:], jnp.float32)
    return (
        jnp.concatenate([values[1:], empty], axis=0),
        jnp.concatenate([empty, values[:-1]], axis=0),
    )


def sources(density, energy_sum, first_sum, root_sum, radian_freq, wavenum, cosine, wind_speed):
    energy = energy_sum + EPSILON
    mean_sigma = energy / (first_sum + EPSILON)
    ratio_k = energy / (root_sum + EPSILON)
    mean_k = ratio_k * ratio_k
    steepness = energy * mean_k * mean_k / STEEP_REF
    decay_rate = WHITECAP * mean_sigma * (wavenum / mean_k) * steepness * steepness
    growth_rate = (
        WIND_COEF
        * radian_freq
        * jnp.maximum(28.0 * USTAR_RATIO * wind_speed * radian_freq / GRAVITY * cosine - 1.0, 0.0)
    )
    return density * (1.0 + growth_rate) / (1.0 + decay_rate)


def local_sources(point_block, wind_block, wind_angle, angles, dtheta):
    band_total = point_block.shape[0]
    band_ids = jnp.arange(band_total).astype(jnp.float32)
    radian_freq, wavenum, courant, turn_rate, band_spread = band_table(band_ids)
    scaled = point_block * (band_spread * dtheta)[:, None, None]
    energy_sum = jnp.sum(scaled, axis=(0, 1))
    first_sum = jnp.sum(scaled / radian_freq[:, None, None], axis=(0, 1))
    root_sum = jnp.sum(scaled / jnp.sqrt(wavenum)[:, None, None], axis=(0, 1))
    energy = energy_sum + EPSILON
    above, below = band_neighbours(point_block)
    delta = quad_delta(point_block, above, below, energy, 1)
    delta_above, delta_below = band_neighbours(delta)
    extra = quad_term(delta, delta_above, delta_below, 1)
    cosine = jnp.cos(angles[:, None] - wind_angle[None, :])
    return (
        sources(
            point_block,
            energy_sum,
            first_sum,
            root_sum,
            radian_freq[:, None, None],
            wavenum[:, None, None],
            cosine,
            wind_block,
        )
        + extra
    )


Y_GROUP = 4


def _z_exchange_kernel(z_count, point_ref, part_ref, lower_ref, upper_ref, gathered_ref,
                       halo_send, halo_recv, gather_send, gather_recv):
    geo = lax.axis_index("geo")
    z_pos = lax.axis_index("z")
    y_pos = lax.axis_index("y")
    group = point_ref.shape[0]
    barrier = pltpu.get_barrier_semaphore()
    for offset in range(1, z_count):
        target = lax.rem(z_pos + offset, z_count)
        pl.semaphore_signal(barrier, inc=1, device_id=(geo, target, y_pos),
                            device_id_type=pl.DeviceIdType.MESH)
    pl.semaphore_wait(barrier, z_count - 1)

    def halo_copy(src_lo, dst_ref, slot, target):
        return pltpu.make_async_remote_copy(
            src_ref=point_ref.at[pl.ds(src_lo, 2)],
            dst_ref=dst_ref,
            send_sem=halo_send.at[slot],
            recv_sem=halo_recv.at[slot],
            device_id=(geo, target, y_pos),
            device_id_type=pl.DeviceIdType.MESH,
        )

    up = halo_copy(group - 2, lower_ref, 0, z_pos + 1)
    down = halo_copy(0, upper_ref, 1, z_pos - 1)

    @pl.when(z_pos < z_count - 1)
    def _():
        up.start()

    @pl.when(z_pos > 0)
    def _():
        down.start()

    copies = []
    for offset in range(1, z_count):
        target = lax.rem(z_pos + offset, z_count)
        copy = pltpu.make_async_remote_copy(
            src_ref=part_ref,
            dst_ref=gathered_ref.at[z_pos],
            send_sem=gather_send.at[offset],
            recv_sem=gather_recv.at[offset],
            device_id=(geo, target, y_pos),
            device_id_type=pl.DeviceIdType.MESH,
        )
        copy.start()
        copies.append(copy)
    gathered_ref[z_pos] = part_ref[...]

    @pl.when(z_pos == 0)
    def _():
        lower_ref[...] = jnp.zeros(lower_ref.shape, lower_ref.dtype)

    @pl.when(z_pos == z_count - 1)
    def _():
        upper_ref[...] = jnp.zeros(upper_ref.shape, upper_ref.dtype)

    for copy in copies:
        copy.wait_send()
        copy.wait_recv()

    @pl.when(z_pos < z_count - 1)
    def _():
        up.wait_send()
        down.wait_recv()

    @pl.when(z_pos > 0)
    def _():
        down.wait_send()
        up.wait_recv()


def z_exchange(point, part, z_count):
    group, dirs, rows, cols = point.shape
    halo = jax.ShapeDtypeStruct((2, dirs, rows, cols), point.dtype)
    vmem = pl.BlockSpec(memory_space=pltpu.VMEM)
    return pl.pallas_call(
        functools.partial(_z_exchange_kernel, z_count),
        out_shape=(halo, halo, jax.ShapeDtypeStruct((z_count,) + part.shape, part.dtype)),
        in_specs=[vmem, vmem],
        out_specs=(vmem, vmem, vmem),
        scratch_shapes=[
            pltpu.SemaphoreType.DMA((2,)),
            pltpu.SemaphoreType.DMA((2,)),
            pltpu.SemaphoreType.DMA((z_count,)),
            pltpu.SemaphoreType.DMA((z_count,)),
        ],
        compiler_params=pltpu.CompilerParams(collective_id=0, has_side_effects=True),
    )(point, part)


def shards(spectrum, land_sea, sea_index, sea_count, wind_speed, wind_dir, slope_x, slope_y):
    local_bands, dir_count, row_count, col_count = spectrum.shape
    z_count = lax.axis_size("z")
    y_count = lax.axis_size("y")
    z_pos = lax.axis_index("z")
    y_pos = lax.axis_index("y")
    spec_pos = z_pos * y_count + y_pos
    dtheta = 2.0 * math.pi / dir_count
    angles = (jnp.arange(dir_count).astype(jnp.float32) + 0.5) * dtheta
    face_angles = jnp.arange(dir_count + 1).astype(jnp.float32) * dtheta
    band_ids = (spec_pos * local_bands + jnp.arange(local_bands)).astype(jnp.float32)
    radian_freq, wavenum, courant, turn_rate, band_spread = band_table(band_ids)
    wet_mask = land_sea.astype(jnp.float32)
    density = spectrum * wet_mask
    padded = extended(density, (("geo", 2),), 2)
    density = (
        advect(padded, (courant[:, None] * jnp.cos(angles)[None, :])[:, :, None, None], 2)
        * wet_mask
    )
    padded = jnp.pad(density, ((0, 0), (0, 0), (0, 0), (2, 2)))
    density = (
        advect(padded, (courant[:, None] * jnp.sin(angles)[None, :])[:, :, None, None], 3)
        * wet_mask
    )
    turning = turn_rate[:, None, None, None] * (
        jnp.sin(face_angles)[None, :, None, None] * slope_x
        - jnp.cos(face_angles)[None, :, None, None] * slope_y
    )
    padded = jnp.concatenate([density[:, -2:], density, density[:, :2]], axis=1)
    floored = jnp.maximum(advect(padded, turning, 1), 0.0)
    y_count = lax.axis_size("y")
    quarters = jnp.transpose(
        floored[0].reshape(dir_count, y_count, row_count // y_count, col_count), (1, 0, 2, 3)
    )
    point = lax.all_to_all(quarters, "y", split_axis=0, concat_axis=0, tiled=True)
    group = point.shape[0]
    part_rows = point.shape[2]
    group_ids = (z_pos * group + jnp.arange(group)).astype(jnp.float32)
    radian_freq, wavenum, courant, turn_rate, band_spread = band_table(group_ids)
    scaled = point * (band_spread * dtheta)[:, None, None, None]
    sums = jnp.stack(
        [
            jnp.sum(scaled, axis=(0, 1)),
            jnp.sum(scaled / radian_freq[:, None, None, None], axis=(0, 1)),
            jnp.sum(scaled / jnp.sqrt(wavenum)[:, None, None, None], axis=(0, 1)),
        ]
    )
    lower, upper = z_halo(point, z_count)
    step = 1
    while step < z_count:
        sums = sums + lax.ppermute(sums, "z", [(i, i ^ step) for i in range(z_count)])
        step *= 2
    energy_sum, first_sum, root_sum = sums[0], sums[1], sums[2]
    energy = energy_sum + EPSILON
    ext = jnp.concatenate([lower, point, upper], axis=0)
    center, plus, minus = ext[1:-1], jnp.roll(ext[2:], -1, axis=1), jnp.roll(ext[:-2], 3, axis=1)
    cubic = center * center * (plus + minus) - 2.0 * center * plus * minus
    extra = (
        -2.0 * cubic[1:-1] + jnp.roll(cubic[:-2], 1, axis=1) + jnp.roll(cubic[2:], -3, axis=1)
    ) * (QUAD_COEF / (energy * energy))
    row_start = y_pos * part_rows
    wind_block = lax.dynamic_slice_in_dim(wind_speed, row_start, part_rows, axis=0)
    wind_angle = lax.dynamic_slice_in_dim(wind_dir, row_start, part_rows, axis=0)
    wet_block = lax.dynamic_slice_in_dim(wet_mask, row_start, part_rows, axis=0)
    cosine = jnp.cos(angles[:, None, None] - wind_angle[None])
    updated = (
        sources(
            point,
            energy_sum,
            first_sum,
            root_sum,
            radian_freq[:, None, None, None],
            wavenum[:, None, None, None],
            cosine,
            wind_block,
        )
        + extra
    ) * wet_block
    return lax.all_to_all(updated, "y", split_axis=0, concat_axis=2, tiled=True)


def solution(mesh):
    geo_count = mesh.shape["geo"]
    spec_count = mesh.shape["spec"]
    local = jax.sharding.Mesh(
        mesh.devices.reshape(geo_count, spec_count // Y_GROUP, Y_GROUP), ("geo", "z", "y")
    )
    spec = ("z", "y")
    placed = (
        P(spec, None, "geo", None),
        P("geo", None),
        P("geo", None),
        P("geo"),
        P("geo", None),
        P("geo", None),
        P("geo", None),
        P("geo", None),
    )
    return jax.shard_map(
        shards, mesh=local, in_specs=placed, out_specs=P(spec, None, "geo", None), check_vma=False
    )
```

```python
import functools
import math

import jax
import jax.numpy as jnp
from jax import lax
from jax.experimental import pallas as pl
from jax.experimental.pallas import tpu as pltpu
from jax.sharding import PartitionSpec as P

GRAVITY = 9.81
BASE_FREQ = 0.035
GROWTH = 1.1
COURANT_TOP = 0.9
TURN_TOP = 1.2
SPACING = 0.1
USTAR_RATIO = 0.035
WIND_COEF = 0.0375
WHITECAP = 0.36
STEEP_REF = 1.6
EPSILON = 1e-06
QUAD_COEF = 100.0


def extended(cells, sides, width):
    for axis, dim in sides:
        count = lax.axis_size(axis)
        ends = count - 1
        head = lax.slice_in_dim(cells, 0, width, axis=dim)
        tail = lax.slice_in_dim(cells, cells.shape[dim] - width, cells.shape[dim], axis=dim)
        cells = jnp.concatenate(
            [
                lax.ppermute(tail, axis, [(i, (i + 1) % count) for i in range(ends)]),
                cells,
                lax.ppermute(head, axis, [((i + 1) % count, i) for i in range(ends)]),
            ],
            axis=dim,
        )
    return cells


def band_table(band_ids):
    growth_factor = jnp.power(GROWTH, band_ids)
    radian_freq = 2.0 * math.pi * BASE_FREQ * growth_factor
    wavenum = radian_freq * radian_freq / GRAVITY
    return (
        radian_freq,
        wavenum,
        COURANT_TOP / growth_factor,
        TURN_TOP / growth_factor,
        SPACING * radian_freq,
    )


def quick_flux(far_left, near_left, near_right, far_right, courant):
    forward = courant >= 0
    upwind = jnp.where(forward, far_left, far_right)
    center = jnp.where(forward, near_left, near_right)
    downwind = jnp.where(forward, near_right, near_left)
    face_value = (
        0.5 * (center + downwind)
        - 0.5 * jnp.abs(courant) * (downwind - center)
        - (1.0 - courant * courant) / 6.0 * (downwind - 2.0 * center + upwind)
    )
    return courant * face_value


def advect(padded, courant, along):
    face_count = padded.shape[along] - 4
    shifted = [
        lax.slice_in_dim(padded, offset, offset + face_count + 1, axis=along) for offset in range(4)
    ]
    face_flux = quick_flux(shifted[0], shifted[1], shifted[2], shifted[3], courant)
    centre_cells = lax.slice_in_dim(padded, 2, 2 + face_count, axis=along)
    upper_flux = lax.slice_in_dim(face_flux, 1, face_count + 1, axis=along)
    lower_flux = lax.slice_in_dim(face_flux, 0, face_count, axis=along)
    return centre_cells - (upper_flux - lower_flux)


def quad_delta(center, above, below, energy, dir_axis):
    plus = jnp.roll(above, -1, axis=dir_axis)
    minus = jnp.roll(below, 3, axis=dir_axis)
    return (
        QUAD_COEF
        * (center * center * (plus + minus) - 2.0 * center * plus * minus)
        / (energy * energy)
    )


def quad_term(delta, delta_above, delta_below, dir_axis):
    return (
        -2.0 * delta
        + jnp.roll(delta_below, 1, axis=dir_axis)
        + jnp.roll(delta_above, -3, axis=dir_axis)
    )


def band_neighbours(values):
    empty = jnp.zeros((1,) + values.shape[1:], jnp.float32)
    return (
        jnp.concatenate([values[1:], empty], axis=0),
        jnp.concatenate([empty, values[:-1]], axis=0),
    )


def sources(density, energy_sum, first_sum, root_sum, radian_freq, wavenum, cosine, wind_speed):
    energy = energy_sum + EPSILON
    mean_sigma = energy / (first_sum + EPSILON)
    ratio_k = energy / (root_sum + EPSILON)
    mean_k = ratio_k * ratio_k
    steepness = energy * mean_k * mean_k / STEEP_REF
    decay_rate = WHITECAP * mean_sigma * (wavenum / mean_k) * steepness * steepness
    growth_rate = (
        WIND_COEF
        * radian_freq
        * jnp.maximum(28.0 * USTAR_RATIO * wind_speed * radian_freq / GRAVITY * cosine - 1.0, 0.0)
    )
    return density * (1.0 + growth_rate) / (1.0 + decay_rate)


def local_sources(point_block, wind_block, wind_angle, angles, dtheta):
    band_total = point_block.shape[0]
    band_ids = jnp.arange(band_total).astype(jnp.float32)
    radian_freq, wavenum, courant, turn_rate, band_spread = band_table(band_ids)
    scaled = point_block * (band_spread * dtheta)[:, None, None]
    energy_sum = jnp.sum(scaled, axis=(0, 1))
    first_sum = jnp.sum(scaled / radian_freq[:, None, None], axis=(0, 1))
    root_sum = jnp.sum(scaled / jnp.sqrt(wavenum)[:, None, None], axis=(0, 1))
    energy = energy_sum + EPSILON
    above, below = band_neighbours(point_block)
    delta = quad_delta(point_block, above, below, energy, 1)
    delta_above, delta_below = band_neighbours(delta)
    extra = quad_term(delta, delta_above, delta_below, 1)
    cosine = jnp.cos(angles[:, None] - wind_angle[None, :])
    return (
        sources(
            point_block,
            energy_sum,
            first_sum,
            root_sum,
            radian_freq[:, None, None],
            wavenum[:, None, None],
            cosine,
            wind_block,
        )
        + extra
    )


Y_GROUP = 4
HALO = 2


def _z_halo_kernel(z_count, point_ref, lower_ref, upper_ref, halo_send, halo_recv):
    geo = lax.axis_index("geo")
    z_pos = lax.axis_index("z")
    y_pos = lax.axis_index("y")
    group = point_ref.shape[0]
    mesh_id = pl.DeviceIdType.MESH
    barrier = pltpu.get_barrier_semaphore()
    for step in (1, z_count - 1):
        pl.semaphore_signal(barrier, inc=1, device_id=(geo, lax.rem(z_pos + step, z_count), y_pos),
                            device_id_type=mesh_id)
    pl.semaphore_wait(barrier, 2)

    def halo_copy(src_lo, dst_ref, slot, target):
        return pltpu.make_async_remote_copy(
            src_ref=point_ref.at[pl.ds(src_lo, HALO)],
            dst_ref=dst_ref,
            send_sem=halo_send.at[slot],
            recv_sem=halo_recv.at[slot],
            device_id=(geo, target, y_pos),
            device_id_type=mesh_id,
        )

    up = halo_copy(group - HALO, lower_ref, 0, lax.rem(z_pos + 1, z_count))
    down = halo_copy(0, upper_ref, 1, lax.rem(z_pos + z_count - 1, z_count))

    @pl.when(z_pos < z_count - 1)
    def _():
        up.start()

    @pl.when(z_pos > 0)
    def _():
        down.start()

    @pl.when(z_pos == 0)
    def _():
        lower_ref[...] = jnp.zeros(lower_ref.shape, lower_ref.dtype)

    @pl.when(z_pos == z_count - 1)
    def _():
        upper_ref[...] = jnp.zeros(upper_ref.shape, upper_ref.dtype)

    @pl.when(z_pos < z_count - 1)
    def _():
        up.wait_send()
        down.wait_recv()

    @pl.when(z_pos > 0)
    def _():
        down.wait_send()
        up.wait_recv()


def z_halo(point, z_count):
    group, dirs, rows, cols = point.shape
    halo = jax.ShapeDtypeStruct((HALO, dirs, rows, cols), point.dtype)
    vmem = pl.BlockSpec(memory_space=pltpu.VMEM)
    return pl.pallas_call(
        functools.partial(_z_halo_kernel, z_count),
        out_shape=(halo, halo),
        in_specs=[pl.BlockSpec(memory_space=pl.ANY)],
        out_specs=(vmem, vmem),
        scratch_shapes=[
            pltpu.SemaphoreType.DMA((2,)),
            pltpu.SemaphoreType.DMA((2,)),
        ],
        compiler_params=pltpu.CompilerParams(collective_id=0, has_side_effects=True),
    )(point)


def extended(cells, sides, width):
    for axis, dim in sides:
        count = lax.axis_size(axis)
        ends = count - 1
        head = lax.slice_in_dim(cells, 0, width, axis=dim)
        tail = lax.slice_in_dim(cells, cells.shape[dim] - width, cells.shape[dim], axis=dim)
        cells = jnp.concatenate(
            [
                lax.ppermute(tail, axis, [(i, (i + 1) % count) for i in range(ends)]),
                cells,
                lax.ppermute(head, axis, [((i + 1) % count, i) for i in range(ends)]),
            ],
            axis=dim,
        )
    return cells


def band_table(band_ids):
    growth_factor = jnp.power(GROWTH, band_ids)
    radian_freq = 2.0 * math.pi * BASE_FREQ * growth_factor
    wavenum = radian_freq * radian_freq / GRAVITY
    return (
        radian_freq,
        wavenum,
        COURANT_TOP / growth_factor,
        TURN_TOP / growth_factor,
        SPACING * radian_freq,
    )


def quick_flux(far_left, near_left, near_right, far_right, courant):
    forward = courant >= 0
    upwind = jnp.where(forward, far_left, far_right)
    center = jnp.where(forward, near_left, near_right)
    downwind = jnp.where(forward, near_right, near_left)
    face_value = (
        0.5 * (center + downwind)
        - 0.5 * jnp.abs(courant) * (downwind - center)
        - (1.0 - courant * courant) / 6.0 * (downwind - 2.0 * center + upwind)
    )
    return courant * face_value


def advect(padded, courant, along):
    face_count = padded.shape[along] - 4
    shifted = [
        lax.slice_in_dim(padded, offset, offset + face_count + 1, axis=along) for offset in range(4)
    ]
    face_flux = quick_flux(shifted[0], shifted[1], shifted[2], shifted[3], courant)
    centre_cells = lax.slice_in_dim(padded, 2, 2 + face_count, axis=along)
    upper_flux = lax.slice_in_dim(face_flux, 1, face_count + 1, axis=along)
    lower_flux = lax.slice_in_dim(face_flux, 0, face_count, axis=along)
    return centre_cells - (upper_flux - lower_flux)


def quad_delta(center, above, below, energy, dir_axis):
    plus = jnp.roll(above, -1, axis=dir_axis)
    minus = jnp.roll(below, 3, axis=dir_axis)
    return (
        QUAD_COEF
        * (center * center * (plus + minus) - 2.0 * center * plus * minus)
        / (energy * energy)
    )


def quad_term(delta, delta_above, delta_below, dir_axis):
    return (
        -2.0 * delta
        + jnp.roll(delta_below, 1, axis=dir_axis)
        + jnp.roll(delta_above, -3, axis=dir_axis)
    )


def band_neighbours(values):
    empty = jnp.zeros((1,) + values.shape[1:], jnp.float32)
    return (
        jnp.concatenate([values[1:], empty], axis=0),
        jnp.concatenate([empty, values[:-1]], axis=0),
    )


def sources(density, energy_sum, first_sum, root_sum, radian_freq, wavenum, cosine, wind_speed):
    energy = energy_sum + EPSILON
    mean_sigma = energy / (first_sum + EPSILON)
    ratio_k = energy / (root_sum + EPSILON)
    mean_k = ratio_k * ratio_k
    steepness = energy * mean_k * mean_k / STEEP_REF
    decay_rate = WHITECAP * mean_sigma * (wavenum / mean_k) * steepness * steepness
    growth_rate = (
        WIND_COEF
        * radian_freq
        * jnp.maximum(28.0 * USTAR_RATIO * wind_speed * radian_freq / GRAVITY * cosine - 1.0, 0.0)
    )
    return density * (1.0 + growth_rate) / (1.0 + decay_rate)


def local_sources(point_block, wind_block, wind_angle, angles, dtheta):
    band_total = point_block.shape[0]
    band_ids = jnp.arange(band_total).astype(jnp.float32)
    radian_freq, wavenum, courant, turn_rate, band_spread = band_table(band_ids)
    scaled = point_block * (band_spread * dtheta)[:, None, None]
    energy_sum = jnp.sum(scaled, axis=(0, 1))
    first_sum = jnp.sum(scaled / radian_freq[:, None, None], axis=(0, 1))
    root_sum = jnp.sum(scaled / jnp.sqrt(wavenum)[:, None, None], axis=(0, 1))
    energy = energy_sum + EPSILON
    above, below = band_neighbours(point_block)
    delta = quad_delta(point_block, above, below, energy, 1)
    delta_above, delta_below = band_neighbours(delta)
    extra = quad_term(delta, delta_above, delta_below, 1)
    cosine = jnp.cos(angles[:, None] - wind_angle[None, :])
    return (
        sources(
            point_block,
            energy_sum,
            first_sum,
            root_sum,
            radian_freq[:, None, None],
            wavenum[:, None, None],
            cosine,
            wind_block,
        )
        + extra
    )


Y_GROUP = 4


def _z_exchange_kernel(z_count, point_ref, part_ref, lower_ref, upper_ref, gathered_ref,
                       halo_send, halo_recv, gather_send, gather_recv):
    geo = lax.axis_index("geo")
    z_pos = lax.axis_index("z")
    y_pos = lax.axis_index("y")
    group = point_ref.shape[0]
    barrier = pltpu.get_barrier_semaphore()
    for offset in range(1, z_count):
        target = lax.rem(z_pos + offset, z_count)
        pl.semaphore_signal(barrier, inc=1, device_id=(geo, target, y_pos),
                            device_id_type=pl.DeviceIdType.MESH)
    pl.semaphore_wait(barrier, z_count - 1)

    def halo_copy(src_lo, dst_ref, slot, target):
        return pltpu.make_async_remote_copy(
            src_ref=point_ref.at[pl.ds(src_lo, 2)],
            dst_ref=dst_ref,
            send_sem=halo_send.at[slot],
            recv_sem=halo_recv.at[slot],
            device_id=(geo, target, y_pos),
            device_id_type=pl.DeviceIdType.MESH,
        )

    up = halo_copy(group - 2, lower_ref, 0, z_pos + 1)
    down = halo_copy(0, upper_ref, 1, z_pos - 1)

    @pl.when(z_pos < z_count - 1)
    def _():
        up.start()

    @pl.when(z_pos > 0)
    def _():
        down.start()

    copies = []
    for offset in range(1, z_count):
        target = lax.rem(z_pos + offset, z_count)
        copy = pltpu.make_async_remote_copy(
            src_ref=part_ref,
            dst_ref=gathered_ref.at[z_pos],
            send_sem=gather_send.at[offset],
            recv_sem=gather_recv.at[offset],
            device_id=(geo, target, y_pos),
            device_id_type=pl.DeviceIdType.MESH,
        )
        copy.start()
        copies.append(copy)
    gathered_ref[z_pos] = part_ref[...]

    @pl.when(z_pos == 0)
    def _():
        lower_ref[...] = jnp.zeros(lower_ref.shape, lower_ref.dtype)

    @pl.when(z_pos == z_count - 1)
    def _():
        upper_ref[...] = jnp.zeros(upper_ref.shape, upper_ref.dtype)

    for copy in copies:
        copy.wait_send()
        copy.wait_recv()

    @pl.when(z_pos < z_count - 1)
    def _():
        up.wait_send()
        down.wait_recv()

    @pl.when(z_pos > 0)
    def _():
        down.wait_send()
        up.wait_recv()


def z_exchange(point, part, z_count):
    group, dirs, rows, cols = point.shape
    halo = jax.ShapeDtypeStruct((2, dirs, rows, cols), point.dtype)
    vmem = pl.BlockSpec(memory_space=pltpu.VMEM)
    return pl.pallas_call(
        functools.partial(_z_exchange_kernel, z_count),
        out_shape=(halo, halo, jax.ShapeDtypeStruct((z_count,) + part.shape, part.dtype)),
        in_specs=[vmem, vmem],
        out_specs=(vmem, vmem, vmem),
        scratch_shapes=[
            pltpu.SemaphoreType.DMA((2,)),
            pltpu.SemaphoreType.DMA((2,)),
            pltpu.SemaphoreType.DMA((z_count,)),
            pltpu.SemaphoreType.DMA((z_count,)),
        ],
        compiler_params=pltpu.CompilerParams(collective_id=0, has_side_effects=True),
    )(point, part)


def shards(spectrum, land_sea, sea_index, sea_count, wind_speed, wind_dir, slope_x, slope_y):
    local_bands, dir_count, row_count, col_count = spectrum.shape
    z_count = lax.axis_size("z")
    y_count = lax.axis_size("y")
    z_pos = lax.axis_index("z")
    y_pos = lax.axis_index("y")
    spec_pos = z_pos * y_count + y_pos
    dtheta = 2.0 * math.pi / dir_count
    angles = (jnp.arange(dir_count).astype(jnp.float32) + 0.5) * dtheta
    face_angles = jnp.arange(dir_count + 1).astype(jnp.float32) * dtheta
    band_ids = (spec_pos * local_bands + jnp.arange(local_bands)).astype(jnp.float32)
    radian_freq, wavenum, courant, turn_rate, band_spread = band_table(band_ids)
    wet_mask = land_sea.astype(jnp.float32)
    density = spectrum * wet_mask
    padded = extended(density, (("geo", 2),), 2)
    density = (
        advect(padded, (courant[:, None] * jnp.cos(angles)[None, :])[:, :, None, None], 2)
        * wet_mask
    )
    padded = jnp.pad(density, ((0, 0), (0, 0), (0, 0), (2, 2)))
    density = (
        advect(padded, (courant[:, None] * jnp.sin(angles)[None, :])[:, :, None, None], 3)
        * wet_mask
    )
    turning = turn_rate[:, None, None, None] * (
        jnp.sin(face_angles)[None, :, None, None] * slope_x
        - jnp.cos(face_angles)[None, :, None, None] * slope_y
    )
    padded = jnp.concatenate([density[:, -2:], density, density[:, :2]], axis=1)
    floored = jnp.maximum(advect(padded, turning, 1), 0.0)
    own_scaled = floored * (band_spread * dtheta)[:, None, None, None]
    tile_sums = jnp.stack(
        [
            jnp.sum(own_scaled, axis=(0, 1)),
            jnp.sum(own_scaled / radian_freq[:, None, None, None], axis=(0, 1)),
            jnp.sum(own_scaled / jnp.sqrt(wavenum)[:, None, None, None], axis=(0, 1)),
        ]
    )
    for axis, size in (("z", z_count), ("y", lax.axis_size("y"))):
        step = 1
        while step < size:
            tile_sums = tile_sums + lax.ppermute(
                tile_sums, axis, [(i, i ^ step) for i in range(size)]
            )
            step *= 2
    point = lax.all_to_all(floored, "y", split_axis=2, concat_axis=0, tiled=True)
    group = point.shape[0]
    part_rows = point.shape[2]
    group_ids = (z_pos * group + jnp.arange(group)).astype(jnp.float32)
    radian_freq, wavenum, courant, turn_rate, band_spread = band_table(group_ids)
    lower, upper = z_halo(point, z_count)
    sums = lax.dynamic_slice_in_dim(tile_sums, y_pos * part_rows, part_rows, axis=1)
    energy_sum, first_sum, root_sum = sums[0], sums[1], sums[2]
    energy = energy_sum + EPSILON
    ext = jnp.concatenate([lower, point, upper], axis=0)
    center, plus, minus = ext[1:-1], jnp.roll(ext[2:], -1, axis=1), jnp.roll(ext[:-2], 3, axis=1)
    cubic = center * center * (plus + minus) - 2.0 * center * plus * minus
    extra = (
        -2.0 * cubic[1:-1] + jnp.roll(cubic[:-2], 1, axis=1) + jnp.roll(cubic[2:], -3, axis=1)
    ) * (QUAD_COEF / (energy * energy))
    row_start = y_pos * part_rows
    wind_block = lax.dynamic_slice_in_dim(wind_speed, row_start, part_rows, axis=0)
    wind_angle = lax.dynamic_slice_in_dim(wind_dir, row_start, part_rows, axis=0)
    wet_block = lax.dynamic_slice_in_dim(wet_mask, row_start, part_rows, axis=0)
    cosine = jnp.cos(angles[:, None, None] - wind_angle[None])
    updated = (
        sources(
            point,
            energy_sum,
            first_sum,
            root_sum,
            radian_freq[:, None, None, None],
            wavenum[:, None, None, None],
            cosine,
            wind_block,
        )
        + extra
    ) * wet_block
    return lax.all_to_all(updated, "y", split_axis=0, concat_axis=2, tiled=True)


def solution(mesh):
    geo_count = mesh.shape["geo"]
    spec_count = mesh.shape["spec"]
    local = jax.sharding.Mesh(
        mesh.devices.reshape(geo_count, spec_count // Y_GROUP, Y_GROUP), ("geo", "z", "y")
    )
    spec = ("z", "y")
    placed = (
        P(spec, None, "geo", None),
        P("geo", None),
        P("geo", None),
        P("geo"),
        P("geo", None),
        P("geo", None),
        P("geo", None),
        P("geo", None),
    )
    return jax.shard_map(
        shards, mesh=local, in_specs=placed, out_specs=P(spec, None, "geo", None), check_vma=False
    )
```

```python
import functools
import math

import jax
import jax.numpy as jnp
from jax import lax
from jax.experimental import pallas as pl
from jax.experimental.pallas import tpu as pltpu
from jax.sharding import PartitionSpec as P

GRAVITY = 9.81
BASE_FREQ = 0.035
GROWTH = 1.1
COURANT_TOP = 0.9
TURN_TOP = 1.2
SPACING = 0.1
USTAR_RATIO = 0.035
WIND_COEF = 0.0375
WHITECAP = 0.36
STEEP_REF = 1.6
EPSILON = 1e-06
QUAD_COEF = 100.0


def extended(cells, sides, width):
    for axis, dim in sides:
        count = lax.axis_size(axis)
        ends = count - 1
        head = lax.slice_in_dim(cells, 0, width, axis=dim)
        tail = lax.slice_in_dim(cells, cells.shape[dim] - width, cells.shape[dim], axis=dim)
        cells = jnp.concatenate(
            [
                lax.ppermute(tail, axis, [(i, (i + 1) % count) for i in range(ends)]),
                cells,
                lax.ppermute(head, axis, [((i + 1) % count, i) for i in range(ends)]),
            ],
            axis=dim,
        )
    return cells


def band_table(band_ids):
    growth_factor = jnp.power(GROWTH, band_ids)
    radian_freq = 2.0 * math.pi * BASE_FREQ * growth_factor
    wavenum = radian_freq * radian_freq / GRAVITY
    return (
        radian_freq,
        wavenum,
        COURANT_TOP / growth_factor,
        TURN_TOP / growth_factor,
        SPACING * radian_freq,
    )


def quick_flux(far_left, near_left, near_right, far_right, courant):
    forward = courant >= 0
    upwind = jnp.where(forward, far_left, far_right)
    center = jnp.where(forward, near_left, near_right)
    downwind = jnp.where(forward, near_right, near_left)
    face_value = (
        0.5 * (center + downwind)
        - 0.5 * jnp.abs(courant) * (downwind - center)
        - (1.0 - courant * courant) / 6.0 * (downwind - 2.0 * center + upwind)
    )
    return courant * face_value


def advect(padded, courant, along):
    face_count = padded.shape[along] - 4
    shifted = [
        lax.slice_in_dim(padded, offset, offset + face_count + 1, axis=along) for offset in range(4)
    ]
    face_flux = quick_flux(shifted[0], shifted[1], shifted[2], shifted[3], courant)
    centre_cells = lax.slice_in_dim(padded, 2, 2 + face_count, axis=along)
    upper_flux = lax.slice_in_dim(face_flux, 1, face_count + 1, axis=along)
    lower_flux = lax.slice_in_dim(face_flux, 0, face_count, axis=along)
    return centre_cells - (upper_flux - lower_flux)


def quad_delta(center, above, below, energy, dir_axis):
    plus = jnp.roll(above, -1, axis=dir_axis)
    minus = jnp.roll(below, 3, axis=dir_axis)
    return (
        QUAD_COEF
        * (center * center * (plus + minus) - 2.0 * center * plus * minus)
        / (energy * energy)
    )


def quad_term(delta, delta_above, delta_below, dir_axis):
    return (
        -2.0 * delta
        + jnp.roll(delta_below, 1, axis=dir_axis)
        + jnp.roll(delta_above, -3, axis=dir_axis)
    )


def band_neighbours(values):
    empty = jnp.zeros((1,) + values.shape[1:], jnp.float32)
    return (
        jnp.concatenate([values[1:], empty], axis=0),
        jnp.concatenate([empty, values[:-1]], axis=0),
    )


def sources(density, energy_sum, first_sum, root_sum, radian_freq, wavenum, cosine, wind_speed):
    energy = energy_sum + EPSILON
    mean_sigma = energy / (first_sum + EPSILON)
    ratio_k = energy / (root_sum + EPSILON)
    mean_k = ratio_k * ratio_k
    steepness = energy * mean_k * mean_k / STEEP_REF
    decay_rate = WHITECAP * mean_sigma * (wavenum / mean_k) * steepness * steepness
    growth_rate = (
        WIND_COEF
        * radian_freq
        * jnp.maximum(28.0 * USTAR_RATIO * wind_speed * radian_freq / GRAVITY * cosine - 1.0, 0.0)
    )
    return density * (1.0 + growth_rate) / (1.0 + decay_rate)


def local_sources(point_block, wind_block, wind_angle, angles, dtheta):
    band_total = point_block.shape[0]
    band_ids = jnp.arange(band_total).astype(jnp.float32)
    radian_freq, wavenum, courant, turn_rate, band_spread = band_table(band_ids)
    scaled = point_block * (band_spread * dtheta)[:, None, None]
    energy_sum = jnp.sum(scaled, axis=(0, 1))
    first_sum = jnp.sum(scaled / radian_freq[:, None, None], axis=(0, 1))
    root_sum = jnp.sum(scaled / jnp.sqrt(wavenum)[:, None, None], axis=(0, 1))
    energy = energy_sum + EPSILON
    above, below = band_neighbours(point_block)
    delta = quad_delta(point_block, above, below, energy, 1)
    delta_above, delta_below = band_neighbours(delta)
    extra = quad_term(delta, delta_above, delta_below, 1)
    cosine = jnp.cos(angles[:, None] - wind_angle[None, :])
    return (
        sources(
            point_block,
            energy_sum,
            first_sum,
            root_sum,
            radian_freq[:, None, None],
            wavenum[:, None, None],
            cosine,
            wind_block,
        )
        + extra
    )


Y_GROUP = 4
HALO = 2


def _z_halo_kernel(z_count, point_ref, sums_ref, lower_ref, upper_ref, pair_ref, halo_send, halo_recv,
                   pair_send, pair_recv):
    geo = lax.axis_index("geo")
    z_pos = lax.axis_index("z")
    y_pos = lax.axis_index("y")
    group = point_ref.shape[0]
    mesh_id = pl.DeviceIdType.MESH
    barrier = pltpu.get_barrier_semaphore()
    for step in (1, z_count - 1):
        pl.semaphore_signal(barrier, inc=1, device_id=(geo, lax.rem(z_pos + step, z_count), y_pos),
                            device_id_type=mesh_id)
    pl.semaphore_wait(barrier, 2)

    def halo_copy(src_lo, dst_ref, slot, target):
        return pltpu.make_async_remote_copy(
            src_ref=point_ref.at[pl.ds(src_lo, HALO)],
            dst_ref=dst_ref,
            send_sem=halo_send.at[slot],
            recv_sem=halo_recv.at[slot],
            device_id=(geo, target, y_pos),
            device_id_type=mesh_id,
        )

    up = halo_copy(group - HALO, lower_ref, 0, lax.rem(z_pos + 1, z_count))
    down = halo_copy(0, upper_ref, 1, lax.rem(z_pos + z_count - 1, z_count))

    pair = pltpu.make_async_remote_copy(
        src_ref=sums_ref,
        dst_ref=pair_ref,
        send_sem=pair_send.at[0],
        recv_sem=pair_recv.at[0],
        device_id=(geo, z_pos + 1 - 2 * lax.rem(z_pos, 2), y_pos),
        device_id_type=mesh_id,
    )
    pair.start()

    @pl.when(z_pos < z_count - 1)
    def _():
        up.start()

    @pl.when(z_pos > 0)
    def _():
        down.start()

    @pl.when(z_pos == 0)
    def _():
        lower_ref[...] = jnp.zeros(lower_ref.shape, lower_ref.dtype)

    @pl.when(z_pos == z_count - 1)
    def _():
        upper_ref[...] = jnp.zeros(upper_ref.shape, upper_ref.dtype)

    pair.wait_send()
    pair.wait_recv()

    @pl.when(z_pos < z_count - 1)
    def _():
        up.wait_send()
        down.wait_recv()

    @pl.when(z_pos > 0)
    def _():
        down.wait_send()
        up.wait_recv()


def z_halo(point, sums, z_count):
    group, dirs, rows, cols = point.shape
    halo = jax.ShapeDtypeStruct((HALO, dirs, rows, cols), point.dtype)
    vmem = pl.BlockSpec(memory_space=pltpu.VMEM)
    hbm = pl.BlockSpec(memory_space=pl.ANY)
    return pl.pallas_call(
        functools.partial(_z_halo_kernel, z_count),
        out_shape=(halo, halo, jax.ShapeDtypeStruct(sums.shape, sums.dtype)),
        in_specs=[hbm, hbm],
        out_specs=(vmem, vmem, vmem),
        scratch_shapes=[
            pltpu.SemaphoreType.DMA((2,)),
            pltpu.SemaphoreType.DMA((2,)),
            pltpu.SemaphoreType.DMA((1,)),
            pltpu.SemaphoreType.DMA((1,)),
        ],
        compiler_params=pltpu.CompilerParams(collective_id=0, has_side_effects=True),
    )(point, sums)


def extended(cells, sides, width):
    for axis, dim in sides:
        count = lax.axis_size(axis)
        ends = count - 1
        head = lax.slice_in_dim(cells, 0, width, axis=dim)
        tail = lax.slice_in_dim(cells, cells.shape[dim] - width, cells.shape[dim], axis=dim)
        cells = jnp.concatenate(
            [
                lax.ppermute(tail, axis, [(i, (i + 1) % count) for i in range(ends)]),
                cells,
                lax.ppermute(head, axis, [((i + 1) % count, i) for i in range(ends)]),
            ],
            axis=dim,
        )
    return cells


def band_table(band_ids):
    growth_factor = jnp.power(GROWTH, band_ids)
    radian_freq = 2.0 * math.pi * BASE_FREQ * growth_factor
    wavenum = radian_freq * radian_freq / GRAVITY
    return (
        radian_freq,
        wavenum,
        COURANT_TOP / growth_factor,
        TURN_TOP / growth_factor,
        SPACING * radian_freq,
    )


def quick_flux(far_left, near_left, near_right, far_right, courant):
    forward = courant >= 0
    upwind = jnp.where(forward, far_left, far_right)
    center = jnp.where(forward, near_left, near_right)
    downwind = jnp.where(forward, near_right, near_left)
    face_value = (
        0.5 * (center + downwind)
        - 0.5 * jnp.abs(courant) * (downwind - center)
        - (1.0 - courant * courant) / 6.0 * (downwind - 2.0 * center + upwind)
    )
    return courant * face_value


def advect(padded, courant, along):
    face_count = padded.shape[along] - 4
    shifted = [
        lax.slice_in_dim(padded, offset, offset + face_count + 1, axis=along) for offset in range(4)
    ]
    face_flux = quick_flux(shifted[0], shifted[1], shifted[2], shifted[3], courant)
    centre_cells = lax.slice_in_dim(padded, 2, 2 + face_count, axis=along)
    upper_flux = lax.slice_in_dim(face_flux, 1, face_count + 1, axis=along)
    lower_flux = lax.slice_in_dim(face_flux, 0, face_count, axis=along)
    return centre_cells - (upper_flux - lower_flux)


def quad_delta(center, above, below, energy, dir_axis):
    plus = jnp.roll(above, -1, axis=dir_axis)
    minus = jnp.roll(below, 3, axis=dir_axis)
    return (
        QUAD_COEF
        * (center * center * (plus + minus) - 2.0 * center * plus * minus)
        / (energy * energy)
    )


def quad_term(delta, delta_above, delta_below, dir_axis):
    return (
        -2.0 * delta
        + jnp.roll(delta_below, 1, axis=dir_axis)
        + jnp.roll(delta_above, -3, axis=dir_axis)
    )


def band_neighbours(values):
    empty = jnp.zeros((1,) + values.shape[1:], jnp.float32)
    return (
        jnp.concatenate([values[1:], empty], axis=0),
        jnp.concatenate([empty, values[:-1]], axis=0),
    )


def sources(density, energy_sum, first_sum, root_sum, radian_freq, wavenum, cosine, wind_speed):
    energy = energy_sum + EPSILON
    mean_sigma = energy / (first_sum + EPSILON)
    ratio_k = energy / (root_sum + EPSILON)
    mean_k = ratio_k * ratio_k
    steepness = energy * mean_k * mean_k / STEEP_REF
    decay_rate = WHITECAP * mean_sigma * (wavenum / mean_k) * steepness * steepness
    growth_rate = (
        WIND_COEF
        * radian_freq
        * jnp.maximum(28.0 * USTAR_RATIO * wind_speed * radian_freq / GRAVITY * cosine - 1.0, 0.0)
    )
    return density * (1.0 + growth_rate) / (1.0 + decay_rate)


def local_sources(point_block, wind_block, wind_angle, angles, dtheta):
    band_total = point_block.shape[0]
    band_ids = jnp.arange(band_total).astype(jnp.float32)
    radian_freq, wavenum, courant, turn_rate, band_spread = band_table(band_ids)
    scaled = point_block * (band_spread * dtheta)[:, None, None]
    energy_sum = jnp.sum(scaled, axis=(0, 1))
    first_sum = jnp.sum(scaled / radian_freq[:, None, None], axis=(0, 1))
    root_sum = jnp.sum(scaled / jnp.sqrt(wavenum)[:, None, None], axis=(0, 1))
    energy = energy_sum + EPSILON
    above, below = band_neighbours(point_block)
    delta = quad_delta(point_block, above, below, energy, 1)
    delta_above, delta_below = band_neighbours(delta)
    extra = quad_term(delta, delta_above, delta_below, 1)
    cosine = jnp.cos(angles[:, None] - wind_angle[None, :])
    return (
        sources(
            point_block,
            energy_sum,
            first_sum,
            root_sum,
            radian_freq[:, None, None],
            wavenum[:, None, None],
            cosine,
            wind_block,
        )
        + extra
    )


Y_GROUP = 4


def _z_exchange_kernel(z_count, point_ref, part_ref, lower_ref, upper_ref, gathered_ref,
                       halo_send, halo_recv, gather_send, gather_recv):
    geo = lax.axis_index("geo")
    z_pos = lax.axis_index("z")
    y_pos = lax.axis_index("y")
    group = point_ref.shape[0]
    barrier = pltpu.get_barrier_semaphore()
    for offset in range(1, z_count):
        target = lax.rem(z_pos + offset, z_count)
        pl.semaphore_signal(barrier, inc=1, device_id=(geo, target, y_pos),
                            device_id_type=pl.DeviceIdType.MESH)
    pl.semaphore_wait(barrier, z_count - 1)

    def halo_copy(src_lo, dst_ref, slot, target):
        return pltpu.make_async_remote_copy(
            src_ref=point_ref.at[pl.ds(src_lo, 2)],
            dst_ref=dst_ref,
            send_sem=halo_send.at[slot],
            recv_sem=halo_recv.at[slot],
            device_id=(geo, target, y_pos),
            device_id_type=pl.DeviceIdType.MESH,
        )

    up = halo_copy(group - 2, lower_ref, 0, z_pos + 1)
    down = halo_copy(0, upper_ref, 1, z_pos - 1)

    @pl.when(z_pos < z_count - 1)
    def _():
        up.start()

    @pl.when(z_pos > 0)
    def _():
        down.start()

    copies = []
    for offset in range(1, z_count):
        target = lax.rem(z_pos + offset, z_count)
        copy = pltpu.make_async_remote_copy(
            src_ref=part_ref,
            dst_ref=gathered_ref.at[z_pos],
            send_sem=gather_send.at[offset],
            recv_sem=gather_recv.at[offset],
            device_id=(geo, target, y_pos),
            device_id_type=pl.DeviceIdType.MESH,
        )
        copy.start()
        copies.append(copy)
    gathered_ref[z_pos] = part_ref[...]

    @pl.when(z_pos == 0)
    def _():
        lower_ref[...] = jnp.zeros(lower_ref.shape, lower_ref.dtype)

    @pl.when(z_pos == z_count - 1)
    def _():
        upper_ref[...] = jnp.zeros(upper_ref.shape, upper_ref.dtype)

    for copy in copies:
        copy.wait_send()
        copy.wait_recv()

    @pl.when(z_pos < z_count - 1)
    def _():
        up.wait_send()
        down.wait_recv()

    @pl.when(z_pos > 0)
    def _():
        down.wait_send()
        up.wait_recv()


def z_exchange(point, part, z_count):
    group, dirs, rows, cols = point.shape
    halo = jax.ShapeDtypeStruct((2, dirs, rows, cols), point.dtype)
    vmem = pl.BlockSpec(memory_space=pltpu.VMEM)
    return pl.pallas_call(
        functools.partial(_z_exchange_kernel, z_count),
        out_shape=(halo, halo, jax.ShapeDtypeStruct((z_count,) + part.shape, part.dtype)),
        in_specs=[vmem, vmem],
        out_specs=(vmem, vmem, vmem),
        scratch_shapes=[
            pltpu.SemaphoreType.DMA((2,)),
            pltpu.SemaphoreType.DMA((2,)),
            pltpu.SemaphoreType.DMA((z_count,)),
            pltpu.SemaphoreType.DMA((z_count,)),
        ],
        compiler_params=pltpu.CompilerParams(collective_id=0, has_side_effects=True),
    )(point, part)


def shards(spectrum, land_sea, sea_index, sea_count, wind_speed, wind_dir, slope_x, slope_y):
    local_bands, dir_count, row_count, col_count = spectrum.shape
    z_count = lax.axis_size("z")
    y_count = lax.axis_size("y")
    z_pos = lax.axis_index("z")
    y_pos = lax.axis_index("y")
    spec_pos = z_pos * y_count + y_pos
    dtheta = 2.0 * math.pi / dir_count
    angles = (jnp.arange(dir_count).astype(jnp.float32) + 0.5) * dtheta
    face_angles = jnp.arange(dir_count + 1).astype(jnp.float32) * dtheta
    band_ids = (spec_pos * local_bands + jnp.arange(local_bands)).astype(jnp.float32)
    radian_freq, wavenum, courant, turn_rate, band_spread = band_table(band_ids)
    wet_mask = land_sea.astype(jnp.float32)
    density = spectrum * wet_mask
    padded = extended(density, (("geo", 2),), 2)
    density = (
        advect(padded, (courant[:, None] * jnp.cos(angles)[None, :])[:, :, None, None], 2)
        * wet_mask
    )
    padded = jnp.pad(density, ((0, 0), (0, 0), (0, 0), (2, 2)))
    density = (
        advect(padded, (courant[:, None] * jnp.sin(angles)[None, :])[:, :, None, None], 3)
        * wet_mask
    )
    turning = turn_rate[:, None, None, None] * (
        jnp.sin(face_angles)[None, :, None, None] * slope_x
        - jnp.cos(face_angles)[None, :, None, None] * slope_y
    )
    padded = jnp.concatenate([density[:, -2:], density, density[:, :2]], axis=1)
    floored = jnp.maximum(advect(padded, turning, 1), 0.0)
    y_count = lax.axis_size("y")
    quarters = jnp.transpose(
        floored[0].reshape(dir_count, y_count, row_count // y_count, col_count), (1, 0, 2, 3)
    )
    point = lax.all_to_all(quarters, "y", split_axis=0, concat_axis=0, tiled=True)
    group = point.shape[0]
    part_rows = point.shape[2]
    group_ids = (z_pos * group + jnp.arange(group)).astype(jnp.float32)
    radian_freq, wavenum, courant, turn_rate, band_spread = band_table(group_ids)
    scaled = point * (band_spread * dtheta)[:, None, None, None]
    sums = jnp.stack(
        [
            jnp.sum(scaled, axis=(0, 1)),
            jnp.sum(scaled / radian_freq[:, None, None, None], axis=(0, 1)),
            jnp.sum(scaled / jnp.sqrt(wavenum)[:, None, None, None], axis=(0, 1)),
        ]
    )
    lower, upper, paired = z_halo(point, sums, z_count)
    sums = sums + paired
    step = 2
    while step < z_count:
        sums = sums + lax.ppermute(sums, "z", [(i, i ^ step) for i in range(z_count)])
        step *= 2
    energy_sum, first_sum, root_sum = sums[0], sums[1], sums[2]
    energy = energy_sum + EPSILON
    ext = jnp.concatenate([lower, point, upper], axis=0)
    center, plus, minus = ext[1:-1], jnp.roll(ext[2:], -1, axis=1), jnp.roll(ext[:-2], 3, axis=1)
    cubic = center * center * (plus + minus) - 2.0 * center * plus * minus
    extra = (
        -2.0 * cubic[1:-1] + jnp.roll(cubic[:-2], 1, axis=1) + jnp.roll(cubic[2:], -3, axis=1)
    ) * (QUAD_COEF / (energy * energy))
    row_start = y_pos * part_rows
    wind_block = lax.dynamic_slice_in_dim(wind_speed, row_start, part_rows, axis=0)
    wind_angle = lax.dynamic_slice_in_dim(wind_dir, row_start, part_rows, axis=0)
    wet_block = lax.dynamic_slice_in_dim(wet_mask, row_start, part_rows, axis=0)
    cosine = jnp.cos(angles[:, None, None] - wind_angle[None])
    updated = (
        sources(
            point,
            energy_sum,
            first_sum,
            root_sum,
            radian_freq[:, None, None, None],
            wavenum[:, None, None, None],
            cosine,
            wind_block,
        )
        + extra
    ) * wet_block
    return lax.all_to_all(updated, "y", split_axis=0, concat_axis=2, tiled=True)


def solution(mesh):
    geo_count = mesh.shape["geo"]
    spec_count = mesh.shape["spec"]
    local = jax.sharding.Mesh(
        mesh.devices.reshape(geo_count, spec_count // Y_GROUP, Y_GROUP), ("geo", "z", "y")
    )
    spec = ("z", "y")
    placed = (
        P(spec, None, "geo", None),
        P("geo", None),
        P("geo", None),
        P("geo"),
        P("geo", None),
        P("geo", None),
        P("geo", None),
        P("geo", None),
    )
    return jax.shard_map(
        shards, mesh=local, in_specs=placed, out_specs=P(spec, None, "geo", None), check_vma=False
    )
```

```python
import functools
import math

import jax
import jax.numpy as jnp
from jax import lax
from jax.experimental import pallas as pl
from jax.experimental.pallas import tpu as pltpu
from jax.sharding import PartitionSpec as P

GRAVITY = 9.81
BASE_FREQ = 0.035
GROWTH = 1.1
COURANT_TOP = 0.9
TURN_TOP = 1.2
SPACING = 0.1
USTAR_RATIO = 0.035
WIND_COEF = 0.0375
WHITECAP = 0.36
STEEP_REF = 1.6
EPSILON = 1e-06
QUAD_COEF = 100.0


def extended(cells, sides, width):
    for axis, dim in sides:
        count = lax.axis_size(axis)
        ends = count - 1
        head = lax.slice_in_dim(cells, 0, width, axis=dim)
        tail = lax.slice_in_dim(cells, cells.shape[dim] - width, cells.shape[dim], axis=dim)
        cells = jnp.concatenate(
            [
                lax.ppermute(tail, axis, [(i, (i + 1) % count) for i in range(ends)]),
                cells,
                lax.ppermute(head, axis, [((i + 1) % count, i) for i in range(ends)]),
            ],
            axis=dim,
        )
    return cells


def band_table(band_ids):
    growth_factor = jnp.power(GROWTH, band_ids)
    radian_freq = 2.0 * math.pi * BASE_FREQ * growth_factor
    wavenum = radian_freq * radian_freq / GRAVITY
    return (
        radian_freq,
        wavenum,
        COURANT_TOP / growth_factor,
        TURN_TOP / growth_factor,
        SPACING * radian_freq,
    )


def quick_flux(far_left, near_left, near_right, far_right, courant):
    forward = courant >= 0
    upwind = jnp.where(forward, far_left, far_right)
    center = jnp.where(forward, near_left, near_right)
    downwind = jnp.where(forward, near_right, near_left)
    face_value = (
        0.5 * (center + downwind)
        - 0.5 * jnp.abs(courant) * (downwind - center)
        - (1.0 - courant * courant) / 6.0 * (downwind - 2.0 * center + upwind)
    )
    return courant * face_value


def advect(padded, courant, along):
    face_count = padded.shape[along] - 4
    shifted = [
        lax.slice_in_dim(padded, offset, offset + face_count + 1, axis=along) for offset in range(4)
    ]
    face_flux = quick_flux(shifted[0], shifted[1], shifted[2], shifted[3], courant)
    centre_cells = lax.slice_in_dim(padded, 2, 2 + face_count, axis=along)
    upper_flux = lax.slice_in_dim(face_flux, 1, face_count + 1, axis=along)
    lower_flux = lax.slice_in_dim(face_flux, 0, face_count, axis=along)
    return centre_cells - (upper_flux - lower_flux)


def quad_delta(center, above, below, energy, dir_axis):
    plus = jnp.roll(above, -1, axis=dir_axis)
    minus = jnp.roll(below, 3, axis=dir_axis)
    return (
        QUAD_COEF
        * (center * center * (plus + minus) - 2.0 * center * plus * minus)
        / (energy * energy)
    )


def quad_term(delta, delta_above, delta_below, dir_axis):
    return (
        -2.0 * delta
        + jnp.roll(delta_below, 1, axis=dir_axis)
        + jnp.roll(delta_above, -3, axis=dir_axis)
    )


def band_neighbours(values):
    empty = jnp.zeros((1,) + values.shape[1:], jnp.float32)
    return (
        jnp.concatenate([values[1:], empty], axis=0),
        jnp.concatenate([empty, values[:-1]], axis=0),
    )


def sources(density, energy_sum, first_sum, root_sum, radian_freq, wavenum, cosine, wind_speed):
    energy = energy_sum + EPSILON
    mean_sigma = energy / (first_sum + EPSILON)
    ratio_k = energy / (root_sum + EPSILON)
    mean_k = ratio_k * ratio_k
    steepness = energy * mean_k * mean_k / STEEP_REF
    decay_rate = WHITECAP * mean_sigma * (wavenum / mean_k) * steepness * steepness
    growth_rate = (
        WIND_COEF
        * radian_freq
        * jnp.maximum(28.0 * USTAR_RATIO * wind_speed * radian_freq / GRAVITY * cosine - 1.0, 0.0)
    )
    return density * (1.0 + growth_rate) / (1.0 + decay_rate)


def local_sources(point_block, wind_block, wind_angle, angles, dtheta):
    band_total = point_block.shape[0]
    band_ids = jnp.arange(band_total).astype(jnp.float32)
    radian_freq, wavenum, courant, turn_rate, band_spread = band_table(band_ids)
    scaled = point_block * (band_spread * dtheta)[:, None, None]
    energy_sum = jnp.sum(scaled, axis=(0, 1))
    first_sum = jnp.sum(scaled / radian_freq[:, None, None], axis=(0, 1))
    root_sum = jnp.sum(scaled / jnp.sqrt(wavenum)[:, None, None], axis=(0, 1))
    energy = energy_sum + EPSILON
    above, below = band_neighbours(point_block)
    delta = quad_delta(point_block, above, below, energy, 1)
    delta_above, delta_below = band_neighbours(delta)
    extra = quad_term(delta, delta_above, delta_below, 1)
    cosine = jnp.cos(angles[:, None] - wind_angle[None, :])
    return (
        sources(
            point_block,
            energy_sum,
            first_sum,
            root_sum,
            radian_freq[:, None, None],
            wavenum[:, None, None],
            cosine,
            wind_block,
        )
        + extra
    )


Y_GROUP = 4
HALO = 2


def _z_halo_kernel(z_count, point_ref, sums_ref, lower_ref, upper_ref, pair_ref, halo_send, halo_recv,
                   pair_send, pair_recv):
    geo = lax.axis_index("geo")
    z_pos = lax.axis_index("z")
    y_pos = lax.axis_index("y")
    group = point_ref.shape[0]
    mesh_id = pl.DeviceIdType.MESH
    barrier = pltpu.get_barrier_semaphore()
    pair_bit = lax.rem(z_pos, 2)
    quad_bit = lax.rem(z_pos // 2, 2)
    partners = [
        z_pos + 1 - 2 * pair_bit,
        z_pos + 2 - 4 * quad_bit,
        z_pos + 1 - 2 * pair_bit + 2 - 4 * quad_bit,
    ]
    for target in [lax.rem(z_pos + 1, z_count), lax.rem(z_pos + z_count - 1, z_count)] + partners[1:]:
        pl.semaphore_signal(barrier, inc=1, device_id=(geo, target, y_pos), device_id_type=mesh_id)
    pl.semaphore_wait(barrier, 4)

    def halo_copy(src_lo, dst_ref, slot, target):
        return pltpu.make_async_remote_copy(
            src_ref=point_ref.at[pl.ds(src_lo, HALO)],
            dst_ref=dst_ref,
            send_sem=halo_send.at[slot],
            recv_sem=halo_recv.at[slot],
            device_id=(geo, target, y_pos),
            device_id_type=mesh_id,
        )

    up = halo_copy(group - HALO, lower_ref, 0, lax.rem(z_pos + 1, z_count))
    down = halo_copy(0, upper_ref, 1, lax.rem(z_pos + z_count - 1, z_count))

    pairs = []
    for index, partner in enumerate(partners):
        pair = pltpu.make_async_remote_copy(
            src_ref=sums_ref,
            dst_ref=pair_ref.at[index],
            send_sem=pair_send.at[index],
            recv_sem=pair_recv.at[index],
            device_id=(geo, partner, y_pos),
            device_id_type=mesh_id,
        )
        pair.start()
        pairs.append(pair)

    @pl.when(z_pos < z_count - 1)
    def _():
        up.start()

    @pl.when(z_pos > 0)
    def _():
        down.start()

    @pl.when(z_pos == 0)
    def _():
        lower_ref[...] = jnp.zeros(lower_ref.shape, lower_ref.dtype)

    @pl.when(z_pos == z_count - 1)
    def _():
        upper_ref[...] = jnp.zeros(upper_ref.shape, upper_ref.dtype)

    for pair in pairs:
        pair.wait_send()
        pair.wait_recv()

    @pl.when(z_pos < z_count - 1)
    def _():
        up.wait_send()
        down.wait_recv()

    @pl.when(z_pos > 0)
    def _():
        down.wait_send()
        up.wait_recv()


def z_halo(point, sums, z_count):
    group, dirs, rows, cols = point.shape
    halo = jax.ShapeDtypeStruct((HALO, dirs, rows, cols), point.dtype)
    vmem = pl.BlockSpec(memory_space=pltpu.VMEM)
    hbm = pl.BlockSpec(memory_space=pl.ANY)
    return pl.pallas_call(
        functools.partial(_z_halo_kernel, z_count),
        out_shape=(halo, halo, jax.ShapeDtypeStruct((3,) + sums.shape, sums.dtype)),
        in_specs=[hbm, hbm],
        out_specs=(vmem, vmem, vmem),
        scratch_shapes=[
            pltpu.SemaphoreType.DMA((2,)),
            pltpu.SemaphoreType.DMA((2,)),
            pltpu.SemaphoreType.DMA((3,)),
            pltpu.SemaphoreType.DMA((3,)),
        ],
        compiler_params=pltpu.CompilerParams(collective_id=0, has_side_effects=True),
    )(point, sums)


def extended(cells, sides, width):
    for axis, dim in sides:
        count = lax.axis_size(axis)
        ends = count - 1
        head = lax.slice_in_dim(cells, 0, width, axis=dim)
        tail = lax.slice_in_dim(cells, cells.shape[dim] - width, cells.shape[dim], axis=dim)
        cells = jnp.concatenate(
            [
                lax.ppermute(tail, axis, [(i, (i + 1) % count) for i in range(ends)]),
                cells,
                lax.ppermute(head, axis, [((i + 1) % count, i) for i in range(ends)]),
            ],
            axis=dim,
        )
    return cells


def band_table(band_ids):
    growth_factor = jnp.power(GROWTH, band_ids)
    radian_freq = 2.0 * math.pi * BASE_FREQ * growth_factor
    wavenum = radian_freq * radian_freq / GRAVITY
    return (
        radian_freq,
        wavenum,
        COURANT_TOP / growth_factor,
        TURN_TOP / growth_factor,
        SPACING * radian_freq,
    )


def quick_flux(far_left, near_left, near_right, far_right, courant):
    forward = courant >= 0
    upwind = jnp.where(forward, far_left, far_right)
    center = jnp.where(forward, near_left, near_right)
    downwind = jnp.where(forward, near_right, near_left)
    face_value = (
        0.5 * (center + downwind)
        - 0.5 * jnp.abs(courant) * (downwind - center)
        - (1.0 - courant * courant) / 6.0 * (downwind - 2.0 * center + upwind)
    )
    return courant * face_value


def advect(padded, courant, along):
    face_count = padded.shape[along] - 4
    shifted = [
        lax.slice_in_dim(padded, offset, offset + face_count + 1, axis=along) for offset in range(4)
    ]
    face_flux = quick_flux(shifted[0], shifted[1], shifted[2], shifted[3], courant)
    centre_cells = lax.slice_in_dim(padded, 2, 2 + face_count, axis=along)
    upper_flux = lax.slice_in_dim(face_flux, 1, face_count + 1, axis=along)
    lower_flux = lax.slice_in_dim(face_flux, 0, face_count, axis=along)
    return centre_cells - (upper_flux - lower_flux)


def quad_delta(center, above, below, energy, dir_axis):
    plus = jnp.roll(above, -1, axis=dir_axis)
    minus = jnp.roll(below, 3, axis=dir_axis)
    return (
        QUAD_COEF
        * (center * center * (plus + minus) - 2.0 * center * plus * minus)
        / (energy * energy)
    )


def quad_term(delta, delta_above, delta_below, dir_axis):
    return (
        -2.0 * delta
        + jnp.roll(delta_below, 1, axis=dir_axis)
        + jnp.roll(delta_above, -3, axis=dir_axis)
    )


def band_neighbours(values):
    empty = jnp.zeros((1,) + values.shape[1:], jnp.float32)
    return (
        jnp.concatenate([values[1:], empty], axis=0),
        jnp.concatenate([empty, values[:-1]], axis=0),
    )


def sources(density, energy_sum, first_sum, root_sum, radian_freq, wavenum, cosine, wind_speed):
    energy = energy_sum + EPSILON
    mean_sigma = energy / (first_sum + EPSILON)
    ratio_k = energy / (root_sum + EPSILON)
    mean_k = ratio_k * ratio_k
    steepness = energy * mean_k * mean_k / STEEP_REF
    decay_rate = WHITECAP * mean_sigma * (wavenum / mean_k) * steepness * steepness
    growth_rate = (
        WIND_COEF
        * radian_freq
        * jnp.maximum(28.0 * USTAR_RATIO * wind_speed * radian_freq / GRAVITY * cosine - 1.0, 0.0)
    )
    return density * (1.0 + growth_rate) / (1.0 + decay_rate)


def local_sources(point_block, wind_block, wind_angle, angles, dtheta):
    band_total = point_block.shape[0]
    band_ids = jnp.arange(band_total).astype(jnp.float32)
    radian_freq, wavenum, courant, turn_rate, band_spread = band_table(band_ids)
    scaled = point_block * (band_spread * dtheta)[:, None, None]
    energy_sum = jnp.sum(scaled, axis=(0, 1))
    first_sum = jnp.sum(scaled / radian_freq[:, None, None], axis=(0, 1))
    root_sum = jnp.sum(scaled / jnp.sqrt(wavenum)[:, None, None], axis=(0, 1))
    energy = energy_sum + EPSILON
    above, below = band_neighbours(point_block)
    delta = quad_delta(point_block, above, below, energy, 1)
    delta_above, delta_below = band_neighbours(delta)
    extra = quad_term(delta, delta_above, delta_below, 1)
    cosine = jnp.cos(angles[:, None] - wind_angle[None, :])
    return (
        sources(
            point_block,
            energy_sum,
            first_sum,
            root_sum,
            radian_freq[:, None, None],
            wavenum[:, None, None],
            cosine,
            wind_block,
        )
        + extra
    )


Y_GROUP = 4


def _z_exchange_kernel(z_count, point_ref, part_ref, lower_ref, upper_ref, gathered_ref,
                       halo_send, halo_recv, gather_send, gather_recv):
    geo = lax.axis_index("geo")
    z_pos = lax.axis_index("z")
    y_pos = lax.axis_index("y")
    group = point_ref.shape[0]
    barrier = pltpu.get_barrier_semaphore()
    for offset in range(1, z_count):
        target = lax.rem(z_pos + offset, z_count)
        pl.semaphore_signal(barrier, inc=1, device_id=(geo, target, y_pos),
                            device_id_type=pl.DeviceIdType.MESH)
    pl.semaphore_wait(barrier, z_count - 1)

    def halo_copy(src_lo, dst_ref, slot, target):
        return pltpu.make_async_remote_copy(
            src_ref=point_ref.at[pl.ds(src_lo, 2)],
            dst_ref=dst_ref,
            send_sem=halo_send.at[slot],
            recv_sem=halo_recv.at[slot],
            device_id=(geo, target, y_pos),
            device_id_type=pl.DeviceIdType.MESH,
        )

    up = halo_copy(group - 2, lower_ref, 0, z_pos + 1)
    down = halo_copy(0, upper_ref, 1, z_pos - 1)

    @pl.when(z_pos < z_count - 1)
    def _():
        up.start()

    @pl.when(z_pos > 0)
    def _():
        down.start()

    copies = []
    for offset in range(1, z_count):
        target = lax.rem(z_pos + offset, z_count)
        copy = pltpu.make_async_remote_copy(
            src_ref=part_ref,
            dst_ref=gathered_ref.at[z_pos],
            send_sem=gather_send.at[offset],
            recv_sem=gather_recv.at[offset],
            device_id=(geo, target, y_pos),
            device_id_type=pl.DeviceIdType.MESH,
        )
        copy.start()
        copies.append(copy)
    gathered_ref[z_pos] = part_ref[...]

    @pl.when(z_pos == 0)
    def _():
        lower_ref[...] = jnp.zeros(lower_ref.shape, lower_ref.dtype)

    @pl.when(z_pos == z_count - 1)
    def _():
        upper_ref[...] = jnp.zeros(upper_ref.shape, upper_ref.dtype)

    for copy in copies:
        copy.wait_send()
        copy.wait_recv()

    @pl.when(z_pos < z_count - 1)
    def _():
        up.wait_send()
        down.wait_recv()

    @pl.when(z_pos > 0)
    def _():
        down.wait_send()
        up.wait_recv()


def z_exchange(point, part, z_count):
    group, dirs, rows, cols = point.shape
    halo = jax.ShapeDtypeStruct((2, dirs, rows, cols), point.dtype)
    vmem = pl.BlockSpec(memory_space=pltpu.VMEM)
    return pl.pallas_call(
        functools.partial(_z_exchange_kernel, z_count),
        out_shape=(halo, halo, jax.ShapeDtypeStruct((z_count,) + part.shape, part.dtype)),
        in_specs=[vmem, vmem],
        out_specs=(vmem, vmem, vmem),
        scratch_shapes=[
            pltpu.SemaphoreType.DMA((2,)),
            pltpu.SemaphoreType.DMA((2,)),
            pltpu.SemaphoreType.DMA((z_count,)),
            pltpu.SemaphoreType.DMA((z_count,)),
        ],
        compiler_params=pltpu.CompilerParams(collective_id=0, has_side_effects=True),
    )(point, part)


def shards(spectrum, land_sea, sea_index, sea_count, wind_speed, wind_dir, slope_x, slope_y):
    local_bands, dir_count, row_count, col_count = spectrum.shape
    z_count = lax.axis_size("z")
    y_count = lax.axis_size("y")
    z_pos = lax.axis_index("z")
    y_pos = lax.axis_index("y")
    spec_pos = z_pos * y_count + y_pos
    dtheta = 2.0 * math.pi / dir_count
    angles = (jnp.arange(dir_count).astype(jnp.float32) + 0.5) * dtheta
    face_angles = jnp.arange(dir_count + 1).astype(jnp.float32) * dtheta
    band_ids = (spec_pos * local_bands + jnp.arange(local_bands)).astype(jnp.float32)
    radian_freq, wavenum, courant, turn_rate, band_spread = band_table(band_ids)
    wet_mask = land_sea.astype(jnp.float32)
    density = spectrum * wet_mask
    padded = extended(density, (("geo", 2),), 2)
    density = (
        advect(padded, (courant[:, None] * jnp.cos(angles)[None, :])[:, :, None, None], 2)
        * wet_mask
    )
    padded = jnp.pad(density, ((0, 0), (0, 0), (0, 0), (2, 2)))
    density = (
        advect(padded, (courant[:, None] * jnp.sin(angles)[None, :])[:, :, None, None], 3)
        * wet_mask
    )
    turning = turn_rate[:, None, None, None] * (
        jnp.sin(face_angles)[None, :, None, None] * slope_x
        - jnp.cos(face_angles)[None, :, None, None] * slope_y
    )
    padded = jnp.concatenate([density[:, -2:], density, density[:, :2]], axis=1)
    floored = jnp.maximum(advect(padded, turning, 1), 0.0)
    y_count = lax.axis_size("y")
    quarters = jnp.transpose(
        floored[0].reshape(dir_count, y_count, row_count // y_count, col_count), (1, 0, 2, 3)
    )
    point = lax.all_to_all(quarters, "y", split_axis=0, concat_axis=0, tiled=True)
    group = point.shape[0]
    part_rows = point.shape[2]
    group_ids = (z_pos * group + jnp.arange(group)).astype(jnp.float32)
    radian_freq, wavenum, courant, turn_rate, band_spread = band_table(group_ids)
    scaled = point * (band_spread * dtheta)[:, None, None, None]
    sums = jnp.stack(
        [
            jnp.sum(scaled, axis=(0, 1)),
            jnp.sum(scaled / radian_freq[:, None, None, None], axis=(0, 1)),
            jnp.sum(scaled / jnp.sqrt(wavenum)[:, None, None, None], axis=(0, 1)),
        ]
    )
    lower, upper, paired = z_halo(point, sums, z_count)
    sums = sums + jnp.sum(paired, axis=0)
    step = 4
    while step < z_count:
        sums = sums + lax.ppermute(sums, "z", [(i, i ^ step) for i in range(z_count)])
        step *= 2
    energy_sum, first_sum, root_sum = sums[0], sums[1], sums[2]
    energy = energy_sum + EPSILON
    ext = jnp.concatenate([lower, point, upper], axis=0)
    center, plus, minus = ext[1:-1], jnp.roll(ext[2:], -1, axis=1), jnp.roll(ext[:-2], 3, axis=1)
    cubic = center * center * (plus + minus) - 2.0 * center * plus * minus
    extra = (
        -2.0 * cubic[1:-1] + jnp.roll(cubic[:-2], 1, axis=1) + jnp.roll(cubic[2:], -3, axis=1)
    ) * (QUAD_COEF / (energy * energy))
    row_start = y_pos * part_rows
    wind_block = lax.dynamic_slice_in_dim(wind_speed, row_start, part_rows, axis=0)
    wind_angle = lax.dynamic_slice_in_dim(wind_dir, row_start, part_rows, axis=0)
    wet_block = lax.dynamic_slice_in_dim(wet_mask, row_start, part_rows, axis=0)
    cosine = jnp.cos(angles[:, None, None] - wind_angle[None])
    updated = (
        sources(
            point,
            energy_sum,
            first_sum,
            root_sum,
            radian_freq[:, None, None, None],
            wavenum[:, None, None, None],
            cosine,
            wind_block,
        )
        + extra
    ) * wet_block
    return lax.all_to_all(updated, "y", split_axis=0, concat_axis=2, tiled=True)


def solution(mesh):
    geo_count = mesh.shape["geo"]
    spec_count = mesh.shape["spec"]
    local = jax.sharding.Mesh(
        mesh.devices.reshape(geo_count, spec_count // Y_GROUP, Y_GROUP), ("geo", "z", "y")
    )
    spec = ("z", "y")
    placed = (
        P(spec, None, "geo", None),
        P("geo", None),
        P("geo", None),
        P("geo"),
        P("geo", None),
        P("geo", None),
        P("geo", None),
        P("geo", None),
    )
    return jax.shard_map(
        shards, mesh=local, in_specs=placed, out_specs=P(spec, None, "geo", None), check_vma=False
    )
```

```python
import functools
import math

import jax
import jax.numpy as jnp
from jax import lax
from jax.experimental import pallas as pl
from jax.experimental.pallas import tpu as pltpu
from jax.sharding import PartitionSpec as P

GRAVITY = 9.81
BASE_FREQ = 0.035
GROWTH = 1.1
COURANT_TOP = 0.9
TURN_TOP = 1.2
SPACING = 0.1
USTAR_RATIO = 0.035
WIND_COEF = 0.0375
WHITECAP = 0.36
STEEP_REF = 1.6
EPSILON = 1e-06
QUAD_COEF = 100.0


def extended(cells, sides, width):
    for axis, dim in sides:
        count = lax.axis_size(axis)
        ends = count - 1
        head = lax.slice_in_dim(cells, 0, width, axis=dim)
        tail = lax.slice_in_dim(cells, cells.shape[dim] - width, cells.shape[dim], axis=dim)
        cells = jnp.concatenate(
            [
                lax.ppermute(tail, axis, [(i, (i + 1) % count) for i in range(ends)]),
                cells,
                lax.ppermute(head, axis, [((i + 1) % count, i) for i in range(ends)]),
            ],
            axis=dim,
        )
    return cells


def band_table(band_ids):
    growth_factor = jnp.power(GROWTH, band_ids)
    radian_freq = 2.0 * math.pi * BASE_FREQ * growth_factor
    wavenum = radian_freq * radian_freq / GRAVITY
    return (
        radian_freq,
        wavenum,
        COURANT_TOP / growth_factor,
        TURN_TOP / growth_factor,
        SPACING * radian_freq,
    )


def quick_flux(far_left, near_left, near_right, far_right, courant):
    forward = courant >= 0
    upwind = jnp.where(forward, far_left, far_right)
    center = jnp.where(forward, near_left, near_right)
    downwind = jnp.where(forward, near_right, near_left)
    face_value = (
        0.5 * (center + downwind)
        - 0.5 * jnp.abs(courant) * (downwind - center)
        - (1.0 - courant * courant) / 6.0 * (downwind - 2.0 * center + upwind)
    )
    return courant * face_value


def advect(padded, courant, along):
    face_count = padded.shape[along] - 4
    shifted = [
        lax.slice_in_dim(padded, offset, offset + face_count + 1, axis=along) for offset in range(4)
    ]
    face_flux = quick_flux(shifted[0], shifted[1], shifted[2], shifted[3], courant)
    centre_cells = lax.slice_in_dim(padded, 2, 2 + face_count, axis=along)
    upper_flux = lax.slice_in_dim(face_flux, 1, face_count + 1, axis=along)
    lower_flux = lax.slice_in_dim(face_flux, 0, face_count, axis=along)
    return centre_cells - (upper_flux - lower_flux)


def quad_delta(center, above, below, energy, dir_axis):
    plus = jnp.roll(above, -1, axis=dir_axis)
    minus = jnp.roll(below, 3, axis=dir_axis)
    return (
        QUAD_COEF
        * (center * center * (plus + minus) - 2.0 * center * plus * minus)
        / (energy * energy)
    )


def quad_term(delta, delta_above, delta_below, dir_axis):
    return (
        -2.0 * delta
        + jnp.roll(delta_below, 1, axis=dir_axis)
        + jnp.roll(delta_above, -3, axis=dir_axis)
    )


def band_neighbours(values):
    empty = jnp.zeros((1,) + values.shape[1:], jnp.float32)
    return (
        jnp.concatenate([values[1:], empty], axis=0),
        jnp.concatenate([empty, values[:-1]], axis=0),
    )


def sources(density, energy_sum, first_sum, root_sum, radian_freq, wavenum, cosine, wind_speed):
    energy = energy_sum + EPSILON
    mean_sigma = energy / (first_sum + EPSILON)
    ratio_k = energy / (root_sum + EPSILON)
    mean_k = ratio_k * ratio_k
    steepness = energy * mean_k * mean_k / STEEP_REF
    decay_rate = WHITECAP * mean_sigma * (wavenum / mean_k) * steepness * steepness
    growth_rate = (
        WIND_COEF
        * radian_freq
        * jnp.maximum(28.0 * USTAR_RATIO * wind_speed * radian_freq / GRAVITY * cosine - 1.0, 0.0)
    )
    return density * (1.0 + growth_rate) / (1.0 + decay_rate)


def local_sources(point_block, wind_block, wind_angle, angles, dtheta):
    band_total = point_block.shape[0]
    band_ids = jnp.arange(band_total).astype(jnp.float32)
    radian_freq, wavenum, courant, turn_rate, band_spread = band_table(band_ids)
    scaled = point_block * (band_spread * dtheta)[:, None, None]
    energy_sum = jnp.sum(scaled, axis=(0, 1))
    first_sum = jnp.sum(scaled / radian_freq[:, None, None], axis=(0, 1))
    root_sum = jnp.sum(scaled / jnp.sqrt(wavenum)[:, None, None], axis=(0, 1))
    energy = energy_sum + EPSILON
    above, below = band_neighbours(point_block)
    delta = quad_delta(point_block, above, below, energy, 1)
    delta_above, delta_below = band_neighbours(delta)
    extra = quad_term(delta, delta_above, delta_below, 1)
    cosine = jnp.cos(angles[:, None] - wind_angle[None, :])
    return (
        sources(
            point_block,
            energy_sum,
            first_sum,
            root_sum,
            radian_freq[:, None, None],
            wavenum[:, None, None],
            cosine,
            wind_block,
        )
        + extra
    )


Y_GROUP = 4
HALO = 2


def _z_halo_kernel(z_count, point_ref, lower_ref, upper_ref, halo_send, halo_recv):
    geo = lax.axis_index("geo")
    z_pos = lax.axis_index("z")
    y_pos = lax.axis_index("y")
    group = point_ref.shape[0]
    mesh_id = pl.DeviceIdType.MESH
    barrier = pltpu.get_barrier_semaphore()
    for step in (1, z_count - 1):
        pl.semaphore_signal(barrier, inc=1, device_id=(geo, lax.rem(z_pos + step, z_count), y_pos),
                            device_id_type=mesh_id)
    pl.semaphore_wait(barrier, 2)

    def halo_copy(src_lo, dst_ref, slot, target):
        return pltpu.make_async_remote_copy(
            src_ref=point_ref.at[pl.ds(src_lo, HALO)],
            dst_ref=dst_ref,
            send_sem=halo_send.at[slot],
            recv_sem=halo_recv.at[slot],
            device_id=(geo, target, y_pos),
            device_id_type=mesh_id,
        )

    up = halo_copy(group - HALO, lower_ref, 0, lax.rem(z_pos + 1, z_count))
    down = halo_copy(0, upper_ref, 1, lax.rem(z_pos + z_count - 1, z_count))

    @pl.when(z_pos < z_count - 1)
    def _():
        up.start()

    @pl.when(z_pos > 0)
    def _():
        down.start()

    @pl.when(z_pos == 0)
    def _():
        lower_ref[...] = jnp.zeros(lower_ref.shape, lower_ref.dtype)

    @pl.when(z_pos == z_count - 1)
    def _():
        upper_ref[...] = jnp.zeros(upper_ref.shape, upper_ref.dtype)

    @pl.when(z_pos < z_count - 1)
    def _():
        up.wait_send()
        down.wait_recv()

    @pl.when(z_pos > 0)
    def _():
        down.wait_send()
        up.wait_recv()


def z_halo(point, z_count):
    group, dirs, rows, cols = point.shape
    halo = jax.ShapeDtypeStruct((HALO, dirs, rows, cols), point.dtype)
    vmem = pl.BlockSpec(memory_space=pltpu.VMEM)
    return pl.pallas_call(
        functools.partial(_z_halo_kernel, z_count),
        out_shape=(halo, halo),
        in_specs=[pl.BlockSpec(memory_space=pl.ANY)],
        out_specs=(vmem, vmem),
        scratch_shapes=[
            pltpu.SemaphoreType.DMA((2,)),
            pltpu.SemaphoreType.DMA((2,)),
        ],
        compiler_params=pltpu.CompilerParams(collective_id=0, has_side_effects=True),
    )(point)


def extended(cells, sides, width):
    for axis, dim in sides:
        count = lax.axis_size(axis)
        ends = count - 1
        head = lax.slice_in_dim(cells, 0, width, axis=dim)
        tail = lax.slice_in_dim(cells, cells.shape[dim] - width, cells.shape[dim], axis=dim)
        cells = jnp.concatenate(
            [
                lax.ppermute(tail, axis, [(i, (i + 1) % count) for i in range(ends)]),
                cells,
                lax.ppermute(head, axis, [((i + 1) % count, i) for i in range(ends)]),
            ],
            axis=dim,
        )
    return cells


def band_table(band_ids):
    growth_factor = jnp.power(GROWTH, band_ids)
    radian_freq = 2.0 * math.pi * BASE_FREQ * growth_factor
    wavenum = radian_freq * radian_freq / GRAVITY
    return (
        radian_freq,
        wavenum,
        COURANT_TOP / growth_factor,
        TURN_TOP / growth_factor,
        SPACING * radian_freq,
    )


def quick_flux(far_left, near_left, near_right, far_right, courant):
    forward = courant >= 0
    upwind = jnp.where(forward, far_left, far_right)
    center = jnp.where(forward, near_left, near_right)
    downwind = jnp.where(forward, near_right, near_left)
    face_value = (
        0.5 * (center + downwind)
        - 0.5 * jnp.abs(courant) * (downwind - center)
        - (1.0 - courant * courant) / 6.0 * (downwind - 2.0 * center + upwind)
    )
    return courant * face_value


def advect(padded, courant, along):
    face_count = padded.shape[along] - 4
    shifted = [
        lax.slice_in_dim(padded, offset, offset + face_count + 1, axis=along) for offset in range(4)
    ]
    face_flux = quick_flux(shifted[0], shifted[1], shifted[2], shifted[3], courant)
    centre_cells = lax.slice_in_dim(padded, 2, 2 + face_count, axis=along)
    upper_flux = lax.slice_in_dim(face_flux, 1, face_count + 1, axis=along)
    lower_flux = lax.slice_in_dim(face_flux, 0, face_count, axis=along)
    return centre_cells - (upper_flux - lower_flux)


def quad_delta(center, above, below, energy, dir_axis):
    plus = jnp.roll(above, -1, axis=dir_axis)
    minus = jnp.roll(below, 3, axis=dir_axis)
    return (
        QUAD_COEF
        * (center * center * (plus + minus) - 2.0 * center * plus * minus)
        / (energy * energy)
    )


def quad_term(delta, delta_above, delta_below, dir_axis):
    return (
        -2.0 * delta
        + jnp.roll(delta_below, 1, axis=dir_axis)
        + jnp.roll(delta_above, -3, axis=dir_axis)
    )


def band_neighbours(values):
    empty = jnp.zeros((1,) + values.shape[1:], jnp.float32)
    return (
        jnp.concatenate([values[1:], empty], axis=0),
        jnp.concatenate([empty, values[:-1]], axis=0),
    )


def sources(density, energy_sum, first_sum, root_sum, radian_freq, wavenum, cosine, wind_speed):
    energy = energy_sum + EPSILON
    mean_sigma = energy / (first_sum + EPSILON)
    ratio_k = energy / (root_sum + EPSILON)
    mean_k = ratio_k * ratio_k
    steepness = energy * mean_k * mean_k / STEEP_REF
    decay_rate = WHITECAP * mean_sigma * (wavenum / mean_k) * steepness * steepness
    growth_rate = (
        WIND_COEF
        * radian_freq
        * jnp.maximum(28.0 * USTAR_RATIO * wind_speed * radian_freq / GRAVITY * cosine - 1.0, 0.0)
    )
    return density * (1.0 + growth_rate) / (1.0 + decay_rate)


def local_sources(point_block, wind_block, wind_angle, angles, dtheta):
    band_total = point_block.shape[0]
    band_ids = jnp.arange(band_total).astype(jnp.float32)
    radian_freq, wavenum, courant, turn_rate, band_spread = band_table(band_ids)
    scaled = point_block * (band_spread * dtheta)[:, None, None]
    energy_sum = jnp.sum(scaled, axis=(0, 1))
    first_sum = jnp.sum(scaled / radian_freq[:, None, None], axis=(0, 1))
    root_sum = jnp.sum(scaled / jnp.sqrt(wavenum)[:, None, None], axis=(0, 1))
    energy = energy_sum + EPSILON
    above, below = band_neighbours(point_block)
    delta = quad_delta(point_block, above, below, energy, 1)
    delta_above, delta_below = band_neighbours(delta)
    extra = quad_term(delta, delta_above, delta_below, 1)
    cosine = jnp.cos(angles[:, None] - wind_angle[None, :])
    return (
        sources(
            point_block,
            energy_sum,
            first_sum,
            root_sum,
            radian_freq[:, None, None],
            wavenum[:, None, None],
            cosine,
            wind_block,
        )
        + extra
    )


Y_GROUP = 4


def _z_exchange_kernel(z_count, point_ref, part_ref, lower_ref, upper_ref, gathered_ref,
                       halo_send, halo_recv, gather_send, gather_recv):
    geo = lax.axis_index("geo")
    z_pos = lax.axis_index("z")
    y_pos = lax.axis_index("y")
    group = point_ref.shape[0]
    barrier = pltpu.get_barrier_semaphore()
    for offset in range(1, z_count):
        target = lax.rem(z_pos + offset, z_count)
        pl.semaphore_signal(barrier, inc=1, device_id=(geo, target, y_pos),
                            device_id_type=pl.DeviceIdType.MESH)
    pl.semaphore_wait(barrier, z_count - 1)

    def halo_copy(src_lo, dst_ref, slot, target):
        return pltpu.make_async_remote_copy(
            src_ref=point_ref.at[pl.ds(src_lo, 2)],
            dst_ref=dst_ref,
            send_sem=halo_send.at[slot],
            recv_sem=halo_recv.at[slot],
            device_id=(geo, target, y_pos),
            device_id_type=pl.DeviceIdType.MESH,
        )

    up = halo_copy(group - 2, lower_ref, 0, z_pos + 1)
    down = halo_copy(0, upper_ref, 1, z_pos - 1)

    @pl.when(z_pos < z_count - 1)
    def _():
        up.start()

    @pl.when(z_pos > 0)
    def _():
        down.start()

    copies = []
    for offset in range(1, z_count):
        target = lax.rem(z_pos + offset, z_count)
        copy = pltpu.make_async_remote_copy(
            src_ref=part_ref,
            dst_ref=gathered_ref.at[z_pos],
            send_sem=gather_send.at[offset],
            recv_sem=gather_recv.at[offset],
            device_id=(geo, target, y_pos),
            device_id_type=pl.DeviceIdType.MESH,
        )
        copy.start()
        copies.append(copy)
    gathered_ref[z_pos] = part_ref[...]

    @pl.when(z_pos == 0)
    def _():
        lower_ref[...] = jnp.zeros(lower_ref.shape, lower_ref.dtype)

    @pl.when(z_pos == z_count - 1)
    def _():
        upper_ref[...] = jnp.zeros(upper_ref.shape, upper_ref.dtype)

    for copy in copies:
        copy.wait_send()
        copy.wait_recv()

    @pl.when(z_pos < z_count - 1)
    def _():
        up.wait_send()
        down.wait_recv()

    @pl.when(z_pos > 0)
    def _():
        down.wait_send()
        up.wait_recv()


def z_exchange(point, part, z_count):
    group, dirs, rows, cols = point.shape
    halo = jax.ShapeDtypeStruct((2, dirs, rows, cols), point.dtype)
    vmem = pl.BlockSpec(memory_space=pltpu.VMEM)
    return pl.pallas_call(
        functools.partial(_z_exchange_kernel, z_count),
        out_shape=(halo, halo, jax.ShapeDtypeStruct((z_count,) + part.shape, part.dtype)),
        in_specs=[vmem, vmem],
        out_specs=(vmem, vmem, vmem),
        scratch_shapes=[
            pltpu.SemaphoreType.DMA((2,)),
            pltpu.SemaphoreType.DMA((2,)),
            pltpu.SemaphoreType.DMA((z_count,)),
            pltpu.SemaphoreType.DMA((z_count,)),
        ],
        compiler_params=pltpu.CompilerParams(collective_id=0, has_side_effects=True),
    )(point, part)


def shards(spectrum, land_sea, sea_index, sea_count, wind_speed, wind_dir, slope_x, slope_y):
    local_bands, dir_count, row_count, col_count = spectrum.shape
    z_count = lax.axis_size("z")
    y_count = lax.axis_size("y")
    z_pos = lax.axis_index("z")
    y_pos = lax.axis_index("y")
    spec_pos = z_pos * y_count + y_pos
    dtheta = 2.0 * math.pi / dir_count
    angles = (jnp.arange(dir_count).astype(jnp.float32) + 0.5) * dtheta
    face_angles = jnp.arange(dir_count + 1).astype(jnp.float32) * dtheta
    band_ids = (spec_pos * local_bands + jnp.arange(local_bands)).astype(jnp.float32)
    radian_freq, wavenum, courant, turn_rate, band_spread = band_table(band_ids)
    wet_mask = land_sea.astype(jnp.float32)
    density = spectrum * wet_mask
    padded = extended(density, (("geo", 2),), 2)
    density = (
        advect(padded, (courant[:, None] * jnp.cos(angles)[None, :])[:, :, None, None], 2)
        * wet_mask
    )
    padded = jnp.pad(density, ((0, 0), (0, 0), (0, 0), (2, 2)))
    density = (
        advect(padded, (courant[:, None] * jnp.sin(angles)[None, :])[:, :, None, None], 3)
        * wet_mask
    )
    turning = turn_rate[:, None, None, None] * (
        jnp.sin(face_angles)[None, :, None, None] * slope_x
        - jnp.cos(face_angles)[None, :, None, None] * slope_y
    )
    padded = jnp.concatenate([density[:, -2:], density, density[:, :2]], axis=1)
    floored = jnp.maximum(advect(padded, turning, 1), 0.0)
    point = lax.all_to_all(floored, "y", split_axis=2, concat_axis=0, tiled=True)
    group = point.shape[0]
    part_rows = point.shape[2]
    group_ids = (z_pos * group + jnp.arange(group)).astype(jnp.float32)
    radian_freq, wavenum, courant, turn_rate, band_spread = band_table(group_ids)
    scaled = point * (band_spread * dtheta)[:, None, None, None]
    sums = jnp.stack(
        [
            jnp.sum(scaled, axis=(0, 1)),
            jnp.sum(scaled / radian_freq[:, None, None, None], axis=(0, 1)),
            jnp.sum(scaled / jnp.sqrt(wavenum)[:, None, None, None], axis=(0, 1)),
        ]
    )
    lower, upper = z_halo(point, z_count)
    step = z_count // 2
    while step >= 1:
        sums = sums + lax.ppermute(sums, "z", [(i, i ^ step) for i in range(z_count)])
        step //= 2
    energy_sum, first_sum, root_sum = sums[0], sums[1], sums[2]
    energy = energy_sum + EPSILON
    ext = jnp.concatenate([lower, point, upper], axis=0)
    center, plus, minus = ext[1:-1], jnp.roll(ext[2:], -1, axis=1), jnp.roll(ext[:-2], 3, axis=1)
    cubic = center * center * (plus + minus) - 2.0 * center * plus * minus
    extra = (
        -2.0 * cubic[1:-1] + jnp.roll(cubic[:-2], 1, axis=1) + jnp.roll(cubic[2:], -3, axis=1)
    ) * (QUAD_COEF / (energy * energy))
    row_start = y_pos * part_rows
    wind_block = lax.dynamic_slice_in_dim(wind_speed, row_start, part_rows, axis=0)
    wind_angle = lax.dynamic_slice_in_dim(wind_dir, row_start, part_rows, axis=0)
    wet_block = lax.dynamic_slice_in_dim(wet_mask, row_start, part_rows, axis=0)
    cosine = jnp.cos(angles[:, None, None] - wind_angle[None])
    updated = (
        sources(
            point,
            energy_sum,
            first_sum,
            root_sum,
            radian_freq[:, None, None, None],
            wavenum[:, None, None, None],
            cosine,
            wind_block,
        )
        + extra
    ) * wet_block
    return lax.all_to_all(updated, "y", split_axis=0, concat_axis=2, tiled=True)


def solution(mesh):
    geo_count = mesh.shape["geo"]
    spec_count = mesh.shape["spec"]
    local = jax.sharding.Mesh(
        mesh.devices.reshape(geo_count, spec_count // Y_GROUP, Y_GROUP), ("geo", "z", "y")
    )
    spec = ("z", "y")
    placed = (
        P(spec, None, "geo", None),
        P("geo", None),
        P("geo", None),
        P("geo"),
        P("geo", None),
        P("geo", None),
        P("geo", None),
        P("geo", None),
    )
    return jax.shard_map(
        shards, mesh=local, in_specs=placed, out_specs=P(spec, None, "geo", None), check_vma=False
    )
```

```python
import functools
import math

import jax
import jax.numpy as jnp
from jax import lax
from jax.experimental import pallas as pl
from jax.experimental.pallas import tpu as pltpu
from jax.sharding import PartitionSpec as P

GRAVITY = 9.81
BASE_FREQ = 0.035
GROWTH = 1.1
COURANT_TOP = 0.9
TURN_TOP = 1.2
SPACING = 0.1
USTAR_RATIO = 0.035
WIND_COEF = 0.0375
WHITECAP = 0.36
STEEP_REF = 1.6
EPSILON = 1e-06
QUAD_COEF = 100.0


def extended(cells, sides, width):
    for axis, dim in sides:
        count = lax.axis_size(axis)
        ends = count - 1
        head = lax.slice_in_dim(cells, 0, width, axis=dim)
        tail = lax.slice_in_dim(cells, cells.shape[dim] - width, cells.shape[dim], axis=dim)
        cells = jnp.concatenate(
            [
                lax.ppermute(tail, axis, [(i, (i + 1) % count) for i in range(ends)]),
                cells,
                lax.ppermute(head, axis, [((i + 1) % count, i) for i in range(ends)]),
            ],
            axis=dim,
        )
    return cells


def band_table(band_ids):
    growth_factor = jnp.power(GROWTH, band_ids)
    radian_freq = 2.0 * math.pi * BASE_FREQ * growth_factor
    wavenum = radian_freq * radian_freq / GRAVITY
    return (
        radian_freq,
        wavenum,
        COURANT_TOP / growth_factor,
        TURN_TOP / growth_factor,
        SPACING * radian_freq,
    )


def quick_flux(far_left, near_left, near_right, far_right, courant):
    forward = courant >= 0
    upwind = jnp.where(forward, far_left, far_right)
    center = jnp.where(forward, near_left, near_right)
    downwind = jnp.where(forward, near_right, near_left)
    face_value = (
        0.5 * (center + downwind)
        - 0.5 * jnp.abs(courant) * (downwind - center)
        - (1.0 - courant * courant) / 6.0 * (downwind - 2.0 * center + upwind)
    )
    return courant * face_value


def advect(padded, courant, along):
    face_count = padded.shape[along] - 4
    shifted = [
        lax.slice_in_dim(padded, offset, offset + face_count + 1, axis=along) for offset in range(4)
    ]
    face_flux = quick_flux(shifted[0], shifted[1], shifted[2], shifted[3], courant)
    centre_cells = lax.slice_in_dim(padded, 2, 2 + face_count, axis=along)
    upper_flux = lax.slice_in_dim(face_flux, 1, face_count + 1, axis=along)
    lower_flux = lax.slice_in_dim(face_flux, 0, face_count, axis=along)
    return centre_cells - (upper_flux - lower_flux)


def quad_delta(center, above, below, energy, dir_axis):
    plus = jnp.roll(above, -1, axis=dir_axis)
    minus = jnp.roll(below, 3, axis=dir_axis)
    return (
        QUAD_COEF
        * (center * center * (plus + minus) - 2.0 * center * plus * minus)
        / (energy * energy)
    )


def quad_term(delta, delta_above, delta_below, dir_axis):
    return (
        -2.0 * delta
        + jnp.roll(delta_below, 1, axis=dir_axis)
        + jnp.roll(delta_above, -3, axis=dir_axis)
    )


def band_neighbours(values):
    empty = jnp.zeros((1,) + values.shape[1:], jnp.float32)
    return (
        jnp.concatenate([values[1:], empty], axis=0),
        jnp.concatenate([empty, values[:-1]], axis=0),
    )


def sources(density, energy_sum, first_sum, root_sum, radian_freq, wavenum, cosine, wind_speed):
    energy = energy_sum + EPSILON
    mean_sigma = energy / (first_sum + EPSILON)
    ratio_k = energy / (root_sum + EPSILON)
    mean_k = ratio_k * ratio_k
    steepness = energy * mean_k * mean_k / STEEP_REF
    decay_rate = WHITECAP * mean_sigma * (wavenum / mean_k) * steepness * steepness
    growth_rate = (
        WIND_COEF
        * radian_freq
        * jnp.maximum(28.0 * USTAR_RATIO * wind_speed * radian_freq / GRAVITY * cosine - 1.0, 0.0)
    )
    return density * (1.0 + growth_rate) / (1.0 + decay_rate)


def local_sources(point_block, wind_block, wind_angle, angles, dtheta):
    band_total = point_block.shape[0]
    band_ids = jnp.arange(band_total).astype(jnp.float32)
    radian_freq, wavenum, courant, turn_rate, band_spread = band_table(band_ids)
    scaled = point_block * (band_spread * dtheta)[:, None, None]
    energy_sum = jnp.sum(scaled, axis=(0, 1))
    first_sum = jnp.sum(scaled / radian_freq[:, None, None], axis=(0, 1))
    root_sum = jnp.sum(scaled / jnp.sqrt(wavenum)[:, None, None], axis=(0, 1))
    energy = energy_sum + EPSILON
    above, below = band_neighbours(point_block)
    delta = quad_delta(point_block, above, below, energy, 1)
    delta_above, delta_below = band_neighbours(delta)
    extra = quad_term(delta, delta_above, delta_below, 1)
    cosine = jnp.cos(angles[:, None] - wind_angle[None, :])
    return (
        sources(
            point_block,
            energy_sum,
            first_sum,
            root_sum,
            radian_freq[:, None, None],
            wavenum[:, None, None],
            cosine,
            wind_block,
        )
        + extra
    )


Y_GROUP = 4
HALO = 2


def _z_halo_kernel(z_count, point_ref, ext_ref, local_sem, halo_send, halo_recv):
    geo = lax.axis_index("geo")
    z_pos = lax.axis_index("z")
    y_pos = lax.axis_index("y")
    group = point_ref.shape[0]
    mesh_id = pl.DeviceIdType.MESH
    barrier = pltpu.get_barrier_semaphore()
    for step in (1, z_count - 1):
        pl.semaphore_signal(barrier, inc=1, device_id=(geo, lax.rem(z_pos + step, z_count), y_pos),
                            device_id_type=mesh_id)
    pl.semaphore_wait(barrier, 2)

    def halo_copy(src_lo, dst_lo, slot, target):
        return pltpu.make_async_remote_copy(
            src_ref=point_ref.at[pl.ds(src_lo, HALO)],
            dst_ref=ext_ref.at[pl.ds(dst_lo, HALO)],
            send_sem=halo_send.at[slot],
            recv_sem=halo_recv.at[slot],
            device_id=(geo, target, y_pos),
            device_id_type=mesh_id,
        )

    up = halo_copy(group - HALO, 0, 0, lax.rem(z_pos + 1, z_count))
    down = halo_copy(0, HALO + group, 1, lax.rem(z_pos + z_count - 1, z_count))

    @pl.when(z_pos < z_count - 1)
    def _():
        up.start()

    @pl.when(z_pos > 0)
    def _():
        down.start()

    local = pltpu.make_async_copy(point_ref, ext_ref.at[pl.ds(HALO, group)], local_sem.at[0])
    local.start()

    @pl.when(z_pos == 0)
    def _():
        ext_ref[pl.ds(0, HALO)] = jnp.zeros((HALO,) + ext_ref.shape[1:], ext_ref.dtype)

    @pl.when(z_pos == z_count - 1)
    def _():
        ext_ref[pl.ds(HALO + group, HALO)] = jnp.zeros((HALO,) + ext_ref.shape[1:], ext_ref.dtype)

    local.wait()

    @pl.when(z_pos < z_count - 1)
    def _():
        up.wait_send()
        down.wait_recv()

    @pl.when(z_pos > 0)
    def _():
        down.wait_send()
        up.wait_recv()


def z_halo(point, z_count):
    group, dirs, rows, cols = point.shape
    vmem = pl.BlockSpec(memory_space=pltpu.VMEM)
    return pl.pallas_call(
        functools.partial(_z_halo_kernel, z_count),
        out_shape=jax.ShapeDtypeStruct((group + 2 * HALO, dirs, rows, cols), point.dtype),
        in_specs=[pl.BlockSpec(memory_space=pl.ANY)],
        out_specs=vmem,
        scratch_shapes=[
            pltpu.SemaphoreType.DMA((1,)),
            pltpu.SemaphoreType.DMA((2,)),
            pltpu.SemaphoreType.DMA((2,)),
        ],
        compiler_params=pltpu.CompilerParams(collective_id=0, has_side_effects=True),
    )(point)


def shards(spectrum, land_sea, sea_index, sea_count, wind_speed, wind_dir, slope_x, slope_y):
    local_bands, dir_count, row_count, col_count = spectrum.shape
    z_count = lax.axis_size("z")
    y_count = lax.axis_size("y")
    z_pos = lax.axis_index("z")
    y_pos = lax.axis_index("y")
    spec_pos = z_pos * y_count + y_pos
    dtheta = 2.0 * math.pi / dir_count
    angles = (jnp.arange(dir_count).astype(jnp.float32) + 0.5) * dtheta
    face_angles = jnp.arange(dir_count + 1).astype(jnp.float32) * dtheta
    band_ids = (spec_pos * local_bands + jnp.arange(local_bands)).astype(jnp.float32)
    radian_freq, wavenum, courant, turn_rate, band_spread = band_table(band_ids)
    wet_mask = land_sea.astype(jnp.float32)
    density = spectrum * wet_mask
    padded = extended(density, (("geo", 2),), 2)
    density = (
        advect(padded, (courant[:, None] * jnp.cos(angles)[None, :])[:, :, None, None], 2)
        * wet_mask
    )
    padded = jnp.pad(density, ((0, 0), (0, 0), (0, 0), (2, 2)))
    density = (
        advect(padded, (courant[:, None] * jnp.sin(angles)[None, :])[:, :, None, None], 3)
        * wet_mask
    )
    turning = turn_rate[:, None, None, None] * (
        jnp.sin(face_angles)[None, :, None, None] * slope_x
        - jnp.cos(face_angles)[None, :, None, None] * slope_y
    )
    padded = jnp.concatenate([density[:, -2:], density, density[:, :2]], axis=1)
    floored = jnp.maximum(advect(padded, turning, 1), 0.0)
    point = lax.all_to_all(floored, "y", split_axis=2, concat_axis=0, tiled=True)
    group = point.shape[0]
    part_rows = point.shape[2]
    group_ids = (z_pos * group + jnp.arange(group)).astype(jnp.float32)
    radian_freq, wavenum, courant, turn_rate, band_spread = band_table(group_ids)
    scaled = point * (band_spread * dtheta)[:, None, None, None]
    sums = jnp.stack(
        [
            jnp.sum(scaled, axis=(0, 1)),
            jnp.sum(scaled / radian_freq[:, None, None, None], axis=(0, 1)),
            jnp.sum(scaled / jnp.sqrt(wavenum)[:, None, None, None], axis=(0, 1)),
        ]
    )
    ext = z_halo(point, z_count)
    step = z_count // 2
    while step >= 1:
        sums = sums + lax.ppermute(sums, "z", [(i, i ^ step) for i in range(z_count)])
        step //= 2
    energy_sum, first_sum, root_sum = sums[0], sums[1], sums[2]
    energy = energy_sum + EPSILON
    center, plus, minus = ext[1:-1], jnp.roll(ext[2:], -1, axis=1), jnp.roll(ext[:-2], 3, axis=1)
    cubic = center * center * (plus + minus) - 2.0 * center * plus * minus
    extra = (
        -2.0 * cubic[1:-1] + jnp.roll(cubic[:-2], 1, axis=1) + jnp.roll(cubic[2:], -3, axis=1)
    ) * (QUAD_COEF / (energy * energy))
    row_start = y_pos * part_rows
    wind_block = lax.dynamic_slice_in_dim(wind_speed, row_start, part_rows, axis=0)
    wind_angle = lax.dynamic_slice_in_dim(wind_dir, row_start, part_rows, axis=0)
    wet_block = lax.dynamic_slice_in_dim(wet_mask, row_start, part_rows, axis=0)
    cosine = jnp.cos(angles[:, None, None] - wind_angle[None])
    updated = (
        sources(
            point,
            energy_sum,
            first_sum,
            root_sum,
            radian_freq[:, None, None, None],
            wavenum[:, None, None, None],
            cosine,
            wind_block,
        )
        + extra
    ) * wet_block
    return lax.all_to_all(updated, "y", split_axis=0, concat_axis=2, tiled=True)


def solution(mesh):
    geo_count = mesh.shape["geo"]
    spec_count = mesh.shape["spec"]
    local = jax.sharding.Mesh(
        mesh.devices.reshape(geo_count, spec_count // Y_GROUP, Y_GROUP), ("geo", "z", "y")
    )
    spec = ("z", "y")
    placed = (
        P(spec, None, "geo", None),
        P("geo", None),
        P("geo", None),
        P("geo"),
        P("geo", None),
        P("geo", None),
        P("geo", None),
        P("geo", None),
    )
    return jax.shard_map(
        shards, mesh=local, in_specs=placed, out_specs=P(spec, None, "geo", None), check_vma=False
    )
```

```python
import functools
import math

import jax
import jax.numpy as jnp
from jax import lax
from jax.experimental import pallas as pl
from jax.experimental.pallas import tpu as pltpu
from jax.sharding import PartitionSpec as P

GRAVITY = 9.81
BASE_FREQ = 0.035
GROWTH = 1.1
COURANT_TOP = 0.9
TURN_TOP = 1.2
SPACING = 0.1
USTAR_RATIO = 0.035
WIND_COEF = 0.0375
WHITECAP = 0.36
STEEP_REF = 1.6
EPSILON = 1e-06
QUAD_COEF = 100.0


def extended(cells, sides, width):
    for axis, dim in sides:
        count = lax.axis_size(axis)
        ends = count - 1
        head = lax.slice_in_dim(cells, 0, width, axis=dim)
        tail = lax.slice_in_dim(cells, cells.shape[dim] - width, cells.shape[dim], axis=dim)
        cells = jnp.concatenate(
            [
                lax.ppermute(tail, axis, [(i, (i + 1) % count) for i in range(ends)]),
                cells,
                lax.ppermute(head, axis, [((i + 1) % count, i) for i in range(ends)]),
            ],
            axis=dim,
        )
    return cells


def band_table(band_ids):
    growth_factor = jnp.power(GROWTH, band_ids)
    radian_freq = 2.0 * math.pi * BASE_FREQ * growth_factor
    wavenum = radian_freq * radian_freq / GRAVITY
    return (
        radian_freq,
        wavenum,
        COURANT_TOP / growth_factor,
        TURN_TOP / growth_factor,
        SPACING * radian_freq,
    )


def quick_flux(far_left, near_left, near_right, far_right, courant):
    forward = courant >= 0
    upwind = jnp.where(forward, far_left, far_right)
    center = jnp.where(forward, near_left, near_right)
    downwind = jnp.where(forward, near_right, near_left)
    face_value = (
        0.5 * (center + downwind)
        - 0.5 * jnp.abs(courant) * (downwind - center)
        - (1.0 - courant * courant) / 6.0 * (downwind - 2.0 * center + upwind)
    )
    return courant * face_value


def advect(padded, courant, along):
    face_count = padded.shape[along] - 4
    shifted = [
        lax.slice_in_dim(padded, offset, offset + face_count + 1, axis=along) for offset in range(4)
    ]
    face_flux = quick_flux(shifted[0], shifted[1], shifted[2], shifted[3], courant)
    centre_cells = lax.slice_in_dim(padded, 2, 2 + face_count, axis=along)
    upper_flux = lax.slice_in_dim(face_flux, 1, face_count + 1, axis=along)
    lower_flux = lax.slice_in_dim(face_flux, 0, face_count, axis=along)
    return centre_cells - (upper_flux - lower_flux)


def quad_delta(center, above, below, energy, dir_axis):
    plus = jnp.roll(above, -1, axis=dir_axis)
    minus = jnp.roll(below, 3, axis=dir_axis)
    return (
        QUAD_COEF
        * (center * center * (plus + minus) - 2.0 * center * plus * minus)
        / (energy * energy)
    )


def quad_term(delta, delta_above, delta_below, dir_axis):
    return (
        -2.0 * delta
        + jnp.roll(delta_below, 1, axis=dir_axis)
        + jnp.roll(delta_above, -3, axis=dir_axis)
    )


def band_neighbours(values):
    empty = jnp.zeros((1,) + values.shape[1:], jnp.float32)
    return (
        jnp.concatenate([values[1:], empty], axis=0),
        jnp.concatenate([empty, values[:-1]], axis=0),
    )


def sources(density, energy_sum, first_sum, root_sum, radian_freq, wavenum, cosine, wind_speed):
    energy = energy_sum + EPSILON
    mean_sigma = energy / (first_sum + EPSILON)
    ratio_k = energy / (root_sum + EPSILON)
    mean_k = ratio_k * ratio_k
    steepness = energy * mean_k * mean_k / STEEP_REF
    decay_rate = WHITECAP * mean_sigma * (wavenum / mean_k) * steepness * steepness
    growth_rate = (
        WIND_COEF
        * radian_freq
        * jnp.maximum(28.0 * USTAR_RATIO * wind_speed * radian_freq / GRAVITY * cosine - 1.0, 0.0)
    )
    return density * (1.0 + growth_rate) / (1.0 + decay_rate)


def local_sources(point_block, wind_block, wind_angle, angles, dtheta):
    band_total = point_block.shape[0]
    band_ids = jnp.arange(band_total).astype(jnp.float32)
    radian_freq, wavenum, courant, turn_rate, band_spread = band_table(band_ids)
    scaled = point_block * (band_spread * dtheta)[:, None, None]
    energy_sum = jnp.sum(scaled, axis=(0, 1))
    first_sum = jnp.sum(scaled / radian_freq[:, None, None], axis=(0, 1))
    root_sum = jnp.sum(scaled / jnp.sqrt(wavenum)[:, None, None], axis=(0, 1))
    energy = energy_sum + EPSILON
    above, below = band_neighbours(point_block)
    delta = quad_delta(point_block, above, below, energy, 1)
    delta_above, delta_below = band_neighbours(delta)
    extra = quad_term(delta, delta_above, delta_below, 1)
    cosine = jnp.cos(angles[:, None] - wind_angle[None, :])
    return (
        sources(
            point_block,
            energy_sum,
            first_sum,
            root_sum,
            radian_freq[:, None, None],
            wavenum[:, None, None],
            cosine,
            wind_block,
        )
        + extra
    )


Y_GROUP = 4
HALO = 2


def _z_halo_kernel(z_count, point_ref, lower_ref, upper_ref, halo_send, halo_recv):
    geo = lax.axis_index("geo")
    z_pos = lax.axis_index("z")
    y_pos = lax.axis_index("y")
    group = point_ref.shape[0]
    mesh_id = pl.DeviceIdType.MESH
    barrier = pltpu.get_barrier_semaphore()
    for step in (1, z_count - 1):
        pl.semaphore_signal(barrier, inc=1, device_id=(geo, lax.rem(z_pos + step, z_count), y_pos),
                            device_id_type=mesh_id)
    pl.semaphore_wait(barrier, 2)

    def halo_copy(src_lo, dst_ref, slot, target):
        return pltpu.make_async_remote_copy(
            src_ref=point_ref.at[pl.ds(src_lo, HALO)],
            dst_ref=dst_ref,
            send_sem=halo_send.at[slot],
            recv_sem=halo_recv.at[slot],
            device_id=(geo, target, y_pos),
            device_id_type=mesh_id,
        )

    up = halo_copy(group - HALO, lower_ref, 0, lax.rem(z_pos + 1, z_count))
    down = halo_copy(0, upper_ref, 1, lax.rem(z_pos + z_count - 1, z_count))

    @pl.when(z_pos < z_count - 1)
    def _():
        up.start()

    @pl.when(z_pos > 0)
    def _():
        down.start()

    @pl.when(z_pos == 0)
    def _():
        lower_ref[...] = jnp.zeros(lower_ref.shape, lower_ref.dtype)

    @pl.when(z_pos == z_count - 1)
    def _():
        upper_ref[...] = jnp.zeros(upper_ref.shape, upper_ref.dtype)

    @pl.when(z_pos < z_count - 1)
    def _():
        up.wait_send()
        down.wait_recv()

    @pl.when(z_pos > 0)
    def _():
        down.wait_send()
        up.wait_recv()


def z_halo(point, z_count):
    group, dirs, rows, cols = point.shape
    halo = jax.ShapeDtypeStruct((HALO, dirs, rows, cols), point.dtype)
    vmem = pl.BlockSpec(memory_space=pltpu.VMEM)
    return pl.pallas_call(
        functools.partial(_z_halo_kernel, z_count),
        out_shape=(halo, halo),
        in_specs=[pl.BlockSpec(memory_space=pl.ANY)],
        out_specs=(vmem, vmem),
        scratch_shapes=[
            pltpu.SemaphoreType.DMA((2,)),
            pltpu.SemaphoreType.DMA((2,)),
        ],
        compiler_params=pltpu.CompilerParams(collective_id=0, has_side_effects=True),
    )(point)


def extended(cells, sides, width):
    for axis, dim in sides:
        count = lax.axis_size(axis)
        ends = count - 1
        head = lax.slice_in_dim(cells, 0, width, axis=dim)
        tail = lax.slice_in_dim(cells, cells.shape[dim] - width, cells.shape[dim], axis=dim)
        cells = jnp.concatenate(
            [
                lax.ppermute(tail, axis, [(i, (i + 1) % count) for i in range(ends)]),
                cells,
                lax.ppermute(head, axis, [((i + 1) % count, i) for i in range(ends)]),
            ],
            axis=dim,
        )
    return cells


def band_table(band_ids):
    growth_factor = jnp.power(GROWTH, band_ids)
    radian_freq = 2.0 * math.pi * BASE_FREQ * growth_factor
    wavenum = radian_freq * radian_freq / GRAVITY
    return (
        radian_freq,
        wavenum,
        COURANT_TOP / growth_factor,
        TURN_TOP / growth_factor,
        SPACING * radian_freq,
    )


def quick_flux(far_left, near_left, near_right, far_right, courant):
    forward = courant >= 0
    upwind = jnp.where(forward, far_left, far_right)
    center = jnp.where(forward, near_left, near_right)
    downwind = jnp.where(forward, near_right, near_left)
    face_value = (
        0.5 * (center + downwind)
        - 0.5 * jnp.abs(courant) * (downwind - center)
        - (1.0 - courant * courant) / 6.0 * (downwind - 2.0 * center + upwind)
    )
    return courant * face_value


def advect(padded, courant, along):
    face_count = padded.shape[along] - 4
    shifted = [
        lax.slice_in_dim(padded, offset, offset + face_count + 1, axis=along) for offset in range(4)
    ]
    face_flux = quick_flux(shifted[0], shifted[1], shifted[2], shifted[3], courant)
    centre_cells = lax.slice_in_dim(padded, 2, 2 + face_count, axis=along)
    upper_flux = lax.slice_in_dim(face_flux, 1, face_count + 1, axis=along)
    lower_flux = lax.slice_in_dim(face_flux, 0, face_count, axis=along)
    return centre_cells - (upper_flux - lower_flux)


def quad_delta(center, above, below, energy, dir_axis):
    plus = jnp.roll(above, -1, axis=dir_axis)
    minus = jnp.roll(below, 3, axis=dir_axis)
    return (
        QUAD_COEF
        * (center * center * (plus + minus) - 2.0 * center * plus * minus)
        / (energy * energy)
    )


def quad_term(delta, delta_above, delta_below, dir_axis):
    return (
        -2.0 * delta
        + jnp.roll(delta_below, 1, axis=dir_axis)
        + jnp.roll(delta_above, -3, axis=dir_axis)
    )


def band_neighbours(values):
    empty = jnp.zeros((1,) + values.shape[1:], jnp.float32)
    return (
        jnp.concatenate([values[1:], empty], axis=0),
        jnp.concatenate([empty, values[:-1]], axis=0),
    )


def sources(density, energy_sum, first_sum, root_sum, radian_freq, wavenum, cosine, wind_speed):
    energy = energy_sum + EPSILON
    mean_sigma = energy / (first_sum + EPSILON)
    ratio_k = energy / (root_sum + EPSILON)
    mean_k = ratio_k * ratio_k
    steepness = energy * mean_k * mean_k / STEEP_REF
    decay_rate = WHITECAP * mean_sigma * (wavenum / mean_k) * steepness * steepness
    growth_rate = (
        WIND_COEF
        * radian_freq
        * jnp.maximum(28.0 * USTAR_RATIO * wind_speed * radian_freq / GRAVITY * cosine - 1.0, 0.0)
    )
    return density * (1.0 + growth_rate) / (1.0 + decay_rate)


def local_sources(point_block, wind_block, wind_angle, angles, dtheta):
    band_total = point_block.shape[0]
    band_ids = jnp.arange(band_total).astype(jnp.float32)
    radian_freq, wavenum, courant, turn_rate, band_spread = band_table(band_ids)
    scaled = point_block * (band_spread * dtheta)[:, None, None]
    energy_sum = jnp.sum(scaled, axis=(0, 1))
    first_sum = jnp.sum(scaled / radian_freq[:, None, None], axis=(0, 1))
    root_sum = jnp.sum(scaled / jnp.sqrt(wavenum)[:, None, None], axis=(0, 1))
    energy = energy_sum + EPSILON
    above, below = band_neighbours(point_block)
    delta = quad_delta(point_block, above, below, energy, 1)
    delta_above, delta_below = band_neighbours(delta)
    extra = quad_term(delta, delta_above, delta_below, 1)
    cosine = jnp.cos(angles[:, None] - wind_angle[None, :])
    return (
        sources(
            point_block,
            energy_sum,
            first_sum,
            root_sum,
            radian_freq[:, None, None],
            wavenum[:, None, None],
            cosine,
            wind_block,
        )
        + extra
    )


Y_GROUP = 4


def _z_exchange_kernel(z_count, point_ref, part_ref, lower_ref, upper_ref, gathered_ref,
                       halo_send, halo_recv, gather_send, gather_recv):
    geo = lax.axis_index("geo")
    z_pos = lax.axis_index("z")
    y_pos = lax.axis_index("y")
    group = point_ref.shape[0]
    barrier = pltpu.get_barrier_semaphore()
    for offset in range(1, z_count):
        target = lax.rem(z_pos + offset, z_count)
        pl.semaphore_signal(barrier, inc=1, device_id=(geo, target, y_pos),
                            device_id_type=pl.DeviceIdType.MESH)
    pl.semaphore_wait(barrier, z_count - 1)

    def halo_copy(src_lo, dst_ref, slot, target):
        return pltpu.make_async_remote_copy(
            src_ref=point_ref.at[pl.ds(src_lo, 2)],
            dst_ref=dst_ref,
            send_sem=halo_send.at[slot],
            recv_sem=halo_recv.at[slot],
            device_id=(geo, target, y_pos),
            device_id_type=pl.DeviceIdType.MESH,
        )

    up = halo_copy(group - 2, lower_ref, 0, z_pos + 1)
    down = halo_copy(0, upper_ref, 1, z_pos - 1)

    @pl.when(z_pos < z_count - 1)
    def _():
        up.start()

    @pl.when(z_pos > 0)
    def _():
        down.start()

    copies = []
    for offset in range(1, z_count):
        target = lax.rem(z_pos + offset, z_count)
        copy = pltpu.make_async_remote_copy(
            src_ref=part_ref,
            dst_ref=gathered_ref.at[z_pos],
            send_sem=gather_send.at[offset],
            recv_sem=gather_recv.at[offset],
            device_id=(geo, target, y_pos),
            device_id_type=pl.DeviceIdType.MESH,
        )
        copy.start()
        copies.append(copy)
    gathered_ref[z_pos] = part_ref[...]

    @pl.when(z_pos == 0)
    def _():
        lower_ref[...] = jnp.zeros(lower_ref.shape, lower_ref.dtype)

    @pl.when(z_pos == z_count - 1)
    def _():
        upper_ref[...] = jnp.zeros(upper_ref.shape, upper_ref.dtype)

    for copy in copies:
        copy.wait_send()
        copy.wait_recv()

    @pl.when(z_pos < z_count - 1)
    def _():
        up.wait_send()
        down.wait_recv()

    @pl.when(z_pos > 0)
    def _():
        down.wait_send()
        up.wait_recv()


def z_exchange(point, part, z_count):
    group, dirs, rows, cols = point.shape
    halo = jax.ShapeDtypeStruct((2, dirs, rows, cols), point.dtype)
    vmem = pl.BlockSpec(memory_space=pltpu.VMEM)
    return pl.pallas_call(
        functools.partial(_z_exchange_kernel, z_count),
        out_shape=(halo, halo, jax.ShapeDtypeStruct((z_count,) + part.shape, part.dtype)),
        in_specs=[vmem, vmem],
        out_specs=(vmem, vmem, vmem),
        scratch_shapes=[
            pltpu.SemaphoreType.DMA((2,)),
            pltpu.SemaphoreType.DMA((2,)),
            pltpu.SemaphoreType.DMA((z_count,)),
            pltpu.SemaphoreType.DMA((z_count,)),
        ],
        compiler_params=pltpu.CompilerParams(collective_id=0, has_side_effects=True),
    )(point, part)


def shards(spectrum, land_sea, sea_index, sea_count, wind_speed, wind_dir, slope_x, slope_y):
    local_bands, dir_count, row_count, col_count = spectrum.shape
    z_count = lax.axis_size("z")
    y_count = lax.axis_size("y")
    z_pos = lax.axis_index("z")
    y_pos = lax.axis_index("y")
    spec_pos = z_pos * y_count + y_pos
    dtheta = 2.0 * math.pi / dir_count
    angles = (jnp.arange(dir_count).astype(jnp.float32) + 0.5) * dtheta
    face_angles = jnp.arange(dir_count + 1).astype(jnp.float32) * dtheta
    band_ids = (spec_pos * local_bands + jnp.arange(local_bands)).astype(jnp.float32)
    radian_freq, wavenum, courant, turn_rate, band_spread = band_table(band_ids)
    wet_mask = land_sea.astype(jnp.float32)
    density = spectrum * wet_mask
    padded = extended(density, (("geo", 2),), 2)
    density = (
        advect(padded, (courant[:, None] * jnp.cos(angles)[None, :])[:, :, None, None], 2)
        * wet_mask
    )
    padded = jnp.pad(density, ((0, 0), (0, 0), (0, 0), (2, 2)))
    density = (
        advect(padded, (courant[:, None] * jnp.sin(angles)[None, :])[:, :, None, None], 3)
        * wet_mask
    )
    turning = turn_rate[:, None, None, None] * (
        jnp.sin(face_angles)[None, :, None, None] * slope_x
        - jnp.cos(face_angles)[None, :, None, None] * slope_y
    )
    padded = jnp.concatenate([density[:, -2:], density, density[:, :2]], axis=1)
    floored = jnp.maximum(advect(padded, turning, 1), 0.0)
    point = lax.all_to_all(floored, "y", split_axis=2, concat_axis=0, tiled=True)
    group = point.shape[0]
    part_rows = point.shape[2]
    group_ids = (z_pos * group + jnp.arange(group)).astype(jnp.float32)
    radian_freq, wavenum, courant, turn_rate, band_spread = band_table(group_ids)
    scaled = point * (band_spread * dtheta)[:, None, None, None]
    sums = jnp.stack(
        [
            jnp.sum(scaled, axis=(0, 1)),
            jnp.sum(scaled / radian_freq[:, None, None, None], axis=(0, 1)),
            jnp.sum(scaled / jnp.sqrt(wavenum)[:, None, None, None], axis=(0, 1)),
        ]
    )
    lower, upper = z_halo(point, z_count)
    step = z_count // 2
    while step >= 1:
        sums = sums + lax.ppermute(sums, "z", [(i, i ^ step) for i in range(z_count)])
        step //= 2
    energy_sum, first_sum, root_sum = sums[0], sums[1], sums[2]
    energy = energy_sum + EPSILON
    ext = jnp.concatenate([lower, point, upper], axis=0)
    center, plus, minus = ext[1:-1], jnp.roll(ext[2:], -1, axis=1), jnp.roll(ext[:-2], 3, axis=1)
    cubic = center * center * (plus + minus) - 2.0 * center * plus * minus
    extra = (
        -2.0 * cubic[1:-1] + jnp.roll(cubic[:-2], 1, axis=1) + jnp.roll(cubic[2:], -3, axis=1)
    ) * (QUAD_COEF / (energy * energy))
    row_start = y_pos * part_rows
    wind_block = lax.dynamic_slice_in_dim(wind_speed, row_start, part_rows, axis=0)
    wind_angle = lax.dynamic_slice_in_dim(wind_dir, row_start, part_rows, axis=0)
    wet_block = lax.dynamic_slice_in_dim(wet_mask, row_start, part_rows, axis=0)
    cosine = jnp.cos(angles[:, None, None] - wind_angle[None])
    updated = (
        sources(
            point,
            energy_sum,
            first_sum,
            root_sum,
            radian_freq[:, None, None, None],
            wavenum[:, None, None, None],
            cosine,
            wind_block,
        )
        + extra
    ) * wet_block
    by_quarter = lax.all_to_all(updated, "y", split_axis=0, concat_axis=0, tiled=True)
    return jnp.transpose(by_quarter, (1, 0, 2, 3)).reshape(1, dir_count, row_count, col_count)


def solution(mesh):
    geo_count = mesh.shape["geo"]
    spec_count = mesh.shape["spec"]
    local = jax.sharding.Mesh(
        mesh.devices.reshape(geo_count, spec_count // Y_GROUP, Y_GROUP), ("geo", "z", "y")
    )
    spec = ("z", "y")
    placed = (
        P(spec, None, "geo", None),
        P("geo", None),
        P("geo", None),
        P("geo"),
        P("geo", None),
        P("geo", None),
        P("geo", None),
        P("geo", None),
    )
    return jax.shard_map(
        shards, mesh=local, in_specs=placed, out_specs=P(spec, None, "geo", None), check_vma=False
    )
```
